32 devices in a mesh: shard: 4 (over z), ctx: 2 (over core), tp: 4 (over y, x).
Axes of the slice: x: 2, y: 2, z: 4, core: 2. Of those that a mesh axis runs over, the one named last changes fastest.
Arguments:
- tokens: bfloat16 [8, 2048, 768], P('shard', 'ctx'), may hold values from -6 to 6
- segment_ids: int32 [8, 2048], P('shard', 'ctx'), may hold values from 0 to 34, as said below
- offsets: int32 [8, 2048], P('shard', 'ctx'), may hold values from 0 to 799, as said below
- qkv_weight: bfloat16 [768, 3, 768], P(('shard', 'ctx'), None, 'tp'), may hold values from -0.3125 to 0.3125
- out_weight: bfloat16 [768, 768], P(('shard', 'ctx'), 'tp'), may hold values from -0.875 to 0.875
- ffn_weight: bfloat16 [768, 2, 3072], P(('shard', 'ctx'), None, 'tp'), may hold values from -0.21875 to 0.21875
- qkv_bias: float32 [3, 768], P(None, 'tp'), may hold values from -3 to 3
- ffn_bias: float32 [3072], P('tp'), may hold values from -3 to 3
- norm_gain: float32 [2, 768], replicated, may hold values from 0.5 to 1.5
- shift_params: float32 [4, 768], replicated, may hold values from -3 to 3
- out_grad: bfloat16 [8, 2048, 768], P('shard', 'ctx'), may hold values from -6 to 6
Outputs:
- outputs: bfloat16 [8, 2048, 768], P('shard', 'ctx')
- grad_tokens: bfloat16 [8, 2048, 768], P('shard', 'ctx')
- grad_qkv_weight: float32 [768, 3, 768], P(('shard', 'ctx'), None, 'tp')
- grad_out_weight: float32 [768, 768], P(('shard', 'ctx'), 'tp')
- grad_ffn_weight: float32 [768, 2, 3072], P(('shard', 'ctx'), None, 'tp')
- grad_qkv_bias: float32 [3, 768], P(None, 'tp')
- grad_ffn_bias: float32 [3072], P('tp')
- grad_norm_gain: float32 [2, 768], replicated
- grad_shift_params: float32 [4, 768], replicated
The draws below stay inside these ranges and needn't reach their ends.
Inputs may be any that keep to these rules, and one draw needn't show every extreme that they name: `segment_ids`: segment numbers start at 0 in each sequence and rise by one where a new document begins. offsets are 0 at a document's first token and rise by one along it; a document has at most 800 tokens, and every document but a sequence's last has at least 60.
All inputs are finite; a program needn't handle non-finite values.
Results may differ from the reference program's by a relative error of at most 0.017.
The reference program's roundings to bfloat16 on the way count: a program that leaves them out, or rounds other values in their place, can miss the bound.
Values may be sent and summed in bfloat16 or wider, within the bound.
No kernel may reach another device: no remote copies, remote signals or barrier semaphores. Data moves between devices by JAX's collectives and lax.ppermute only.
A program may use at most 192 MiB of HBM per device.

```python
import jax
import jax.numpy as jnp
from jax import lax

D = 768
HEADS = 12
HEAD = 64
FF = 3072
SEQ = 2048
DOC_LEAST = 60
DOC_MOST = 800
SEQS = 8


def document_layout(key):
    base_key = jax.random.fold_in(key, 11)
    doc_count = SEQ // DOC_LEAST + 1
    lengths = jax.random.randint(jax.random.fold_in(base_key, 1), (SEQS, doc_count), DOC_LEAST, DOC_MOST + 1)
    longest = jax.random.randint(jax.random.fold_in(base_key, 2), (), 0, SEQS)
    shortest = (longest + 1) % SEQS
    row_index = jnp.arange(SEQS)[:, None]
    col_index = jnp.arange(doc_count)[None, :]
    lengths = jnp.where((row_index == longest) & (col_index == 0), DOC_MOST, lengths)
    lengths = jnp.where(row_index == shortest, DOC_LEAST, lengths)
    doc_ends = jnp.cumsum(lengths, axis=1)
    places = jnp.arange(SEQ)
    segment = jnp.sum((doc_ends[:, None, :] <= places[None, :, None]).astype(jnp.int32), axis=2)
    doc_starts = doc_ends - lengths
    doc_begin = jnp.take_along_axis(doc_starts, segment, axis=1)
    return (segment.astype(jnp.int32), (places[None, :] - doc_begin).astype(jnp.int32))


def draw_segment_ids(key, part):
    return document_layout(key)[0]


def draw_offsets(key, part):
    return document_layout(key)[1]


def raised(array, stream_key, source, target, blocks, factor):
    def block_of(position):
        return (jnp.arange(array.shape[position]) // (array.shape[position] // blocks)).reshape((-1,) + (1,) * (array.ndim - 1 - position))

    near = jax.random.permutation(stream_key, blocks)[block_of(target)]
    second = (block_of(target) + blocks // 2) % blocks
    return jnp.where((block_of(source) == near) | (block_of(source) == second), factor * array, array)


def steps_of(key, dims, split, low, high):
    loudness, own = 1.0, jax.random.fold_in(key, 6)
    for axis_at, blocks in split:
        heights = jnp.exp(jax.random.uniform(jax.random.fold_in(own, axis_at), (blocks,), jnp.float32, low / len(split), high / len(split)))
        loudness = loudness * jnp.repeat(heights, dims[axis_at] // blocks).reshape([-1 if axis == axis_at else 1 for axis in range(len(dims))])
    return loudness


def normal_values(stream_key, extent, deviation, reach, cuts=(), kind=jnp.bfloat16):
    result = deviation * jax.random.normal(stream_key, extent, jnp.float32)
    if cuts:
        result = result * steps_of(stream_key, extent, cuts, -0.22, 0.18)
    return jnp.clip(result, -reach, reach).astype(kind)


def gaussian_with(own_key, shape, scale, bound, shards, heavy, held_as=jnp.bfloat16):
    array = scale * jax.random.normal(own_key, shape, jnp.float32)
    if shards:
        array = array * steps_of(own_key, shape, shards, -0.22, 0.18)
    return jnp.clip(raised(array, jax.random.fold_in(own_key, 3), *heavy), -bound, bound).astype(held_as)


def setup_inputs(seed: int = 0) -> dict:
    seeds = jax.random.split(jax.random.key(seed), 12)
    return {
        "tokens": gaussian_with(seeds[0], (SEQS, SEQ, D), 1.0, 6.0, ((0, 4), (1, 2)), (0, 2, 4, 2.0)),
        "segment_ids": draw_segment_ids(jax.random.fold_in(seeds[11], 71), 0),
        "offsets": draw_offsets(jax.random.fold_in(seeds[11], 71), 0),
        "qkv_weight": normal_values(seeds[3], (D, 3, D), (D // 2) ** -0.5, 0.3125, ((0, 8), (2, 4))),
        "out_weight": normal_values(seeds[4], (D, D), (D // 16) ** -0.5, 0.875, ((0, 8), (1, 4))),
        "ffn_weight": normal_values(seeds[5], (D, 2, FF), D ** -0.5, 0.21875, ((0, 8), (2, 4))),
        "qkv_bias": normal_values(seeds[6], (3, D), 0.5, 3.0, ((1, 4),), jnp.float32),
        "ffn_bias": normal_values(seeds[7], (FF,), 0.5, 3.0, ((0, 4),), jnp.float32),
        "norm_gain": jnp.clip(1.0 + 0.1 * jax.random.normal(seeds[8], (2, D), jnp.float32), 0.5, 1.5),
        "shift_params": normal_values(seeds[9], (4, D), 0.5, 3.0, (), jnp.float32),
        "out_grad": gaussian_with(seeds[10], (SEQS, SEQ, D), 1.0, 6.0, ((0, 4), (1, 2)), (0, 2, 4, 2.0)),
    }


HIGHEST = lax.Precision.HIGHEST
EPSILON = 1e-12

@jax.custom_vjp
def low(v):
    return lax.optimization_barrier(v.astype(jnp.bfloat16)).astype(jnp.float32)

@jax.custom_vjp
def low_back(v):
    return v

def low_keep(v):
    return (low(v), None)

def low_pass(kept, grad):
    return (grad,)

def back_keep(v):
    return (v, None)

def back_low(kept, grad):
    return (low(grad),)
low.defvjp(low_keep, low_pass)
low_back.defvjp(back_keep, back_low)

def rotate_pairs(values, offsets, direction):
    half_size = values.shape[-1] // 2
    frequency = 10000.0 ** (-2.0 * jnp.arange(half_size, dtype=jnp.float32) / values.shape[-1])
    angles = offsets.astype(jnp.float32)[:, None] * frequency[None, :]
    cosine = jnp.cos(angles)[:, None, :]
    sine_part = direction * jnp.sin(angles)[:, None, :]
    paired = values.reshape(values.shape[:-1] + (half_size, 2))
    even_part = paired[..., 0]
    odd_part = paired[..., 1]
    turned = jnp.stack([even_part * cosine - odd_part * sine_part, even_part * sine_part + odd_part * cosine], axis=-1)
    return turned.reshape(values.shape)

def layer_norm(rows_in, gain_row, shift_row):
    centre = rows_in - lax.optimization_barrier(jnp.mean(rows_in, axis=-1, keepdims=True))
    spread = lax.optimization_barrier(jnp.mean(centre * centre, axis=-1, keepdims=True))
    return centre * lax.rsqrt(spread + EPSILON) * gain_row + shift_row

def one_sequence(inputs, segment, offsets, qkv_weight, out_weight, ffn_weight, qkv_bias, ffn_bias, norm_gain, shift_params):
    length = inputs.shape[0]
    projected = jnp.einsum('sd,dke->kse', inputs, qkv_weight, precision=HIGHEST) + qkv_bias[:, None, :]
    projected = low_back(projected)
    per_head = projected.reshape(3, length, HEADS, HEAD)
    queries = low(rotate_pairs(per_head[0], offsets, 1.0))
    keys = low(rotate_pairs(per_head[1], offsets, 1.0))
    values = low(per_head[2])
    scores = jnp.einsum('shd,thd->hst', queries, keys, precision=HIGHEST) * HEAD ** (-0.5)
    scores = low_back(scores)
    same_doc = (segment[:, None] == segment[None, :])[None]
    scores = jnp.where(same_doc, scores, -1e+30)
    probs = jax.nn.softmax(scores, axis=-1)
    context = jnp.einsum('hst,thd->shd', low(probs), values, precision=HIGHEST).reshape(length, HEADS * HEAD)
    context = low(low_back(context))
    attended = low_back(jnp.einsum('se,de->sd', context, out_weight, precision=HIGHEST))
    normed = layer_norm(inputs + attended + shift_params[2], norm_gain[0], shift_params[0])
    hidden_in = jnp.dot(low(normed), ffn_weight[:, 0, :], precision=HIGHEST) + ffn_bias
    hidden_in = low_back(hidden_in)
    activated = low(jax.nn.gelu(hidden_in, approximate=False))
    returned = low_back(jnp.einsum('sf,df->sd', activated, ffn_weight[:, 1, :], precision=HIGHEST))
    return layer_norm(normed + returned + shift_params[3], norm_gain[1], shift_params[1])

def reference(tokens, segment_ids, offsets, qkv_weight, out_weight, ffn_weight, qkv_bias, ffn_bias, norm_gain, shift_params, out_grad):
    parameters = tuple((parameter.astype(jnp.float32) for parameter in (qkv_weight, out_weight, ffn_weight, qkv_bias, ffn_bias, norm_gain, shift_params)))

    def forward(inputs, weights):

        def seq_step(one_item):
            return one_sequence(one_item[0], one_item[1], one_item[2], *weights)
        return lax.map(jax.checkpoint(seq_step), (inputs, segment_ids, offsets))
    outputs, pullback = jax.vjp(forward, tokens.astype(jnp.float32), parameters)
    grad_inputs, grad_params = pullback(out_grad.astype(jnp.float32))
    return (outputs.astype(jnp.bfloat16), grad_inputs.astype(jnp.bfloat16), grad_params[0], grad_params[1], grad_params[2], grad_params[3], grad_params[4], grad_params[5], grad_params[6])
```

```python
from functools import partial

import jax
import jax.numpy as jnp
import numpy as np
from jax import lax
from jax.experimental import pallas as pl
from jax.experimental.pallas import tpu as pltpu
from jax.sharding import PartitionSpec as P

HEAD = 64
WIDE = 256
BLOCK = 256
CHUNK = 256
EPSILON = 1e-12
F32 = jnp.float32
BF = jnp.bfloat16
NEG = -1e30


def swap_pairs(x):
    lane=lax.broadcasted_iota(jnp.int32,x.shape,1)
    n=x.shape[1]
    return jnp.where(lane%2==0, pltpu.roll(x,n-1,1), pltpu.roll(x,1,1))

def nt(a,b): return lax.dot_general(a,b,(((1,),(1,)),((),())),preferred_element_type=F32)
def nn(a,b): return lax.dot_general(a,b,(((1,),(0,)),((),())),preferred_element_type=F32)

def stack_heads(x, heads):
    lane=lax.broadcasted_iota(jnp.int32,x.shape,1)//HEAD
    return jnp.concatenate([jnp.where(lane==h,x,jnp.zeros_like(x)) for h in range(heads)],axis=0)

def fwd_kernel(heads, bounds, tok, w, bias, cos, sin, segc, segr, q_o, k_o, v_o, ctx_o, lse_o, o32_o, s_sc, m_sc, l_sc, qc_sc, vm_sc):
    i=pl.program_id(0)
    length=tok.shape[0]
    rows=heads*BLOCK
    @pl.when(i==0)
    def _():
        def step(r,_):
            sl=pl.ds(pl.multiple_of(r*BLOCK,BLOCK),BLOCK)
            c=cos[sl,:]; s=sin[sl,:]
            c=jnp.concatenate([c,c],axis=1); s=jnp.concatenate([s,s],axis=1)
            x=tok[sl,:]
            p=nn(x,w[:,0:WIDE])+bias[0:1,:]
            q_o[sl,:]=((p*c+swap_pairs(p)*s).astype(BF).astype(F32)*(HEAD**-0.5)).astype(BF)
            p=nn(x,w[:,WIDE:2*WIDE])+bias[1:2,:]
            k_o[sl,:]=(p*c+swap_pairs(p)*s).astype(BF)
            p=(nn(x,w[:,2*WIDE:3*WIDE])+bias[2:3,:]).astype(BF)
            v_o[sl,:]=p
            lane=lax.broadcasted_iota(jnp.int32,p.shape,1)//HEAD
            for h in range(heads):
                vm_sc[h,sl,:]=jnp.where(lane==h,p,jnp.zeros_like(p))
            return 0
        lax.fori_loop(0,length//BLOCK,step,0)
    start=bounds[0,i]; count=bounds[1,i]
    q=q_o[pl.ds(pl.multiple_of(i*BLOCK,BLOCK),BLOCK),:]
    qc_sc[...]=stack_heads(q,heads)
    seg_q=segc[...]
    m_sc[...]=jnp.full(m_sc.shape,NEG,F32)
    l_sc[...]=jnp.zeros(l_sc.shape,F32)
    def at(j): return pl.ds(pl.multiple_of(start+j*CHUNK,128),CHUNK)
    def pass1(j,_):
        s=nt(qc_sc[...],k_o[at(j),:])
        keep=seg_q==segr[0:1,at(j)]
        for h in range(heads):
            sh=jnp.where(keep,s[h*BLOCK:(h+1)*BLOCK,:],NEG)
            s_sc[j,h*BLOCK:(h+1)*BLOCK,:]=sh
            m_sc[h*BLOCK:(h+1)*BLOCK,:]=jnp.maximum(m_sc[h*BLOCK:(h+1)*BLOCK,:],jnp.maximum(sh[:,:128],sh[:,128:]))
        return 0
    lax.fori_loop(0,count,pass1,0)
    m_sc[...]=jnp.broadcast_to(jnp.max(m_sc[...],axis=1,keepdims=True),m_sc.shape)
    def pass2(j,_):
        for h in range(heads):
            hs=slice(h*BLOCK,(h+1)*BLOCK)
            m=m_sc[hs,:]
            e=jnp.exp(s_sc[j,hs,:]-jnp.concatenate([m,m],axis=1))
            s_sc[j,hs,:]=e
            l_sc[hs,:]+=e[:,:128]+e[:,128:]
        return 0
    lax.fori_loop(0,count,pass2,0)
    total=jnp.sum(l_sc[...],axis=1,keepdims=True)
    lse=m_sc[:,0:1]+jnp.log(total)
    l_sc[...]=jnp.broadcast_to(1.0/total,l_sc.shape)
    lane=lax.broadcasted_iota(jnp.int32,(BLOCK,128),1)
    tile=jnp.zeros((BLOCK,128),F32)
    for h in range(heads):
        tile=jnp.where(lane==h,lse[h*BLOCK:(h+1)*BLOCK,:],tile)
    lse_o[...]=tile.T[0:8,:]
    o32_o[...]=jnp.zeros(o32_o.shape,F32)
    def pass3(j,_):
        ps=[];vs=[]
        for h in range(heads):
            hs=slice(h*BLOCK,(h+1)*BLOCK)
            inv=l_sc[hs,:]
            ps.append((s_sc[j,hs,:]*jnp.concatenate([inv,inv],axis=1)).astype(BF))
            vs.append(vm_sc[h,at(j),:])
        o32_o[...]+=nn(jnp.concatenate(ps,axis=1),jnp.concatenate(vs,axis=0))
        return 0
    lax.fori_loop(0,count,pass3,0)
    ctx_o[...]=o32_o[:,:heads*HEAD].astype(BF)

def attention_forward(bounds,tok,w,bias,cos,sin,segc,segr,heads):
    length,width=tok.shape
    nq=length//BLOCK; nch=length//CHUNK
    full=lambda shape: pl.BlockSpec(shape,lambda i:(0,)*len(shape),pipeline_mode=pl.Buffered(1))
    return pl.pallas_call(
        partial(fwd_kernel,heads),
        grid=(nq,),
        in_specs=[pl.BlockSpec(memory_space=pltpu.SMEM),full((length,width)),full(w.shape),full(bias.shape),full(cos.shape),full(sin.shape),
                  pl.BlockSpec((BLOCK,1),lambda i:(i,0)),full(segr.shape)],
        out_specs=[full((length,WIDE)),full((length,WIDE)),full((length,WIDE)),
                   pl.BlockSpec((BLOCK,heads*HEAD),lambda i:(i,0)),pl.BlockSpec((8,BLOCK),lambda i:(0,i))],
        out_shape=[jax.ShapeDtypeStruct((length,WIDE),BF)]*3+[jax.ShapeDtypeStruct((length,heads*HEAD),BF),jax.ShapeDtypeStruct((8,length),F32)],
        scratch_shapes=[pltpu.VMEM((BLOCK,WIDE),F32),pltpu.VMEM((nch,heads*BLOCK,CHUNK),F32),pltpu.VMEM((heads*BLOCK,128),F32),pltpu.VMEM((heads*BLOCK,128),F32),
                        pltpu.VMEM((heads*BLOCK,WIDE),BF),pltpu.VMEM((heads,length,WIDE),BF)],
        compiler_params=pltpu.CompilerParams(dimension_semantics=("arbitrary",),vmem_limit_bytes=56*1024*1024),
        name="attention_forward",
    )(bounds,tok,w,bias,cos,sin,segc,segr)

def bwd_kernel(heads, bounds, q, k, kt, v, do, lse, segc, segr, cos, sin, g_o, gb_o, dk_sc, dv_sc, qc_sc, dc_sc, dq_sc, p_sc, dp_sc, dl_sc):
    i=pl.program_id(0)
    length=k.shape[0]
    @pl.when(i==0)
    def _():
        dk_sc[...]=jnp.zeros(dk_sc.shape,F32)
        dv_sc[...]=jnp.zeros(dv_sc.shape,F32)
        gb_o[...]=jnp.zeros(gb_o.shape,F32)
    start=bounds[0,i]; count=bounds[1,i]
    qc_sc[...]=stack_heads(q[...],heads)
    d=do[...]
    dz=jnp.concatenate([d,jnp.zeros((BLOCK,WIDE-d.shape[1]),BF)],axis=1)
    dc_sc[...]=stack_heads(dz,heads)
    dq_sc[...]=jnp.zeros(dq_sc.shape,F32)
    seg_q=segr[0:1,pl.ds(pl.multiple_of(i*BLOCK,BLOCK),BLOCK)]
    dl_sc[...]=jnp.zeros(dl_sc.shape,F32)
    def at(j): return pl.ds(pl.multiple_of(start+j*CHUNK,128),CHUNK)
    def pass1(j,_):
        s=nt(k[at(j),:],qc_sc[...])
        dp=nt(v[at(j),:],dc_sc[...])
        keep=segc[at(j),:]==seg_q
        for h in range(heads):
            hs=slice(h*BLOCK,(h+1)*BLOCK)
            p=jnp.exp(jnp.where(keep,s[:,hs],NEG)-lse[h:h+1,:])
            p_sc[j,:,hs]=p
            dp_sc[j,:,hs]=dp[:,hs]
            dl_sc[:,hs]+=jnp.sum((p*dp[:,hs]).reshape(CHUNK//8,8,BLOCK),axis=0)
        return 0
    lax.fori_loop(0,count,pass1,0)
    delta=jnp.sum(dl_sc[...],axis=0,keepdims=True)
    def pass2(j,_):
        ps=[];dss=[]
        for h in range(heads):
            hs=slice(h*BLOCK,(h+1)*BLOCK)
            p=p_sc[j,:,hs]
            ds=(p*(dp_sc[j,:,hs]-delta[:,hs])).astype(BF)
            ps.append(p.astype(BF)); dss.append(ds)
            dq_sc[h*HEAD:(h+1)*HEAD,:]+=nn(kt[h*HEAD:(h+1)*HEAD,at(j)],ds)
        dv_sc[at(j),:]+=nn(jnp.concatenate(ps,axis=1),dc_sc[...])
        dk_sc[at(j),:]+=nn(jnp.concatenate(dss,axis=1),qc_sc[...])
        return 0
    lax.fori_loop(0,count,pass2,0)
    def turn(x,sl):
        c=cos[sl,:]; s=sin[sl,:]
        c=jnp.concatenate([c,c],axis=1); s=jnp.concatenate([s,s],axis=1)
        return (x*c-swap_pairs(x)*s).astype(BF)
    own=pl.ds(pl.multiple_of(i*BLOCK,BLOCK),BLOCK)
    dq=turn(dq_sc[...].T*(HEAD**-0.5),own)
    g_o[own,0:WIDE]=dq
    gb_o[0:1,0:WIDE]+=jnp.sum(dq.astype(F32),axis=0,keepdims=True)
    @pl.when(i==pl.num_programs(0)-1)
    def _():
        def fin(r,_):
            sl=pl.ds(pl.multiple_of(r*BLOCK,BLOCK),BLOCK)
            dk=turn(dk_sc[sl,:],sl)
            g_o[sl,WIDE:2*WIDE]=dk
            gb_o[0:1,WIDE:2*WIDE]+=jnp.sum(dk.astype(F32),axis=0,keepdims=True)
            dv=dv_sc[sl,:].astype(BF)
            g_o[sl,2*WIDE:]=dv
            gb_o[0:1,2*WIDE:]+=jnp.sum(dv.astype(F32),axis=0,keepdims=True)
            return 0
        lax.fori_loop(0,length//BLOCK,fin,0)

def attention_backward(bounds,q,k,kt,v,do,lse,segc,segr,cos,sin,heads):
    length=k.shape[0]; nq=length//BLOCK
    full=lambda shape: pl.BlockSpec(shape,lambda i:(0,)*len(shape),pipeline_mode=pl.Buffered(1))
    return pl.pallas_call(
        partial(bwd_kernel,heads),
        grid=(nq,),
        in_specs=[pl.BlockSpec(memory_space=pltpu.SMEM),pl.BlockSpec((BLOCK,WIDE),lambda i:(i,0)),full(k.shape),full(kt.shape),full(v.shape),
                  pl.BlockSpec((BLOCK,heads*HEAD),lambda i:(i,0)),pl.BlockSpec((8,BLOCK),lambda i:(0,i)),
                  full(segc.shape),full(segr.shape),full(cos.shape),full(sin.shape)],
        out_specs=[full((length,3*WIDE)),full((8,3*WIDE))],
        out_shape=[jax.ShapeDtypeStruct((length,3*WIDE),BF),jax.ShapeDtypeStruct((8,3*WIDE),F32)],
        scratch_shapes=[pltpu.VMEM((length,WIDE),F32),pltpu.VMEM((length,WIDE),F32),pltpu.VMEM((heads*BLOCK,WIDE),BF),pltpu.VMEM((heads*BLOCK,WIDE),BF),pltpu.VMEM((WIDE,BLOCK),F32)]+[pltpu.VMEM((length//CHUNK,CHUNK,heads*BLOCK),F32)]*2+[pltpu.VMEM((8,heads*BLOCK),F32)],
        compiler_params=pltpu.CompilerParams(dimension_semantics=("arbitrary",),vmem_limit_bytes=56*1024*1024),
        name="attention_backward",
    )(bounds,q,k,kt,v,do,lse,segc,segr,cos,sin)


def rotation_tables(offsets):
    lane = np.arange(128)
    frequency = (10000.0 ** (-2.0 * (lane % HEAD // 2) / HEAD)).astype(np.float32)
    angles = offsets.astype(F32)[:, None] * frequency[None, :]
    sign = np.where(lane % 2 == 0, -1.0, 1.0).astype(np.float32)
    return jnp.cos(angles), jnp.sin(angles) * sign


def key_bounds(segment):
    length = segment.shape[0]
    first, last = segment[::BLOCK], segment[BLOCK - 1 :: BLOCK]
    low = jnp.sum(segment[None, :] < first[:, None], axis=1)
    high = jnp.sum(segment[None, :] <= last[:, None], axis=1)
    low = low // 128 * 128
    count = (high - low + CHUNK - 1) // CHUNK
    return jnp.stack([jnp.minimum(low, length - CHUNK * count), count]).astype(jnp.int32)


def swap_ctx(x):
    return lax.ppermute(x, "ctx", [(0, 1), (1, 0)])


def swap_tp(x, k):
    return lax.ppermute(x, "tp", [(i, i ^ k) for i in range(4)])


def swap_shard(x, k):
    return lax.ppermute(x, "shard", [(i, i ^ k) for i in range(4)])


def order_four(parts, index):
    a, b, c, d = parts
    odd, high = index % 2 == 1, index // 2 == 1
    a, b = jnp.where(odd, b, a), jnp.where(odd, a, b)
    c, d = jnp.where(odd, d, c), jnp.where(odd, c, d)
    return jnp.stack([jnp.where(high, c, a), jnp.where(high, d, b), jnp.where(high, a, c), jnp.where(high, b, d)])


def gather_shard(x):
    if lax.axis_size("shard") != 4:
        return lax.all_gather(x, "shard", axis=0)
    return order_four([x] + [swap_shard(x, k) for k in (1, 2, 3)], lax.axis_index("shard"))


def scatter_shard(x):
    if lax.axis_size("shard") != 4:
        return lax.psum_scatter(x, "shard", scatter_dimension=0)
    z = lax.axis_index("shard")
    total = lax.dynamic_index_in_dim(x, z, 0, keepdims=False)
    for k in (1, 2, 3):
        piece = lax.dynamic_index_in_dim(x, z ^ k, 0, keepdims=False).astype(BF)
        total = total + swap_shard(piece, k).astype(F32)
    return total


def sum_shard(x):
    if lax.axis_size("shard") != 4:
        return lax.psum(x, "shard")
    x = x + swap_shard(x, 1)
    return x + swap_shard(x, 2)


def gather_tp(x):
    half = x.shape[0] // 2
    one, two = swap_tp(x, 1), swap_tp(x, 2)
    three = jnp.concatenate([swap_tp(one[:half], 2), swap_tp(two[half:], 1)])
    return [x, one, two, three]


def scatter_tp(parts):
    own, one, two, three = parts
    half = own.shape[0] // 2
    low, high = three[:half].astype(BF), three[half:].astype(BF)
    low, high = swap_tp(low, 2), swap_tp(high, 1)
    one = jnp.concatenate([one[:half] + low.astype(F32), one[half:]]).astype(BF)
    two = jnp.concatenate([two[:half], two[half:] + high.astype(F32)]).astype(BF)
    return own + swap_tp(one, 1).astype(F32) + swap_tp(two, 2).astype(F32)


def exchange_tp(parts):
    return [parts[0]] + [swap_tp(parts[k], k) for k in (1, 2, 3)]


def three_rows(x):
    high = lax.reduce_precision(x, 8, 7)
    middle = lax.reduce_precision(x - high, 8, 7)
    return jnp.stack([high, middle, x - high - middle]).astype(BF)


def norm_parts(rows_in):
    centre = rows_in - jnp.mean(rows_in, axis=-1, keepdims=True)
    inverse_root = lax.rsqrt(jnp.mean(centre * centre, axis=-1, keepdims=True) + EPSILON)
    return (centre * inverse_root, inverse_root)


def norm_back(grad_in, scaled, inverse_root, gain_row):
    grad_scaled = grad_in * gain_row
    term_mean = jnp.mean(grad_scaled, axis=-1, keepdims=True)
    term_along = jnp.mean(grad_scaled * scaled, axis=-1, keepdims=True)
    return inverse_root * (grad_scaled - term_mean - scaled * term_along)


def contract_last(left, right):
    return lax.dot_general(left, right, (((1,), (1,)), ((), ())), preferred_element_type=F32)


def contract_first(left, right):
    return lax.dot_general(left, right, (((0,), (0,)), ((), ())), preferred_element_type=F32)


def body(tokens, segment_ids, offsets, qkv_weight, out_weight, ffn_weight, qkv_bias, ffn_bias, norm_gain, shift_params, out_grad):
    t, c = lax.axis_index("tp"), lax.axis_index("ctx")
    shards = lax.axis_size("shard")
    half_len, width = tokens.shape[1:]
    rows, _, part = qkv_weight.shape
    hidden = ffn_weight.shape[2]
    heads = part // HEAD
    length = 2 * half_len
    share = length // 4
    hh = hidden // 2
    first_core = c == 0

    def take(x, index):
        return lax.dynamic_index_in_dim(x, index, 0, keepdims=False)

    def by_core(own, other):
        return jnp.where(first_core, jnp.stack([own, other]), jnp.stack([other, own]))

    def whole(x):
        return by_core(take(x, c), swap_ctx(take(x, 1 - c))).reshape((length,) + x.shape[2:])

    qkv_rows = gather_shard(qkv_weight.reshape(rows, 3 * part))
    tok = whole(tokens)
    marks = whole(jnp.stack([segment_ids, offsets], axis=-1))
    segment, places = marks[:, 0], marks[:, 1]
    grad_block = out_grad.reshape(2, 2, share, width)
    grad_own = take(take(grad_block, c), t % 2)
    grad_far = swap_ctx(take(take(grad_block, 1 - c), t % 2))
    grad_top = jnp.where(t // 2 == c, grad_own, grad_far).astype(F32)

    rest = jnp.concatenate([ffn_weight.reshape(rows, 2 * hidden), out_weight], axis=1)
    rest_rows = gather_shard(rest)

    def rows_of(x):
        return by_core(x, swap_ctx(x)).transpose(1, 0, 2, 3).reshape(width, x.shape[-1])

    qkv_own = rows_of(qkv_rows).reshape(width, 3, part)
    qkv_pad = jnp.pad(qkv_own, ((0, 0), (0, 0), (0, WIDE - part))).reshape(width, 3 * WIDE)
    bias_pad = jnp.pad(qkv_bias, ((0, 0), (0, WIDE - part)))

    rest_own = rows_of(rest_rows)
    ups, downs = rest_own[:, :hidden], rest_own[:, hidden : 2 * hidden]

    def half_of(x, index):
        return lax.dynamic_slice_in_dim(x, index * hh, hh, x.ndim - 1)

    def pack(core):
        feed = jnp.concatenate([half_of(ups, core), half_of(downs, core)], axis=1)
        out_part = lax.dynamic_index_in_dim(rest_own.reshape(shards, 2, rows, -1), core, 1, keepdims=False)
        out_part = out_part[:, :, 2 * hidden :].reshape(-1, hidden)
        bias = three_rows(half_of(ffn_bias, core)).reshape(-1)
        bias = jnp.pad(bias, (0, 16 * hidden - bias.shape[0])).reshape(16, hidden)
        return jnp.concatenate([feed, out_part, bias], axis=0)

    mine = jnp.stack(gather_tp(pack(c)))
    far = jnp.concatenate([pack(1 - c)[None], swap_ctx(mine[1:])])
    packs = [mine, far]
    n_out = shards * rows * part // hidden

    def join(cut):
        return jnp.concatenate([cut(p[k]) for p in packs for k in range(4)], axis=-1)

    up_all = join(lambda p: p[:width, :hh])
    down_all = join(lambda p: p[:width, hh:])

    def bias_of(p):
        three = p[width + n_out :].reshape(-1)[: 3 * hh].reshape(3, hh).astype(F32)
        return three[0] + three[1] + three[2]

    bias_all = join(bias_of)

    def out_of(k):
        own, other = (p[k][width : width + n_out].reshape(shards, rows, part) for p in packs)
        return by_core(own, other).transpose(1, 0, 2, 3).reshape(width, part)

    out_all = jnp.concatenate([out_of(k) for k in range(4)], axis=1)

    cosine, sine = rotation_tables(places)
    bounds = key_bounds(segment)
    seg_column = segment[:, None]
    seg_row = jnp.broadcast_to(segment[None, :], (8, length))
    q, k_rows, v_rows, context, log_total = attention_forward(
        bounds, tok, qkv_pad, bias_pad, cosine, sine, seg_column, seg_row, heads
    )

    blocks = context.reshape(4, share, part)
    context_all = jnp.concatenate(exchange_tp([take(blocks, t ^ k) for k in range(4)]), axis=1)
    tok_block = take(tok.reshape(4, share, width), t)
    attended = contract_last(context_all, out_all)
    first_scaled, first_root = norm_parts(tok_block.astype(F32) + attended + shift_params[2])
    normed = first_scaled * norm_gain[0] + shift_params[0]
    normed_b = normed.astype(BF)
    hidden_in = jnp.dot(normed_b, up_all, preferred_element_type=F32) + bias_all
    activated, gelu_pull = jax.vjp(partial(jax.nn.gelu, approximate=False), hidden_in)
    activated_b = activated.astype(BF)
    returned = contract_last(activated_b, down_all)
    second_scaled, second_root = norm_parts(normed + returned + shift_params[3])
    layer_out = (second_scaled * norm_gain[1] + shift_params[1]).astype(BF)

    def spread(block):
        full = order_four(gather_tp(block), t).reshape(2, half_len, width)
        own, other = take(full, c), swap_ctx(take(full, 1 - c))
        return by_core(own, other)

    outputs = spread(layer_out)

    grad_second = norm_back(grad_top, second_scaled, second_root, norm_gain[1])
    grad_second_b = grad_second.astype(BF)
    grad_act = jnp.dot(grad_second_b, down_all, preferred_element_type=F32)
    grad_hidden = gelu_pull(grad_act)[0].astype(BF)
    grad_normed = grad_second + contract_last(grad_hidden, up_all)
    grad_first = norm_back(grad_normed, first_scaled, first_root, norm_gain[0])
    grad_first_b = grad_first.astype(BF)
    grad_context = jnp.dot(grad_first_b, out_all, preferred_element_type=F32).astype(BF)
    grad_parts = exchange_tp([grad_context[:, k * part : (k + 1) * part] for k in range(4)])
    grad_heads = order_four(grad_parts, t).reshape(length, part)

    grad_proj, bias_sums = attention_backward(
        bounds, q, k_rows, k_rows.T, v_rows, grad_heads, log_total, seg_column, seg_row, cosine, sine, heads
    )

    branch = contract_last(grad_proj, qkv_pad).reshape(4, share, width)
    grad_branch = scatter_tp([take(branch, t ^ k) for k in range(4)])
    grad_tokens = spread((grad_first + grad_branch).astype(BF))

    grad_up = contract_first(normed_b, grad_hidden)
    grad_down = contract_first(grad_second_b, activated_b)
    grad_out = contract_first(grad_first_b, context_all)
    near, apart = slice(0, 4 * hh), slice(4 * hh, 8 * hh)
    got = swap_ctx(jnp.stack([grad_up[:, apart], grad_down[:, apart]]).astype(BF)).astype(F32)
    grad_up, grad_down = grad_up[:, near] + got[0], grad_down[:, near] + got[1]
    grad_out = grad_out.reshape(shards, 2, rows, width).transpose(1, 0, 2, 3)
    grad_out = take(grad_out, c) + swap_ctx(take(grad_out, 1 - c).astype(BF)).astype(F32)

    def bundle(k):
        at = slice(k * hh, (k + 1) * hh)
        feed = jnp.concatenate([grad_up[:, at], grad_down[:, at]], axis=1).reshape(shards, 2 * rows, hidden)
        out_part = grad_out[:, :, k * part : (k + 1) * part].reshape(shards, rows * part // hidden, hidden)
        return jnp.concatenate([feed, out_part], axis=1)

    summed = scatter_shard(scatter_tp([bundle(k) for k in range(4)]))
    grad_out_weight = summed[2 * rows :].reshape(rows, part)
    feed = summed[: 2 * rows].reshape(2, rows, hidden)
    feed = by_core(take(feed, c), swap_ctx(take(feed, 1 - c))).reshape(2, rows, 2, hh)
    grad_ffn_weight = feed.transpose(1, 2, 0, 3).reshape(rows, 2, hidden)

    grad_qkv = contract_first(tok, grad_proj).reshape(shards, 2, rows, 3, WIDE)[..., :part]
    grad_qkv = grad_qkv.transpose(1, 0, 2, 3, 4).reshape(2, shards, rows, 3 * part)
    grad_qkv = take(grad_qkv, c) + swap_ctx(take(grad_qkv, 1 - c).astype(BF)).astype(F32)
    grad_qkv_weight = scatter_shard(grad_qkv).reshape(rows, 3, part)

    sums = jnp.sum(grad_hidden.astype(F32), axis=0).reshape(2, 4, hh)
    sums = by_core(sums[0], sums[1])
    sums = order_four([sums[:, k] for k in range(4)], t).reshape(-1)
    small = jnp.concatenate(
        [sums]
        + [
            jnp.sum(x, axis=0)
            for x in (
                grad_normed * first_scaled,
                grad_top * second_scaled,
                grad_normed,
                grad_top,
                grad_first,
                grad_second,
            )
        ]
    ).reshape(-1, 128)
    for k in (1, 2):
        small = small + swap_tp(small, k)
    small = sum_shard(small + swap_ctx(small)).reshape(-1)
    grad_ffn_bias = lax.dynamic_slice_in_dim(small, t * hidden, hidden, 0)
    vectors = small[4 * hidden :].reshape(6, width)
    grad_qkv_bias = bias_sums[0].reshape(3, WIDE)[:, :part]
    grad_qkv_bias = sum_shard(grad_qkv_bias + swap_ctx(grad_qkv_bias))
    return (
        outputs,
        grad_tokens,
        grad_qkv_weight,
        grad_out_weight,
        grad_ffn_weight,
        grad_qkv_bias,
        grad_ffn_bias,
        vectors[:2],
        vectors[2:],
    )


def solution(mesh):
    return jax.shard_map(
        body,
        mesh=mesh,
        in_specs=(
            P("shard", "ctx", None),
            P("shard", "ctx"),
            P("shard", "ctx"),
            P(("shard", "ctx"), None, "tp"),
            P(("shard", "ctx"), "tp"),
            P(("shard", "ctx"), None, "tp"),
            P(None, "tp"),
            P("tp"),
            P(),
            P(),
            P("shard", "ctx", None),
        ),
        out_specs=(
            P("shard", "ctx", None),
            P("shard", "ctx", None),
            P(("shard", "ctx"), None, "tp"),
            P(("shard", "ctx"), "tp"),
            P(("shard", "ctx"), None, "tp"),
            P(None, "tp"),
            P("tp"),
            P(),
            P(),
        ),
        check_vma=False,
    )
```

```python
from functools import partial

import jax
import jax.numpy as jnp
import numpy as np
from jax import lax
from jax.experimental import pallas as pl
from jax.experimental.pallas import tpu as pltpu
from jax.sharding import PartitionSpec as P

HEAD = 64
WIDE = 256
BLOCK = 256
CHUNK = 256
EPSILON = 1e-12
F32 = jnp.float32
BF = jnp.bfloat16
NEG = -1e30


def swap_pairs(x):
    lane = lax.broadcasted_iota(jnp.int32, x.shape, 1)
    n = x.shape[1]
    return jnp.where(lane % 2 == 0, pltpu.roll(x, n - 1, 1), pltpu.roll(x, 1, 1))


def nt(a, b):
    return lax.dot_general(a, b, (((1,), (1,)), ((), ())), preferred_element_type=F32)


def nn(a, b):
    return lax.dot_general(a, b, (((1,), (0,)), ((), ())), preferred_element_type=F32)


def twice(x):
    return jnp.concatenate([x, x], axis=1)


def lanes_of_heads(x, heads):
    lane = lax.broadcasted_iota(jnp.int32, x.shape, 1) // HEAD
    return [jnp.where(lane == h, x, jnp.zeros_like(x)) for h in range(heads)]


def whole_block(shape, buffers=1):
    return pl.BlockSpec(shape, lambda *_: (0,) * len(shape), pipeline_mode=pl.Buffered(buffers))


def smem():
    return pl.BlockSpec(memory_space=pltpu.SMEM)


def params(mib):
    return pltpu.CompilerParams(dimension_semantics=("arbitrary",), vmem_limit_bytes=mib * 1024 * 1024)


def qkv_kernel(count, part, place, *refs):
    pieces = refs[:count]
    bias, own, other, cos, sin, q_o, k_o, v_o, kt_o, w_o = refs[count:]
    piece_rows = pieces[0].shape[0]
    pad = jnp.zeros((piece_rows, WIDE - part), BF)
    for n in range(count):
        sl = pl.ds(pl.multiple_of(place[n], 16), piece_rows)
        for m in range(3):
            w_o[sl, m * WIDE : (m + 1) * WIDE] = jnp.concatenate([pieces[n][:, m * part : (m + 1) * part], pad], axis=1)
    half_len = other.shape[0]

    def run(x, sl):
        c, s = twice(cos[sl, :]), twice(sin[sl, :])
        p = nn(x, w_o[:, 0:WIDE]) + bias[0:1, :]
        q_o[sl, :] = ((p * c + swap_pairs(p) * s).astype(BF).astype(F32) * (HEAD**-0.5)).astype(BF)
        p = nn(x, w_o[:, WIDE : 2 * WIDE]) + bias[1:2, :]
        k = (p * c + swap_pairs(p) * s).astype(BF)
        k_o[sl, :] = k
        kt_o[:, sl] = k.T
        v_o[sl, :] = (nn(x, w_o[:, 2 * WIDE : 3 * WIDE]) + bias[2:3, :]).astype(BF)

    def step(r, _):
        rows = pl.ds(pl.multiple_of(r * BLOCK, BLOCK), BLOCK)
        core = place[count]
        run(own[0, rows, :], pl.ds(pl.multiple_of(core * half_len + r * BLOCK, BLOCK), BLOCK))
        run(other[rows, :], pl.ds(pl.multiple_of((1 - core) * half_len + r * BLOCK, BLOCK), BLOCK))
        return 0

    lax.fori_loop(0, half_len // BLOCK, step, 0)


def project_qkv(place, pieces, bias, tokens, other, cos, sin, part):
    half_len, width = other.shape
    length, count = 2 * half_len, len(pieces)
    cost = pl.CostEstimate(flops=2 * length * width * 3 * WIDE, bytes_accessed=12 * 2**20, transcendentals=0)
    return pl.pallas_call(
        partial(qkv_kernel, count, part),
        grid_spec=pltpu.PrefetchScalarGridSpec(
            num_scalar_prefetch=1,
            grid=(1,),
            in_specs=[whole_block(p.shape) for p in pieces]
            + [whole_block(bias.shape), pl.BlockSpec((1, half_len, width), lambda i, s: (s[count], 0, 0))]
            + [whole_block(x.shape) for x in (other, cos, sin)],
            out_specs=[whole_block((length, WIDE))] * 3 + [whole_block((WIDE, length)), whole_block((width, 3 * WIDE))],
        ),
        out_shape=[jax.ShapeDtypeStruct((length, WIDE), BF)] * 3
        + [jax.ShapeDtypeStruct((WIDE, length), BF), jax.ShapeDtypeStruct((width, 3 * WIDE), BF)],
        compiler_params=params(32),
        cost_estimate=cost,
        name="project_qkv",
    )(place, *pieces, bias, tokens, other, cos, sin)


def forward_kernel(heads, place, q, k, v, segc, segr, ctx_o, lse_o, acc, s_sc, m_sc, l_sc, qc_sc):
    i = place[0] + pl.program_id(0)
    start, count = place[1 + 2 * i], place[2 + 2 * i]
    qc_sc[...] = jnp.concatenate(lanes_of_heads(q[...], heads), axis=0)
    seg_q = segc[...]
    m_sc[...] = jnp.full(m_sc.shape, NEG, F32)
    l_sc[...] = jnp.zeros(l_sc.shape, F32)

    def at(j):
        return pl.ds(pl.multiple_of(start + j * CHUNK, 128), CHUNK)

    def of(h):
        return slice(h * BLOCK, (h + 1) * BLOCK)

    def pass1(j, _):
        s = nt(qc_sc[...], k[at(j), :])
        keep = seg_q == segr[0:1, at(j)]
        for h in range(heads):
            sh = jnp.where(keep, s[of(h), :], NEG)
            s_sc[j, of(h), :] = sh
            m_sc[of(h), :] = jnp.maximum(m_sc[of(h), :], jnp.maximum(sh[:, :128], sh[:, 128:]))
        return 0

    lax.fori_loop(0, count, pass1, 0)
    m_sc[...] = jnp.broadcast_to(jnp.max(m_sc[...], axis=1, keepdims=True), m_sc.shape)

    def pass2(j, _):
        for h in range(heads):
            e = jnp.exp(s_sc[j, of(h), :] - twice(m_sc[of(h), :]))
            s_sc[j, of(h), :] = e
            l_sc[of(h), :] += e[:, :128] + e[:, 128:]
        return 0

    lax.fori_loop(0, count, pass2, 0)
    total = jnp.sum(l_sc[...], axis=1, keepdims=True)
    lse = m_sc[:, 0:1] + jnp.log(total)
    l_sc[...] = jnp.broadcast_to(1.0 / total, l_sc.shape)
    lane = lax.broadcasted_iota(jnp.int32, (BLOCK, 128), 1)
    tile = jnp.zeros((BLOCK, 128), F32)
    for h in range(heads):
        tile = jnp.where(lane == h, lse[of(h), :], tile)
    lse_o[...] = tile.T[0:8, :]
    acc[...] = jnp.zeros(acc.shape, F32)

    def pass3(j, _):
        ps = [(s_sc[j, of(h), :] * twice(l_sc[of(h), :])).astype(BF) for h in range(heads)]
        acc[...] += nn(jnp.concatenate(ps, axis=1), jnp.concatenate(lanes_of_heads(v[at(j), :], heads), axis=0))
        return 0

    lax.fori_loop(0, count, pass3, 0)
    ctx_o[...] = acc[:, : heads * HEAD].astype(BF)


def attention_forward(place, q, k, v, segc, segr, heads, share):
    length = q.shape[0]
    grid = share // BLOCK
    rows = lambda i, s: (s[0] + i, 0)
    flops = 4 * share * 1024 * heads * WIDE
    return pl.pallas_call(
        partial(forward_kernel, heads),
        grid_spec=pltpu.PrefetchScalarGridSpec(
            num_scalar_prefetch=1,
            grid=(grid,),
            in_specs=[
                pl.BlockSpec((BLOCK, WIDE), rows),
                whole_block(k.shape),
                whole_block(v.shape),
                pl.BlockSpec((BLOCK, 1), rows),
                whole_block(segr.shape),
            ],
            out_specs=[pl.BlockSpec((BLOCK, heads * HEAD), lambda i, s: (i, 0)), pl.BlockSpec((8, BLOCK), lambda i, s: (0, i))],
            scratch_shapes=[
                pltpu.VMEM((BLOCK, WIDE), F32),
                pltpu.VMEM((length // CHUNK, heads * BLOCK, CHUNK), F32),
                pltpu.VMEM((heads * BLOCK, 128), F32),
                pltpu.VMEM((heads * BLOCK, 128), F32),
                pltpu.VMEM((heads * BLOCK, WIDE), BF),
            ],
        ),
        out_shape=[jax.ShapeDtypeStruct((share, heads * HEAD), BF), jax.ShapeDtypeStruct((8, share), F32)],
        compiler_params=params(24),
        cost_estimate=pl.CostEstimate(flops=flops * 6, bytes_accessed=4 * 2**20, transcendentals=share * 1024 * heads),
        name="attention_forward",
    )(place, q, k, v, segc, segr)


def backward_kernel(heads, place, q, k, kt, v, do, lse, segc, segr, cos, sin, g_o, gb_o, dk_sc, dv_sc, qc_sc, dc_sc, dq_sc, p_sc, dp_sc, dl_sc):
    step_at = pl.program_id(0)
    i = step_at ^ place[0]
    length = k.shape[0]

    @pl.when(step_at == 0)
    def _():
        dk_sc[...] = jnp.zeros(dk_sc.shape, F32)
        dv_sc[...] = jnp.zeros(dv_sc.shape, F32)
        gb_o[...] = jnp.zeros(gb_o.shape, F32)

    start, count = place[1 + 2 * i], place[2 + 2 * i]
    qc_sc[...] = jnp.concatenate(lanes_of_heads(q[...], heads), axis=0)
    d = do[0]
    d = jnp.concatenate([d, jnp.zeros((BLOCK, WIDE - d.shape[1]), BF)], axis=1)
    dc_sc[...] = jnp.concatenate(lanes_of_heads(d, heads), axis=0)
    dq_sc[...] = jnp.zeros(dq_sc.shape, F32)
    own = pl.ds(pl.multiple_of(i * BLOCK, BLOCK), BLOCK)
    seg_q = segr[0:1, own]
    dl_sc[...] = jnp.zeros(dl_sc.shape, F32)

    def at(j):
        return pl.ds(pl.multiple_of(start + j * CHUNK, 128), CHUNK)

    def of(h):
        return slice(h * BLOCK, (h + 1) * BLOCK)

    def pass1(j, _):
        s = nt(k[at(j), :], qc_sc[...])
        dp = nt(v[at(j), :], dc_sc[...])
        keep = segc[at(j), :] == seg_q
        for h in range(heads):
            p = jnp.exp(jnp.where(keep, s[:, of(h)], NEG) - lse[h : h + 1, :])
            p_sc[j, :, of(h)] = p
            dp_sc[j, :, of(h)] = dp[:, of(h)]
            dl_sc[:, of(h)] += jnp.sum((p * dp[:, of(h)]).reshape(CHUNK // 8, 8, BLOCK), axis=0)
        return 0

    lax.fori_loop(0, count, pass1, 0)
    delta = jnp.sum(dl_sc[...], axis=0, keepdims=True)

    def pass2(j, _):
        ps, dss = [], []
        for h in range(heads):
            p = p_sc[j, :, of(h)]
            ds = (p * (dp_sc[j, :, of(h)] - delta[:, of(h)])).astype(BF)
            ps.append(p.astype(BF))
            dss.append(ds)
            dq_sc[h * HEAD : (h + 1) * HEAD, :] += nn(kt[h * HEAD : (h + 1) * HEAD, at(j)], ds)
        dv_sc[at(j), :] += nn(jnp.concatenate(ps, axis=1), dc_sc[...])
        dk_sc[at(j), :] += nn(jnp.concatenate(dss, axis=1), qc_sc[...])
        return 0

    lax.fori_loop(0, count, pass2, 0)

    def turn(x, sl):
        return (x * twice(cos[sl, :]) - swap_pairs(x) * twice(sin[sl, :])).astype(BF)

    def put(x, sl, m):
        g_o[sl, m * WIDE : (m + 1) * WIDE] = x
        gb_o[0:1, m * WIDE : (m + 1) * WIDE] += jnp.sum(x.astype(F32), axis=0, keepdims=True)

    put(turn(dq_sc[...].T * (HEAD**-0.5), own), own, 0)

    @pl.when(step_at == pl.num_programs(0) - 1)
    def _():
        def last(r, _):
            sl = pl.ds(pl.multiple_of(r * BLOCK, BLOCK), BLOCK)
            put(turn(dk_sc[sl, :], sl), sl, 1)
            put(dv_sc[sl, :].astype(BF), sl, 2)
            return 0

        lax.fori_loop(0, length // BLOCK, last, 0)


def attention_backward(place, q, k, kt, v, do, lse, segc, segr, cos, sin, heads):
    length = k.shape[0]
    steps, per = length // BLOCK, do.shape[1] // BLOCK
    flops = 10 * length * 1024 * heads * WIDE
    return pl.pallas_call(
        partial(backward_kernel, heads),
        grid_spec=pltpu.PrefetchScalarGridSpec(
            num_scalar_prefetch=1,
            grid=(steps,),
            in_specs=[
                pl.BlockSpec((BLOCK, WIDE), lambda i, s: (i ^ s[0], 0)),
                whole_block(k.shape),
                whole_block(kt.shape),
                whole_block(v.shape),
                pl.BlockSpec((1, BLOCK, heads * HEAD), lambda i, s: (i // per, i % per, 0)),
                pl.BlockSpec((8, BLOCK), lambda i, s: (0, i)),
                whole_block(segc.shape),
                whole_block(segr.shape),
                whole_block(cos.shape),
                whole_block(sin.shape),
            ],
            out_specs=[whole_block((length, 3 * WIDE)), whole_block((8, 3 * WIDE))],
            scratch_shapes=[pltpu.VMEM((length, WIDE), F32)] * 2
            + [pltpu.VMEM((heads * BLOCK, WIDE), BF)] * 2
            + [pltpu.VMEM((WIDE, BLOCK), F32)]
            + [pltpu.VMEM((length // CHUNK, CHUNK, heads * BLOCK), F32)] * 2
            + [pltpu.VMEM((8, heads * BLOCK), F32)],
        ),
        out_shape=[jax.ShapeDtypeStruct((length, 3 * WIDE), BF), jax.ShapeDtypeStruct((8, 3 * WIDE), F32)],
        compiler_params=params(44),
        cost_estimate=pl.CostEstimate(flops=flops * 4, bytes_accessed=16 * 2**20, transcendentals=length * 1024 * heads),
        name="attention_backward",
    )(place, q, k, kt, v, do, lse, segc, segr, cos, sin)


def fetches(place, pieces, w_feed, w_out, sems, per):
    out = []
    for n, (group, ref, lead) in enumerate(pieces):
        m = n % per
        src = ref if lead is None else ref.at[lead]
        rows = w_feed.shape[1] // per
        feed = w_feed.shape[2]
        sl = pl.ds(pl.multiple_of(place[m], 16), rows)
        a = pltpu.make_async_copy(src.at[0:rows, feed:], w_out.at[group, sl, :], sems.at[0, n])
        b = pltpu.make_async_copy(src.at[0:rows, 0:feed], w_feed.at[group, sl, :], sems.at[1, n])
        out.append((group, a, b))
    return out


def row_mean(x):
    return jnp.mean(x, axis=1, keepdims=True)


def gelu_parts(x):
    e = jnp.exp(x * x * -0.5)
    t = 1.0 / (1.0 + (0.3275911 * 0.7071067811865476) * jnp.abs(x))
    p = t * (0.254829592 + t * (-0.284496736 + t * (1.421413741 + t * (-1.453152027 + t * 1.061405429))))
    tail = 0.5 * p * e
    phi = jnp.where(x >= 0, 1.0 - tail, tail)
    return phi, phi + x * e * 0.3989422804014327


ROWS = 256


def feed_kernel(layout, per, place, *refs):
    arrays = refs[: layout[0]]
    (c0, c1, c2, c3, tokb, gtop, vec, bias, out_o, gs_o, gsb_o, fs_o, nb_o, act_o, gp_o, root_o, sum_o, w_feed, w_out, acc, normed, sems) = refs[layout[0] :]
    pieces = [(g, arrays[a], lead) for g, a, lead in layout[1]]
    copies = fetches(place, pieces, w_feed, w_out, sems, per)
    k = pl.program_id(0)
    share = tokb.shape[0]
    chunks = [pl.ds(r * ROWS, ROWS) for r in range(share // ROWS)]

    @pl.when(k == 0)
    def _():
        for _, a, _ in copies:
            a.start()
        for _, _, b in copies:
            b.start()
        for _, a, _ in copies:
            a.wait()
        for sl in chunks:
            x = tokb[sl, :].astype(F32) + vec[4:5, :]
            for n, ctx in enumerate((c0, c1, c2, c3)):
                x = x + nt(ctx[sl, :], w_out[n])
            x = x - row_mean(x)
            root = lax.rsqrt(row_mean(x * x) + EPSILON)
            x = x * root
            fs_o[sl, :] = x
            root_o[sl, :] = jnp.broadcast_to(root, (ROWS, 128))
            y = x * vec[0:1, :] + vec[2:3, :]
            normed[sl, :] = y
            nb_o[sl, :] = y.astype(BF)
            acc[sl, :] = y + vec[5:6, :]

    for group in range(4):

        @pl.when(k == group)
        def _():
            for g, _, b in copies:
                if g == group:
                    b.wait()

    hidden = act_o.shape[2]

    def rows_step(r, _):
        sl = pl.ds(pl.multiple_of(r * ROWS, ROWS), ROWS)
        h = nn(nb_o[sl, :], w_feed[k, :, 0:hidden]) + bias[pl.ds(k, 1), :]
        phi, slope = gelu_parts(h)
        a = (h * phi).astype(BF)
        act_o[0, sl, :] = a
        gp_o[0, sl, :] = slope
        acc[sl, :] += nt(a, w_feed[k, :, hidden:])
        return 0

    lax.fori_loop(0, share // ROWS, rows_step, 0)

    @pl.when(k == 3)
    def _():
        total = [jnp.zeros((1, tokb.shape[1]), F32)] * 3
        for sl in chunks:
            x = acc[sl, :]
            x = x - row_mean(x)
            root = lax.rsqrt(row_mean(x * x) + EPSILON)
            x = x * root
            out_o[sl, :] = (x * vec[1:2, :] + vec[3:4, :]).astype(BF)
            g = gtop[sl, :].astype(F32)
            gg = g * vec[1:2, :]
            gs = root * (gg - row_mean(gg) - x * row_mean(gg * x))
            gs_o[sl, :] = gs
            gsb_o[sl, :] = gs.astype(BF)
            for n, y in enumerate((g * x, g, gs)):
                total[n] = total[n] + jnp.sum(y, axis=0, keepdims=True)
        sum_o[...] = jnp.concatenate(total + [jnp.zeros((5, tokb.shape[1]), F32)], axis=0)


def layout_of(groups):
    arrays, pieces = [], []
    for k, group in enumerate(groups):
        for x in group:
            if x.ndim == 2:
                pieces.append((k, len(arrays), None))
            else:
                pieces += [(k, len(arrays), n) for n in range(x.shape[0])]
            arrays.append(x)
    return arrays, (len(arrays), pieces), len(pieces) // 4


def feed_forward(place, groups, contexts, tokb, gtop, vec, bias):
    arrays, layout, per = layout_of(groups)
    share, width = tokb.shape
    part, hidden = contexts[0].shape[1], bias.shape[1]
    block = lambda: pl.BlockSpec((1, share, hidden), lambda i, s: (i, 0, 0))
    sd = jax.ShapeDtypeStruct
    return pl.pallas_call(
        partial(feed_kernel, layout, per),
        grid_spec=pltpu.PrefetchScalarGridSpec(
            num_scalar_prefetch=1,
            grid=(4,),
            in_specs=[pl.BlockSpec(memory_space=pl.ANY)] * len(arrays)
            + [whole_block(x.shape) for x in (*contexts, tokb, gtop, vec, bias)],
            out_specs=[whole_block((share, width))] * 5
            + [block(), block(), whole_block((share, 128)), whole_block((8, width))],
            scratch_shapes=[
                pltpu.VMEM((4, width, 2 * hidden), BF),
                pltpu.VMEM((4, width, part), BF),
                pltpu.VMEM((share, width), F32),
                pltpu.VMEM((share, width), F32),
                pltpu.SemaphoreType.DMA((2, len(layout[1]))),
            ],
        ),
        out_shape=[
            sd((share, width), BF),
            sd((share, width), F32),
            sd((share, width), BF),
            sd((share, width), F32),
            sd((share, width), BF),
            sd((4, share, hidden), BF),
            sd((4, share, hidden), F32),
            sd((share, 128), F32),
            sd((8, width), F32),
        ],
        compiler_params=params(48),
        cost_estimate=pl.CostEstimate(flops=4 * share * width * 4 * hidden * 2, bytes_accessed=24 * 2**20, transcendentals=share * 4 * hidden),
        name="feed_forward",
    )(place, *arrays, *contexts, tokb, gtop, vec, bias)


def feed_back_kernel(layout, per, place, *refs):
    arrays = refs[: layout[0]]
    (gs, gsb, fs, gp, root, vec, gf_o, gfb_o, gc0, gc1, gc2, gc3, gh_o, ghs_o, sum_o, w_feed, w_out, acc, sems) = refs[layout[0] :]
    pieces = [(g, arrays[a], lead) for g, a, lead in layout[1]]
    copies = fetches(place, pieces, w_feed, w_out, sems, per)
    k = pl.program_id(0)
    share, width = gs.shape
    hidden = gh_o.shape[2]

    @pl.when(k == 0)
    def _():
        for _, _, b in copies:
            b.start()
        for _, a, _ in copies:
            a.start()

    for group in range(4):

        @pl.when(k == group)
        def _():
            for g, _, b in copies:
                if g == group:
                    b.wait()

    @pl.when(k == 0)
    def _():
        acc[...] = gs[...]

    def rows_step(r, total):
        sl = pl.ds(pl.multiple_of(r * ROWS, ROWS), ROWS)
        g = (nn(gsb[sl, :], w_feed[k, :, hidden:]) * gp[0, sl, :]).astype(BF)
        gh_o[0, sl, :] = g
        acc[sl, :] += nt(g, w_feed[k, :, 0:hidden])
        return total + jnp.sum(g.astype(F32), axis=0, keepdims=True)

    total = lax.fori_loop(0, share // ROWS, rows_step, jnp.zeros((1, hidden), F32))
    ghs_o[0] = jnp.broadcast_to(total, (8, hidden))

    @pl.when(k == 3)
    def _():
        for _, a, _ in copies:
            a.wait()
        sums = [jnp.zeros((1, width), F32)] * 3
        for r in range(share // ROWS):
            sl = pl.ds(r * ROWS, ROWS)
            gn = acc[sl, :]
            x = fs[sl, :]
            gg = gn * vec[0:1, :]
            gf = root[sl, 0:1] * (gg - row_mean(gg) - x * row_mean(gg * x))
            gf_o[sl, :] = gf
            b = gf.astype(BF)
            gfb_o[sl, :] = b
            for n, o in enumerate((gc0, gc1, gc2, gc3)):
                o[sl, :] = nn(b, w_out[n]).astype(BF)
            for n, y in enumerate((gn * x, gn, gf)):
                sums[n] = sums[n] + jnp.sum(y, axis=0, keepdims=True)
        sum_o[...] = jnp.concatenate(sums + [jnp.zeros((5, width), F32)], axis=0)


def feed_back(place, groups, gs, gsb, fs, gp, root, vec, part):
    arrays, layout, per = layout_of(groups)
    share, width = gs.shape
    hidden = gp.shape[2]
    block = lambda: pl.BlockSpec((1, share, hidden), lambda i, s: (i, 0, 0))
    sd = jax.ShapeDtypeStruct
    return pl.pallas_call(
        partial(feed_back_kernel, layout, per),
        grid_spec=pltpu.PrefetchScalarGridSpec(
            num_scalar_prefetch=1,
            grid=(4,),
            in_specs=[pl.BlockSpec(memory_space=pl.ANY)] * len(arrays)
            + [whole_block(gs.shape), whole_block(gsb.shape), whole_block(fs.shape), block(), whole_block(root.shape), whole_block(vec.shape)],
            out_specs=[whole_block((share, width))] * 2
            + [whole_block((share, part))] * 4
            + [block(), pl.BlockSpec((1, 8, hidden), lambda i, s: (i, 0, 0)), whole_block((8, width))],
            scratch_shapes=[
                pltpu.VMEM((4, width, 2 * hidden), BF),
                pltpu.VMEM((4, width, part), BF),
                pltpu.VMEM((share, width), F32),
                pltpu.SemaphoreType.DMA((2, len(layout[1]))),
            ],
        ),
        out_shape=[sd((share, width), F32), sd((share, width), BF)]
        + [sd((share, part), BF)] * 4
        + [sd((4, share, hidden), BF), sd((4, 8, hidden), F32), sd((8, width), F32)],
        compiler_params=params(48),
        cost_estimate=pl.CostEstimate(flops=4 * share * width * 4 * hidden * 2, bytes_accessed=24 * 2**20, transcendentals=0),
        name="feed_back",
    )(place, *arrays, gs, gsb, fs, gp, root, vec)


def split_rows(place, per, acc, source, near_o, far_o, lead, cols):
    if per == 1:
        near_o[(*lead, slice(None), cols)] = acc[:, source].astype(near_o.dtype)
        return
    rows = acc.shape[0] // per
    for n in range(per // 2):
        near, far = (pl.ds(pl.multiple_of(place[m], 16), rows) for m in (n, per // 2 + n))
        near_o[(*lead, n, slice(None), cols)] = acc[near, source].astype(near_o.dtype)
        far_o[(*lead, n, slice(None), cols)] = acc[far, source].astype(BF)


def weights_kernel(per, place, nb, gsb, gfb, c0, c1, c2, c3, gh, act, *refs):
    outs = refs[:-5]
    near_o, far_o = outs if per > 1 else (outs[0], None)
    nbt, gst, gft, acc, acc_out = refs[-5:]
    k = pl.program_id(0)

    @pl.when(k == 0)
    def _():
        nbt[...] = nb[...].T
        gst[...] = gsb[...].T
        gft[...] = gfb[...].T

    hidden = gh.shape[2]
    part = c0.shape[1]
    acc[...] = nn(nbt[...], gh[0])
    split_rows(place, per, acc, slice(None), near_o, far_o, (0,), slice(0, hidden))
    acc[...] = nn(gst[...], act[0])
    split_rows(place, per, acc, slice(None), near_o, far_o, (0,), slice(hidden, 2 * hidden))
    for n, ctx in enumerate((c0, c1, c2, c3)):

        @pl.when(k == n)
        def _(ctx=ctx):
            acc_out[...] = nn(gft[...], ctx[...])

    split_rows(place, per, acc_out, slice(None), near_o, far_o, (0,), slice(2 * hidden, 2 * hidden + part))


def weight_grads(place, per, nb, gsb, gfb, contexts, gh, act):
    share, width = nb.shape
    hidden, part = gh.shape[2], contexts[0].shape[1]
    block = lambda: pl.BlockSpec((1, share, hidden), lambda i, s: (i, 0, 0))
    cols = 2 * hidden + part
    if per > 1:
        shape = (4, per // 2, width // per, cols)
        outs = [jax.ShapeDtypeStruct(shape, BF)] * 2
        specs = [pl.BlockSpec((1,) + shape[1:], lambda i, s: (i, 0, 0, 0))] * 2
    else:
        outs = [jax.ShapeDtypeStruct((4, width, cols), BF)]
        specs = [pl.BlockSpec((1, width, cols), lambda i, s: (i, 0, 0))]
    return pl.pallas_call(
        partial(weights_kernel, per),
        grid_spec=pltpu.PrefetchScalarGridSpec(
            num_scalar_prefetch=1,
            grid=(4,),
            in_specs=[whole_block(x.shape) for x in (nb, gsb, gfb, *contexts)] + [block(), block()],
            out_specs=specs,
            scratch_shapes=[pltpu.VMEM((width, share), BF)] * 3 + [pltpu.VMEM((width, hidden), F32), pltpu.VMEM((width, part), F32)],
        ),
        out_shape=outs,
        compiler_params=params(40),
        cost_estimate=pl.CostEstimate(flops=4 * share * width * 4 * hidden, bytes_accessed=20 * 2**20, transcendentals=0),
        name="weight_grads",
    )(place, nb, gsb, gfb, *contexts, gh, act)


def qkv_weights_kernel(per, part, place, own, other, g, *refs):
    near_o, far_o = refs[:2] if per > 1 else (refs[0], None)
    acc = refs[-1]
    half_len = other.shape[0]
    core = place[per]
    rows = 512

    acc[...] = jnp.zeros(acc.shape, F32)

    def step(r, _):
        at = pl.ds(pl.multiple_of(r * rows, rows), rows)
        a = g[pl.ds(pl.multiple_of(core * half_len + r * rows, rows), rows), :]
        b = g[pl.ds(pl.multiple_of((1 - core) * half_len + r * rows, rows), rows), :]
        acc[...] += nn(own[0, at, :].T, a) + nn(other[at, :].T, b)
        return 0

    lax.fori_loop(0, half_len // rows, step, 0)
    for m in range(3):
        split_rows(place, per, acc, slice(m * WIDE, m * WIDE + part), near_o, far_o, (), slice(m * part, (m + 1) * part))


def qkv_weight_grads(place, per, tokens, other, g, part):
    half_len, width = other.shape
    if per > 1:
        shape = (per // 2, width // per, 3 * part)
        outs = [jax.ShapeDtypeStruct(shape, F32), jax.ShapeDtypeStruct(shape, BF)]
    else:
        outs = [jax.ShapeDtypeStruct((width, 3 * part), F32)]
    return pl.pallas_call(
        partial(qkv_weights_kernel, per, part),
        grid_spec=pltpu.PrefetchScalarGridSpec(
            num_scalar_prefetch=1,
            grid=(1,),
            in_specs=[pl.BlockSpec((1, half_len, width), lambda i, s: (s[per], 0, 0)), whole_block(other.shape), whole_block(g.shape)],
            out_specs=[whole_block(o.shape) for o in outs],
            scratch_shapes=[pltpu.VMEM((width, 3 * WIDE), F32)],
        ),
        out_shape=outs,
        compiler_params=params(32),
        cost_estimate=pl.CostEstimate(flops=4 * half_len * width * 3 * WIDE, bytes_accessed=8 * 2**20, transcendentals=0),
        name="qkv_weight_grads",
    )(place, tokens, other, g)


def rotation_tables(offsets):
    lane = np.arange(128)
    frequency = (10000.0 ** (-2.0 * (lane % HEAD // 2) / HEAD)).astype(np.float32)
    angles = offsets.astype(F32)[:, None] * frequency[None, :]
    sign = np.where(lane % 2 == 0, -1.0, 1.0).astype(np.float32)
    return jnp.cos(angles), jnp.sin(angles) * sign


def key_bounds(segment):
    length = segment.shape[0]
    first, last = segment[::BLOCK], segment[BLOCK - 1 :: BLOCK]
    low = jnp.sum(segment[None, :] < first[:, None], axis=1)
    high = jnp.sum(segment[None, :] <= last[:, None], axis=1)
    low = low // 128 * 128
    count = (high - low + CHUNK - 1) // CHUNK
    return jnp.stack([jnp.minimum(low, length - CHUNK * count), count], axis=1).reshape(-1).astype(jnp.int32)


def swap_ctx(x):
    return lax.ppermute(x, "ctx", [(0, 1), (1, 0)])


def swap_tp(x, k):
    return lax.ppermute(x, "tp", [(i, i ^ k) for i in range(4)])


def swap_shard(x, k):
    return lax.ppermute(x, "shard", [(i, i ^ k) for i in range(4)])


def order_four(parts, index):
    a, b, c, d = parts
    odd, high = index % 2 == 1, index // 2 == 1
    a, b = jnp.where(odd, b, a), jnp.where(odd, a, b)
    c, d = jnp.where(odd, d, c), jnp.where(odd, c, d)
    return jnp.stack([jnp.where(high, c, a), jnp.where(high, d, b), jnp.where(high, a, c), jnp.where(high, b, d)])


def sum_shard(x):
    if lax.axis_size("shard") != 4:
        return lax.psum(x, "shard")
    x = x + swap_shard(x, 1)
    return x + swap_shard(x, 2)


def gather_tp(x, half):
    one, two = swap_tp(x, 1), swap_tp(x, 2)
    three = jnp.concatenate([swap_tp(one[:half], 2), swap_tp(two[half:], 1)])
    return [x, one, two, three]


def scatter_tp(parts):
    own, one, two, three = parts
    half = own.shape[0] // 2
    low, high = three[:half].astype(BF), three[half:].astype(BF)
    low, high = swap_tp(low, 2), swap_tp(high, 1)
    one = jnp.concatenate([one[:half] + low.astype(F32), one[half:]]).astype(BF)
    two = jnp.concatenate([two[:half], two[half:] + high.astype(F32)]).astype(BF)
    return own + swap_tp(one, 1).astype(F32) + swap_tp(two, 2).astype(F32)


def three_rows(x):
    high = lax.reduce_precision(x, 8, 7)
    middle = lax.reduce_precision(x - high, 8, 7)
    return jnp.stack([high, middle, x - high - middle]).astype(BF)


def contract_last(left, right):
    return lax.dot_general(left, right, (((1,), (1,)), ((), ())), preferred_element_type=F32)


def body(tokens, segment_ids, offsets, qkv_weight, out_weight, ffn_weight, qkv_bias, ffn_bias, norm_gain, shift_params, out_grad):
    t, c, z = lax.axis_index("tp"), lax.axis_index("ctx"), lax.axis_index("shard")
    shards = lax.axis_size("shard")
    half_len, width = tokens.shape[1:]
    rows, _, part = qkv_weight.shape
    hidden = ffn_weight.shape[2]
    heads = part // HEAD
    length = 2 * half_len
    share = length // 4
    first_core = c == 0
    direct = shards == 4

    def take(x, index):
        return lax.dynamic_index_in_dim(x, index, 0, keepdims=False)

    def by_core(own, other):
        return jnp.where(first_core, jnp.stack([own, other]), jnp.stack([other, own]))

    feed = jnp.concatenate([ffn_weight.reshape(rows, 2 * hidden), out_weight], axis=1)
    bias_rows = jnp.pad(three_rows(ffn_bias), ((0, 13), (0, hidden + part)))
    qkv_rows = qkv_weight.reshape(rows, 3 * part)
    other_tokens = swap_ctx(take(tokens, 1 - c))
    if direct:
        place = jnp.stack([((z ^ j) * 2 + (c ^ f)) * rows for f in (0, 1) for j in range(4)] + [c]).astype(jnp.int32)
        near = [qkv_rows] + [swap_shard(qkv_rows, j) for j in (1, 2, 3)]
        qkv_pieces = near + [swap_ctx(x) for x in near]
        own = gather_tp(jnp.concatenate([feed, bias_rows]), rows // 2)
        far = jnp.concatenate([swap_shard(feed, j) for j in (1, 2, 3)])
        far = gather_tp(far, 3 * rows // 2)
        lifted = [x.reshape(3, rows, -1) for x in far]
        groups = [[own[k], lifted[k], swap_ctx(own[k]), swap_ctx(lifted[k])] for k in range(4)]
        bias_all = [x[rows : rows + 3, :hidden] for x in own]
    else:
        place = jnp.stack([jnp.zeros_like(c), c]).astype(jnp.int32)
        qkv_pieces = [lax.all_gather(qkv_rows, ("shard", "ctx"), axis=0, tiled=True)]
        full = lax.all_gather(feed, ("shard", "ctx"), axis=0, tiled=True)
        full = gather_tp(jnp.concatenate([full, bias_rows]), width // 2)
        groups = [[x] for x in full]
        bias_all = [x[width : width + 3, :hidden] for x in full]
    per = len(qkv_pieces)
    bias_all = jnp.stack([jnp.sum(x.astype(F32), axis=0) for x in bias_all])
    bias_pad = jnp.pad(qkv_bias, ((0, 0), (0, WIDE - part)))
    vec = jnp.concatenate([norm_gain, shift_params, jnp.zeros((2, width), F32)])

    marks = jnp.stack([segment_ids, offsets])
    marks = by_core(take(marks.swapaxes(0, 1), c), swap_ctx(take(marks.swapaxes(0, 1), 1 - c)))
    segment, places = marks[:, 0].reshape(length), marks[:, 1].reshape(length)
    halves = lambda x: x.reshape(2, 2, share, width)
    here = t // 2 == c
    tok_block = jnp.where(here, take(take(halves(tokens), c), t % 2), take(other_tokens.reshape(2, share, width), t % 2))
    grad_block = halves(out_grad)
    grad_far = swap_ctx(take(take(grad_block, 1 - c), t % 2))
    grad_top = jnp.where(here, take(take(grad_block, c), t % 2), grad_far)

    cosine, sine = rotation_tables(places)
    bounds = key_bounds(segment)
    seg_column = segment[:, None]
    seg_row = jnp.broadcast_to(segment[None, :], (8, length))
    q, k_rows, v_rows, k_turned, qkv_wide = project_qkv(place, qkv_pieces, bias_pad, tokens, other_tokens, cosine, sine, part)

    contexts, log_totals = [None] * 4, [None] * 4
    for j in (3, 1, 2, 0):
        spot = jnp.concatenate([((t ^ j) * (share // BLOCK))[None].astype(jnp.int32), bounds])
        context, log_totals[j] = attention_forward(spot, q, k_rows, v_rows, seg_column, seg_row, heads, share)
        contexts[j] = swap_tp(context, j) if j else context
    log_total = jnp.concatenate(log_totals, axis=1)

    layer_out, grad_second, grad_second_b, first_scaled, normed_b, activated, slope, root, sums_two = feed_forward(
        place, groups, contexts, tok_block, grad_top, vec, bias_all
    )

    def spread(block):
        a, b, d, e = gather_tp(block, share // 2)
        odd = t % 2 == 1
        mine = jnp.where(odd, jnp.stack([b, a]), jnp.stack([a, b]))
        rest = jnp.where(odd, jnp.stack([e, d]), jnp.stack([d, e]))
        keep, send = jnp.where(here, mine, rest), jnp.where(here, rest, mine)
        return by_core(keep, swap_ctx(send)).reshape(2, half_len, width)

    outputs = spread(layer_out)

    grad_first, grad_first_b, g0, g1, g2, g3, grad_hidden, hidden_sums, sums_one = feed_back(
        place, groups, grad_second, grad_second_b, first_scaled, slope, root, vec, part
    )
    grad_heads = jnp.stack([g0, swap_tp(g1, 1), swap_tp(g2, 2), swap_tp(g3, 3)])

    grads = weight_grads(place, per, normed_b, grad_second_b, grad_first_b, contexts, grad_hidden, activated)
    if direct:
        got = swap_ctx(grads[1])
        summed = scatter_tp([grads[0][k].astype(F32) + got[k].astype(F32) for k in range(4)])
        total = summed[0]
        for j in (1, 2, 3):
            total = total + swap_shard(summed[j].astype(BF), j).astype(F32)
    else:
        summed = scatter_tp([grads[0][k].astype(F32) for k in range(4)])
        total = lax.psum_scatter(summed, ("shard", "ctx"), scatter_dimension=0, tiled=True)
    grad_ffn_weight = total[:, : 2 * hidden].reshape(rows, 2, hidden)
    grad_out_weight = total[:, 2 * hidden :]

    spot = jnp.concatenate([(t * (share // BLOCK))[None].astype(jnp.int32), bounds])
    grad_proj, bias_sums = attention_backward(
        spot, q, k_rows, k_turned, v_rows, grad_heads, log_total, seg_column, seg_row, cosine, sine, heads
    )
    proj_blocks = grad_proj.reshape(4, share, 3 * WIDE)
    branch = [contract_last(take(proj_blocks, t ^ k), qkv_wide) for k in range(4)]
    grad_tokens = spread((grad_first + scatter_tp(branch)).astype(BF))

    grads = qkv_weight_grads(place, per, tokens, other_tokens, grad_proj, part)
    if direct:
        summed = grads[0] + swap_ctx(grads[1]).astype(F32)
        total = summed[0]
        for j in (1, 2, 3):
            total = total + swap_shard(summed[j].astype(BF), j).astype(F32)
    else:
        total = lax.psum_scatter(grads[0], ("shard", "ctx"), scatter_dimension=0, tiled=True)
    grad_qkv_weight = total.reshape(rows, 3, part)

    sums = order_four([hidden_sums[k, 0] for k in range(4)], t).reshape(4 * hidden)
    vectors = jnp.stack([sums_one[0], sums_two[0], sums_one[1], sums_two[1], sums_one[2], sums_two[2]])
    small = jnp.concatenate([sums, vectors.reshape(-1)]).reshape(-1, 128)
    for k in (1, 2):
        small = small + swap_tp(small, k)
    small = sum_shard(small + swap_ctx(small))
    cut = 4 * hidden // 128
    grad_ffn_bias = take(small[:cut].reshape(4, hidden), t)
    vectors = small[cut:].reshape(6, width)
    grad_qkv_bias = bias_sums[0].reshape(3, WIDE)[:, :part]
    grad_qkv_bias = sum_shard(grad_qkv_bias + swap_ctx(grad_qkv_bias))
    return (
        outputs,
        grad_tokens,
        grad_qkv_weight,
        grad_out_weight,
        grad_ffn_weight,
        grad_qkv_bias,
        grad_ffn_bias,
        vectors[:2],
        vectors[2:],
    )


def solution(mesh):
    return jax.shard_map(
        body,
        mesh=mesh,
        in_specs=(
            P("shard", "ctx", None),
            P("shard", "ctx"),
            P("shard", "ctx"),
            P(("shard", "ctx"), None, "tp"),
            P(("shard", "ctx"), "tp"),
            P(("shard", "ctx"), None, "tp"),
            P(None, "tp"),
            P("tp"),
            P(),
            P(),
            P("shard", "ctx", None),
        ),
        out_specs=(
            P("shard", "ctx", None),
            P("shard", "ctx", None),
            P(("shard", "ctx"), None, "tp"),
            P(("shard", "ctx"), "tp"),
            P(("shard", "ctx"), None, "tp"),
            P(None, "tp"),
            P("tp"),
            P(),
            P(),
        ),
        check_vma=False,
    )
```

```python
from functools import partial

import jax
import jax.numpy as jnp
import numpy as np
from jax import lax
from jax.experimental import pallas as pl
from jax.experimental.pallas import tpu as pltpu
from jax.sharding import PartitionSpec as P

HEAD = 64
WIDE = 256
BLOCK = 256
CHUNK = 256
EPSILON = 1e-12
F32 = jnp.float32
BF = jnp.bfloat16
NEG = -1e30
COST = pl.CostEstimate(flops=0, bytes_accessed=0, transcendentals=0)


def swap_pairs(x):
    lane = lax.broadcasted_iota(jnp.int32, x.shape, 1)
    n = x.shape[1]
    return jnp.where(lane % 2 == 0, pltpu.roll(x, n - 1, 1), pltpu.roll(x, 1, 1))


def nt(a, b):
    return lax.dot_general(a, b, (((1,), (1,)), ((), ())), preferred_element_type=F32)


def nn(a, b):
    return lax.dot_general(a, b, (((1,), (0,)), ((), ())), preferred_element_type=F32)


def twice(x):
    return jnp.concatenate([x, x], axis=1)


def lanes_of_heads(x, heads):
    lane = lax.broadcasted_iota(jnp.int32, x.shape, 1) // HEAD
    return [jnp.where(lane == h, x, jnp.zeros_like(x)) for h in range(heads)]


def whole_block(shape, buffers=1):
    return pl.BlockSpec(shape, lambda *_: (0,) * len(shape), pipeline_mode=pl.Buffered(buffers))


def smem():
    return pl.BlockSpec(memory_space=pltpu.SMEM)


def params(mib):
    return pltpu.CompilerParams(dimension_semantics=("arbitrary",), vmem_limit_bytes=mib * 1024 * 1024)


def qkv_kernel(count, per, part, place, *refs):
    pieces = []
    for x in refs[:count]:
        pieces += [x] if len(x.shape) == 2 else [x.at[n] for n in range(x.shape[0])]
    bias, own, other, cos, sin, q_o, k_o, v_o, kt_o, w_o = refs[count:]
    piece_rows = pieces[0].shape[0]
    pad = jnp.zeros((piece_rows, WIDE - part), BF)
    for n in range(per):
        sl = pl.ds(pl.multiple_of(place[n], 16), piece_rows)
        for m in range(3):
            w_o[sl, m * WIDE : (m + 1) * WIDE] = jnp.concatenate([pieces[n][:, m * part : (m + 1) * part], pad], axis=1)
    half_len = other.shape[0]

    def run(x, sl):
        c, s = twice(cos[sl, :]), twice(sin[sl, :])
        p = nn(x, w_o[:, 0:WIDE]) + bias[0:1, :]
        q_o[sl, :] = ((p * c + swap_pairs(p) * s).astype(BF).astype(F32) * (HEAD**-0.5)).astype(BF)
        p = nn(x, w_o[:, WIDE : 2 * WIDE]) + bias[1:2, :]
        k = (p * c + swap_pairs(p) * s).astype(BF)
        k_o[sl, :] = k
        kt_o[:, sl] = k.T
        v_o[sl, :] = (nn(x, w_o[:, 2 * WIDE : 3 * WIDE]) + bias[2:3, :]).astype(BF)

    def step(r, _):
        rows = pl.ds(pl.multiple_of(r * BLOCK, BLOCK), BLOCK)
        core = place[per]
        run(own[0, rows, :], pl.ds(pl.multiple_of(core * half_len + r * BLOCK, BLOCK), BLOCK))
        run(other[rows, :], pl.ds(pl.multiple_of((1 - core) * half_len + r * BLOCK, BLOCK), BLOCK))
        return 0

    lax.fori_loop(0, half_len // BLOCK, step, 0)


def project_qkv(place, pieces, per, bias, tokens, other, cos, sin, part):
    half_len, width = other.shape
    length, count = 2 * half_len, len(pieces)
    return pl.pallas_call(
        partial(qkv_kernel, count, per, part),
        grid_spec=pltpu.PrefetchScalarGridSpec(
            num_scalar_prefetch=1,
            grid=(1,),
            in_specs=[whole_block(p.shape) for p in pieces]
            + [whole_block(bias.shape), pl.BlockSpec((1, half_len, width), lambda i, s: (s[per], 0, 0))]
            + [whole_block(x.shape) for x in (other, cos, sin)],
            out_specs=[whole_block((length, WIDE))] * 3 + [whole_block((WIDE, length)), whole_block((width, 3 * WIDE))],
        ),
        out_shape=[jax.ShapeDtypeStruct((length, WIDE), BF)] * 3
        + [jax.ShapeDtypeStruct((WIDE, length), BF), jax.ShapeDtypeStruct((width, 3 * WIDE), BF)],
        compiler_params=params(32),
        cost_estimate=COST,
        name="project_qkv",
    )(place, *pieces, bias, tokens, other, cos, sin)


def forward_kernel(heads, place, q, k, v, segc, segr, ctx_o, lse_o, acc, s_sc, m_sc, l_sc, qc_sc):
    i = place[0] + pl.program_id(0)
    start, count = place[1 + 2 * i], place[2 + 2 * i]
    qc_sc[...] = jnp.concatenate(lanes_of_heads(q[...], heads), axis=0)
    seg_q = segc[...]
    m_sc[...] = jnp.full(m_sc.shape, NEG, F32)
    l_sc[...] = jnp.zeros(l_sc.shape, F32)

    def at(j):
        return pl.ds(pl.multiple_of(start + j * CHUNK, 128), CHUNK)

    def of(h):
        return slice(h * BLOCK, (h + 1) * BLOCK)

    def pass1(j, _):
        s = nt(qc_sc[...], k[at(j), :])
        keep = seg_q == segr[0:1, at(j)]
        for h in range(heads):
            sh = jnp.where(keep, s[of(h), :], NEG)
            s_sc[j, of(h), :] = sh
            m_sc[of(h), :] = jnp.maximum(m_sc[of(h), :], jnp.maximum(sh[:, :128], sh[:, 128:]))
        return 0

    lax.fori_loop(0, count, pass1, 0)
    m_sc[...] = jnp.broadcast_to(jnp.max(m_sc[...], axis=1, keepdims=True), m_sc.shape)

    def pass2(j, _):
        for h in range(heads):
            e = jnp.exp(s_sc[j, of(h), :] - twice(m_sc[of(h), :]))
            s_sc[j, of(h), :] = e
            l_sc[of(h), :] += e[:, :128] + e[:, 128:]
        return 0

    lax.fori_loop(0, count, pass2, 0)
    total = jnp.sum(l_sc[...], axis=1, keepdims=True)
    lse = m_sc[:, 0:1] + jnp.log(total)
    l_sc[...] = jnp.broadcast_to(1.0 / total, l_sc.shape)
    lane = lax.broadcasted_iota(jnp.int32, (BLOCK, 128), 1)
    tile = jnp.zeros((BLOCK, 128), F32)
    for h in range(heads):
        tile = jnp.where(lane == h, lse[of(h), :], tile)
    lse_o[...] = tile.T[0:8, :]
    acc[...] = jnp.zeros(acc.shape, F32)

    def pass3(j, _):
        ps = [(s_sc[j, of(h), :] * twice(l_sc[of(h), :])).astype(BF) for h in range(heads)]
        acc[...] += nn(jnp.concatenate(ps, axis=1), jnp.concatenate(lanes_of_heads(v[at(j), :], heads), axis=0))
        return 0

    lax.fori_loop(0, count, pass3, 0)
    ctx_o[...] = acc[:, : heads * HEAD].astype(BF)


def attention_forward(place, q, k, v, segc, segr, heads, share):
    length = q.shape[0]
    grid = share // BLOCK
    rows = lambda i, s: (s[0] + i, 0)
    return pl.pallas_call(
        partial(forward_kernel, heads),
        grid_spec=pltpu.PrefetchScalarGridSpec(
            num_scalar_prefetch=1,
            grid=(grid,),
            in_specs=[
                pl.BlockSpec((BLOCK, WIDE), rows),
                whole_block(k.shape),
                whole_block(v.shape),
                pl.BlockSpec((BLOCK, 1), rows),
                whole_block(segr.shape),
            ],
            out_specs=[pl.BlockSpec((BLOCK, heads * HEAD), lambda i, s: (i, 0)), pl.BlockSpec((8, BLOCK), lambda i, s: (0, i))],
            scratch_shapes=[
                pltpu.VMEM((BLOCK, WIDE), F32),
                pltpu.VMEM((length // CHUNK, heads * BLOCK, CHUNK), F32),
                pltpu.VMEM((heads * BLOCK, 128), F32),
                pltpu.VMEM((heads * BLOCK, 128), F32),
                pltpu.VMEM((heads * BLOCK, WIDE), BF),
            ],
        ),
        out_shape=[jax.ShapeDtypeStruct((share, heads * HEAD), BF), jax.ShapeDtypeStruct((8, share), F32)],
        compiler_params=params(16),
        cost_estimate=COST,
        name="attention_forward",
    )(place, q, k, v, segc, segr)


def backward_kernel(heads, place, q, k, kt, v, do, lse, segc, segr, cos, sin, g_o, gb_o, dk_sc, dv_sc, qc_sc, dc_sc, dq_sc, p_sc, dp_sc, dl_sc):
    step_at = pl.program_id(0)
    i = step_at ^ place[0]
    length = k.shape[0]

    @pl.when(step_at == 0)
    def _():
        dk_sc[...] = jnp.zeros(dk_sc.shape, F32)
        dv_sc[...] = jnp.zeros(dv_sc.shape, F32)
        gb_o[...] = jnp.zeros(gb_o.shape, F32)

    start, count = place[1 + 2 * i], place[2 + 2 * i]
    qc_sc[...] = jnp.concatenate(lanes_of_heads(q[...], heads), axis=0)
    d = do[0]
    d = jnp.concatenate([d, jnp.zeros((BLOCK, WIDE - d.shape[1]), BF)], axis=1)
    dc_sc[...] = jnp.concatenate(lanes_of_heads(d, heads), axis=0)
    dq_sc[...] = jnp.zeros(dq_sc.shape, F32)
    own = pl.ds(pl.multiple_of(i * BLOCK, BLOCK), BLOCK)
    seg_q = segr[0:1, own]
    dl_sc[...] = jnp.zeros(dl_sc.shape, F32)

    def at(j):
        return pl.ds(pl.multiple_of(start + j * CHUNK, 128), CHUNK)

    def of(h):
        return slice(h * BLOCK, (h + 1) * BLOCK)

    def pass1(j, _):
        s = nt(k[at(j), :], qc_sc[...])
        dp = nt(v[at(j), :], dc_sc[...])
        keep = segc[at(j), :] == seg_q
        for h in range(heads):
            p = jnp.exp(jnp.where(keep, s[:, of(h)], NEG) - lse[h : h + 1, :])
            p_sc[j, :, of(h)] = p
            dp_sc[j, :, of(h)] = dp[:, of(h)]
            dl_sc[:, of(h)] += jnp.sum((p * dp[:, of(h)]).reshape(CHUNK // 8, 8, BLOCK), axis=0)
        return 0

    lax.fori_loop(0, count, pass1, 0)
    delta = jnp.sum(dl_sc[...], axis=0, keepdims=True)

    def pass2(j, _):
        ps, dss = [], []
        for h in range(heads):
            p = p_sc[j, :, of(h)]
            ds = (p * (dp_sc[j, :, of(h)] - delta[:, of(h)])).astype(BF)
            ps.append(p.astype(BF))
            dss.append(ds)
            dq_sc[h * HEAD : (h + 1) * HEAD, :] += nn(kt[h * HEAD : (h + 1) * HEAD, at(j)], ds)
        dv_sc[at(j), :] += nn(jnp.concatenate(ps, axis=1), dc_sc[...])
        dk_sc[at(j), :] += nn(jnp.concatenate(dss, axis=1), qc_sc[...])
        return 0

    lax.fori_loop(0, count, pass2, 0)

    def turn(x, sl):
        return (x * twice(cos[sl, :]) - swap_pairs(x) * twice(sin[sl, :])).astype(BF)

    def put(x, sl, m):
        g_o[sl, m * WIDE : (m + 1) * WIDE] = x
        gb_o[0:1, m * WIDE : (m + 1) * WIDE] += jnp.sum(x.astype(F32), axis=0, keepdims=True)

    put(turn(dq_sc[...].T * (HEAD**-0.5), own), own, 0)

    @pl.when(step_at == pl.num_programs(0) - 1)
    def _():
        def last(r, _):
            sl = pl.ds(pl.multiple_of(r * BLOCK, BLOCK), BLOCK)
            put(turn(dk_sc[sl, :], sl), sl, 1)
            put(dv_sc[sl, :].astype(BF), sl, 2)
            return 0

        lax.fori_loop(0, length // BLOCK, last, 0)


def attention_backward(place, q, k, kt, v, do, lse, segc, segr, cos, sin, heads):
    length = k.shape[0]
    steps, per = length // BLOCK, do.shape[1] // BLOCK
    return pl.pallas_call(
        partial(backward_kernel, heads),
        grid_spec=pltpu.PrefetchScalarGridSpec(
            num_scalar_prefetch=1,
            grid=(steps,),
            in_specs=[
                pl.BlockSpec((BLOCK, WIDE), lambda i, s: (i ^ s[0], 0)),
                whole_block(k.shape),
                whole_block(kt.shape),
                whole_block(v.shape),
                pl.BlockSpec((1, BLOCK, heads * HEAD), lambda i, s: (i // per, i % per, 0)),
                pl.BlockSpec((8, BLOCK), lambda i, s: (0, i)),
                whole_block(segc.shape),
                whole_block(segr.shape),
                whole_block(cos.shape),
                whole_block(sin.shape),
            ],
            out_specs=[whole_block((length, 3 * WIDE)), whole_block((8, 3 * WIDE))],
            scratch_shapes=[pltpu.VMEM((length, WIDE), F32)] * 2
            + [pltpu.VMEM((heads * BLOCK, WIDE), BF)] * 2
            + [pltpu.VMEM((WIDE, BLOCK), F32)]
            + [pltpu.VMEM((length // CHUNK, CHUNK, heads * BLOCK), F32)] * 2
            + [pltpu.VMEM((8, heads * BLOCK), F32)],
        ),
        out_shape=[jax.ShapeDtypeStruct((length, 3 * WIDE), BF), jax.ShapeDtypeStruct((8, 3 * WIDE), F32)],
        compiler_params=params(32),
        cost_estimate=COST,
        name="attention_backward",
    )(place, q, k, kt, v, do, lse, segc, segr, cos, sin)


def out_copies(place, gathered, w_out, sems):
    here = place[place.shape[0] - 1]
    feed = gathered.shape[2] - w_out.shape[2]
    return [pltpu.make_async_copy(gathered.at[here ^ k, :, feed:], w_out.at[k], sems.at[k]) for k in range(4)]


def row_mean(x):
    return jnp.mean(x, axis=1, keepdims=True)


def gelu_parts(x):
    e = jnp.exp(x * x * -0.5)
    t = 1.0 / (1.0 + (0.3275911 * 0.7071067811865476) * jnp.abs(x))
    p = t * (0.254829592 + t * (-0.284496736 + t * (1.421413741 + t * (-1.453152027 + t * 1.061405429))))
    tail = 0.5 * p * e
    phi = jnp.where(x >= 0, 1.0 - tail, tail)
    return phi, phi + x * e * 0.3989422804014327


ROWS = 256


def feed_kernel(place, gathered, w, c0, c1, c2, c3, tokb, gtop, vec, bias, *refs):
    (out_o, gs_o, gsb_o, fs_o, nbt_o, gst_o, act_o, gp_o, root_o, sum_o, nb_o, w_out, acc, normed, sems) = refs
    copies = out_copies(place, gathered, w_out, sems)
    k = pl.program_id(0)
    share = tokb.shape[0]
    part = c0.shape[1]
    chunks = [pl.ds(r * ROWS, ROWS) for r in range(share // ROWS)]

    @pl.when(k == 0)
    def _():
        for copy in copies:
            copy.start()
        for copy in copies:
            copy.wait()
        for sl in chunks:
            x = tokb[sl, :].astype(F32) + vec[4:5, :]
            for n, ctx in enumerate((c0, c1, c2, c3)):
                x = x + nt(ctx[sl, :], w_out[n, :, 0:part])
            x = x - row_mean(x)
            root = lax.rsqrt(row_mean(x * x) + EPSILON)
            x = x * root
            fs_o[sl, :] = x
            root_o[sl, :] = jnp.broadcast_to(root, (ROWS, 128))
            y = x * vec[0:1, :] + vec[2:3, :]
            normed[sl, :] = y
            nb_o[sl, :] = y.astype(BF)
            nbt_o[:, sl] = y.astype(BF).T
            acc[sl, :] = y + vec[5:6, :]

    hidden = act_o.shape[2]

    def rows_step(r, _):
        sl = pl.ds(pl.multiple_of(r * ROWS, ROWS), ROWS)
        h = nn(nb_o[sl, :], w[0, :, 0:hidden]) + bias[pl.ds(k, 1), :]
        phi, slope = gelu_parts(h)
        a = (h * phi).astype(BF)
        act_o[0, sl, :] = a
        gp_o[0, sl, :] = slope
        acc[sl, :] += nt(a, w[0, :, hidden:])
        return 0

    lax.fori_loop(0, share // ROWS, rows_step, 0)

    @pl.when(k == 3)
    def _():
        total = [jnp.zeros((1, tokb.shape[1]), F32)] * 3
        for sl in chunks:
            x = acc[sl, :]
            x = x - row_mean(x)
            root = lax.rsqrt(row_mean(x * x) + EPSILON)
            x = x * root
            out_o[sl, :] = (x * vec[1:2, :] + vec[3:4, :]).astype(BF)
            g = gtop[sl, :].astype(F32)
            gg = g * vec[1:2, :]
            gs = root * (gg - row_mean(gg) - x * row_mean(gg * x))
            gs_o[sl, :] = gs
            gsb_o[sl, :] = gs.astype(BF)
            gst_o[:, sl] = gs.astype(BF).T
            for n, y in enumerate((g * x, g, gs)):
                total[n] = total[n] + jnp.sum(y, axis=0, keepdims=True)
        sum_o[...] = jnp.concatenate(total + [jnp.zeros((5, tokb.shape[1]), F32)], axis=0)


def feed_specs(place, gathered, hidden):
    width, last = gathered.shape[1], place.shape[0] - 1
    return [pl.BlockSpec(memory_space=pl.ANY), pl.BlockSpec((1, width, 2 * hidden), lambda i, s: (s[last] ^ i, 0, 0))]


def feed_forward(place, gathered, contexts, tokb, gtop, vec, bias):
    share, width = tokb.shape
    hidden = bias.shape[1]
    block = lambda: pl.BlockSpec((1, share, hidden), lambda i, s: (i, 0, 0))
    sd = jax.ShapeDtypeStruct
    return pl.pallas_call(
        feed_kernel,
        grid_spec=pltpu.PrefetchScalarGridSpec(
            num_scalar_prefetch=1,
            grid=(4,),
            in_specs=feed_specs(place, gathered, hidden) + [whole_block(x.shape) for x in (*contexts, tokb, gtop, vec, bias)],
            out_specs=[whole_block((share, width))] * 4
            + [whole_block((width, share))] * 2
            + [block(), block(), whole_block((share, 128)), whole_block((8, width))],
            scratch_shapes=[
                pltpu.VMEM((share, width), BF),
                pltpu.VMEM((4, width, gathered.shape[2] - 2 * hidden), BF),
                pltpu.VMEM((share, width), F32),
                pltpu.VMEM((share, width), F32),
                pltpu.SemaphoreType.DMA((4,)),
            ],
        ),
        out_shape=[
            sd((share, width), BF),
            sd((share, width), F32),
            sd((share, width), BF),
            sd((share, width), F32),
            sd((width, share), BF),
            sd((width, share), BF),
            sd((4, share, hidden), BF),
            sd((4, share, hidden), F32),
            sd((share, 128), F32),
            sd((8, width), F32),
        ],
        compiler_params=params(32),
        cost_estimate=COST,
        name="feed_forward",
    )(place, gathered, gathered, *contexts, tokb, gtop, vec, bias)


def feed_back_kernel(place, gathered, w, gs, gsb, fs, gp, root, vec, *refs):
    (gf_o, gft_o, gc0, gc1, gc2, gc3, gh_o, ghs_o, sum_o, w_out, acc, sems) = refs
    copies = out_copies(place, gathered, w_out, sems)
    k = pl.program_id(0)
    share, width = gs.shape
    hidden, part = gh_o.shape[2], gc0.shape[1]

    @pl.when(k == 0)
    def _():
        for copy in copies:
            copy.start()
        acc[...] = gs[...]

    def rows_step(r, total):
        sl = pl.ds(pl.multiple_of(r * ROWS, ROWS), ROWS)
        g = (nn(gsb[sl, :], w[0, :, hidden:]) * gp[0, sl, :]).astype(BF)
        gh_o[0, sl, :] = g
        acc[sl, :] += nt(g, w[0, :, 0:hidden])
        return total + jnp.sum(g.astype(F32), axis=0, keepdims=True)

    total = lax.fori_loop(0, share // ROWS, rows_step, jnp.zeros((1, hidden), F32))
    ghs_o[0] = jnp.broadcast_to(total, (8, hidden))

    @pl.when(k == 3)
    def _():
        for copy in copies:
            copy.wait()
        sums = [jnp.zeros((1, width), F32)] * 3
        for r in range(share // ROWS):
            sl = pl.ds(r * ROWS, ROWS)
            gn = acc[sl, :]
            x = fs[sl, :]
            gg = gn * vec[0:1, :]
            gf = root[sl, 0:1] * (gg - row_mean(gg) - x * row_mean(gg * x))
            gf_o[sl, :] = gf
            b = gf.astype(BF)
            gft_o[:, sl] = b.T
            for n, o in enumerate((gc0, gc1, gc2, gc3)):
                o[sl, :] = nn(b, w_out[n, :, 0:part]).astype(BF)
            for n, y in enumerate((gn * x, gn, gf)):
                sums[n] = sums[n] + jnp.sum(y, axis=0, keepdims=True)
        sum_o[...] = jnp.concatenate(sums + [jnp.zeros((5, width), F32)], axis=0)


def feed_back(place, gathered, gs, gsb, fs, gp, root, vec, part):
    share, width = gs.shape
    hidden = gp.shape[2]
    block = lambda: pl.BlockSpec((1, share, hidden), lambda i, s: (i, 0, 0))
    sd = jax.ShapeDtypeStruct
    return pl.pallas_call(
        feed_back_kernel,
        grid_spec=pltpu.PrefetchScalarGridSpec(
            num_scalar_prefetch=1,
            grid=(4,),
            in_specs=feed_specs(place, gathered, hidden)
            + [whole_block(gs.shape), whole_block(gsb.shape), whole_block(fs.shape), block(), whole_block(root.shape), whole_block(vec.shape)],
            out_specs=[whole_block((share, width)), whole_block((width, share))]
            + [whole_block((share, part))] * 4
            + [block(), pl.BlockSpec((1, 8, hidden), lambda i, s: (i, 0, 0)), whole_block((8, width))],
            scratch_shapes=[
                pltpu.VMEM((4, width, gathered.shape[2] - 2 * hidden), BF),
                pltpu.VMEM((share, width), F32),
                pltpu.SemaphoreType.DMA((4,)),
            ],
        ),
        out_shape=[sd((share, width), F32), sd((width, share), BF)]
        + [sd((share, part), BF)] * 4
        + [sd((4, share, hidden), BF), sd((4, 8, hidden), F32), sd((8, width), F32)],
        compiler_params=params(28),
        cost_estimate=COST,
        name="feed_back",
    )(place, gathered, gathered, gs, gsb, fs, gp, root, vec)


def split_rows(place, per, acc, source, near_o, far_o, lead, cols):
    if per == 1:
        near_o[(*lead, slice(None), cols)] = acc[:, source].astype(near_o.dtype)
        return
    rows = acc.shape[0] // per
    for n in range(per // 2):
        near, far = (pl.ds(pl.multiple_of(place[m], 16), rows) for m in (n, per // 2 + n))
        near_o[(*lead, n, slice(None), cols)] = acc[near, source].astype(near_o.dtype)
        far_o[(*lead, n, slice(None), cols)] = acc[far, source].astype(BF)


def weights_kernel(per, place, nbt, gst, gh, act, *refs):
    hh = gh.shape[2]
    if per > 1:
        near_o, far_o, acc = refs
        for n, (left, right) in enumerate(((nbt, gh), (gst, act))):
            acc[...] = nn(left[...], right[0])
            split_rows(place, per, acc, slice(None), near_o, far_o, (0,), slice(n * hh, (n + 1) * hh))
        return
    *more, out = refs
    out[0, :, 0:hh] = nn(nbt[...], gh[0]).astype(BF)
    out[0, :, hh : 2 * hh] = nn(gst[...], act[0]).astype(BF)
    if more:
        gft, ctx = more
        out[0, :, 2 * hh :] = nn(gft[...], ctx[0]).astype(BF)


def weight_grads(place, per, side, nbt, gst, gh, act, *more):
    width, share = nbt.shape
    hh = gh.shape[2] // 2
    here = len(place.shape) and place.shape[0] - 1
    block = pl.BlockSpec((1, share, hh), lambda i, s: (i, 0, side))
    cols = 2 * hh
    ins = [whole_block(nbt.shape), whole_block(gst.shape), block, block]
    if more:
        part = more[1].shape[2]
        cols += part
        ins += [whole_block(more[0].shape), pl.BlockSpec((1, share, part), lambda i, s: (i, 0, 0))]
    if per > 1:
        shape = (4, per // 2, width // per, cols)
        outs = [jax.ShapeDtypeStruct(shape, BF)] * 2
        specs = [pl.BlockSpec((1,) + shape[1:], lambda i, s: (i, 0, 0, 0))] * 2
        scratch = [pltpu.VMEM((width, hh), F32)]
    else:
        outs = [jax.ShapeDtypeStruct((4, width, cols), BF)]
        specs = [pl.BlockSpec((1, width, cols), lambda i, s: (i ^ s[here], 0, 0))]
        scratch = []
    return pl.pallas_call(
        partial(weights_kernel, per),
        grid_spec=pltpu.PrefetchScalarGridSpec(
            num_scalar_prefetch=1,
            grid=(4,),
            in_specs=ins,
            out_specs=specs,
            scratch_shapes=scratch,
        ),
        out_shape=outs,
        compiler_params=params(20),
        cost_estimate=COST,
        name="weight_grads",
    )(place, nbt, gst, gh, act, *more)


def qkv_weights_kernel(per, part, place, own, other, g, *refs):
    near_o, far_o = refs[:2] if per > 1 else (refs[0], None)
    acc = refs[-1]
    half_len = other.shape[0]
    core = place[per]
    rows = 512

    acc[...] = jnp.zeros(acc.shape, F32)

    def step(r, _):
        at = pl.ds(pl.multiple_of(r * rows, rows), rows)
        a = g[pl.ds(pl.multiple_of(core * half_len + r * rows, rows), rows), :]
        b = g[pl.ds(pl.multiple_of((1 - core) * half_len + r * rows, rows), rows), :]
        acc[...] += nn(own[0, at, :].T, a) + nn(other[at, :].T, b)
        return 0

    lax.fori_loop(0, half_len // rows, step, 0)
    for m in range(3):
        split_rows(place, per, acc, slice(m * WIDE, m * WIDE + part), near_o, far_o, (), slice(m * part, (m + 1) * part))


def qkv_weight_grads(place, per, tokens, other, g, part):
    half_len, width = other.shape
    if per > 1:
        shape = (per // 2, width // per, 3 * part)
        outs = [jax.ShapeDtypeStruct(shape, F32), jax.ShapeDtypeStruct(shape, BF)]
    else:
        outs = [jax.ShapeDtypeStruct((width, 3 * part), F32)]
    return pl.pallas_call(
        partial(qkv_weights_kernel, per, part),
        grid_spec=pltpu.PrefetchScalarGridSpec(
            num_scalar_prefetch=1,
            grid=(1,),
            in_specs=[pl.BlockSpec((1, half_len, width), lambda i, s: (s[per], 0, 0)), whole_block(other.shape), whole_block(g.shape)],
            out_specs=[whole_block(o.shape) for o in outs],
            scratch_shapes=[pltpu.VMEM((width, 3 * WIDE), F32)],
        ),
        out_shape=outs,
        compiler_params=params(32),
        cost_estimate=COST,
        name="qkv_weight_grads",
    )(place, tokens, other, g)


def rotation_tables(offsets):
    lane = np.arange(128)
    frequency = (10000.0 ** (-2.0 * (lane % HEAD // 2) / HEAD)).astype(np.float32)
    angles = offsets.astype(F32)[:, None] * frequency[None, :]
    sign = np.where(lane % 2 == 0, -1.0, 1.0).astype(np.float32)
    return jnp.cos(angles), jnp.sin(angles) * sign


def key_bounds(segment):
    length = segment.shape[0]
    first, last = segment[::BLOCK], segment[BLOCK - 1 :: BLOCK]
    low = jnp.sum(segment[None, :] < first[:, None], axis=1)
    high = jnp.sum(segment[None, :] <= last[:, None], axis=1)
    low = low // 128 * 128
    count = (high - low + CHUNK - 1) // CHUNK
    return jnp.stack([jnp.minimum(low, length - CHUNK * count), count], axis=1).reshape(-1).astype(jnp.int32)


def swap_ctx(x):
    return lax.ppermute(x, "ctx", [(0, 1), (1, 0)])


def swap_tp(x, k):
    return lax.ppermute(x, "tp", [(i, i ^ k) for i in range(4)])


def swap_shard(x, k):
    return lax.ppermute(x, "shard", [(i, i ^ k) for i in range(4)])


def order_four(parts, index):
    a, b, c, d = parts
    odd, high = index % 2 == 1, index // 2 == 1
    a, b = jnp.where(odd, b, a), jnp.where(odd, a, b)
    c, d = jnp.where(odd, d, c), jnp.where(odd, c, d)
    return jnp.stack([jnp.where(high, c, a), jnp.where(high, d, b), jnp.where(high, a, c), jnp.where(high, b, d)])


def after(x, *others):
    return lax.optimization_barrier((x, others))[0]


def sum_shard(x):
    if lax.axis_size("shard") != 4:
        return lax.psum(x, "shard")
    x = x + swap_shard(x, 1)
    return x + swap_shard(x, 2)


def gather_tp(x, half):
    one, two = swap_tp(x, 1), swap_tp(x, 2)
    three = jnp.concatenate([swap_tp(one[:half], 2), swap_tp(two[half:], 1)])
    return [x, one, two, three]


def scatter_tp(parts):
    own, one, two, three = parts
    half = own.shape[0] // 2
    low, high = three[:half].astype(BF), three[half:].astype(BF)
    low, high = swap_tp(low, 2), swap_tp(high, 1)
    one = jnp.concatenate([one[:half] + low.astype(F32), one[half:]]).astype(BF)
    two = jnp.concatenate([two[:half], two[half:] + high.astype(F32)]).astype(BF)
    return own + swap_tp(one, 1).astype(F32) + swap_tp(two, 2).astype(F32)


def three_rows(x):
    high = lax.reduce_precision(x, 8, 7)
    middle = lax.reduce_precision(x - high, 8, 7)
    return jnp.stack([high, middle, x - high - middle]).astype(BF)


def contract_last(left, right):
    return lax.dot_general(left, right, (((1,), (1,)), ((), ())), preferred_element_type=F32)


def body(tokens, segment_ids, offsets, qkv_weight, out_weight, ffn_weight, qkv_bias, ffn_bias, norm_gain, shift_params, out_grad):
    t, c, z = lax.axis_index("tp"), lax.axis_index("ctx"), lax.axis_index("shard")
    shards = lax.axis_size("shard")
    half_len, width = tokens.shape[1:]
    rows, _, part = qkv_weight.shape
    hidden = ffn_weight.shape[2]
    heads = part // HEAD
    length = 2 * half_len
    share = length // 4
    first_core = c == 0
    direct = shards == 4

    def take(x, index):
        return lax.dynamic_index_in_dim(x, index, 0, keepdims=False)

    def by_core(own, other):
        return jnp.where(first_core, jnp.stack([own, other]), jnp.stack([other, own]))

    hh = hidden // 2
    row = z * 2 + c
    bias_terms = lax.dynamic_slice_in_dim(three_rows(ffn_bias), row * rows, rows, 1).T
    extra = jnp.pad(bias_terms, ((0, 0), (0, 256 - part - 3)))
    gathered = jnp.concatenate([ffn_weight.reshape(rows, 2 * hidden), out_weight, extra], axis=1)
    gathered = lax.all_gather(gathered, ("tp", "shard", "ctx"), axis=0, tiled=True).reshape(4, width, 2 * hidden + 256)
    qkv_rows = qkv_weight.reshape(rows, 3 * part)
    other_tokens = swap_ctx(take(tokens, 1 - c))
    if direct:
        places = [((z ^ j) * 2 + (c ^ f)) * rows for f in (0, 1) for j in range(4)]
        near = [qkv_rows] + [swap_shard(qkv_rows, j) for j in (1, 2, 3)]
        qkv_pieces = [*near, swap_ctx(jnp.stack(near))]
    else:
        places = [jnp.zeros_like(c)]
        qkv_pieces = [lax.all_gather(qkv_rows, ("shard", "ctx"), axis=0, tiled=True)]
    per = len(places)
    place = jnp.stack(places + [c, t]).astype(jnp.int32)
    bias_pad = jnp.pad(qkv_bias, ((0, 0), (0, WIDE - part)))
    vec = jnp.concatenate([norm_gain, shift_params, jnp.zeros((2, width), F32)])

    marks = jnp.stack([segment_ids, offsets])
    marks = by_core(take(marks.swapaxes(0, 1), c), swap_ctx(take(marks.swapaxes(0, 1), 1 - c)))
    segment, places = marks[:, 0].reshape(length), marks[:, 1].reshape(length)
    halves = lambda x: x.reshape(2, 2, share, width)
    here = t // 2 == c
    tok_block = jnp.where(here, take(take(halves(tokens), c), t % 2), take(other_tokens.reshape(2, share, width), t % 2))
    grad_block = halves(out_grad)
    grad_far = swap_ctx(take(take(grad_block, 1 - c), t % 2))
    grad_top = jnp.where(here, take(take(grad_block, c), t % 2), grad_far)

    cosine, sine = rotation_tables(places)
    bounds = key_bounds(segment)
    seg_column = segment[:, None]
    seg_row = jnp.broadcast_to(segment[None, :], (8, length))
    q, k_rows, v_rows, k_turned, qkv_wide = project_qkv(place, qkv_pieces, per, bias_pad, tokens, other_tokens, cosine, sine, part)

    contexts, log_totals = [None] * 4, [None] * 4

    def forward(j, q):
        spot = jnp.concatenate([((t ^ j) * (share // BLOCK))[None].astype(jnp.int32), bounds])
        context, log_totals[j] = attention_forward(spot, q, k_rows, v_rows, seg_column, seg_row, heads, share)
        contexts[j] = swap_tp(context, j) if j else context

    forward(3, q)
    q_next, log_totals[3] = lax.optimization_barrier((q, log_totals[3]))
    forward(1, q_next)
    q_next, log_totals[1], contexts[3] = lax.optimization_barrier((q, log_totals[1], contexts[3]))
    forward(2, q_next)
    q_next, log_totals[2], contexts[1] = lax.optimization_barrier((q, log_totals[2], contexts[1]))
    forward(0, q_next)
    log_total = jnp.concatenate(log_totals, axis=1)
    terms = gathered[:, :, 2 * hidden + part : 2 * hidden + part + 3].astype(F32)
    bias_all = order_four(list(jnp.sum(terms, axis=2)), t)

    (
        layer_out,
        grad_second,
        grad_second_b,
        first_scaled,
        normed_t,
        second_t,
        activated,
        slope,
        root,
        sums_two,
    ) = feed_forward(place, gathered, contexts, tok_block, grad_top, vec, bias_all)

    def finish_spread(full):
        keep, send = take(full, c), take(full, 1 - c)
        return by_core(keep, swap_ctx(send))

    out_blocks = [layer_out, swap_tp(layer_out, 1), swap_tp(layer_out, 2)]

    grad_first, first_t, g0, g1, g2, g3, grad_hidden, hidden_sums, sums_one = feed_back(
        place, gathered, grad_second, grad_second_b, first_scaled, slope, root, vec, part
    )
    heads_grads = [g0, swap_tp(g1, 1), swap_tp(g2, 2), swap_tp(g3, 3)]

    contexts = jnp.stack(contexts)
    normed_t, out_blocks = lax.optimization_barrier((normed_t, out_blocks))
    made = weight_grads(place, per, 1, normed_t, second_t, grad_hidden, activated)
    normed_t, made, heads_grads[1] = lax.optimization_barrier((normed_t, made, heads_grads[1]))
    whole = weight_grads(place, 1, 0, normed_t, second_t, grad_hidden, activated, first_t, contexts)[0]
    whole = lax.psum_scatter(whole.reshape(-1, 2 * hh + part), ("tp", "shard", "ctx"), scatter_dimension=0, tiled=True)
    whole = whole.astype(F32)
    grad_heads = jnp.stack(heads_grads)

    spot = jnp.concatenate([(t * (share // BLOCK))[None].astype(jnp.int32), bounds])
    if direct:
        got = swap_ctx(made[1])
        packs = [made[0][k].astype(F32) + got[k].astype(F32) for k in range(4)]
        low, high = packs[3][:2].astype(BF), packs[3][2:].astype(BF)
        grad_heads, low, high = lax.optimization_barrier((grad_heads, low, high))
        low, high = swap_tp(low, 2), swap_tp(high, 1)
    corner = [swap_tp(out_blocks[1][: share // 2], 2), swap_tp(out_blocks[2][share // 2 :], 1)]
    grad_proj, bias_sums = attention_backward(
        spot, q, k_rows, k_turned, v_rows, grad_heads, log_total, seg_column, seg_row, cosine, sine, heads
    )
    proj_blocks = grad_proj.reshape(4, share, 3 * WIDE)
    corner, proj_blocks = lax.optimization_barrier((corner, proj_blocks))
    out_blocks = [*out_blocks, jnp.concatenate(corner)]
    branch = {3: contract_last(take(proj_blocks, t ^ 3), qkv_wide)}
    if direct:
        branch[3], low, high = lax.optimization_barrier((branch[3], low, high))
        one = jnp.concatenate([packs[1][:2] + low.astype(F32), packs[1][2:]]).astype(BF)
        two = jnp.concatenate([packs[2][:2], packs[2][2:] + high.astype(F32)]).astype(BF)
        summed = packs[0] + swap_tp(one, 1).astype(F32) + swap_tp(two, 2).astype(F32)
        total = summed[0]
        for j in (1, 2, 3):
            total = total + swap_shard(summed[j].astype(BF), j).astype(F32)
    else:
        total = lax.psum_scatter(made[0].reshape(-1, 2 * hh), ("tp", "shard", "ctx"), scatter_dimension=0, tiled=True).astype(F32)
    grad_up = jnp.concatenate([whole[:, :hh], total[:, :hh]], axis=1)
    grad_down = jnp.concatenate([whole[:, hh : 2 * hh], total[:, hh:]], axis=1)
    grad_ffn_weight = jnp.stack([grad_up, grad_down], axis=1)
    grad_out_weight = whole[:, 2 * hh :]

    for k in (1, 2, 0):
        branch[k] = contract_last(take(proj_blocks, t ^ k), qkv_wide)
    grad_branch = scatter_tp([branch[k] for k in range(4)])
    grad_blocks = gather_tp((grad_first + grad_branch).astype(BF), share // 2)
    grad_full = order_four(grad_blocks, t).reshape(2, half_len, width)

    grads = qkv_weight_grads(after(place, branch[0]), per, tokens, other_tokens, grad_proj, part)
    if direct:
        summed = grads[0] + swap_ctx(grads[1]).astype(F32)
        total = summed[0]
        for j in (1, 2, 3):
            total = total + swap_shard(summed[j].astype(BF), j).astype(F32)
    else:
        total = lax.psum_scatter(grads[0], ("shard", "ctx"), scatter_dimension=0, tiled=True)
    grad_qkv_weight = total.reshape(rows, 3, part)

    sums = order_four([hidden_sums[k, 0] for k in range(4)], t).reshape(4 * hidden)
    vectors = jnp.stack([sums_one[0], sums_two[0], sums_one[1], sums_two[1], sums_one[2], sums_two[2]])
    mine = bias_sums[0].reshape(3, WIDE)
    others = jnp.where(jnp.arange(4)[:, None, None] == t, mine[None], 0.0)
    small = jnp.concatenate([sums, vectors.reshape(-1), others.reshape(-1)]).reshape(-1, 128)
    for k in (1, 2):
        small = small + swap_tp(small, k)
    small = sum_shard(small + swap_ctx(small))
    cut, end = 4 * hidden // 128, (4 * hidden + 6 * width) // 128
    grad_ffn_bias = take(small[:cut].reshape(4, hidden), t)
    vectors = small[cut:end].reshape(6, width)
    grad_qkv_bias = take(small[end:].reshape(4, 3, WIDE), t)[:, :part]
    outputs = finish_spread(order_four(out_blocks, t).reshape(2, half_len, width))
    grad_tokens = finish_spread(grad_full)
    return (
        outputs,
        grad_tokens,
        grad_qkv_weight,
        grad_out_weight,
        grad_ffn_weight,
        grad_qkv_bias,
        grad_ffn_bias,
        vectors[:2],
        vectors[2:],
    )


def solution(mesh):
    return jax.shard_map(
        body,
        mesh=mesh,
        in_specs=(
            P("shard", "ctx", None),
            P("shard", "ctx"),
            P("shard", "ctx"),
            P(("shard", "ctx"), None, "tp"),
            P(("shard", "ctx"), "tp"),
            P(("shard", "ctx"), None, "tp"),
            P(None, "tp"),
            P("tp"),
            P(),
            P(),
            P("shard", "ctx", None),
        ),
        out_specs=(
            P("shard", "ctx", None),
            P("shard", "ctx", None),
            P(("shard", "ctx"), None, "tp"),
            P(("shard", "ctx"), "tp"),
            P(("shard", "ctx"), None, "tp"),
            P(None, "tp"),
            P("tp"),
            P(),
            P(),
        ),
        check_vma=False,
    )
```

```python
from functools import partial

import jax
import jax.numpy as jnp
import numpy as np
from jax import lax
from jax.experimental import pallas as pl
from jax.experimental.pallas import tpu as pltpu
from jax.sharding import PartitionSpec as P

HEAD = 64
WIDE = 256
BLOCK = 256
CHUNK = 256
EPSILON = 1e-12
F32 = jnp.float32
BF = jnp.bfloat16
NEG = -1e30
COST = pl.CostEstimate(flops=0, bytes_accessed=0, transcendentals=0)


def swap_pairs(x):
    lane = lax.broadcasted_iota(jnp.int32, x.shape, 1)
    n = x.shape[1]
    return jnp.where(lane % 2 == 0, pltpu.roll(x, n - 1, 1), pltpu.roll(x, 1, 1))


def nt(a, b):
    return lax.dot_general(a, b, (((1,), (1,)), ((), ())), preferred_element_type=F32)


def nn(a, b):
    return lax.dot_general(a, b, (((1,), (0,)), ((), ())), preferred_element_type=F32)


def twice(x):
    return jnp.concatenate([x, x], axis=1)


def lanes_of_heads(x, heads):
    lane = lax.broadcasted_iota(jnp.int32, x.shape, 1) // HEAD
    return [jnp.where(lane == h, x, jnp.zeros_like(x)) for h in range(heads)]


def whole_block(shape, buffers=1):
    return pl.BlockSpec(shape, lambda *_: (0,) * len(shape), pipeline_mode=pl.Buffered(buffers))


def smem():
    return pl.BlockSpec(memory_space=pltpu.SMEM)


def params(mib):
    return pltpu.CompilerParams(dimension_semantics=("arbitrary",), vmem_limit_bytes=mib * 1024 * 1024)


def qkv_kernel(count, per, part, place, *refs):
    pieces = []
    for x in refs[:count]:
        pieces += [x] if len(x.shape) == 2 else [x.at[n] for n in range(x.shape[0])]
    bias, own, other, cos, sin, q_o, k_o, v_o, kt_o, w_o = refs[count:]
    piece_rows = pieces[0].shape[0]
    pad = jnp.zeros((piece_rows, WIDE - part), BF)
    for n in range(per):
        sl = pl.ds(pl.multiple_of(place[n], 16), piece_rows)
        for m in range(3):
            w_o[sl, m * WIDE : (m + 1) * WIDE] = jnp.concatenate([pieces[n][:, m * part : (m + 1) * part], pad], axis=1)
    half_len = other.shape[0]

    def run(x, sl):
        c, s = twice(cos[sl, :]), twice(sin[sl, :])
        p = nn(x, w_o[:, 0:WIDE]) + bias[0:1, :]
        q_o[sl, :] = ((p * c + swap_pairs(p) * s).astype(BF).astype(F32) * (HEAD**-0.5)).astype(BF)
        p = nn(x, w_o[:, WIDE : 2 * WIDE]) + bias[1:2, :]
        k = (p * c + swap_pairs(p) * s).astype(BF)
        k_o[sl, :] = k
        kt_o[:, sl] = k.T
        v_o[sl, :] = (nn(x, w_o[:, 2 * WIDE : 3 * WIDE]) + bias[2:3, :]).astype(BF)

    def step(r, _):
        rows = pl.ds(pl.multiple_of(r * BLOCK, BLOCK), BLOCK)
        core = place[per]
        run(own[0, rows, :], pl.ds(pl.multiple_of(core * half_len + r * BLOCK, BLOCK), BLOCK))
        run(other[rows, :], pl.ds(pl.multiple_of((1 - core) * half_len + r * BLOCK, BLOCK), BLOCK))
        return 0

    lax.fori_loop(0, half_len // BLOCK, step, 0)


def project_qkv(place, pieces, per, bias, tokens, other, cos, sin, part):
    half_len, width = other.shape
    length, count = 2 * half_len, len(pieces)
    return pl.pallas_call(
        partial(qkv_kernel, count, per, part),
        grid_spec=pltpu.PrefetchScalarGridSpec(
            num_scalar_prefetch=1,
            grid=(1,),
            in_specs=[whole_block(p.shape) for p in pieces]
            + [whole_block(bias.shape), pl.BlockSpec((1, half_len, width), lambda i, s: (s[per], 0, 0))]
            + [whole_block(x.shape) for x in (other, cos, sin)],
            out_specs=[whole_block((length, WIDE))] * 3 + [whole_block((WIDE, length)), whole_block((width, 3 * WIDE))],
        ),
        out_shape=[jax.ShapeDtypeStruct((length, WIDE), BF)] * 3
        + [jax.ShapeDtypeStruct((WIDE, length), BF), jax.ShapeDtypeStruct((width, 3 * WIDE), BF)],
        compiler_params=params(32),
        cost_estimate=COST,
        name="project_qkv",
    )(place, *pieces, bias, tokens, other, cos, sin)


def forward_kernel(heads, place, q, k, v, segc, segr, ctx_o, lse_o, acc, s_sc, m_sc, l_sc, qc_sc):
    i = place[0] + pl.program_id(0)
    start, count = place[1 + 2 * i], place[2 + 2 * i]
    qc_sc[...] = jnp.concatenate(lanes_of_heads(q[...], heads), axis=0)
    seg_q = segc[...]
    m_sc[...] = jnp.full(m_sc.shape, NEG, F32)
    l_sc[...] = jnp.zeros(l_sc.shape, F32)

    def at(j):
        return pl.ds(pl.multiple_of(start + j * CHUNK, 128), CHUNK)

    def of(h):
        return slice(h * BLOCK, (h + 1) * BLOCK)

    def pass1(j, _):
        s = nt(qc_sc[...], k[at(j), :])
        keep = seg_q == segr[0:1, at(j)]
        for h in range(heads):
            sh = jnp.where(keep, s[of(h), :], NEG)
            s_sc[j, of(h), :] = sh
            m_sc[of(h), :] = jnp.maximum(m_sc[of(h), :], jnp.maximum(sh[:, :128], sh[:, 128:]))
        return 0

    lax.fori_loop(0, count, pass1, 0)
    m_sc[...] = jnp.broadcast_to(jnp.max(m_sc[...], axis=1, keepdims=True), m_sc.shape)

    def pass2(j, _):
        for h in range(heads):
            e = jnp.exp(s_sc[j, of(h), :] - twice(m_sc[of(h), :]))
            s_sc[j, of(h), :] = e
            l_sc[of(h), :] += e[:, :128] + e[:, 128:]
        return 0

    lax.fori_loop(0, count, pass2, 0)
    total = jnp.sum(l_sc[...], axis=1, keepdims=True)
    lse = m_sc[:, 0:1] + jnp.log(total)
    l_sc[...] = jnp.broadcast_to(1.0 / total, l_sc.shape)
    lane = lax.broadcasted_iota(jnp.int32, (BLOCK, 128), 1)
    tile = jnp.zeros((BLOCK, 128), F32)
    for h in range(heads):
        tile = jnp.where(lane == h, lse[of(h), :], tile)
    lse_o[...] = tile.T[0:8, :]
    acc[...] = jnp.zeros(acc.shape, F32)

    def pass3(j, _):
        ps = [(s_sc[j, of(h), :] * twice(l_sc[of(h), :])).astype(BF) for h in range(heads)]
        acc[...] += nn(jnp.concatenate(ps, axis=1), jnp.concatenate(lanes_of_heads(v[at(j), :], heads), axis=0))
        return 0

    lax.fori_loop(0, count, pass3, 0)
    ctx_o[...] = acc[:, : heads * HEAD].astype(BF)


def attention_forward(place, q, k, v, segc, segr, heads, share):
    length = q.shape[0]
    grid = share // BLOCK
    rows = lambda i, s: (s[0] + i, 0)
    return pl.pallas_call(
        partial(forward_kernel, heads),
        grid_spec=pltpu.PrefetchScalarGridSpec(
            num_scalar_prefetch=1,
            grid=(grid,),
            in_specs=[
                pl.BlockSpec((BLOCK, WIDE), rows),
                whole_block(k.shape),
                whole_block(v.shape),
                pl.BlockSpec((BLOCK, 1), rows),
                whole_block(segr.shape),
            ],
            out_specs=[pl.BlockSpec((BLOCK, heads * HEAD), lambda i, s: (i, 0)), pl.BlockSpec((8, BLOCK), lambda i, s: (0, i))],
            scratch_shapes=[
                pltpu.VMEM((BLOCK, WIDE), F32),
                pltpu.VMEM((length // CHUNK, heads * BLOCK, CHUNK), F32),
                pltpu.VMEM((heads * BLOCK, 128), F32),
                pltpu.VMEM((heads * BLOCK, 128), F32),
                pltpu.VMEM((heads * BLOCK, WIDE), BF),
            ],
        ),
        out_shape=[jax.ShapeDtypeStruct((share, heads * HEAD), BF), jax.ShapeDtypeStruct((8, share), F32)],
        compiler_params=params(16),
        cost_estimate=COST,
        name="attention_forward",
    )(place, q, k, v, segc, segr)


def backward_kernel(heads, place, q, k, kt, v, do, lse, segc, segr, cos, sin, g_o, gb_o, dk_sc, dv_sc, qc_sc, dc_sc, dq_sc, p_sc, dp_sc, dl_sc):
    step_at = pl.program_id(0)
    i = step_at ^ place[0]
    length = k.shape[0]

    @pl.when(step_at == 0)
    def _():
        dk_sc[...] = jnp.zeros(dk_sc.shape, F32)
        dv_sc[...] = jnp.zeros(dv_sc.shape, F32)
        gb_o[...] = jnp.zeros(gb_o.shape, F32)

    start, count = place[1 + 2 * i], place[2 + 2 * i]
    qc_sc[...] = jnp.concatenate(lanes_of_heads(q[...], heads), axis=0)
    d = do[0]
    d = jnp.concatenate([d, jnp.zeros((BLOCK, WIDE - d.shape[1]), BF)], axis=1)
    dc_sc[...] = jnp.concatenate(lanes_of_heads(d, heads), axis=0)
    dq_sc[...] = jnp.zeros(dq_sc.shape, F32)
    own = pl.ds(pl.multiple_of(i * BLOCK, BLOCK), BLOCK)
    seg_q = segr[0:1, own]
    dl_sc[...] = jnp.zeros(dl_sc.shape, F32)

    def at(j):
        return pl.ds(pl.multiple_of(start + j * CHUNK, 128), CHUNK)

    def of(h):
        return slice(h * BLOCK, (h + 1) * BLOCK)

    def pass1(j, _):
        s = nt(k[at(j), :], qc_sc[...])
        dp = nt(v[at(j), :], dc_sc[...])
        keep = segc[at(j), :] == seg_q
        for h in range(heads):
            p = jnp.exp(jnp.where(keep, s[:, of(h)], NEG) - lse[h : h + 1, :])
            p_sc[j, :, of(h)] = p
            dp_sc[j, :, of(h)] = dp[:, of(h)]
            dl_sc[:, of(h)] += jnp.sum((p * dp[:, of(h)]).reshape(CHUNK // 8, 8, BLOCK), axis=0)
        return 0

    lax.fori_loop(0, count, pass1, 0)
    delta = jnp.sum(dl_sc[...], axis=0, keepdims=True)

    def pass2(j, _):
        ps, dss = [], []
        for h in range(heads):
            p = p_sc[j, :, of(h)]
            ds = (p * (dp_sc[j, :, of(h)] - delta[:, of(h)])).astype(BF)
            ps.append(p.astype(BF))
            dss.append(ds)
            dq_sc[h * HEAD : (h + 1) * HEAD, :] += nn(kt[h * HEAD : (h + 1) * HEAD, at(j)], ds)
        dv_sc[at(j), :] += nn(jnp.concatenate(ps, axis=1), dc_sc[...])
        dk_sc[at(j), :] += nn(jnp.concatenate(dss, axis=1), qc_sc[...])
        return 0

    lax.fori_loop(0, count, pass2, 0)

    def turn(x, sl):
        return (x * twice(cos[sl, :]) - swap_pairs(x) * twice(sin[sl, :])).astype(BF)

    def put(x, sl, m):
        g_o[sl, m * WIDE : (m + 1) * WIDE] = x
        gb_o[0:1, m * WIDE : (m + 1) * WIDE] += jnp.sum(x.astype(F32), axis=0, keepdims=True)

    put(turn(dq_sc[...].T * (HEAD**-0.5), own), own, 0)

    @pl.when(step_at == pl.num_programs(0) - 1)
    def _():
        def last(r, _):
            sl = pl.ds(pl.multiple_of(r * BLOCK, BLOCK), BLOCK)
            put(turn(dk_sc[sl, :], sl), sl, 1)
            put(dv_sc[sl, :].astype(BF), sl, 2)
            return 0

        lax.fori_loop(0, length // BLOCK, last, 0)


def attention_backward(place, q, k, kt, v, do, lse, segc, segr, cos, sin, heads):
    length = k.shape[0]
    steps, per = length // BLOCK, do.shape[1] // BLOCK
    return pl.pallas_call(
        partial(backward_kernel, heads),
        grid_spec=pltpu.PrefetchScalarGridSpec(
            num_scalar_prefetch=1,
            grid=(steps,),
            in_specs=[
                pl.BlockSpec((BLOCK, WIDE), lambda i, s: (i ^ s[0], 0)),
                whole_block(k.shape),
                whole_block(kt.shape),
                whole_block(v.shape),
                pl.BlockSpec((1, BLOCK, heads * HEAD), lambda i, s: (i // per, i % per, 0)),
                pl.BlockSpec((8, BLOCK), lambda i, s: (0, i)),
                whole_block(segc.shape),
                whole_block(segr.shape),
                whole_block(cos.shape),
                whole_block(sin.shape),
            ],
            out_specs=[whole_block((length, 3 * WIDE)), whole_block((8, 3 * WIDE))],
            scratch_shapes=[pltpu.VMEM((length, WIDE), F32)] * 2
            + [pltpu.VMEM((heads * BLOCK, WIDE), BF)] * 2
            + [pltpu.VMEM((WIDE, BLOCK), F32)]
            + [pltpu.VMEM((length // CHUNK, CHUNK, heads * BLOCK), F32)] * 2
            + [pltpu.VMEM((8, heads * BLOCK), F32)],
        ),
        out_shape=[jax.ShapeDtypeStruct((length, 3 * WIDE), BF), jax.ShapeDtypeStruct((8, 3 * WIDE), F32)],
        compiler_params=params(32),
        cost_estimate=COST,
        name="attention_backward",
    )(place, q, k, kt, v, do, lse, segc, segr, cos, sin)


def out_copies(place, gathered, w_out, sems):
    here = place[place.shape[0] - 1]
    feed = gathered.shape[2] - w_out.shape[2]
    return [pltpu.make_async_copy(gathered.at[here ^ k, :, feed:], w_out.at[k], sems.at[k]) for k in range(4)]


def row_mean(x):
    return jnp.mean(x, axis=1, keepdims=True)


def gelu_parts(x):
    e = jnp.exp(x * x * -0.5)
    t = 1.0 / (1.0 + (0.3275911 * 0.7071067811865476) * jnp.abs(x))
    p = t * (0.254829592 + t * (-0.284496736 + t * (1.421413741 + t * (-1.453152027 + t * 1.061405429))))
    tail = 0.5 * p * e
    phi = jnp.where(x >= 0, 1.0 - tail, tail)
    return phi, phi + x * e * 0.3989422804014327


ROWS = 256


def feed_kernel(place, gathered, w, c0, c1, c2, c3, tokb, gtop, vec, bias, *refs):
    (out_o, gs_o, gsb_o, fs_o, nbt_o, gst_o, act_o, gp_o, root_o, sum_o, nb_o, w_out, acc, normed, sems) = refs
    copies = out_copies(place, gathered, w_out, sems)
    k = pl.program_id(0)
    share = tokb.shape[0]
    part = c0.shape[1]
    chunks = [pl.ds(r * ROWS, ROWS) for r in range(share // ROWS)]

    @pl.when(k == 0)
    def _():
        for copy in copies:
            copy.start()
        for copy in copies:
            copy.wait()
        for sl in chunks:
            x = tokb[sl, :].astype(F32) + vec[4:5, :]
            for n, ctx in enumerate((c0, c1, c2, c3)):
                x = x + nt(ctx[sl, :], w_out[n, :, 0:part])
            x = x - row_mean(x)
            root = lax.rsqrt(row_mean(x * x) + EPSILON)
            x = x * root
            fs_o[sl, :] = x
            root_o[sl, :] = jnp.broadcast_to(root, (ROWS, 128))
            y = x * vec[0:1, :] + vec[2:3, :]
            normed[sl, :] = y
            nb_o[sl, :] = y.astype(BF)
            nbt_o[:, sl] = y.astype(BF).T
            acc[sl, :] = y + vec[5:6, :]

    hidden = act_o.shape[2]

    def rows_step(r, _):
        sl = pl.ds(pl.multiple_of(r * ROWS, ROWS), ROWS)
        h = nn(nb_o[sl, :], w[0, :, 0:hidden]) + bias[pl.ds(k, 1), :]
        phi, slope = gelu_parts(h)
        a = (h * phi).astype(BF)
        act_o[0, sl, :] = a
        gp_o[0, sl, :] = slope
        acc[sl, :] += nt(a, w[0, :, hidden:])
        return 0

    lax.fori_loop(0, share // ROWS, rows_step, 0, unroll=True)

    @pl.when(k == 3)
    def _():
        total = [jnp.zeros((1, tokb.shape[1]), F32)] * 3
        for sl in chunks:
            x = acc[sl, :]
            x = x - row_mean(x)
            root = lax.rsqrt(row_mean(x * x) + EPSILON)
            x = x * root
            out_o[sl, :] = (x * vec[1:2, :] + vec[3:4, :]).astype(BF)
            g = gtop[sl, :].astype(F32)
            gg = g * vec[1:2, :]
            gs = root * (gg - row_mean(gg) - x * row_mean(gg * x))
            gs_o[sl, :] = gs
            gsb_o[sl, :] = gs.astype(BF)
            gst_o[:, sl] = gs.astype(BF).T
            for n, y in enumerate((g * x, g, gs)):
                total[n] = total[n] + jnp.sum(y, axis=0, keepdims=True)
        sum_o[...] = jnp.concatenate(total + [jnp.zeros((5, tokb.shape[1]), F32)], axis=0)


def feed_specs(place, gathered, hidden):
    width, last = gathered.shape[1], place.shape[0] - 1
    return [pl.BlockSpec(memory_space=pl.ANY), pl.BlockSpec((1, width, 2 * hidden), lambda i, s: (s[last] ^ i, 0, 0))]


def feed_forward(place, gathered, contexts, tokb, gtop, vec, bias):
    share, width = tokb.shape
    hidden = bias.shape[1]
    block = lambda: pl.BlockSpec((1, share, hidden), lambda i, s: (i, 0, 0))
    sd, far = jax.ShapeDtypeStruct, pltpu.HBM
    return pl.pallas_call(
        feed_kernel,
        grid_spec=pltpu.PrefetchScalarGridSpec(
            num_scalar_prefetch=1,
            grid=(4,),
            in_specs=feed_specs(place, gathered, hidden) + [whole_block(x.shape) for x in (*contexts, tokb, gtop, vec, bias)],
            out_specs=[whole_block((share, width))] * 4
            + [whole_block((width, share))] * 2
            + [block(), block(), whole_block((share, 128)), whole_block((8, width))],
            scratch_shapes=[
                pltpu.VMEM((share, width), BF),
                pltpu.VMEM((4, width, gathered.shape[2] - 2 * hidden), BF),
                pltpu.VMEM((share, width), F32),
                pltpu.VMEM((share, width), F32),
                pltpu.SemaphoreType.DMA((4,)),
            ],
        ),
        out_shape=[
            sd((share, width), BF),
            sd((share, width), F32),
            sd((share, width), BF),
            sd((share, width), F32),
            far((width, share), BF),
            far((width, share), BF),
            far((4, share, hidden), BF),
            far((4, share, hidden), F32),
            sd((share, 128), F32),
            sd((8, width), F32),
        ],
        compiler_params=params(32),
        cost_estimate=COST,
        name="feed_forward",
    )(place, gathered, gathered, *contexts, tokb, gtop, vec, bias)


def feed_back_kernel(place, gathered, w, gs, gsb, fs, gp, root, vec, *refs):
    (gf_o, gft_o, gc0, gc1, gc2, gc3, gh_o, ghs_o, sum_o, w_out, acc, sems) = refs
    copies = out_copies(place, gathered, w_out, sems)
    k = pl.program_id(0)
    share, width = gs.shape
    hidden, part = gh_o.shape[2], gc0.shape[1]

    @pl.when(k == 0)
    def _():
        for copy in copies:
            copy.start()
        acc[...] = gs[...]

    def rows_step(r, total):
        sl = pl.ds(pl.multiple_of(r * ROWS, ROWS), ROWS)
        g = (nn(gsb[sl, :], w[0, :, hidden:]) * gp[0, sl, :]).astype(BF)
        gh_o[0, sl, :] = g
        acc[sl, :] += nt(g, w[0, :, 0:hidden])
        return total + jnp.sum(g.astype(F32), axis=0, keepdims=True)

    total = lax.fori_loop(0, share // ROWS, rows_step, jnp.zeros((1, hidden), F32), unroll=True)
    ghs_o[0] = jnp.broadcast_to(total, (8, hidden))

    @pl.when(k == 3)
    def _():
        for copy in copies:
            copy.wait()
        sums = [jnp.zeros((1, width), F32)] * 3
        for r in range(share // ROWS):
            sl = pl.ds(r * ROWS, ROWS)
            gn = acc[sl, :]
            x = fs[sl, :]
            gg = gn * vec[0:1, :]
            gf = root[sl, 0:1] * (gg - row_mean(gg) - x * row_mean(gg * x))
            gf_o[sl, :] = gf
            b = gf.astype(BF)
            gft_o[:, sl] = b.T
            for n, o in enumerate((gc0, gc1, gc2, gc3)):
                o[sl, :] = nn(b, w_out[n, :, 0:part]).astype(BF)
            for n, y in enumerate((gn * x, gn, gf)):
                sums[n] = sums[n] + jnp.sum(y, axis=0, keepdims=True)
        sum_o[...] = jnp.concatenate(sums + [jnp.zeros((5, width), F32)], axis=0)


def feed_back(place, gathered, gs, gsb, fs, gp, root, vec, part):
    share, width = gs.shape
    hidden = gp.shape[2]
    block = lambda: pl.BlockSpec((1, share, hidden), lambda i, s: (i, 0, 0))
    sd, far = jax.ShapeDtypeStruct, pltpu.HBM
    return pl.pallas_call(
        feed_back_kernel,
        grid_spec=pltpu.PrefetchScalarGridSpec(
            num_scalar_prefetch=1,
            grid=(4,),
            in_specs=feed_specs(place, gathered, hidden)
            + [whole_block(gs.shape), whole_block(gsb.shape), whole_block(fs.shape), block(), whole_block(root.shape), whole_block(vec.shape)],
            out_specs=[whole_block((share, width)), whole_block((width, share))]
            + [whole_block((share, part))] * 4
            + [block(), pl.BlockSpec((1, 8, hidden), lambda i, s: (i, 0, 0)), whole_block((8, width))],
            scratch_shapes=[
                pltpu.VMEM((4, width, gathered.shape[2] - 2 * hidden), BF),
                pltpu.VMEM((share, width), F32),
                pltpu.SemaphoreType.DMA((4,)),
            ],
        ),
        out_shape=[far((share, width), F32), far((width, share), BF)]
        + [sd((share, part), BF)] * 4
        + [far((4, share, hidden), BF), sd((4, 8, hidden), F32), sd((8, width), F32)],
        compiler_params=params(28),
        cost_estimate=COST,
        name="feed_back",
    )(place, gathered, gathered, gs, gsb, fs, gp, root, vec)


def split_rows(place, per, acc, source, near_o, far_o, lead, cols):
    if per == 1:
        near_o[(*lead, slice(None), cols)] = acc[:, source].astype(near_o.dtype)
        return
    rows = acc.shape[0] // per
    for n in range(per // 2):
        near, far = (pl.ds(pl.multiple_of(place[m], 16), rows) for m in (n, per // 2 + n))
        near_o[(*lead, n, slice(None), cols)] = acc[near, source].astype(near_o.dtype)
        far_o[(*lead, n, slice(None), cols)] = acc[far, source].astype(BF)


def weights_kernel(per, place, nbt, gst, gft, ctx, gh, act, *refs):
    hh = gh.shape[2] // 2
    if per > 1:
        near_o, far_o, out, acc = refs
    else:
        other, out = refs
    for n, (left, right) in enumerate(((nbt, gh), (gst, act))):
        made = nn(left[...], right[0])
        out[0, :, n * hh : (n + 1) * hh] = made[:, 0:hh].astype(BF)
        if per > 1:
            acc[...] = made[:, hh:]
            split_rows(place, per, acc, slice(None), near_o, far_o, (0,), slice(n * hh, (n + 1) * hh))
        else:
            other[0, :, n * hh : (n + 1) * hh] = made[:, hh:].astype(BF)
    out[0, :, 2 * hh :] = nn(gft[...], ctx[0]).astype(BF)


def weight_grads(place, per, nbt, gst, gft, contexts, gh, act):
    width, share = nbt.shape
    hidden, part = gh.shape[2], contexts.shape[2]
    last = place.shape[0] - 1
    block = lambda cols: pl.BlockSpec((1, share, cols), lambda i, s: (i, 0, 0))
    ordered = lambda cols: pl.BlockSpec((1, width, cols), lambda i, s: (i ^ s[last], 0, 0))
    if per > 1:
        shape = (4, per // 2, width // per, hidden)
        outs = [jax.ShapeDtypeStruct(shape, BF)] * 2
        specs = [pl.BlockSpec((1,) + shape[1:], lambda i, s: (i, 0, 0, 0))] * 2
        scratch = [pltpu.VMEM((width, hidden // 2), F32)]
    else:
        outs = [jax.ShapeDtypeStruct((4, width, hidden), BF)]
        specs = [ordered(hidden)]
        scratch = []
    return pl.pallas_call(
        partial(weights_kernel, per),
        grid_spec=pltpu.PrefetchScalarGridSpec(
            num_scalar_prefetch=1,
            grid=(4,),
            in_specs=[whole_block(x.shape) for x in (nbt, gst, gft)] + [block(part), block(hidden), block(hidden)],
            out_specs=specs + [ordered(hidden + part)],
            scratch_shapes=scratch,
        ),
        out_shape=outs + [jax.ShapeDtypeStruct((4, width, hidden + part), BF)],
        compiler_params=params(58),
        cost_estimate=COST,
        name="weight_grads",
    )(place, nbt, gst, gft, contexts, gh, act)


def qkv_weights_kernel(per, part, place, own, other, g, *refs):
    near_o, far_o = refs[:2] if per > 1 else (refs[0], None)
    acc = refs[-1]
    half_len = other.shape[0]
    core = place[per]
    rows = 512

    acc[...] = jnp.zeros(acc.shape, F32)

    def step(r, _):
        at = pl.ds(pl.multiple_of(r * rows, rows), rows)
        a = g[pl.ds(pl.multiple_of(core * half_len + r * rows, rows), rows), :]
        b = g[pl.ds(pl.multiple_of((1 - core) * half_len + r * rows, rows), rows), :]
        acc[...] += nn(own[0, at, :].T, a) + nn(other[at, :].T, b)
        return 0

    lax.fori_loop(0, half_len // rows, step, 0)
    for m in range(3):
        split_rows(place, per, acc, slice(m * WIDE, m * WIDE + part), near_o, far_o, (), slice(m * part, (m + 1) * part))


def qkv_weight_grads(place, per, tokens, other, g, part):
    half_len, width = other.shape
    if per > 1:
        shape = (per // 2, width // per, 3 * part)
        outs = [jax.ShapeDtypeStruct(shape, F32), jax.ShapeDtypeStruct(shape, BF)]
    else:
        outs = [jax.ShapeDtypeStruct((width, 3 * part), F32)]
    return pl.pallas_call(
        partial(qkv_weights_kernel, per, part),
        grid_spec=pltpu.PrefetchScalarGridSpec(
            num_scalar_prefetch=1,
            grid=(1,),
            in_specs=[pl.BlockSpec((1, half_len, width), lambda i, s: (s[per], 0, 0)), whole_block(other.shape), whole_block(g.shape)],
            out_specs=[whole_block(o.shape) for o in outs],
            scratch_shapes=[pltpu.VMEM((width, 3 * WIDE), F32)],
        ),
        out_shape=outs,
        compiler_params=params(32),
        cost_estimate=COST,
        name="qkv_weight_grads",
    )(place, tokens, other, g)


def branch_kernel(place, *refs):
    count = (len(refs) - 1) // 2
    w = refs[count]
    for g, o in zip(refs[:count], refs[count + 1 :]):
        rows = 256
        for r in range(g.shape[0] // rows):
            sl = slice(r * rows, (r + 1) * rows)
            o[sl, :] = nt(g[sl, :], w[...]).astype(o.dtype)


def branch(place, blocks, kinds, g, w):
    share, last = g.shape[0] // 4, place.shape[0] - 1
    return pl.pallas_call(
        branch_kernel,
        grid_spec=pltpu.PrefetchScalarGridSpec(
            num_scalar_prefetch=1,
            grid=(1,),
            in_specs=[pl.BlockSpec((share, g.shape[1]), lambda i, s, k=k: (s[last] ^ k, 0)) for k in blocks] + [whole_block(w.shape)],
            out_specs=[whole_block((share, w.shape[0]))] * len(blocks),
        ),
        out_shape=[jax.ShapeDtypeStruct((share, w.shape[0]), kind) for kind in kinds],
        compiler_params=params(24),
        cost_estimate=COST,
        name="branch",
    )(place, *[g] * len(blocks), w)


def split_kernel(place, *refs):
    keep, send, last = refs[5], refs[6], place.shape[0] - 1
    share = refs[0].shape[0]
    core, here = place[last - 1], place[last]

    def put(out, sl, k):
        if k < 3:
            out[sl, :] = refs[k][...]
        else:
            half = share // 2
            out[pl.ds(pl.multiple_of(sl.start, half), half), :] = refs[3][...]
            out[pl.ds(pl.multiple_of(sl.start + half, half), half), :] = refs[4][...]

    for k in range(4):
        owner = here ^ k
        sl = pl.ds(pl.multiple_of(owner % 2 * share, share), share)
        mine = owner // 2 == core

        @pl.when(mine)
        def _(k=k, sl=sl):
            put(keep, sl, k)

        @pl.when(jnp.logical_not(mine))
        def _(k=k, sl=sl):
            put(send, sl, k)


def split_halves(place, blocks):
    share, width = blocks[0].shape
    shape = (2 * share, width)
    return pl.pallas_call(
        split_kernel,
        grid_spec=pltpu.PrefetchScalarGridSpec(
            num_scalar_prefetch=1,
            grid=(1,),
            in_specs=[whole_block(x.shape) for x in blocks],
            out_specs=[whole_block(shape)] * 2,
        ),
        out_shape=[jax.ShapeDtypeStruct(shape, blocks[0].dtype)] * 2,
        compiler_params=params(12),
        cost_estimate=COST,
        name="split_halves",
    )(place, *blocks)


def join_kernel(place, keep, other, out):
    @pl.when(pl.program_id(0) == place[place.shape[0] - 2])
    def _():
        out[0] = keep[...]

    @pl.when(pl.program_id(0) != place[place.shape[0] - 2])
    def _():
        out[0] = other[...]


def join_halves(place, keep, other):
    return pl.pallas_call(
        join_kernel,
        grid_spec=pltpu.PrefetchScalarGridSpec(
            num_scalar_prefetch=1,
            grid=(2,),
            in_specs=[whole_block(keep.shape), whole_block(other.shape)],
            out_specs=pl.BlockSpec((1,) + keep.shape, lambda i, s: (i, 0, 0)),
        ),
        out_shape=jax.ShapeDtypeStruct((2,) + keep.shape, keep.dtype),
        compiler_params=params(16),
        cost_estimate=COST,
        name="join_halves",
    )(place, keep, other)


def collect_kernel(place, hidden_sums, one, two, bias, out):
    here = place[place.shape[0] - 1]
    out[...] = jnp.zeros(out.shape, F32)
    for k in range(4):
        out[pl.ds(here ^ k, 1), :] = hidden_sums[k, 0:1, :]
    for n, (x, row) in enumerate(((one, 0), (two, 0), (one, 1), (two, 1), (one, 2), (two, 2))):
        out[4 + n : 5 + n, :] = x[row : row + 1, :]
    out[pl.ds(10 + here, 1), :] = bias[0:1, :]


def collect(place, hidden_sums, one, two, bias):
    return pl.pallas_call(
        collect_kernel,
        grid_spec=pltpu.PrefetchScalarGridSpec(
            num_scalar_prefetch=1,
            grid=(1,),
            in_specs=[whole_block(x.shape) for x in (hidden_sums, one, two, bias)],
            out_specs=whole_block((16, one.shape[1])),
        ),
        out_shape=jax.ShapeDtypeStruct((16, one.shape[1]), F32),
        compiler_params=params(8),
        cost_estimate=COST,
        name="collect",
    )(place, hidden_sums, one, two, bias)


def settle_kernel(count, *refs):
    ins, outs = refs[:count], refs[count:]
    for j, out in enumerate(outs):
        total = ins[0][j].astype(F32)
        for x in ins[1:]:
            total = total + x[j].astype(F32)
        out[...] = total.astype(out.dtype)


def settle(*stacks):
    shape = stacks[0].shape
    vmem = pl.BlockSpec(memory_space=pltpu.VMEM)
    return pl.pallas_call(
        partial(settle_kernel, len(stacks)),
        in_specs=[vmem] * len(stacks),
        out_specs=[vmem] * shape[0],
        out_shape=[jax.ShapeDtypeStruct(shape[1:], F32 if j == 0 else BF) for j in range(shape[0])],
        compiler_params=pltpu.CompilerParams(vmem_limit_bytes=16 * 1024 * 1024),
        cost_estimate=COST,
        name="settle",
    )(*stacks)


def finish_kernel(*refs):
    out = refs[-1]
    total = refs[0][...]
    for x in refs[1:-1]:
        total = total + x[...].astype(F32)
    out[...] = total


def finish(*parts):
    vmem = pl.BlockSpec(memory_space=pltpu.VMEM)
    return pl.pallas_call(
        finish_kernel,
        in_specs=[vmem] * len(parts),
        out_specs=vmem,
        out_shape=jax.ShapeDtypeStruct(parts[0].shape, F32),
        compiler_params=pltpu.CompilerParams(vmem_limit_bytes=8 * 1024 * 1024),
        cost_estimate=COST,
        name="finish",
    )(*parts)


def block_kernel(own, first, one, two, out):
    out[...] = (own[...] + first[...] + one[...].astype(F32) + two[...].astype(F32)).astype(BF)


def add_block(own, first, one, two):
    vmem = pl.BlockSpec(memory_space=pltpu.VMEM)
    return pl.pallas_call(
        block_kernel,
        in_specs=[vmem] * 4,
        out_specs=vmem,
        out_shape=jax.ShapeDtypeStruct(own.shape, BF),
        compiler_params=pltpu.CompilerParams(vmem_limit_bytes=12 * 1024 * 1024),
        cost_estimate=COST,
        name="add_block",
    )(own, first, one, two)


def relay_kernel(one, two, low, high, one_o, two_o):
    half = low.shape[0]
    one_o[0:half, :] = (one[0:half, :] + low[...].astype(F32)).astype(BF)
    one_o[half:, :] = one[half:, :].astype(BF)
    two_o[0:half, :] = two[0:half, :].astype(BF)
    two_o[half:, :] = (two[half:, :] + high[...].astype(F32)).astype(BF)


def relay(one, two, low, high):
    return pl.pallas_call(
        relay_kernel,
        in_specs=[pl.BlockSpec(memory_space=pltpu.VMEM)] * 4,
        out_specs=[pl.BlockSpec(memory_space=pltpu.VMEM)] * 2,
        out_shape=[jax.ShapeDtypeStruct(one.shape, BF)] * 2,
        compiler_params=pltpu.CompilerParams(vmem_limit_bytes=16 * 1024 * 1024),
        cost_estimate=COST,
        name="relay",
    )(one, two, low, high)


def rotation_tables(offsets):
    lane = np.arange(128)
    frequency = (10000.0 ** (-2.0 * (lane % HEAD // 2) / HEAD)).astype(np.float32)
    angles = offsets.astype(F32)[:, None] * frequency[None, :]
    sign = np.where(lane % 2 == 0, -1.0, 1.0).astype(np.float32)
    return jnp.cos(angles), jnp.sin(angles) * sign


def key_bounds(segment):
    length = segment.shape[0]
    first, last = segment[::BLOCK], segment[BLOCK - 1 :: BLOCK]
    low = jnp.sum(segment[None, :] < first[:, None], axis=1)
    high = jnp.sum(segment[None, :] <= last[:, None], axis=1)
    low = low // 128 * 128
    count = (high - low + CHUNK - 1) // CHUNK
    return jnp.stack([jnp.minimum(low, length - CHUNK * count), count], axis=1).reshape(-1).astype(jnp.int32)


def swap_ctx(x):
    return lax.ppermute(x, "ctx", [(0, 1), (1, 0)])


def swap_tp(x, k):
    return lax.ppermute(x, "tp", [(i, i ^ k) for i in range(4)])


def swap_shard(x, k):
    return lax.ppermute(x, "shard", [(i, i ^ k) for i in range(4)])


def order_four(parts, index):
    a, b, c, d = parts
    odd, high = index % 2 == 1, index // 2 == 1
    a, b = jnp.where(odd, b, a), jnp.where(odd, a, b)
    c, d = jnp.where(odd, d, c), jnp.where(odd, c, d)
    return jnp.stack([jnp.where(high, c, a), jnp.where(high, d, b), jnp.where(high, a, c), jnp.where(high, b, d)])


def after(x, *others):
    return lax.optimization_barrier((x, others))[0]


def sum_shard(x):
    if lax.axis_size("shard") != 4:
        return lax.psum(x, "shard")
    x = x + swap_shard(x, 1)
    return x + swap_shard(x, 2)


def gather_tp(x, half):
    one, two = swap_tp(x, 1), swap_tp(x, 2)
    three = jnp.concatenate([swap_tp(one[:half], 2), swap_tp(two[half:], 1)])
    return [x, one, two, three]


def scatter_tp(parts):
    own, one, two, three = parts
    half = own.shape[0] // 2
    low, high = three[:half].astype(BF), three[half:].astype(BF)
    low, high = swap_tp(low, 2), swap_tp(high, 1)
    one = jnp.concatenate([one[:half] + low.astype(F32), one[half:]]).astype(BF)
    two = jnp.concatenate([two[:half], two[half:] + high.astype(F32)]).astype(BF)
    return own + swap_tp(one, 1).astype(F32) + swap_tp(two, 2).astype(F32)


def three_rows(x):
    high = lax.reduce_precision(x, 8, 7)
    middle = lax.reduce_precision(x - high, 8, 7)
    return jnp.stack([high, middle, x - high - middle]).astype(BF)


def contract_last(left, right):
    return lax.dot_general(left, right, (((1,), (1,)), ((), ())), preferred_element_type=F32)


def body(tokens, segment_ids, offsets, qkv_weight, out_weight, ffn_weight, qkv_bias, ffn_bias, norm_gain, shift_params, out_grad):
    t, c, z = lax.axis_index("tp"), lax.axis_index("ctx"), lax.axis_index("shard")
    shards = lax.axis_size("shard")
    half_len, width = tokens.shape[1:]
    rows, _, part = qkv_weight.shape
    hidden = ffn_weight.shape[2]
    heads = part // HEAD
    length = 2 * half_len
    share = length // 4
    first_core = c == 0
    direct = shards == 4

    def take(x, index):
        return lax.dynamic_index_in_dim(x, index, 0, keepdims=False)

    def by_core(own, other):
        return jnp.where(first_core, jnp.stack([own, other]), jnp.stack([other, own]))

    hh = hidden // 2
    row = z * 2 + c
    bias_terms = lax.dynamic_slice_in_dim(three_rows(ffn_bias), row * rows, rows, 1).T
    extra = jnp.pad(bias_terms, ((0, 0), (0, 256 - part - 3)))
    gathered = jnp.concatenate([ffn_weight.reshape(rows, 2 * hidden), out_weight, extra], axis=1)
    gathered = lax.all_gather(gathered, ("tp", "shard", "ctx"), axis=0, tiled=True).reshape(4, width, 2 * hidden + 256)
    qkv_rows = qkv_weight.reshape(rows, 3 * part)
    other_tokens = swap_ctx(take(tokens, 1 - c))
    if direct:
        places = [((z ^ j) * 2 + (c ^ f)) * rows for f in (0, 1) for j in range(4)]
        near = [qkv_rows] + [swap_shard(qkv_rows, j) for j in (1, 2, 3)]
        qkv_pieces = [*near, swap_ctx(jnp.stack(near))]
    else:
        places = [jnp.zeros_like(c)]
        qkv_pieces = [lax.all_gather(qkv_rows, ("shard", "ctx"), axis=0, tiled=True)]
    per = len(places)
    place = jnp.stack(places + [c, t]).astype(jnp.int32)
    bias_pad = jnp.pad(qkv_bias, ((0, 0), (0, WIDE - part)))
    vec = jnp.concatenate([norm_gain, shift_params, jnp.zeros((2, width), F32)])

    marks = jnp.stack([segment_ids, offsets])
    marks = by_core(take(marks.swapaxes(0, 1), c), swap_ctx(take(marks.swapaxes(0, 1), 1 - c)))
    segment, places = marks[:, 0].reshape(length), marks[:, 1].reshape(length)
    halves = lambda x: x.reshape(2, 2, share, width)
    here = t // 2 == c
    tok_block = jnp.where(here, take(take(halves(tokens), c), t % 2), take(other_tokens.reshape(2, share, width), t % 2))
    grad_block = halves(out_grad)
    grad_far = swap_ctx(take(take(grad_block, 1 - c), t % 2))
    grad_top = jnp.where(here, take(take(grad_block, c), t % 2), grad_far)

    cosine, sine = rotation_tables(places)
    bounds = key_bounds(segment)
    seg_column = segment[:, None]
    seg_row = jnp.broadcast_to(segment[None, :], (8, length))
    q, k_rows, v_rows, k_turned, qkv_wide = project_qkv(place, qkv_pieces, per, bias_pad, tokens, other_tokens, cosine, sine, part)

    contexts, log_totals = [None] * 4, [None] * 4

    def forward(j, q):
        spot = jnp.concatenate([((t ^ j) * (share // BLOCK))[None].astype(jnp.int32), bounds])
        context, log_totals[j] = attention_forward(spot, q, k_rows, v_rows, seg_column, seg_row, heads, share)
        contexts[j] = swap_tp(context, j) if j else context

    forward(3, q)
    q_next, log_totals[3] = lax.optimization_barrier((q, log_totals[3]))
    forward(1, q_next)
    q_next, log_totals[1], contexts[3] = lax.optimization_barrier((q, log_totals[1], contexts[3]))
    forward(2, q_next)
    q_next, log_totals[2], contexts[1] = lax.optimization_barrier((q, log_totals[2], contexts[1]))
    forward(0, q_next)
    log_total = jnp.concatenate(log_totals, axis=1)
    terms = gathered[:, :, 2 * hidden + part : 2 * hidden + part + 3].astype(F32)
    bias_all = order_four(list(jnp.sum(terms, axis=2)), t)

    (
        layer_out,
        grad_second,
        grad_second_b,
        first_scaled,
        normed_t,
        second_t,
        activated,
        slope,
        root,
        sums_two,
    ) = feed_forward(place, gathered, contexts, tok_block, grad_top, vec, bias_all)

    barrier = lax.optimization_barrier
    out_blocks = [layer_out, swap_tp(layer_out, 1), swap_tp(layer_out, 2)]

    grad_first, first_t, g0, g1, g2, g3, grad_hidden, hidden_sums, sums_one = feed_back(
        place, gathered, grad_second, grad_second_b, first_scaled, slope, root, vec, part
    )
    heads_grads = [g0, swap_tp(g1, 1), swap_tp(g2, 2), swap_tp(g3, 3)]

    contexts = jnp.stack(contexts)
    *made, whole = weight_grads(place, per, normed_t, second_t, first_t, contexts, grad_hidden, activated)
    made, whole, heads_grads, out_blocks = barrier((made, whole, heads_grads, out_blocks))
    whole = lax.psum_scatter(whole.reshape(-1, 2 * hh + part), ("tp", "shard", "ctx"), scatter_dimension=0, tiled=True)
    corner = [swap_tp(out_blocks[1][: share // 2], 2), swap_tp(out_blocks[2][share // 2 :], 1)]
    grad_heads = jnp.stack(heads_grads)
    if direct:
        got = swap_ctx(made[1])
        grad_heads, got = barrier((grad_heads, got))
        packs = [made[0][k].astype(F32) + got[k].astype(F32) for k in range(4)]
        sent = [packs[k].astype(BF) for k in (1, 2, 3)]
        grad_heads, sent = barrier((grad_heads, sent))
        sent = [swap_tp(sent[k - 1], k) for k in (1, 2, 3)]

    spot = jnp.concatenate([(t * (share // BLOCK))[None].astype(jnp.int32), bounds])
    grad_proj, bias_sums = attention_backward(
        spot, q, k_rows, k_turned, v_rows, grad_heads, log_total, seg_column, seg_row, cosine, sine, heads
    )
    grad_proj, bias_sums, corner, hidden_sums, sums_one, sums_two = barrier((grad_proj, bias_sums, corner, hidden_sums, sums_one, sums_two))
    if direct:
        grad_proj, sent, packs[0] = barrier((grad_proj, sent, packs[0]))

    three = branch(place, (3,), (BF,), grad_proj, qkv_wide)[0]
    three, grad_proj, corner, bias_sums = barrier((three, grad_proj, corner, bias_sums))
    low, high = swap_tp(three[: share // 2], 2), swap_tp(three[share // 2 :], 1)
    one, two, own = branch(place, (1, 2, 0), (F32, F32, F32), grad_proj, qkv_wide)
    keep, send = split_halves(place, [*out_blocks, *corner])
    small = collect(place, hidden_sums, sums_one, sums_two, bias_sums)
    low, high, one, two, own, keep, send, grad_proj, small = barrier((low, high, one, two, own, keep, send, grad_proj, small))

    one, two = relay(one, two, low, high)
    one, two, send, keep, grad_proj, small = barrier((one, two, send, keep, grad_proj, small))
    one, two = swap_tp(one, 1), swap_tp(two, 2)
    grads = qkv_weight_grads(place, per, tokens, other_tokens, grad_proj, part)
    outputs = join_halves(place, keep, swap_ctx(send))
    small = sum_shard(small + swap_ctx(small))
    if direct:
        summed, *pieces = settle(packs[0], *sent)
        qkv_sum, *qkv_pieces = settle(grads[0], swap_ctx(grads[1]))
        one, two, own, small, outputs, summed, pieces, qkv_sum, qkv_pieces = barrier(
            (one, two, own, small, outputs, summed, pieces, qkv_sum, qkv_pieces)
        )
    else:
        one, two, own, small, outputs = barrier((one, two, own, small, outputs))

    block = add_block(own, grad_first, one, two)
    ready = [block, swap_tp(block, 1), swap_tp(block, 2)]
    small = small + swap_tp(small, 1)
    if direct:
        total = finish(summed, *[swap_shard(pieces[j - 1], j) for j in (1, 2, 3)])
        ready, total, small, qkv_pieces = barrier((ready, total, small, qkv_pieces))
    corner = [swap_tp(ready[1][: share // 2], 2), swap_tp(ready[2][share // 2 :], 1)]
    if direct:
        qkv_total = finish(qkv_sum, *[swap_shard(qkv_pieces[j - 1], j) for j in (1, 2, 3)])
    else:
        qkv_total = lax.psum_scatter(grads[0], ("shard", "ctx"), scatter_dimension=0, tiled=True)
        total = lax.psum_scatter(made[0].reshape(-1, 2 * hh), ("tp", "shard", "ctx"), scatter_dimension=0, tiled=True).astype(F32)
    small = small + swap_tp(small, 2)
    qkv_total = qkv_total.reshape(rows, 3, part)
    corner, qkv_total, total, small = barrier((corner, qkv_total, total, small))
    keep, send = split_halves(place, [*ready, *corner])
    grad_tokens = join_halves(place, keep, swap_ctx(send))

    grad_qkv_weight = qkv_total
    whole = whole.astype(F32)
    grad_up = jnp.concatenate([whole[:, :hh], total[:, :hh]], axis=1)
    grad_down = jnp.concatenate([whole[:, hh : 2 * hh], total[:, hh:]], axis=1)
    grad_ffn_weight = jnp.stack([grad_up, grad_down], axis=1)
    grad_out_weight = whole[:, 2 * hh :]
    grad_ffn_bias = take(small, t)
    vectors = small[4:10]
    grad_qkv_bias = take(small[10:14], t).reshape(3, WIDE)[:, :part]
    return (
        outputs,
        grad_tokens,
        grad_qkv_weight,
        grad_out_weight,
        grad_ffn_weight,
        grad_qkv_bias,
        grad_ffn_bias,
        vectors[:2],
        vectors[2:],
    )


def solution(mesh):
    return jax.shard_map(
        body,
        mesh=mesh,
        in_specs=(
            P("shard", "ctx", None),
            P("shard", "ctx"),
            P("shard", "ctx"),
            P(("shard", "ctx"), None, "tp"),
            P(("shard", "ctx"), "tp"),
            P(("shard", "ctx"), None, "tp"),
            P(None, "tp"),
            P("tp"),
            P(),
            P(),
            P("shard", "ctx", None),
        ),
        out_specs=(
            P("shard", "ctx", None),
            P("shard", "ctx", None),
            P(("shard", "ctx"), None, "tp"),
            P(("shard", "ctx"), "tp"),
            P(("shard", "ctx"), None, "tp"),
            P(None, "tp"),
            P("tp"),
            P(),
            P(),
        ),
        check_vma=False,
    )
```

```python
from functools import partial

import jax
import jax.numpy as jnp
import numpy as np
from jax import lax
from jax.experimental import pallas as pl
from jax.experimental.pallas import tpu as pltpu
from jax.sharding import PartitionSpec as P

HEAD = 64
WIDE = 256
BLOCK = 256
CHUNK = 256
EPSILON = 1e-12
F32 = jnp.float32
BF = jnp.bfloat16
NEG = -1e30
COST = pl.CostEstimate(flops=0, bytes_accessed=0, transcendentals=0)


def swap_pairs(x):
    lane = lax.broadcasted_iota(jnp.int32, x.shape, 1)
    n = x.shape[1]
    return jnp.where(lane % 2 == 0, pltpu.roll(x, n - 1, 1), pltpu.roll(x, 1, 1))


def nt(a, b):
    return lax.dot_general(a, b, (((1,), (1,)), ((), ())), preferred_element_type=F32)


def nn(a, b):
    return lax.dot_general(a, b, (((1,), (0,)), ((), ())), preferred_element_type=F32)


def twice(x):
    return jnp.concatenate([x, x], axis=1)


def lanes_of_heads(x, heads):
    lane = lax.broadcasted_iota(jnp.int32, x.shape, 1) // HEAD
    return [jnp.where(lane == h, x, jnp.zeros_like(x)) for h in range(heads)]


def whole_block(shape, buffers=1):
    return pl.BlockSpec(shape, lambda *_: (0,) * len(shape), pipeline_mode=pl.Buffered(buffers))


def smem():
    return pl.BlockSpec(memory_space=pltpu.SMEM)


def params(mib):
    return pltpu.CompilerParams(dimension_semantics=("arbitrary",), vmem_limit_bytes=mib * 1024 * 1024)


def qkv_kernel(count, per, part, place, *refs):
    pieces = []
    for x in refs[:count]:
        pieces += [x] if len(x.shape) == 2 else [x.at[n] for n in range(x.shape[0])]
    bias, own, other, cos, sin, q_o, k_o, v_o, kt_o, qt_o, w_o = refs[count:]
    piece_rows = pieces[0].shape[0]
    pad = jnp.zeros((piece_rows, WIDE - part), BF)
    for n in range(per):
        sl = pl.ds(pl.multiple_of(place[n], 16), piece_rows)
        for m in range(3):
            w_o[sl, m * WIDE : (m + 1) * WIDE] = jnp.concatenate([pieces[n][:, m * part : (m + 1) * part], pad], axis=1)
    half_len = other.shape[0]

    def run(x, sl):
        c, s = twice(cos[sl, :]), twice(sin[sl, :])
        p = nn(x, w_o[:, 0:WIDE]) + bias[0:1, :]
        q = ((p * c + swap_pairs(p) * s).astype(BF).astype(F32) * (HEAD**-0.5)).astype(BF)
        q_o[sl, :] = q
        qt_o[:, sl] = q.T
        p = nn(x, w_o[:, WIDE : 2 * WIDE]) + bias[1:2, :]
        k = (p * c + swap_pairs(p) * s).astype(BF)
        k_o[sl, :] = k
        kt_o[:, sl] = k.T
        v_o[sl, :] = (nn(x, w_o[:, 2 * WIDE : 3 * WIDE]) + bias[2:3, :]).astype(BF)

    def step(r, _):
        rows = pl.ds(pl.multiple_of(r * BLOCK, BLOCK), BLOCK)
        core = place[per]
        run(own[0, rows, :], pl.ds(pl.multiple_of(core * half_len + r * BLOCK, BLOCK), BLOCK))
        run(other[rows, :], pl.ds(pl.multiple_of((1 - core) * half_len + r * BLOCK, BLOCK), BLOCK))
        return 0

    lax.fori_loop(0, half_len // BLOCK, step, 0)


def project_qkv(place, pieces, per, bias, tokens, other, cos, sin, part):
    half_len, width = other.shape
    length, count = 2 * half_len, len(pieces)
    return pl.pallas_call(
        partial(qkv_kernel, count, per, part),
        grid_spec=pltpu.PrefetchScalarGridSpec(
            num_scalar_prefetch=1,
            grid=(1,),
            in_specs=[whole_block(p.shape) for p in pieces]
            + [whole_block(bias.shape), pl.BlockSpec((1, half_len, width), lambda i, s: (s[per], 0, 0))]
            + [whole_block(x.shape) for x in (other, cos, sin)],
            out_specs=[whole_block((length, WIDE))] * 3 + [whole_block((WIDE, length))] * 2 + [whole_block((width, 3 * WIDE))],
        ),
        out_shape=[jax.ShapeDtypeStruct((length, WIDE), BF)] * 3
        + [jax.ShapeDtypeStruct((WIDE, length), BF)] * 2
        + [jax.ShapeDtypeStruct((width, 3 * WIDE), BF)],
        compiler_params=params(32),
        cost_estimate=COST,
        name="project_qkv",
    )(place, *pieces, bias, tokens, other, cos, sin)


def forward_kernel(heads, place, q, k, v, segc, segr, ctx_o, lse_o, full_o, acc, s_sc, m_sc, l_sc, qc_sc):
    i = place[0] + pl.program_id(0)
    start, count = place[1 + 2 * i], place[2 + 2 * i]
    qc_sc[...] = jnp.concatenate(lanes_of_heads(q[...], heads), axis=0)
    seg_q = segc[...]
    m_sc[...] = jnp.full(m_sc.shape, NEG, F32)
    l_sc[...] = jnp.zeros(l_sc.shape, F32)

    def at(j):
        return pl.ds(pl.multiple_of(start + j * CHUNK, 128), CHUNK)

    def of(h):
        return slice(h * BLOCK, (h + 1) * BLOCK)

    def pass1(j, _):
        s = nt(qc_sc[...], k[at(j), :])
        keep = seg_q == segr[0:1, at(j)]
        for h in range(heads):
            sh = jnp.where(keep, s[of(h), :], NEG)
            s_sc[j, of(h), :] = sh
            m_sc[of(h), :] = jnp.maximum(m_sc[of(h), :], jnp.maximum(sh[:, :128], sh[:, 128:]))
        return 0

    lax.fori_loop(0, count, pass1, 0)
    m_sc[...] = jnp.broadcast_to(jnp.max(m_sc[...], axis=1, keepdims=True), m_sc.shape)

    def pass2(j, _):
        for h in range(heads):
            e = jnp.exp(s_sc[j, of(h), :] - twice(m_sc[of(h), :]))
            s_sc[j, of(h), :] = e
            l_sc[of(h), :] += e[:, :128] + e[:, 128:]
        return 0

    lax.fori_loop(0, count, pass2, 0)
    total = jnp.sum(l_sc[...], axis=1, keepdims=True)
    lse = m_sc[:, 0:1] + jnp.log(total)
    l_sc[...] = jnp.broadcast_to(1.0 / total, l_sc.shape)
    lane = lax.broadcasted_iota(jnp.int32, (BLOCK, 128), 1)
    tile = jnp.zeros((BLOCK, 128), F32)
    for h in range(heads):
        tile = jnp.where(lane == h, lse[of(h), :], tile)
    lse_o[...] = tile.T[0:8, :]
    acc[...] = jnp.zeros(acc.shape, F32)
    full_o[...] = jnp.zeros(full_o.shape, F32)

    def pass3(j, _):
        ps, less = [], []
        for h in range(heads):
            p = s_sc[j, of(h), :] * twice(l_sc[of(h), :])
            b = p.astype(BF)
            ps.append(b)
            less.append((p - b.astype(F32)).astype(BF))
        vs = jnp.concatenate(lanes_of_heads(v[at(j), :], heads), axis=0)
        acc[...] += nn(jnp.concatenate(ps, axis=1), vs)
        full_o[...] += nn(jnp.concatenate(less, axis=1), vs)
        return 0

    lax.fori_loop(0, count, pass3, 0)
    ctx_o[...] = acc[:, : heads * HEAD].astype(BF)
    full_o[...] += acc[...]


def attention_forward(place, q, k, v, segc, segr, heads, share):
    length = q.shape[0]
    grid = share // BLOCK
    rows = lambda i, s: (s[0] + i, 0)
    return pl.pallas_call(
        partial(forward_kernel, heads),
        grid_spec=pltpu.PrefetchScalarGridSpec(
            num_scalar_prefetch=1,
            grid=(grid,),
            in_specs=[
                pl.BlockSpec((BLOCK, WIDE), rows),
                whole_block(k.shape),
                whole_block(v.shape),
                pl.BlockSpec((BLOCK, 1), rows),
                whole_block(segr.shape),
            ],
            out_specs=[
                pl.BlockSpec((BLOCK, heads * HEAD), lambda i, s: (i, 0)),
                pl.BlockSpec((8, BLOCK), lambda i, s: (0, i)),
                pl.BlockSpec((BLOCK, WIDE), lambda i, s: (i, 0)),
            ],
            scratch_shapes=[
                pltpu.VMEM((BLOCK, WIDE), F32),
                pltpu.VMEM((length // CHUNK, heads * BLOCK, CHUNK), F32),
                pltpu.VMEM((heads * BLOCK, 128), F32),
                pltpu.VMEM((heads * BLOCK, 128), F32),
                pltpu.VMEM((heads * BLOCK, WIDE), BF),
            ],
        ),
        out_shape=[
            jax.ShapeDtypeStruct((share, heads * HEAD), BF),
            jax.ShapeDtypeStruct((8, share), F32),
            jax.ShapeDtypeStruct((share, WIDE), F32),
        ],
        compiler_params=params(16),
        cost_estimate=COST,
        name="attention_forward",
    )(place, q, k, v, segc, segr)


def backward_kernel(heads, place, q, qt, k, kt, v, d0, d1, d2, d3, full, lse, segc, segr, cos, sin, g_o, gb_o, dk_sc, dv_sc, qc_sc, dc_sc, dq_sc, d_sc, dt_sc):
    step_at = pl.program_id(0)
    i = step_at ^ place[0]
    length = k.shape[0]
    part = d0.shape[1]
    per = d0.shape[0] // BLOCK

    @pl.when(step_at == 0)
    def _():
        dk_sc[...] = jnp.zeros(dk_sc.shape, F32)
        dv_sc[...] = jnp.zeros(dv_sc.shape, F32)
        gb_o[...] = jnp.zeros(gb_o.shape, F32)
        d_sc[...] = jnp.zeros(d_sc.shape, BF)

    for n, d in enumerate((d0, d1, d2, d3)):

        @pl.when(step_at // per == n)
        def _(d=d):
            d_sc[:, 0:part] = d[pl.ds(pl.multiple_of(step_at % per * BLOCK, BLOCK), BLOCK), :]

    start, count = place[1 + 2 * i], place[2 + 2 * i]
    qc_sc[...] = jnp.concatenate(lanes_of_heads(q[...], heads), axis=0)
    dz = d_sc[...]
    dc_sc[...] = jnp.concatenate(lanes_of_heads(dz, heads), axis=0)
    dt_sc[...] = dz.T
    dq_sc[...] = jnp.zeros(dq_sc.shape, F32)
    own = pl.ds(pl.multiple_of(i * BLOCK, BLOCK), BLOCK)
    seg_q = segr[0:1, own]
    row = lax.broadcasted_iota(jnp.int32, (8, WIDE), 0)
    lane = lax.broadcasted_iota(jnp.int32, (8, WIDE), 1) // HEAD
    pick = jnp.where(row == lane, 1.0, 0.0).astype(F32)
    delta = lax.dot_general(
        pick, dz.astype(F32) * full[...], (((1,), (1,)), ((), ())), preferred_element_type=F32, precision=lax.Precision.HIGHEST
    )

    def of(h):
        return slice(h * BLOCK, (h + 1) * BLOCK)

    def step(j, _):
        at = pl.ds(pl.multiple_of(start + j * CHUNK, 128), CHUNK)
        s = nt(k[at, :], qc_sc[...])
        dp = nt(v[at, :], dc_sc[...])
        keep = segc[at, :] == seg_q
        for h in range(heads):
            mine = slice(h * HEAD, (h + 1) * HEAD)
            p = jnp.exp(jnp.where(keep, s[:, of(h)], NEG) - lse[h : h + 1, :])
            ds = (p * (dp[:, of(h)] - delta[h : h + 1, :])).astype(BF)
            dq_sc[mine, :] += nn(kt[mine, at], ds)
            dv_sc[mine, at] += nt(dt_sc[mine, :], p.astype(BF))
            dk_sc[mine, at] += nt(qt[mine, :], ds)
        return 0

    def pair(j, _):
        step(2 * j, 0)
        step(2 * j + 1, 0)
        return 0

    lax.fori_loop(0, count // 2, pair, 0)

    @pl.when(count % 2 == 1)
    def _():
        step(count - 1, 0)

    def turn(x, sl):
        return (x * twice(cos[sl, :]) - swap_pairs(x) * twice(sin[sl, :])).astype(BF)

    def put(x, sl, m):
        g_o[sl, m * WIDE : (m + 1) * WIDE] = x
        gb_o[0:1, m * WIDE : (m + 1) * WIDE] += jnp.sum(x.astype(F32), axis=0, keepdims=True)

    put(turn(dq_sc[...].T * (HEAD**-0.5), own), own, 0)

    @pl.when(step_at == pl.num_programs(0) - 1)
    def _():
        def last(r, _):
            sl = pl.ds(pl.multiple_of(r * BLOCK, BLOCK), BLOCK)
            put(turn(dk_sc[:, sl].T, sl), sl, 1)
            put(dv_sc[:, sl].astype(BF).T, sl, 2)
            return 0

        lax.fori_loop(0, length // BLOCK, last, 0)


def attention_backward(place, q, qt, k, kt, v, do, full, lse, segc, segr, cos, sin, heads):
    length = k.shape[0]
    return pl.pallas_call(
        partial(backward_kernel, heads),
        grid_spec=pltpu.PrefetchScalarGridSpec(
            num_scalar_prefetch=1,
            grid=(length // BLOCK,),
            in_specs=[
                pl.BlockSpec((BLOCK, WIDE), lambda i, s: (i ^ s[0], 0)),
                pl.BlockSpec((WIDE, BLOCK), lambda i, s: (0, i ^ s[0])),
                whole_block(k.shape),
                whole_block(kt.shape),
                whole_block(v.shape),
                *[whole_block(d.shape) for d in do],
                pl.BlockSpec((BLOCK, WIDE), lambda i, s: (i, 0)),
                pl.BlockSpec((8, BLOCK), lambda i, s: (0, i)),
                whole_block(segc.shape),
                whole_block(segr.shape),
                whole_block(cos.shape),
                whole_block(sin.shape),
            ],
            out_specs=[whole_block((length, 3 * WIDE)), whole_block((8, 3 * WIDE))],
            scratch_shapes=[pltpu.VMEM((WIDE, length), F32)] * 2
            + [pltpu.VMEM((heads * BLOCK, WIDE), BF)] * 2
            + [pltpu.VMEM((WIDE, BLOCK), F32), pltpu.VMEM((BLOCK, WIDE), BF), pltpu.VMEM((WIDE, BLOCK), BF)],
        ),
        out_shape=[jax.ShapeDtypeStruct((length, 3 * WIDE), BF), jax.ShapeDtypeStruct((8, 3 * WIDE), F32)],
        compiler_params=params(28),
        cost_estimate=COST,
        name="attention_backward",
    )(place, q, qt, k, kt, v, *do, full, lse, segc, segr, cos, sin)


def out_copies(place, gathered, w_out, sems):
    here = place[place.shape[0] - 1]
    feed = gathered.shape[2] - w_out.shape[2]
    return [pltpu.make_async_copy(gathered.at[here ^ k, :, feed:], w_out.at[k], sems.at[k]) for k in range(4)]


def row_mean(x):
    return jnp.mean(x, axis=1, keepdims=True)


def gelu_parts(x):
    e = jnp.exp(x * x * -0.5)
    t = 1.0 / (1.0 + (0.3275911 * 0.7071067811865476) * jnp.abs(x))
    p = t * (0.254829592 + t * (-0.284496736 + t * (1.421413741 + t * (-1.453152027 + t * 1.061405429))))
    tail = 0.5 * p * e
    phi = jnp.where(x >= 0, 1.0 - tail, tail)
    return phi, phi + x * e * 0.3989422804014327


ROWS = 256


def feed_kernel(place, gathered, w, c0, c1, c2, c3, tokb, gtop, vec, bias, *refs):
    (out_o, gs_o, gsb_o, fs_o, nbt_o, gst_o, act_o, gp_o, root_o, sum_o, nb_o, w_out, acc, normed, sems) = refs
    copies = out_copies(place, gathered, w_out, sems)
    k = pl.program_id(0)
    share = tokb.shape[0]
    part = c0.shape[1]
    chunks = [pl.ds(r * ROWS, ROWS) for r in range(share // ROWS)]

    @pl.when(k == 0)
    def _():
        for copy in copies:
            copy.start()
        for copy in copies:
            copy.wait()
        for sl in chunks:
            x = tokb[sl, :].astype(F32) + vec[4:5, :]
            for n, ctx in enumerate((c0, c1, c2, c3)):
                x = x + nt(ctx[sl, :], w_out[n, :, 0:part])
            x = x - row_mean(x)
            root = lax.rsqrt(row_mean(x * x) + EPSILON)
            x = x * root
            fs_o[sl, :] = x
            root_o[sl, :] = jnp.broadcast_to(root, (ROWS, 128))
            y = x * vec[0:1, :] + vec[2:3, :]
            normed[sl, :] = y
            nb_o[sl, :] = y.astype(BF)
            nbt_o[:, sl] = y.astype(BF).T
            acc[sl, :] = y + vec[5:6, :]

    hidden = act_o.shape[2]

    def rows_step(r, _):
        sl = pl.ds(pl.multiple_of(r * ROWS, ROWS), ROWS)
        h = nn(nb_o[sl, :], w[0, :, 0:hidden]) + bias[pl.ds(k, 1), :]
        phi, slope = gelu_parts(h)
        a = (h * phi).astype(BF)
        act_o[0, sl, :] = a
        gp_o[0, sl, :] = slope
        acc[sl, :] += nt(a, w[0, :, hidden:])
        return 0

    lax.fori_loop(0, share // ROWS, rows_step, 0, unroll=True)

    @pl.when(k == 3)
    def _():
        total = [jnp.zeros((1, tokb.shape[1]), F32)] * 3
        for sl in chunks:
            x = acc[sl, :]
            x = x - row_mean(x)
            root = lax.rsqrt(row_mean(x * x) + EPSILON)
            x = x * root
            out_o[sl, :] = (x * vec[1:2, :] + vec[3:4, :]).astype(BF)
            g = gtop[sl, :].astype(F32)
            gg = g * vec[1:2, :]
            gs = root * (gg - row_mean(gg) - x * row_mean(gg * x))
            gs_o[sl, :] = gs
            gsb_o[sl, :] = gs.astype(BF)
            gst_o[:, sl] = gs.astype(BF).T
            for n, y in enumerate((g * x, g, gs)):
                total[n] = total[n] + jnp.sum(y, axis=0, keepdims=True)
        sum_o[...] = jnp.concatenate(total + [jnp.zeros((5, tokb.shape[1]), F32)], axis=0)


def feed_specs(place, gathered, hidden):
    width, last = gathered.shape[1], place.shape[0] - 1
    return [pl.BlockSpec(memory_space=pl.ANY), pl.BlockSpec((1, width, 2 * hidden), lambda i, s: (s[last] ^ i, 0, 0))]


def feed_forward(place, gathered, contexts, tokb, gtop, vec, bias):
    share, width = tokb.shape
    hidden = bias.shape[1]
    block = lambda: pl.BlockSpec((1, share, hidden), lambda i, s: (i, 0, 0))
    sd, far = jax.ShapeDtypeStruct, pltpu.HBM
    return pl.pallas_call(
        feed_kernel,
        grid_spec=pltpu.PrefetchScalarGridSpec(
            num_scalar_prefetch=1,
            grid=(4,),
            in_specs=feed_specs(place, gathered, hidden) + [whole_block(x.shape) for x in (*contexts, tokb, gtop, vec, bias)],
            out_specs=[whole_block((share, width))] * 4
            + [whole_block((width, share))] * 2
            + [block(), block(), whole_block((share, 128)), whole_block((8, width))],
            scratch_shapes=[
                pltpu.VMEM((share, width), BF),
                pltpu.VMEM((4, width, gathered.shape[2] - 2 * hidden), BF),
                pltpu.VMEM((share, width), F32),
                pltpu.VMEM((share, width), F32),
                pltpu.SemaphoreType.DMA((4,)),
            ],
        ),
        out_shape=[
            sd((share, width), BF),
            sd((share, width), F32),
            sd((share, width), BF),
            sd((share, width), F32),
            far((width, share), BF),
            far((width, share), BF),
            far((4, share, hidden), BF),
            far((4, share, hidden), F32),
            sd((share, 128), F32),
            sd((8, width), F32),
        ],
        compiler_params=params(54),
        cost_estimate=COST,
        name="feed_forward",
    )(place, gathered, gathered, *contexts, tokb, gtop, vec, bias)


def feed_back_kernel(place, gathered, w, gs, gsb, fs, gp, root, vec, *refs):
    (gf_o, gft_o, gc0, gc1, gc2, gc3, gh_o, ghs_o, sum_o, w_out, acc, sems) = refs
    copies = out_copies(place, gathered, w_out, sems)
    k = pl.program_id(0)
    share, width = gs.shape
    hidden, part = gh_o.shape[2], gc0.shape[1]

    @pl.when(k == 0)
    def _():
        for copy in copies:
            copy.start()
        acc[...] = gs[...]

    def rows_step(r, total):
        sl = pl.ds(pl.multiple_of(r * ROWS, ROWS), ROWS)
        g = (nn(gsb[sl, :], w[0, :, hidden:]) * gp[0, sl, :]).astype(BF)
        gh_o[0, sl, :] = g
        acc[sl, :] += nt(g, w[0, :, 0:hidden])
        return total + jnp.sum(g.astype(F32), axis=0, keepdims=True)

    total = lax.fori_loop(0, share // ROWS, rows_step, jnp.zeros((1, hidden), F32), unroll=True)
    ghs_o[0] = jnp.broadcast_to(total, (8, hidden))

    @pl.when(k == 3)
    def _():
        for copy in copies:
            copy.wait()
        sums = [jnp.zeros((1, width), F32)] * 3
        for r in range(share // ROWS):
            sl = pl.ds(r * ROWS, ROWS)
            gn = acc[sl, :]
            x = fs[sl, :]
            gg = gn * vec[0:1, :]
            gf = root[sl, 0:1] * (gg - row_mean(gg) - x * row_mean(gg * x))
            gf_o[sl, :] = gf
            b = gf.astype(BF)
            gft_o[:, sl] = b.T
            for n, o in enumerate((gc0, gc1, gc2, gc3)):
                o[sl, :] = nn(b, w_out[n, :, 0:part]).astype(BF)
            for n, y in enumerate((gn * x, gn, gf)):
                sums[n] = sums[n] + jnp.sum(y, axis=0, keepdims=True)
        sum_o[...] = jnp.concatenate(sums + [jnp.zeros((5, width), F32)], axis=0)


def feed_back(place, gathered, gs, gsb, fs, gp, root, vec, part):
    share, width = gs.shape
    hidden = gp.shape[2]
    block = lambda: pl.BlockSpec((1, share, hidden), lambda i, s: (i, 0, 0))
    sd, far = jax.ShapeDtypeStruct, pltpu.HBM
    return pl.pallas_call(
        feed_back_kernel,
        grid_spec=pltpu.PrefetchScalarGridSpec(
            num_scalar_prefetch=1,
            grid=(4,),
            in_specs=feed_specs(place, gathered, hidden)
            + [whole_block(gs.shape), whole_block(gsb.shape), whole_block(fs.shape), block(), whole_block(root.shape), whole_block(vec.shape)],
            out_specs=[whole_block((share, width)), whole_block((width, share))]
            + [whole_block((share, part))] * 4
            + [block(), pl.BlockSpec((1, 8, hidden), lambda i, s: (i, 0, 0)), whole_block((8, width))],
            scratch_shapes=[
                pltpu.VMEM((4, width, gathered.shape[2] - 2 * hidden), BF),
                pltpu.VMEM((share, width), F32),
                pltpu.SemaphoreType.DMA((4,)),
            ],
        ),
        out_shape=[far((share, width), F32), far((width, share), BF)]
        + [sd((share, part), BF)] * 4
        + [far((4, share, hidden), BF), sd((4, 8, hidden), F32), sd((8, width), F32)],
        compiler_params=params(54),
        cost_estimate=COST,
        name="feed_back",
    )(place, gathered, gathered, gs, gsb, fs, gp, root, vec)


def split_rows(place, per, acc, source, near_o, far_o, lead, cols):
    if per == 1:
        near_o[(*lead, slice(None), cols)] = acc[:, source].astype(near_o.dtype)
        return
    rows = acc.shape[0] // per
    for n in range(per // 2):
        near, far = (pl.ds(pl.multiple_of(place[m], 16), rows) for m in (n, per // 2 + n))
        near_o[(*lead, n, slice(None), cols)] = acc[near, source].astype(near_o.dtype)
        far_o[(*lead, n, slice(None), cols)] = acc[far, source].astype(BF)


def weights_kernel(per, place, nbt, gst, gft, ctx, gh, act, *refs):
    hh = gh.shape[2] // 2
    if per > 1:
        near_o, far_o, out, acc = refs
    else:
        other, out = refs
    for n, (left, right) in enumerate(((nbt, gh), (gst, act))):
        made = nn(left[...], right[0])
        out[0, :, n * hh : (n + 1) * hh] = made[:, 0:hh].astype(BF)
        if per > 1:
            acc[...] = made[:, hh:]
            split_rows(place, per, acc, slice(None), near_o, far_o, (0,), slice(n * hh, (n + 1) * hh))
        else:
            other[0, :, n * hh : (n + 1) * hh] = made[:, hh:].astype(BF)
    out[0, :, 2 * hh :] = nn(gft[...], ctx[0]).astype(BF)


def weight_grads(place, per, nbt, gst, gft, contexts, gh, act):
    width, share = nbt.shape
    hidden, part = gh.shape[2], contexts.shape[2]
    last = place.shape[0] - 1
    block = lambda cols: pl.BlockSpec((1, share, cols), lambda i, s: (i, 0, 0))
    ordered = lambda cols: pl.BlockSpec((1, width, cols), lambda i, s: (i ^ s[last], 0, 0))
    if per > 1:
        shape = (4, per // 2, width // per, hidden)
        outs = [jax.ShapeDtypeStruct(shape, BF)] * 2
        specs = [pl.BlockSpec((1,) + shape[1:], lambda i, s: (i, 0, 0, 0))] * 2
        scratch = [pltpu.VMEM((width, hidden // 2), F32)]
    else:
        outs = [jax.ShapeDtypeStruct((4, width, hidden), BF)]
        specs = [ordered(hidden)]
        scratch = []
    return pl.pallas_call(
        partial(weights_kernel, per),
        grid_spec=pltpu.PrefetchScalarGridSpec(
            num_scalar_prefetch=1,
            grid=(4,),
            in_specs=[whole_block(x.shape) for x in (nbt, gst, gft)] + [block(part), block(hidden), block(hidden)],
            out_specs=specs + [ordered(hidden + part)],
            scratch_shapes=scratch,
        ),
        out_shape=outs + [jax.ShapeDtypeStruct((4, width, hidden + part), BF)],
        compiler_params=params(58),
        cost_estimate=COST,
        name="weight_grads",
    )(place, nbt, gst, gft, contexts, gh, act)


def qkv_weights_kernel(per, part, place, own, other, g, *refs):
    near_o, far_o = refs[:2] if per > 1 else (refs[0], None)
    acc = refs[-1]
    half_len = other.shape[0]
    core = place[per]
    rows = 512

    acc[...] = jnp.zeros(acc.shape, F32)

    def step(r, _):
        at = pl.ds(pl.multiple_of(r * rows, rows), rows)
        a = g[pl.ds(pl.multiple_of(core * half_len + r * rows, rows), rows), :]
        b = g[pl.ds(pl.multiple_of((1 - core) * half_len + r * rows, rows), rows), :]
        acc[...] += nn(own[0, at, :].T, a) + nn(other[at, :].T, b)
        return 0

    lax.fori_loop(0, half_len // rows, step, 0)
    for m in range(3):
        split_rows(place, per, acc, slice(m * WIDE, m * WIDE + part), near_o, far_o, (), slice(m * part, (m + 1) * part))


def qkv_weight_grads(place, per, tokens, other, g, part):
    half_len, width = other.shape
    if per > 1:
        shape = (per // 2, width // per, 3 * part)
        outs = [jax.ShapeDtypeStruct(shape, F32), jax.ShapeDtypeStruct(shape, BF)]
    else:
        outs = [jax.ShapeDtypeStruct((width, 3 * part), F32)]
    return pl.pallas_call(
        partial(qkv_weights_kernel, per, part),
        grid_spec=pltpu.PrefetchScalarGridSpec(
            num_scalar_prefetch=1,
            grid=(1,),
            in_specs=[pl.BlockSpec((1, half_len, width), lambda i, s: (s[per], 0, 0)), whole_block(other.shape), whole_block(g.shape)],
            out_specs=[whole_block(o.shape) for o in outs],
            scratch_shapes=[pltpu.VMEM((width, 3 * WIDE), F32)],
        ),
        out_shape=outs,
        compiler_params=params(32),
        cost_estimate=COST,
        name="qkv_weight_grads",
    )(place, tokens, other, g)


def branch_kernel(place, *refs):
    count = (len(refs) - 1) // 2
    w = refs[count]
    for g, o in zip(refs[:count], refs[count + 1 :]):
        rows = 256
        for r in range(g.shape[0] // rows):
            sl = slice(r * rows, (r + 1) * rows)
            o[sl, :] = nt(g[sl, :], w[...]).astype(o.dtype)


def branch(place, blocks, kinds, g, w):
    share, last = g.shape[0] // 4, place.shape[0] - 1
    return pl.pallas_call(
        branch_kernel,
        grid_spec=pltpu.PrefetchScalarGridSpec(
            num_scalar_prefetch=1,
            grid=(1,),
            in_specs=[pl.BlockSpec((share, g.shape[1]), lambda i, s, k=k: (s[last] ^ k, 0)) for k in blocks] + [whole_block(w.shape)],
            out_specs=[whole_block((share, w.shape[0]))] * len(blocks),
        ),
        out_shape=[jax.ShapeDtypeStruct((share, w.shape[0]), kind) for kind in kinds],
        compiler_params=params(24),
        cost_estimate=COST,
        name="branch",
    )(place, *[g] * len(blocks), w)


def pick_kernel(place, near, *refs):
    far, (keep, send) = refs[:-2], refs[-2:]
    last = place.shape[0] - 1
    mine = place[last] // 2 == place[last - 1]

    def put(out, parts):
        rows = out.shape[0] // len(parts)
        for n, x in enumerate(parts):
            out[n * rows : (n + 1) * rows, :] = x[...]

    @pl.when(mine)
    def _():
        put(keep, [near])
        put(send, far)

    @pl.when(jnp.logical_not(mine))
    def _():
        put(keep, far)
        put(send, [near])


def pick(place, near, *far):
    return pl.pallas_call(
        pick_kernel,
        grid_spec=pltpu.PrefetchScalarGridSpec(
            num_scalar_prefetch=1,
            grid=(1,),
            in_specs=[whole_block(x.shape) for x in (near, *far)],
            out_specs=[whole_block(near.shape)] * 2,
        ),
        out_shape=[jax.ShapeDtypeStruct(near.shape, near.dtype)] * 2,
        compiler_params=params(8),
        cost_estimate=COST,
        name="pick",
    )(place, near, *far)


def join_kernel(place, keep_a, keep_b, other_a, other_b, out):
    last = place.shape[0] - 1
    mine = pl.program_id(0) == place[last - 1]
    same = pl.program_id(1) == place[last] % 2
    for x, own, even in ((keep_a, True, True), (keep_b, True, False), (other_a, False, True), (other_b, False, False)):

        @pl.when(jnp.logical_and(mine == own, same == even))
        def _(x=x):
            out[0] = x[...]


def join(place, keeps, others):
    share, width = keeps[0].shape
    return pl.pallas_call(
        join_kernel,
        grid_spec=pltpu.PrefetchScalarGridSpec(
            num_scalar_prefetch=1,
            grid=(2, 2),
            in_specs=[whole_block((share, width))] * 4,
            out_specs=pl.BlockSpec((1, share, width), lambda i, j, s: (i, j, 0)),
        ),
        out_shape=jax.ShapeDtypeStruct((2, 2 * share, width), keeps[0].dtype),
        compiler_params=pltpu.CompilerParams(dimension_semantics=("arbitrary", "arbitrary"), vmem_limit_bytes=12 * 1024 * 1024),
        cost_estimate=COST,
        name="join",
    )(place, *keeps, *others)


def relay_kernel(one, two, low, high, one_o, two_o):
    half = low.shape[0]
    one_o[0:half, :] = (one[0:half, :] + low[...].astype(F32)).astype(BF)
    one_o[half:, :] = one[half:, :].astype(BF)
    two_o[0:half, :] = two[0:half, :].astype(BF)
    two_o[half:, :] = (two[half:, :] + high[...].astype(F32)).astype(BF)


def relay(one, two, low, high):
    return pl.pallas_call(
        relay_kernel,
        in_specs=[pl.BlockSpec(memory_space=pltpu.VMEM)] * 4,
        out_specs=[pl.BlockSpec(memory_space=pltpu.VMEM)] * 2,
        out_shape=[jax.ShapeDtypeStruct(one.shape, BF)] * 2,
        compiler_params=pltpu.CompilerParams(vmem_limit_bytes=16 * 1024 * 1024),
        cost_estimate=COST,
        name="relay",
    )(one, two, low, high)


def collect_kernel(place, hidden_sums, one, two, bias, out):
    here = place[place.shape[0] - 1]
    out[...] = jnp.zeros(out.shape, F32)
    for k in range(4):
        out[pl.ds(here ^ k, 1), :] = hidden_sums[k, 0:1, :]
    for n, (x, row) in enumerate(((one, 0), (two, 0), (one, 1), (two, 1), (one, 2), (two, 2))):
        out[4 + n : 5 + n, :] = x[row : row + 1, :]
    out[pl.ds(10 + here, 1), :] = bias[0:1, :]


def collect(place, hidden_sums, one, two, bias):
    return pl.pallas_call(
        collect_kernel,
        grid_spec=pltpu.PrefetchScalarGridSpec(
            num_scalar_prefetch=1,
            grid=(1,),
            in_specs=[whole_block(x.shape) for x in (hidden_sums, one, two, bias)],
            out_specs=whole_block((16, one.shape[1])),
        ),
        out_shape=jax.ShapeDtypeStruct((16, one.shape[1]), F32),
        compiler_params=params(8),
        cost_estimate=COST,
        name="collect",
    )(place, hidden_sums, one, two, bias)


def settle_kernel(count, *refs):
    ins, outs = refs[:count], refs[count:]
    for j, out in enumerate(outs):
        total = ins[0][j].astype(F32)
        for x in ins[1:]:
            total = total + x[j].astype(F32)
        out[...] = total.astype(out.dtype)


def settle(*stacks):
    shape = stacks[0].shape
    vmem = pl.BlockSpec(memory_space=pltpu.VMEM)
    return pl.pallas_call(
        partial(settle_kernel, len(stacks)),
        in_specs=[vmem] * len(stacks),
        out_specs=[vmem] * shape[0],
        out_shape=[jax.ShapeDtypeStruct(shape[1:], F32 if j == 0 else BF) for j in range(shape[0])],
        compiler_params=pltpu.CompilerParams(vmem_limit_bytes=16 * 1024 * 1024),
        cost_estimate=COST,
        name="settle",
    )(*stacks)


def finish_kernel(parts, *refs):
    out = refs[-1]
    total = refs[0][...]
    for x in refs[1:-1]:
        total = total + x[...].astype(F32)
    if parts == 1:
        out[...] = total
    else:
        cols = total.shape[1] // parts
        for m in range(parts):
            out[:, m, :] = total[:, m * cols : (m + 1) * cols]


def finish(parts, *pieces):
    vmem = pl.BlockSpec(memory_space=pltpu.VMEM)
    rows, cols = pieces[0].shape
    return pl.pallas_call(
        partial(finish_kernel, parts),
        in_specs=[vmem] * len(pieces),
        out_specs=vmem,
        out_shape=jax.ShapeDtypeStruct((rows, cols) if parts == 1 else (rows, parts, cols // parts), F32),
        compiler_params=pltpu.CompilerParams(vmem_limit_bytes=8 * 1024 * 1024),
        cost_estimate=COST,
        name="finish",
    )(*pieces)


def place_kernel(whole, rest, feed_o, out_o):
    hh = rest.shape[1] // 2
    for m in range(2):
        feed_o[:, m, 0:hh] = whole[:, m * hh : (m + 1) * hh].astype(F32)
        feed_o[:, m, hh:] = rest[:, m * hh : (m + 1) * hh]
    out_o[...] = whole[:, 2 * hh :].astype(F32)


def place_feed(whole, rest):
    vmem = pl.BlockSpec(memory_space=pltpu.VMEM)
    rows, cols = rest.shape
    return pl.pallas_call(
        place_kernel,
        in_specs=[vmem] * 2,
        out_specs=[vmem] * 2,
        out_shape=[jax.ShapeDtypeStruct((rows, 2, cols), F32), jax.ShapeDtypeStruct((rows, whole.shape[1] - cols), F32)],
        compiler_params=pltpu.CompilerParams(vmem_limit_bytes=8 * 1024 * 1024),
        cost_estimate=COST,
        name="place_feed",
    )(whole, rest)


def block_kernel(own, first, one, two, out):
    out[...] = (own[...] + first[...] + one[...].astype(F32) + two[...].astype(F32)).astype(BF)


def add_block(own, first, one, two):
    vmem = pl.BlockSpec(memory_space=pltpu.VMEM)
    return pl.pallas_call(
        block_kernel,
        in_specs=[vmem] * 4,
        out_specs=vmem,
        out_shape=jax.ShapeDtypeStruct(own.shape, BF),
        compiler_params=pltpu.CompilerParams(vmem_limit_bytes=12 * 1024 * 1024),
        cost_estimate=COST,
        name="add_block",
    )(own, first, one, two)


def relay_kernel(one, two, low, high, one_o, two_o):
    half = low.shape[0]
    one_o[0:half, :] = (one[0:half, :] + low[...].astype(F32)).astype(BF)
    one_o[half:, :] = one[half:, :].astype(BF)
    two_o[0:half, :] = two[0:half, :].astype(BF)
    two_o[half:, :] = (two[half:, :] + high[...].astype(F32)).astype(BF)


def relay(one, two, low, high):
    return pl.pallas_call(
        relay_kernel,
        in_specs=[pl.BlockSpec(memory_space=pltpu.VMEM)] * 4,
        out_specs=[pl.BlockSpec(memory_space=pltpu.VMEM)] * 2,
        out_shape=[jax.ShapeDtypeStruct(one.shape, BF)] * 2,
        compiler_params=pltpu.CompilerParams(vmem_limit_bytes=16 * 1024 * 1024),
        cost_estimate=COST,
        name="relay",
    )(one, two, low, high)


def rotation_tables(offsets):
    lane = np.arange(128)
    frequency = (10000.0 ** (-2.0 * (lane % HEAD // 2) / HEAD)).astype(np.float32)
    angles = offsets.astype(F32)[:, None] * frequency[None, :]
    sign = np.where(lane % 2 == 0, -1.0, 1.0).astype(np.float32)
    return jnp.cos(angles), jnp.sin(angles) * sign


def key_bounds(segment):
    length = segment.shape[0]
    first, last = segment[::BLOCK], segment[BLOCK - 1 :: BLOCK]
    low = jnp.sum(segment[None, :] < first[:, None], axis=1)
    high = jnp.sum(segment[None, :] <= last[:, None], axis=1)
    low = low // 128 * 128
    count = (high - low + CHUNK - 1) // CHUNK
    return jnp.stack([jnp.minimum(low, length - CHUNK * count), count], axis=1).reshape(-1).astype(jnp.int32)


def swap_ctx(x):
    return lax.ppermute(x, "ctx", [(0, 1), (1, 0)])


def swap_tp(x, k):
    return lax.ppermute(x, "tp", [(i, i ^ k) for i in range(4)])


def swap_shard(x, k):
    return lax.ppermute(x, "shard", [(i, i ^ k) for i in range(4)])


def order_four(parts, index):
    a, b, c, d = parts
    odd, high = index % 2 == 1, index // 2 == 1
    a, b = jnp.where(odd, b, a), jnp.where(odd, a, b)
    c, d = jnp.where(odd, d, c), jnp.where(odd, c, d)
    return jnp.stack([jnp.where(high, c, a), jnp.where(high, d, b), jnp.where(high, a, c), jnp.where(high, b, d)])


def after(x, *others):
    return lax.optimization_barrier((x, others))[0]


def gather_tp(x, half):
    one, two = swap_tp(x, 1), swap_tp(x, 2)
    three = jnp.concatenate([swap_tp(one[:half], 2), swap_tp(two[half:], 1)])
    return [x, one, two, three]


def scatter_tp(parts):
    own, one, two, three = parts
    half = own.shape[0] // 2
    low, high = three[:half].astype(BF), three[half:].astype(BF)
    low, high = swap_tp(low, 2), swap_tp(high, 1)
    one = jnp.concatenate([one[:half] + low.astype(F32), one[half:]]).astype(BF)
    two = jnp.concatenate([two[:half], two[half:] + high.astype(F32)]).astype(BF)
    return own + swap_tp(one, 1).astype(F32) + swap_tp(two, 2).astype(F32)


def three_rows(x):
    high = lax.reduce_precision(x, 8, 7)
    middle = lax.reduce_precision(x - high, 8, 7)
    return jnp.stack([high, middle, x - high - middle]).astype(BF)


def contract_last(left, right):
    return lax.dot_general(left, right, (((1,), (1,)), ((), ())), preferred_element_type=F32)


def body(tokens, segment_ids, offsets, qkv_weight, out_weight, ffn_weight, qkv_bias, ffn_bias, norm_gain, shift_params, out_grad):
    t, c, z = lax.axis_index("tp"), lax.axis_index("ctx"), lax.axis_index("shard")
    shards = lax.axis_size("shard")
    half_len, width = tokens.shape[1:]
    rows, _, part = qkv_weight.shape
    hidden = ffn_weight.shape[2]
    heads = part // HEAD
    length = 2 * half_len
    share = length // 4
    first_core = c == 0
    direct = shards == 4

    def take(x, index):
        return lax.dynamic_index_in_dim(x, index, 0, keepdims=False)

    def by_core(own, other):
        return jnp.where(first_core, jnp.stack([own, other]), jnp.stack([other, own]))

    hh = hidden // 2
    gathered = jnp.concatenate([ffn_weight.reshape(rows, 2 * hidden), out_weight], axis=1)
    gathered = lax.all_gather(gathered, ("tp", "shard", "ctx"), axis=0, tiled=True).reshape(4, width, 2 * hidden + part)
    bias_all = ffn_bias.reshape(1, hidden)
    bias_all = jnp.concatenate([bias_all] + [swap_tp(bias_all, k) for k in (1, 2, 3)])
    qkv_rows = qkv_weight.reshape(rows, 3 * part)
    other_tokens = swap_ctx(take(tokens, 1 - c))
    if direct:
        places = [((z ^ j) * 2 + (c ^ f)) * rows for f in (0, 1) for j in range(4)]
        near = [qkv_rows] + [swap_shard(qkv_rows, j) for j in (1, 2, 3)]
        qkv_pieces = [*near, swap_ctx(jnp.stack(near))]
    else:
        places = [jnp.zeros_like(c)]
        qkv_pieces = [lax.all_gather(qkv_rows, ("shard", "ctx"), axis=0, tiled=True)]
    per = len(places)
    place = jnp.stack(places + [c, t]).astype(jnp.int32)
    bias_pad = jnp.pad(qkv_bias, ((0, 0), (0, WIDE - part)))
    vec = jnp.concatenate([norm_gain, shift_params, jnp.zeros((2, width), F32)])

    marks = jnp.stack([segment_ids, offsets])
    marks = by_core(take(marks.swapaxes(0, 1), c), swap_ctx(take(marks.swapaxes(0, 1), 1 - c)))
    segment, places = marks[:, 0].reshape(length), marks[:, 1].reshape(length)
    halves = lambda x: x.reshape(2, 2, share, width)
    here = t // 2 == c
    tok_block = jnp.where(here, take(take(halves(tokens), c), t % 2), take(other_tokens.reshape(2, share, width), t % 2))
    grad_block = halves(out_grad)
    grad_far = swap_ctx(take(take(grad_block, 1 - c), t % 2))
    grad_top = jnp.where(here, take(take(grad_block, c), t % 2), grad_far)

    cosine, sine = rotation_tables(places)
    bounds = key_bounds(segment)
    seg_column = segment[:, None]
    seg_row = jnp.broadcast_to(segment[None, :], (8, length))
    q, k_rows, v_rows, k_turned, q_turned, qkv_wide = project_qkv(place, qkv_pieces, per, bias_pad, tokens, other_tokens, cosine, sine, part)

    contexts, log_totals, fulls = [None] * 4, [None] * 4, [None] * 4

    def forward(j, q):
        spot = jnp.concatenate([((t ^ j) * (share // BLOCK))[None].astype(jnp.int32), bounds])
        context, log_totals[j], fulls[j] = attention_forward(spot, q, k_rows, v_rows, seg_column, seg_row, heads, share)
        contexts[j] = swap_tp(context, j) if j else context

    forward(3, q)
    q_next, log_totals[3] = lax.optimization_barrier((q, log_totals[3]))
    forward(1, q_next)
    q_next, log_totals[1], contexts[3] = lax.optimization_barrier((q, log_totals[1], contexts[3]))
    forward(2, q_next)
    q_next, log_totals[2], contexts[1] = lax.optimization_barrier((q, log_totals[2], contexts[1]))
    forward(0, q_next)
    stacked = jnp.stack(contexts)
    tok_block, log_total, full, stacked = lax.optimization_barrier(
        (tok_block, jnp.concatenate(log_totals, axis=1), jnp.concatenate(fulls), stacked)
    )

    layer_out, grad_second, grad_second_b, first_scaled, normed_t, second_t, activated, slope, root, sums_two = feed_forward(
        place, gathered, contexts, tok_block, grad_top, vec, bias_all
    )

    barrier = lax.optimization_barrier
    out_blocks = [layer_out, swap_tp(layer_out, 1), swap_tp(layer_out, 2)]

    grad_first, first_t, g0, g1, g2, g3, grad_hidden, hidden_sums, sums_one = feed_back(
        place, gathered, grad_second, grad_second_b, first_scaled, slope, root, vec, part
    )
    heads_grads = [g0, swap_tp(g1, 1), swap_tp(g2, 2), swap_tp(g3, 3)]

    *made, whole = weight_grads(place, per, normed_t, second_t, first_t, stacked, grad_hidden, activated)
    made, whole, heads_grads, out_blocks = barrier((made, whole, heads_grads, out_blocks))
    whole = lax.psum_scatter(whole.reshape(-1, 2 * hh + part), ("tp", "shard", "ctx"), scatter_dimension=0, tiled=True)
    grad_heads = heads_grads
    corner = [out_blocks[1][: share // 2], out_blocks[2][share // 2 :]]
    if direct:
        got = swap_ctx(made[1])
        grad_heads, got, corner = barrier((grad_heads, got, corner))
        packs = [made[0][k].astype(F32) + got[k].astype(F32) for k in range(4)]
        sent = [packs[k].astype(BF) for k in (1, 2, 3)]
        grad_heads, sent = barrier((grad_heads, sent))
        sent = [swap_tp(sent[k - 1], k) for k in (1, 2, 3)]
    corner = [swap_tp(corner[0], 2), swap_tp(corner[1], 1)]

    spot = jnp.concatenate([(t * (share // BLOCK))[None].astype(jnp.int32), bounds])
    grad_proj, bias_sums = attention_backward(
        spot, q, q_turned, k_rows, k_turned, v_rows, grad_heads, full, log_total, seg_column, seg_row, cosine, sine, heads
    )
    grad_proj, bias_sums, corner, hidden_sums, sums_one, sums_two = barrier((grad_proj, bias_sums, corner, hidden_sums, sums_one, sums_two))
    if direct:
        grad_proj, sent, packs[0] = barrier((grad_proj, sent, packs[0]))

    three = branch(place, (3,), (BF,), grad_proj, qkv_wide)[0]
    three, grad_proj, corner, bias_sums = barrier((three, grad_proj, corner, bias_sums))
    low, high = swap_tp(three[: share // 2], 2), swap_tp(three[share // 2 :], 1)
    one, two, own = branch(place, (1, 2, 0), (F32, F32, F32), grad_proj, qkv_wide)
    keep_a, send_a = pick(place, out_blocks[0], out_blocks[2])
    keep_b, send_b = pick(place, out_blocks[1], *corner)
    small = collect(place, hidden_sums, sums_one, sums_two, bias_sums)
    outs = [keep_a, keep_b, send_a, send_b]
    low, high, one, two, own, outs, grad_proj, small = barrier((low, high, one, two, own, outs, grad_proj, small))

    one, two = relay(one, two, low, high)
    one, two, outs, grad_proj, small = barrier((one, two, outs, grad_proj, small))
    one, two = swap_tp(one, 1), swap_tp(two, 2)
    grads = qkv_weight_grads(place, per, tokens, other_tokens, grad_proj, part)
    outputs = join(place, outs[:2], [swap_ctx(outs[2]), swap_ctx(outs[3])])

    def send_shards(pieces, small, k):
        moved = [swap_shard(pieces[j - 1], j) for j in (1, 2, 3)]
        moved[0], small = barrier((moved[0], small))
        return moved, small + swap_tp(small, k)

    if direct:
        summed, *pieces = settle(packs[0], *sent)
        small = small + swap_ctx(small)
        small = small + swap_shard(small, 1)
        small = small + swap_shard(small, 2)
        qkv_sum, *qkv_pieces = settle(grads[0], swap_ctx(grads[1]))
        one, two, own, small, outputs, summed, pieces, qkv_sum, qkv_pieces = barrier(
            (one, two, own, small, outputs, summed, pieces, qkv_sum, qkv_pieces)
        )
    else:
        one, two, own, small, outputs = barrier((one, two, own, small, outputs))

    block = add_block(own, grad_first, one, two)
    ready = [block, swap_tp(block, 1), swap_tp(block, 2)]
    if direct:
        moved, small = send_shards(pieces, small, 1)
        total = finish(1, summed, *moved)
        ready, total, small, qkv_pieces = barrier((ready, total, small, qkv_pieces))
        moved, small = send_shards(qkv_pieces, small, 2)
        qkv_total = finish(3, qkv_sum, *moved)
    else:
        qkv_total = lax.psum_scatter(grads[0], ("shard", "ctx"), scatter_dimension=0, tiled=True).reshape(rows, 3, part)
        total = lax.psum_scatter(made[0].reshape(-1, 2 * hh), ("tp", "shard", "ctx"), scatter_dimension=0, tiled=True).astype(F32)
    corner = [swap_tp(ready[1][: share // 2], 2), swap_tp(ready[2][share // 2 :], 1)]
    keep_a, send_a = pick(place, ready[0], ready[2])
    other_a = swap_ctx(send_a)
    grad_ffn_weight, grad_out_weight = place_feed(whole, total)
    small = small if direct else lax.psum(small, ("shard", "ctx", "tp"))
    corner, grad_ffn_weight, grad_out_weight, small, keep_a, other_a, qkv_total = barrier(
        (corner, grad_ffn_weight, grad_out_weight, small, keep_a, other_a, qkv_total)
    )
    keep_b, send_b = pick(place, ready[1], *corner)
    grad_tokens = join(place, [keep_a, keep_b], [other_a, swap_ctx(send_b)])

    grad_qkv_weight = qkv_total
    grad_ffn_bias = take(small, t)
    vectors = small[4:10]
    grad_qkv_bias = take(small[10:14], t).reshape(3, WIDE)[:, :part]
    return (
        outputs,
        grad_tokens,
        grad_qkv_weight,
        grad_out_weight,
        grad_ffn_weight,
        grad_qkv_bias,
        grad_ffn_bias,
        vectors[:2],
        vectors[2:],
    )


def solution(mesh):
    return jax.shard_map(
        body,
        mesh=mesh,
        in_specs=(
            P("shard", "ctx", None),
            P("shard", "ctx"),
            P("shard", "ctx"),
            P(("shard", "ctx"), None, "tp"),
            P(("shard", "ctx"), "tp"),
            P(("shard", "ctx"), None, "tp"),
            P(None, "tp"),
            P("tp"),
            P(),
            P(),
            P("shard", "ctx", None),
        ),
        out_specs=(
            P("shard", "ctx", None),
            P("shard", "ctx", None),
            P(("shard", "ctx"), None, "tp"),
            P(("shard", "ctx"), "tp"),
            P(("shard", "ctx"), None, "tp"),
            P(None, "tp"),
            P("tp"),
            P(),
            P(),
        ),
        check_vma=False,
    )
```

```python
from functools import partial

import jax
import jax.numpy as jnp
import numpy as np
from jax import lax
from jax.experimental import pallas as pl
from jax.experimental.pallas import tpu as pltpu
from jax.sharding import PartitionSpec as P

HEAD = 64
WIDE = 256
BLOCK = 256
CHUNK = 256
EPSILON = 1e-12
F32 = jnp.float32
BF = jnp.bfloat16
NEG = -1e30
COST = pl.CostEstimate(flops=0, bytes_accessed=0, transcendentals=0)


def swap_pairs(x):
    lane = lax.broadcasted_iota(jnp.int32, x.shape, 1)
    n = x.shape[1]
    return jnp.where(lane % 2 == 0, pltpu.roll(x, n - 1, 1), pltpu.roll(x, 1, 1))


def nt(a, b):
    return lax.dot_general(a, b, (((1,), (1,)), ((), ())), preferred_element_type=F32)


def nn(a, b):
    return lax.dot_general(a, b, (((1,), (0,)), ((), ())), preferred_element_type=F32)


def twice(x):
    return jnp.concatenate([x, x], axis=1)


def lanes_of_heads(x, heads):
    lane = lax.broadcasted_iota(jnp.int32, x.shape, 1) // HEAD
    return [jnp.where(lane == h, x, jnp.zeros_like(x)) for h in range(heads)]


def whole_block(shape, buffers=1):
    return pl.BlockSpec(shape, lambda *_: (0,) * len(shape), pipeline_mode=pl.Buffered(buffers))


def smem():
    return pl.BlockSpec(memory_space=pltpu.SMEM)


def params(mib):
    return pltpu.CompilerParams(dimension_semantics=("arbitrary",), vmem_limit_bytes=mib * 1024 * 1024)


def qkv_kernel(count, per, part, place, *refs):
    pieces = []
    for x in refs[:count]:
        pieces += [x] if len(x.shape) == 2 else [x.at[n] for n in range(x.shape[0])]
    bias, own, other, cos, sin, q_o, k_o, v_o, kt_o, qt_o, w_o = refs[count:]
    piece_rows = pieces[0].shape[0]
    pad = jnp.zeros((piece_rows, WIDE - part), BF)
    for n in range(per):
        sl = pl.ds(pl.multiple_of(place[n], 16), piece_rows)
        for m in range(3):
            w_o[sl, m * WIDE : (m + 1) * WIDE] = jnp.concatenate([pieces[n][:, m * part : (m + 1) * part], pad], axis=1)
    half_len = other.shape[0]

    def run(x, sl):
        c, s = twice(cos[sl, :]), twice(sin[sl, :])
        p = nn(x, w_o[:, 0:WIDE]) + bias[0:1, :]
        q = ((p * c + swap_pairs(p) * s).astype(BF).astype(F32) * (HEAD**-0.5)).astype(BF)
        q_o[sl, :] = q
        qt_o[:, sl] = q.T
        p = nn(x, w_o[:, WIDE : 2 * WIDE]) + bias[1:2, :]
        k = (p * c + swap_pairs(p) * s).astype(BF)
        k_o[sl, :] = k
        kt_o[:, sl] = k.T
        v_o[sl, :] = (nn(x, w_o[:, 2 * WIDE : 3 * WIDE]) + bias[2:3, :]).astype(BF)

    def step(r, _):
        rows = pl.ds(pl.multiple_of(r * BLOCK, BLOCK), BLOCK)
        core = place[per]
        run(own[0, rows, :], pl.ds(pl.multiple_of(core * half_len + r * BLOCK, BLOCK), BLOCK))
        run(other[rows, :], pl.ds(pl.multiple_of((1 - core) * half_len + r * BLOCK, BLOCK), BLOCK))
        return 0

    lax.fori_loop(0, half_len // BLOCK, step, 0)


def project_qkv(place, pieces, per, bias, tokens, other, cos, sin, part):
    half_len, width = other.shape
    length, count = 2 * half_len, len(pieces)
    return pl.pallas_call(
        partial(qkv_kernel, count, per, part),
        grid_spec=pltpu.PrefetchScalarGridSpec(
            num_scalar_prefetch=1,
            grid=(1,),
            in_specs=[whole_block(p.shape) for p in pieces]
            + [whole_block(bias.shape), pl.BlockSpec((1, half_len, width), lambda i, s: (s[per], 0, 0))]
            + [whole_block(x.shape) for x in (other, cos, sin)],
            out_specs=[whole_block((length, WIDE))] * 3 + [whole_block((WIDE, length))] * 2 + [whole_block((width, 3 * WIDE))],
        ),
        out_shape=[jax.ShapeDtypeStruct((length, WIDE), BF)] * 3
        + [jax.ShapeDtypeStruct((WIDE, length), BF)] * 2
        + [jax.ShapeDtypeStruct((width, 3 * WIDE), BF)],
        compiler_params=params(32),
        cost_estimate=COST,
        name="project_qkv",
    )(place, *pieces, bias, tokens, other, cos, sin)


def forward_kernel(heads, place, q, k, v, segc, segr, ctx_o, lse_o, full_o, acc, s_sc, m_sc, l_sc, qc_sc):
    i = place[0] + pl.program_id(0)
    start, count = place[1 + 2 * i], place[2 + 2 * i]
    qc_sc[...] = jnp.concatenate(lanes_of_heads(q[...], heads), axis=0)
    seg_q = segc[...]
    m_sc[...] = jnp.full(m_sc.shape, NEG, F32)
    l_sc[...] = jnp.zeros(l_sc.shape, F32)

    def at(j):
        return pl.ds(pl.multiple_of(start + j * CHUNK, 128), CHUNK)

    def of(h):
        return slice(h * BLOCK, (h + 1) * BLOCK)

    def pass1(j, _):
        s = nt(qc_sc[...], k[at(j), :])
        keep = seg_q == segr[0:1, at(j)]
        for h in range(heads):
            sh = jnp.where(keep, s[of(h), :], NEG)
            s_sc[j, of(h), :] = sh
            m_sc[of(h), :] = jnp.maximum(m_sc[of(h), :], jnp.maximum(sh[:, :128], sh[:, 128:]))
        return 0

    lax.fori_loop(0, count, pass1, 0)
    m_sc[...] = jnp.broadcast_to(jnp.max(m_sc[...], axis=1, keepdims=True), m_sc.shape)

    def pass2(j, _):
        for h in range(heads):
            e = jnp.exp(s_sc[j, of(h), :] - twice(m_sc[of(h), :]))
            s_sc[j, of(h), :] = e
            l_sc[of(h), :] += e[:, :128] + e[:, 128:]
        return 0

    lax.fori_loop(0, count, pass2, 0)
    total = jnp.sum(l_sc[...], axis=1, keepdims=True)
    lse = m_sc[:, 0:1] + jnp.log(total)
    l_sc[...] = jnp.broadcast_to(1.0 / total, l_sc.shape)
    lane = lax.broadcasted_iota(jnp.int32, (BLOCK, 128), 1)
    tile = jnp.zeros((BLOCK, 128), F32)
    for h in range(heads):
        tile = jnp.where(lane == h, lse[of(h), :], tile)
    lse_o[...] = tile.T[0:8, :]
    acc[...] = jnp.zeros(acc.shape, F32)
    full_o[...] = jnp.zeros(full_o.shape, F32)

    def pass3(j, _):
        ps, less = [], []
        for h in range(heads):
            p = s_sc[j, of(h), :] * twice(l_sc[of(h), :])
            b = p.astype(BF)
            ps.append(b)
            less.append((p - b.astype(F32)).astype(BF))
        vs = jnp.concatenate(lanes_of_heads(v[at(j), :], heads), axis=0)
        acc[...] += nn(jnp.concatenate(ps, axis=1), vs)
        full_o[...] += nn(jnp.concatenate(less, axis=1), vs)
        return 0

    lax.fori_loop(0, count, pass3, 0)
    ctx_o[...] = acc[:, : heads * HEAD].astype(BF)
    full_o[...] += acc[...]


def attention_forward(place, q, k, v, segc, segr, heads, share):
    length = q.shape[0]
    grid = share // BLOCK
    rows = lambda i, s: (s[0] + i, 0)
    return pl.pallas_call(
        partial(forward_kernel, heads),
        grid_spec=pltpu.PrefetchScalarGridSpec(
            num_scalar_prefetch=1,
            grid=(grid,),
            in_specs=[
                pl.BlockSpec((BLOCK, WIDE), rows),
                whole_block(k.shape),
                whole_block(v.shape),
                pl.BlockSpec((BLOCK, 1), rows),
                whole_block(segr.shape),
            ],
            out_specs=[
                pl.BlockSpec((BLOCK, heads * HEAD), lambda i, s: (i, 0)),
                pl.BlockSpec((8, BLOCK), lambda i, s: (0, i)),
                pl.BlockSpec((BLOCK, WIDE), lambda i, s: (i, 0)),
            ],
            scratch_shapes=[
                pltpu.VMEM((BLOCK, WIDE), F32),
                pltpu.VMEM((length // CHUNK, heads * BLOCK, CHUNK), F32),
                pltpu.VMEM((heads * BLOCK, 128), F32),
                pltpu.VMEM((heads * BLOCK, 128), F32),
                pltpu.VMEM((heads * BLOCK, WIDE), BF),
            ],
        ),
        out_shape=[
            jax.ShapeDtypeStruct((share, heads * HEAD), BF),
            jax.ShapeDtypeStruct((8, share), F32),
            jax.ShapeDtypeStruct((share, WIDE), F32),
        ],
        compiler_params=params(16),
        cost_estimate=COST,
        name="attention_forward",
    )(place, q, k, v, segc, segr)


def backward_kernel(heads, place, q, qt, k, kt, v, d0, d1, d2, d3, full, lse, segc, segr, cos, sin, g_o, gb_o, dk_sc, dv_sc, qc_sc, dc_sc, dq_sc, d_sc, dt_sc, qs_sc):
    step_at = pl.program_id(0)
    blocks = k.shape[0] // BLOCK

    @pl.when(step_at < blocks)
    def _():
        backward_rows(heads, place, q, qt, k, kt, v, (d0, d1, d2, d3), full, lse, segc, segr, dk_sc, dv_sc, qc_sc, dc_sc, dq_sc, d_sc, dt_sc, qs_sc)

    @pl.when(step_at == 0)
    def _():
        gb_o[...] = jnp.zeros(gb_o.shape, F32)

    @pl.when(step_at >= blocks)
    def _():
        at = pl.ds(pl.multiple_of((step_at - blocks) * BLOCK, BLOCK), BLOCK)

        def turn(x):
            return (x * twice(cos[...]) - swap_pairs(x) * twice(sin[...])).astype(BF)

        def put(x, m):
            g_o[:, m * WIDE : (m + 1) * WIDE] = x
            gb_o[0:1, m * WIDE : (m + 1) * WIDE] += jnp.sum(x.astype(F32), axis=0, keepdims=True)

        put(turn(qs_sc[:, at].T * (HEAD**-0.5)), 0)
        put(turn(dk_sc[:, at].T), 1)
        put(dv_sc[:, at].astype(BF).T, 2)


def backward_rows(heads, place, q, qt, k, kt, v, do, full, lse, segc, segr, dk_sc, dv_sc, qc_sc, dc_sc, dq_sc, d_sc, dt_sc, qs_sc):
    step_at = pl.program_id(0)
    i = step_at ^ place[0]
    part = do[0].shape[1]
    per = do[0].shape[0] // BLOCK

    @pl.when(step_at == 0)
    def _():
        dk_sc[...] = jnp.zeros(dk_sc.shape, F32)
        dv_sc[...] = jnp.zeros(dv_sc.shape, F32)
        d_sc[...] = jnp.zeros(d_sc.shape, BF)

    for n, d in enumerate(do):

        @pl.when(step_at // per == n)
        def _(d=d):
            d_sc[:, 0:part] = d[pl.ds(pl.multiple_of(step_at % per * BLOCK, BLOCK), BLOCK), :]

    start, count = place[1 + 2 * i], place[2 + 2 * i]
    qc_sc[...] = jnp.concatenate(lanes_of_heads(q[...], heads), axis=0)
    dz = d_sc[...]
    dc_sc[...] = jnp.concatenate(lanes_of_heads(dz, heads), axis=0)
    dt_sc[...] = dz.T
    dq_sc[...] = jnp.zeros(dq_sc.shape, F32)
    own = pl.ds(pl.multiple_of(i * BLOCK, BLOCK), BLOCK)
    seg_q = segr[0:1, own]
    row = lax.broadcasted_iota(jnp.int32, (8, WIDE), 0)
    lane = lax.broadcasted_iota(jnp.int32, (8, WIDE), 1) // HEAD
    pick = jnp.where(row == lane, 1.0, 0.0).astype(F32)
    delta = lax.dot_general(
        pick, dz.astype(F32) * full[...], (((1,), (1,)), ((), ())), preferred_element_type=F32, precision=lax.Precision.HIGHEST
    )

    def of(h):
        return slice(h * BLOCK, (h + 1) * BLOCK)

    def step(j, _):
        at = pl.ds(pl.multiple_of(start + j * CHUNK, 128), CHUNK)
        s = nt(k[at, :], qc_sc[...])
        dp = nt(v[at, :], dc_sc[...])
        keep = segc[at, :] == seg_q
        for h in range(heads):
            mine = slice(h * HEAD, (h + 1) * HEAD)
            p = jnp.exp(jnp.where(keep, s[:, of(h)], NEG) - lse[h : h + 1, :])
            ds = (p * (dp[:, of(h)] - delta[h : h + 1, :])).astype(BF)
            dq_sc[mine, :] += nn(kt[mine, at], ds)
            dv_sc[mine, at] += nt(dt_sc[mine, :], p.astype(BF))
            dk_sc[mine, at] += nt(qt[mine, :], ds)
        return 0

    def pair(j, _):
        step(2 * j, 0)
        step(2 * j + 1, 0)
        return 0

    lax.fori_loop(0, count // 2, pair, 0)

    @pl.when(count % 2 == 1)
    def _():
        step(count - 1, 0)

    qs_sc[:, own] = dq_sc[...]


def attention_backward(place, q, qt, k, kt, v, do, full, lse, segc, segr, cos, sin, heads):
    length = k.shape[0]
    blocks = length // BLOCK
    first = lambda i: jnp.minimum(i, blocks - 1)
    second = lambda i: jnp.maximum(i - blocks, 0)
    return pl.pallas_call(
        partial(backward_kernel, heads),
        grid_spec=pltpu.PrefetchScalarGridSpec(
            num_scalar_prefetch=1,
            grid=(2 * blocks,),
            in_specs=[
                pl.BlockSpec((BLOCK, WIDE), lambda i, s: (first(i) ^ s[0], 0)),
                pl.BlockSpec((WIDE, BLOCK), lambda i, s: (0, first(i) ^ s[0])),
                whole_block(k.shape),
                whole_block(kt.shape),
                whole_block(v.shape),
                *[whole_block(d.shape) for d in do],
                pl.BlockSpec((BLOCK, WIDE), lambda i, s: (first(i), 0)),
                pl.BlockSpec((8, BLOCK), lambda i, s: (0, first(i))),
                whole_block(segc.shape),
                whole_block(segr.shape),
                pl.BlockSpec((BLOCK, 128), lambda i, s: (second(i), 0)),
                pl.BlockSpec((BLOCK, 128), lambda i, s: (second(i), 0)),
            ],
            out_specs=[pl.BlockSpec((BLOCK, 3 * WIDE), lambda i, s: (second(i), 0)), whole_block((8, 3 * WIDE))],
            scratch_shapes=[pltpu.VMEM((WIDE, length), F32)] * 2
            + [pltpu.VMEM((heads * BLOCK, WIDE), BF)] * 2
            + [pltpu.VMEM((WIDE, BLOCK), F32), pltpu.VMEM((BLOCK, WIDE), BF), pltpu.VMEM((WIDE, BLOCK), BF)]
            + [pltpu.VMEM((WIDE, length), F32)],
        ),
        out_shape=[jax.ShapeDtypeStruct((length, 3 * WIDE), BF), jax.ShapeDtypeStruct((8, 3 * WIDE), F32)],
        compiler_params=params(28),
        cost_estimate=COST,
        name="attention_backward",
    )(place, q, qt, k, kt, v, *do, full, lse, segc, segr, cos, sin)


def out_copies(place, gathered, w_out, sems):
    here = place[place.shape[0] - 1]
    feed = gathered.shape[2] - w_out.shape[2]
    return [pltpu.make_async_copy(gathered.at[here ^ k, :, feed:], w_out.at[k], sems.at[k]) for k in range(4)]


def row_mean(x):
    return jnp.mean(x, axis=1, keepdims=True)


def gelu_parts(x):
    e = jnp.exp2(x * x * (-0.5 * 1.4426950408889634))
    t = 1.0 / (1.0 + (0.3275911 * 0.7071067811865476) * jnp.abs(x))
    p = t * (0.127414796 + t * (-0.142248368 + t * (0.7107068705 + t * (-0.7265760135 + t * 0.5307027145))))
    tail = p * e
    phi = jnp.where(x >= 0, 1.0 - tail, tail)
    return phi, phi + x * e * 0.3989422804014327


ROWS = 512


def feed_kernel(place, gathered, w, c0, c1, c2, c3, tokb, gtop, vec, bias, *refs):
    (out_o, gs_o, gsb_o, fs_o, nbt_o, gst_o, act_o, gp_o, root_o, sum_o, nb_o, w_out, acc, normed, sems) = refs
    copies = out_copies(place, gathered, w_out, sems)
    k = pl.program_id(0)
    share = tokb.shape[0]
    part = c0.shape[1]
    chunks = [pl.ds(r * ROWS, ROWS) for r in range(share // ROWS)]

    @pl.when(k == 0)
    def _():
        for copy in copies:
            copy.start()
        for copy in copies:
            copy.wait()
        for sl in chunks:
            x = tokb[sl, :].astype(F32) + vec[4:5, :]
            for n, ctx in enumerate((c0, c1, c2, c3)):
                x = x + nt(ctx[sl, :], w_out[n, :, 0:part])
            x = x - row_mean(x)
            root = lax.rsqrt(row_mean(x * x) + EPSILON)
            x = x * root
            fs_o[sl, :] = x
            root_o[sl, :] = jnp.broadcast_to(root, (ROWS, 128))
            y = x * vec[0:1, :] + vec[2:3, :]
            normed[sl, :] = y
            nb_o[sl, :] = y.astype(BF)
            nbt_o[:, sl] = y.astype(BF).T
            acc[sl, :] = y + vec[5:6, :]

    hidden = act_o.shape[2]

    def rows_step(r, _):
        sl = pl.ds(pl.multiple_of(r * ROWS, ROWS), ROWS)
        h = nn(nb_o[sl, :], w[0, :, 0:hidden]) + bias[pl.ds(k, 1), :]
        phi, slope = gelu_parts(h)
        a = (h * phi).astype(BF)
        act_o[0, sl, :] = a
        gp_o[0, sl, :] = slope
        acc[sl, :] += nt(a, w[0, :, hidden:])
        return 0

    lax.fori_loop(0, share // ROWS, rows_step, 0, unroll=True)

    @pl.when(k == 3)
    def _():
        total = [jnp.zeros((1, tokb.shape[1]), F32)] * 3
        for sl in chunks:
            x = acc[sl, :]
            x = x - row_mean(x)
            root = lax.rsqrt(row_mean(x * x) + EPSILON)
            x = x * root
            out_o[sl, :] = (x * vec[1:2, :] + vec[3:4, :]).astype(BF)
            g = gtop[sl, :].astype(F32)
            gg = g * vec[1:2, :]
            gs = root * (gg - row_mean(gg) - x * row_mean(gg * x))
            gs_o[sl, :] = gs
            gsb_o[sl, :] = gs.astype(BF)
            gst_o[:, sl] = gs.astype(BF).T
            for n, y in enumerate((g * x, g, gs)):
                total[n] = total[n] + jnp.sum(y, axis=0, keepdims=True)
        sum_o[...] = jnp.concatenate(total + [jnp.zeros((5, tokb.shape[1]), F32)], axis=0)


def feed_specs(place, gathered, hidden):
    width, last = gathered.shape[1], place.shape[0] - 1
    return [pl.BlockSpec(memory_space=pl.ANY), pl.BlockSpec((1, width, 2 * hidden), lambda i, s: (s[last] ^ i, 0, 0))]


def feed_forward(place, gathered, contexts, tokb, gtop, vec, bias):
    share, width = tokb.shape
    hidden = bias.shape[1]
    block = lambda: pl.BlockSpec((1, share, hidden), lambda i, s: (i, 0, 0))
    sd, far = jax.ShapeDtypeStruct, pltpu.HBM
    return pl.pallas_call(
        feed_kernel,
        grid_spec=pltpu.PrefetchScalarGridSpec(
            num_scalar_prefetch=1,
            grid=(4,),
            in_specs=feed_specs(place, gathered, hidden) + [whole_block(x.shape) for x in (*contexts, tokb, gtop, vec, bias)],
            out_specs=[whole_block((share, width))] * 4
            + [whole_block((width, share))] * 2
            + [block(), block(), whole_block((share, 128)), whole_block((8, width))],
            scratch_shapes=[
                pltpu.VMEM((share, width), BF),
                pltpu.VMEM((4, width, gathered.shape[2] - 2 * hidden), BF),
                pltpu.VMEM((share, width), F32),
                pltpu.VMEM((share, width), F32),
                pltpu.SemaphoreType.DMA((4,)),
            ],
        ),
        out_shape=[
            sd((share, width), BF),
            sd((share, width), F32),
            sd((share, width), BF),
            sd((share, width), F32),
            far((width, share), BF),
            far((width, share), BF),
            far((4, share, hidden), BF),
            far((4, share, hidden), F32),
            sd((share, 128), F32),
            sd((8, width), F32),
        ],
        compiler_params=params(54),
        cost_estimate=COST,
        name="feed_forward",
    )(place, gathered, gathered, *contexts, tokb, gtop, vec, bias)


def feed_back_kernel(place, gathered, w, gs, gsb, fs, gp, root, vec, *refs):
    (gf_o, gft_o, gc0, gc1, gc2, gc3, gh_o, ghs_o, sum_o, w_out, acc, sems) = refs
    copies = out_copies(place, gathered, w_out, sems)
    k = pl.program_id(0)
    share, width = gs.shape
    hidden, part = gh_o.shape[2], gc0.shape[1]

    @pl.when(k == 0)
    def _():
        for copy in copies:
            copy.start()
        acc[...] = gs[...]

    def rows_step(r, total):
        sl = pl.ds(pl.multiple_of(r * ROWS, ROWS), ROWS)
        g = (nn(gsb[sl, :], w[0, :, hidden:]) * gp[0, sl, :]).astype(BF)
        gh_o[0, sl, :] = g
        acc[sl, :] += nt(g, w[0, :, 0:hidden])
        return total + jnp.sum(g.astype(F32), axis=0, keepdims=True)

    total = lax.fori_loop(0, share // ROWS, rows_step, jnp.zeros((1, hidden), F32), unroll=True)
    ghs_o[0] = jnp.broadcast_to(total, (8, hidden))

    @pl.when(k == 3)
    def _():
        for copy in copies:
            copy.wait()
        sums = [jnp.zeros((1, width), F32)] * 3
        for r in range(share // ROWS):
            sl = pl.ds(r * ROWS, ROWS)
            gn = acc[sl, :]
            x = fs[sl, :]
            gg = gn * vec[0:1, :]
            gf = root[sl, 0:1] * (gg - row_mean(gg) - x * row_mean(gg * x))
            gf_o[sl, :] = gf
            b = gf.astype(BF)
            gft_o[:, sl] = b.T
            for n, o in enumerate((gc0, gc1, gc2, gc3)):
                o[sl, :] = nn(b, w_out[n, :, 0:part]).astype(BF)
            for n, y in enumerate((gn * x, gn, gf)):
                sums[n] = sums[n] + jnp.sum(y, axis=0, keepdims=True)
        sum_o[...] = jnp.concatenate(sums + [jnp.zeros((5, width), F32)], axis=0)


def feed_back(place, gathered, gs, gsb, fs, gp, root, vec, part):
    share, width = gs.shape
    hidden = gp.shape[2]
    block = lambda: pl.BlockSpec((1, share, hidden), lambda i, s: (i, 0, 0))
    sd, far = jax.ShapeDtypeStruct, pltpu.HBM
    return pl.pallas_call(
        feed_back_kernel,
        grid_spec=pltpu.PrefetchScalarGridSpec(
            num_scalar_prefetch=1,
            grid=(4,),
            in_specs=feed_specs(place, gathered, hidden)
            + [whole_block(gs.shape), whole_block(gsb.shape), whole_block(fs.shape), block(), whole_block(root.shape), whole_block(vec.shape)],
            out_specs=[whole_block((share, width)), whole_block((width, share))]
            + [whole_block((share, part))] * 4
            + [block(), pl.BlockSpec((1, 8, hidden), lambda i, s: (i, 0, 0)), whole_block((8, width))],
            scratch_shapes=[
                pltpu.VMEM((4, width, gathered.shape[2] - 2 * hidden), BF),
                pltpu.VMEM((share, width), F32),
                pltpu.SemaphoreType.DMA((4,)),
            ],
        ),
        out_shape=[far((share, width), F32), far((width, share), BF)]
        + [sd((share, part), BF)] * 4
        + [far((4, share, hidden), BF), sd((4, 8, hidden), F32), sd((8, width), F32)],
        compiler_params=params(54),
        cost_estimate=COST,
        name="feed_back",
    )(place, gathered, gathered, gs, gsb, fs, gp, root, vec)


def split_rows(place, per, acc, source, near_o, far_o, lead, cols):
    if per == 1:
        near_o[(*lead, slice(None), cols)] = acc[:, source].astype(near_o.dtype)
        return
    rows = acc.shape[0] // per
    for n in range(per // 2):
        near, far = (pl.ds(pl.multiple_of(place[m], 16), rows) for m in (n, per // 2 + n))
        near_o[(*lead, n, slice(None), cols)] = acc[near, source].astype(near_o.dtype)
        far_o[(*lead, n, slice(None), cols)] = acc[far, source].astype(BF)


def weights_kernel(per, place, nbt, gst, gft, ctx, gh, act, *refs):
    hh = gh.shape[2] // 2
    if per > 1:
        near_o, far_o, out, acc = refs
    else:
        other, out = refs
    for n, (left, right) in enumerate(((nbt, gh), (gst, act))):
        made = nn(left[...], right[0])
        out[0, :, n * hh : (n + 1) * hh] = made[:, 0:hh].astype(BF)
        if per > 1:
            acc[...] = made[:, hh:]
            split_rows(place, per, acc, slice(None), near_o, far_o, (0,), slice(n * hh, (n + 1) * hh))
        else:
            other[0, :, n * hh : (n + 1) * hh] = made[:, hh:].astype(BF)
    out[0, :, 2 * hh :] = nn(gft[...], ctx[0]).astype(BF)


def weight_grads(place, per, nbt, gst, gft, contexts, gh, act):
    width, share = nbt.shape
    hidden, part = gh.shape[2], contexts.shape[2]
    last = place.shape[0] - 1
    block = lambda cols: pl.BlockSpec((1, share, cols), lambda i, s: (i, 0, 0))
    ordered = lambda cols: pl.BlockSpec((1, width, cols), lambda i, s: (i ^ s[last], 0, 0))
    if per > 1:
        shape = (4, per // 2, width // per, hidden)
        outs = [jax.ShapeDtypeStruct(shape, BF)] * 2
        specs = [pl.BlockSpec((1,) + shape[1:], lambda i, s: (i, 0, 0, 0))] * 2
        scratch = [pltpu.VMEM((width, hidden // 2), F32)]
    else:
        outs = [jax.ShapeDtypeStruct((4, width, hidden), BF)]
        specs = [ordered(hidden)]
        scratch = []
    return pl.pallas_call(
        partial(weights_kernel, per),
        grid_spec=pltpu.PrefetchScalarGridSpec(
            num_scalar_prefetch=1,
            grid=(4,),
            in_specs=[whole_block(x.shape) for x in (nbt, gst, gft)] + [block(part), block(hidden), block(hidden)],
            out_specs=specs + [ordered(hidden + part)],
            scratch_shapes=scratch,
        ),
        out_shape=outs + [jax.ShapeDtypeStruct((4, width, hidden + part), BF)],
        compiler_params=params(58),
        cost_estimate=COST,
        name="weight_grads",
    )(place, nbt, gst, gft, contexts, gh, act)


def qkv_weights_kernel(per, part, place, own, other, g, *refs):
    near_o, far_o = refs[:2] if per > 1 else (refs[0], None)
    acc = refs[-1]
    half_len = other.shape[0]
    core = place[per]
    rows = 512

    acc[...] = jnp.zeros(acc.shape, F32)

    def step(r, _):
        at = pl.ds(pl.multiple_of(r * rows, rows), rows)
        a = g[pl.ds(pl.multiple_of(core * half_len + r * rows, rows), rows), :]
        b = g[pl.ds(pl.multiple_of((1 - core) * half_len + r * rows, rows), rows), :]
        acc[...] += nn(own[0, at, :].T, a) + nn(other[at, :].T, b)
        return 0

    lax.fori_loop(0, half_len // rows, step, 0)
    for m in range(3):
        split_rows(place, per, acc, slice(m * WIDE, m * WIDE + part), near_o, far_o, (), slice(m * part, (m + 1) * part))


def qkv_weight_grads(place, per, tokens, other, g, part):
    half_len, width = other.shape
    if per > 1:
        shape = (per // 2, width // per, 3 * part)
        outs = [jax.ShapeDtypeStruct(shape, F32), jax.ShapeDtypeStruct(shape, BF)]
    else:
        outs = [jax.ShapeDtypeStruct((width, 3 * part), F32)]
    return pl.pallas_call(
        partial(qkv_weights_kernel, per, part),
        grid_spec=pltpu.PrefetchScalarGridSpec(
            num_scalar_prefetch=1,
            grid=(1,),
            in_specs=[pl.BlockSpec((1, half_len, width), lambda i, s: (s[per], 0, 0)), whole_block(other.shape), whole_block(g.shape)],
            out_specs=[whole_block(o.shape) for o in outs],
            scratch_shapes=[pltpu.VMEM((width, 3 * WIDE), F32)],
        ),
        out_shape=outs,
        compiler_params=params(32),
        cost_estimate=COST,
        name="qkv_weight_grads",
    )(place, tokens, other, g)


def branch_kernel(place, *refs):
    count = (len(refs) - 1) // 2
    w = refs[count]
    for g, o in zip(refs[:count], refs[count + 1 :]):
        rows = 256
        for r in range(g.shape[0] // rows):
            sl = slice(r * rows, (r + 1) * rows)
            o[sl, :] = nt(g[sl, :], w[...]).astype(o.dtype)


def branch(place, blocks, kinds, g, w):
    share, last = g.shape[0] // 4, place.shape[0] - 1
    return pl.pallas_call(
        branch_kernel,
        grid_spec=pltpu.PrefetchScalarGridSpec(
            num_scalar_prefetch=1,
            grid=(1,),
            in_specs=[pl.BlockSpec((share, g.shape[1]), lambda i, s, k=k: (s[last] ^ k, 0)) for k in blocks] + [whole_block(w.shape)],
            out_specs=[whole_block((share, w.shape[0]))] * len(blocks),
        ),
        out_shape=[jax.ShapeDtypeStruct((share, w.shape[0]), kind) for kind in kinds],
        compiler_params=params(24),
        cost_estimate=COST,
        name="branch",
    )(place, *[g] * len(blocks), w)


def pick_kernel(place, near, *refs):
    far, (keep, send) = refs[:-2], refs[-2:]
    last = place.shape[0] - 1
    mine = place[last] // 2 == place[last - 1]

    def put(out, parts):
        rows = out.shape[0] // len(parts)
        for n, x in enumerate(parts):
            out[n * rows : (n + 1) * rows, :] = x[...]

    @pl.when(mine)
    def _():
        put(keep, [near])
        put(send, far)

    @pl.when(jnp.logical_not(mine))
    def _():
        put(keep, far)
        put(send, [near])


def pick(place, near, *far):
    return pl.pallas_call(
        pick_kernel,
        grid_spec=pltpu.PrefetchScalarGridSpec(
            num_scalar_prefetch=1,
            grid=(1,),
            in_specs=[whole_block(x.shape) for x in (near, *far)],
            out_specs=[whole_block(near.shape)] * 2,
        ),
        out_shape=[jax.ShapeDtypeStruct(near.shape, near.dtype)] * 2,
        compiler_params=params(8),
        cost_estimate=COST,
        name="pick",
    )(place, near, *far)


def join_kernel(place, keep_a, keep_b, other_a, other_b, out):
    last = place.shape[0] - 1
    mine = pl.program_id(0) == place[last - 1]
    same = pl.program_id(1) == place[last] % 2
    for x, own, even in ((keep_a, True, True), (keep_b, True, False), (other_a, False, True), (other_b, False, False)):

        @pl.when(jnp.logical_and(mine == own, same == even))
        def _(x=x):
            out[0] = x[...]


def join(place, keeps, others):
    share, width = keeps[0].shape
    return pl.pallas_call(
        join_kernel,
        grid_spec=pltpu.PrefetchScalarGridSpec(
            num_scalar_prefetch=1,
            grid=(2, 2),
            in_specs=[whole_block((share, width))] * 4,
            out_specs=pl.BlockSpec((1, share, width), lambda i, j, s: (i, j, 0)),
        ),
        out_shape=jax.ShapeDtypeStruct((2, 2 * share, width), keeps[0].dtype),
        compiler_params=pltpu.CompilerParams(dimension_semantics=("arbitrary", "arbitrary"), vmem_limit_bytes=12 * 1024 * 1024),
        cost_estimate=COST,
        name="join",
    )(place, *keeps, *others)


def relay_kernel(one, two, low, high, one_o, two_o):
    half = low.shape[0]
    one_o[0:half, :] = (one[0:half, :] + low[...].astype(F32)).astype(BF)
    one_o[half:, :] = one[half:, :].astype(BF)
    two_o[0:half, :] = two[0:half, :].astype(BF)
    two_o[half:, :] = (two[half:, :] + high[...].astype(F32)).astype(BF)


def relay(one, two, low, high):
    return pl.pallas_call(
        relay_kernel,
        in_specs=[pl.BlockSpec(memory_space=pltpu.VMEM)] * 4,
        out_specs=[pl.BlockSpec(memory_space=pltpu.VMEM)] * 2,
        out_shape=[jax.ShapeDtypeStruct(one.shape, BF)] * 2,
        compiler_params=pltpu.CompilerParams(vmem_limit_bytes=16 * 1024 * 1024),
        cost_estimate=COST,
        name="relay",
    )(one, two, low, high)


def collect_kernel(place, hidden_sums, one, two, bias, out):
    here = place[place.shape[0] - 1]
    out[...] = jnp.zeros(out.shape, F32)
    for k in range(4):
        out[pl.ds(here ^ k, 1), :] = hidden_sums[k, 0:1, :]
    for n, (x, row) in enumerate(((one, 0), (two, 0), (one, 1), (two, 1), (one, 2), (two, 2))):
        out[4 + n : 5 + n, :] = x[row : row + 1, :]
    out[pl.ds(10 + here, 1), :] = bias[0:1, :]


def collect(place, hidden_sums, one, two, bias):
    return pl.pallas_call(
        collect_kernel,
        grid_spec=pltpu.PrefetchScalarGridSpec(
            num_scalar_prefetch=1,
            grid=(1,),
            in_specs=[whole_block(x.shape) for x in (hidden_sums, one, two, bias)],
            out_specs=whole_block((16, one.shape[1])),
        ),
        out_shape=jax.ShapeDtypeStruct((16, one.shape[1]), F32),
        compiler_params=params(8),
        cost_estimate=COST,
        name="collect",
    )(place, hidden_sums, one, two, bias)


def settle_kernel(count, *refs):
    ins, outs = refs[:count], refs[count:]
    for j, out in enumerate(outs):
        total = ins[0][j].astype(F32)
        for x in ins[1:]:
            total = total + x[j].astype(F32)
        out[...] = total.astype(out.dtype)


def settle(*stacks):
    shape = stacks[0].shape
    vmem = pl.BlockSpec(memory_space=pltpu.VMEM)
    return pl.pallas_call(
        partial(settle_kernel, len(stacks)),
        in_specs=[vmem] * len(stacks),
        out_specs=[vmem] * shape[0],
        out_shape=[jax.ShapeDtypeStruct(shape[1:], F32 if j == 0 else BF) for j in range(shape[0])],
        compiler_params=pltpu.CompilerParams(vmem_limit_bytes=16 * 1024 * 1024),
        cost_estimate=COST,
        name="settle",
    )(*stacks)


def finish_kernel(parts, *refs):
    out = refs[-1]
    total = refs[0][...]
    for x in refs[1:-1]:
        total = total + x[...].astype(F32)
    if parts == 1:
        out[...] = total
    else:
        cols = total.shape[1] // parts
        for m in range(parts):
            out[:, m, :] = total[:, m * cols : (m + 1) * cols]


def finish(parts, *pieces):
    vmem = pl.BlockSpec(memory_space=pltpu.VMEM)
    rows, cols = pieces[0].shape
    return pl.pallas_call(
        partial(finish_kernel, parts),
        in_specs=[vmem] * len(pieces),
        out_specs=vmem,
        out_shape=jax.ShapeDtypeStruct((rows, cols) if parts == 1 else (rows, parts, cols // parts), F32),
        compiler_params=pltpu.CompilerParams(vmem_limit_bytes=8 * 1024 * 1024),
        cost_estimate=COST,
        name="finish",
    )(*pieces)


def place_kernel(whole, rest, feed_o, out_o):
    hh = rest.shape[1] // 2
    for m in range(2):
        feed_o[:, m, 0:hh] = whole[:, m * hh : (m + 1) * hh].astype(F32)
        feed_o[:, m, hh:] = rest[:, m * hh : (m + 1) * hh]
    out_o[...] = whole[:, 2 * hh :].astype(F32)


def place_feed(whole, rest):
    vmem = pl.BlockSpec(memory_space=pltpu.VMEM)
    rows, cols = rest.shape
    return pl.pallas_call(
        place_kernel,
        in_specs=[vmem] * 2,
        out_specs=[vmem] * 2,
        out_shape=[jax.ShapeDtypeStruct((rows, 2, cols), F32), jax.ShapeDtypeStruct((rows, whole.shape[1] - cols), F32)],
        compiler_params=pltpu.CompilerParams(vmem_limit_bytes=8 * 1024 * 1024),
        cost_estimate=COST,
        name="place_feed",
    )(whole, rest)


def block_kernel(own, first, one, two, out):
    out[...] = (own[...] + first[...] + one[...].astype(F32) + two[...].astype(F32)).astype(BF)


def add_block(own, first, one, two):
    vmem = pl.BlockSpec(memory_space=pltpu.VMEM)
    return pl.pallas_call(
        block_kernel,
        in_specs=[vmem] * 4,
        out_specs=vmem,
        out_shape=jax.ShapeDtypeStruct(own.shape, BF),
        compiler_params=pltpu.CompilerParams(vmem_limit_bytes=12 * 1024 * 1024),
        cost_estimate=COST,
        name="add_block",
    )(own, first, one, two)


def relay_kernel(one, two, low, high, one_o, two_o):
    half = low.shape[0]
    one_o[0:half, :] = (one[0:half, :] + low[...].astype(F32)).astype(BF)
    one_o[half:, :] = one[half:, :].astype(BF)
    two_o[0:half, :] = two[0:half, :].astype(BF)
    two_o[half:, :] = (two[half:, :] + high[...].astype(F32)).astype(BF)


def relay(one, two, low, high):
    return pl.pallas_call(
        relay_kernel,
        in_specs=[pl.BlockSpec(memory_space=pltpu.VMEM)] * 4,
        out_specs=[pl.BlockSpec(memory_space=pltpu.VMEM)] * 2,
        out_shape=[jax.ShapeDtypeStruct(one.shape, BF)] * 2,
        compiler_params=pltpu.CompilerParams(vmem_limit_bytes=16 * 1024 * 1024),
        cost_estimate=COST,
        name="relay",
    )(one, two, low, high)


def rotation_tables(offsets):
    lane = np.arange(128)
    frequency = (10000.0 ** (-2.0 * (lane % HEAD // 2) / HEAD)).astype(np.float32)
    angles = offsets.astype(F32)[:, None] * frequency[None, :]
    sign = np.where(lane % 2 == 0, -1.0, 1.0).astype(np.float32)
    return jnp.cos(angles), jnp.sin(angles) * sign


def key_bounds(segment):
    length = segment.shape[0]
    first, last = segment[::BLOCK], segment[BLOCK - 1 :: BLOCK]
    low = jnp.sum(segment[None, :] < first[:, None], axis=1)
    high = jnp.sum(segment[None, :] <= last[:, None], axis=1)
    low = low // 128 * 128
    count = (high - low + CHUNK - 1) // CHUNK
    return jnp.stack([jnp.minimum(low, length - CHUNK * count), count], axis=1).reshape(-1).astype(jnp.int32)


def swap_ctx(x):
    return lax.ppermute(x, "ctx", [(0, 1), (1, 0)])


def swap_tp(x, k):
    return lax.ppermute(x, "tp", [(i, i ^ k) for i in range(4)])


def swap_shard(x, k):
    return lax.ppermute(x, "shard", [(i, i ^ k) for i in range(4)])


def order_four(parts, index):
    a, b, c, d = parts
    odd, high = index % 2 == 1, index // 2 == 1
    a, b = jnp.where(odd, b, a), jnp.where(odd, a, b)
    c, d = jnp.where(odd, d, c), jnp.where(odd, c, d)
    return jnp.stack([jnp.where(high, c, a), jnp.where(high, d, b), jnp.where(high, a, c), jnp.where(high, b, d)])


def after(x, *others):
    return lax.optimization_barrier((x, others))[0]


def gather_tp(x, half):
    one, two = swap_tp(x, 1), swap_tp(x, 2)
    three = jnp.concatenate([swap_tp(one[:half], 2), swap_tp(two[half:], 1)])
    return [x, one, two, three]


def scatter_tp(parts):
    own, one, two, three = parts
    half = own.shape[0] // 2
    low, high = three[:half].astype(BF), three[half:].astype(BF)
    low, high = swap_tp(low, 2), swap_tp(high, 1)
    one = jnp.concatenate([one[:half] + low.astype(F32), one[half:]]).astype(BF)
    two = jnp.concatenate([two[:half], two[half:] + high.astype(F32)]).astype(BF)
    return own + swap_tp(one, 1).astype(F32) + swap_tp(two, 2).astype(F32)


def three_rows(x):
    high = lax.reduce_precision(x, 8, 7)
    middle = lax.reduce_precision(x - high, 8, 7)
    return jnp.stack([high, middle, x - high - middle]).astype(BF)


def contract_last(left, right):
    return lax.dot_general(left, right, (((1,), (1,)), ((), ())), preferred_element_type=F32)


def body(tokens, segment_ids, offsets, qkv_weight, out_weight, ffn_weight, qkv_bias, ffn_bias, norm_gain, shift_params, out_grad):
    t, c, z = lax.axis_index("tp"), lax.axis_index("ctx"), lax.axis_index("shard")
    shards = lax.axis_size("shard")
    half_len, width = tokens.shape[1:]
    rows, _, part = qkv_weight.shape
    hidden = ffn_weight.shape[2]
    heads = part // HEAD
    length = 2 * half_len
    share = length // 4
    first_core = c == 0
    direct = shards == 4

    def take(x, index):
        return lax.dynamic_index_in_dim(x, index, 0, keepdims=False)

    def by_core(own, other):
        return jnp.where(first_core, jnp.stack([own, other]), jnp.stack([other, own]))

    hh = hidden // 2
    gathered = jnp.concatenate([ffn_weight.reshape(rows, 2 * hidden), out_weight], axis=1)
    gathered = lax.all_gather(gathered, ("tp", "shard", "ctx"), axis=0, tiled=True).reshape(4, width, 2 * hidden + part)
    bias_all = ffn_bias.reshape(1, hidden)
    bias_all = jnp.concatenate([bias_all] + [swap_tp(bias_all, k) for k in (1, 2, 3)])
    qkv_rows = qkv_weight.reshape(rows, 3 * part)
    other_tokens = swap_ctx(take(tokens, 1 - c))
    if direct:
        places = [((z ^ j) * 2 + (c ^ f)) * rows for f in (0, 1) for j in range(4)]
        near = [qkv_rows] + [swap_shard(qkv_rows, j) for j in (1, 2, 3)]
        qkv_pieces = [*near, swap_ctx(jnp.stack(near))]
    else:
        places = [jnp.zeros_like(c)]
        qkv_pieces = [lax.all_gather(qkv_rows, ("shard", "ctx"), axis=0, tiled=True)]
    per = len(places)
    place = jnp.stack(places + [c, t]).astype(jnp.int32)
    bias_pad = jnp.pad(qkv_bias, ((0, 0), (0, WIDE - part)))
    vec = jnp.concatenate([norm_gain, shift_params, jnp.zeros((2, width), F32)])

    marks = jnp.stack([segment_ids, offsets])
    marks = by_core(take(marks.swapaxes(0, 1), c), swap_ctx(take(marks.swapaxes(0, 1), 1 - c)))
    segment, places = marks[:, 0].reshape(length), marks[:, 1].reshape(length)
    halves = lambda x: x.reshape(2, 2, share, width)
    here = t // 2 == c
    tok_block = jnp.where(here, take(take(halves(tokens), c), t % 2), take(other_tokens.reshape(2, share, width), t % 2))
    grad_block = halves(out_grad)
    grad_far = swap_ctx(take(take(grad_block, 1 - c), t % 2))
    grad_top = jnp.where(here, take(take(grad_block, c), t % 2), grad_far)

    cosine, sine = rotation_tables(places)
    bounds = key_bounds(segment)
    seg_column = segment[:, None]
    seg_row = jnp.broadcast_to(segment[None, :], (8, length))
    q, k_rows, v_rows, k_turned, q_turned, qkv_wide = project_qkv(place, qkv_pieces, per, bias_pad, tokens, other_tokens, cosine, sine, part)

    contexts, log_totals, fulls = [None] * 4, [None] * 4, [None] * 4

    def forward(j, q):
        spot = jnp.concatenate([((t ^ j) * (share // BLOCK))[None].astype(jnp.int32), bounds])
        context, log_totals[j], fulls[j] = attention_forward(spot, q, k_rows, v_rows, seg_column, seg_row, heads, share)
        contexts[j] = swap_tp(context, j) if j else context

    forward(3, q)
    q_next, log_totals[3] = lax.optimization_barrier((q, log_totals[3]))
    forward(1, q_next)
    q_next, log_totals[1], contexts[3] = lax.optimization_barrier((q, log_totals[1], contexts[3]))
    forward(2, q_next)
    q_next, log_totals[2], contexts[1] = lax.optimization_barrier((q, log_totals[2], contexts[1]))
    forward(0, q_next)
    stacked = jnp.stack(contexts)
    tok_block, log_total, full, stacked = lax.optimization_barrier(
        (tok_block, jnp.concatenate(log_totals, axis=1), jnp.concatenate(fulls), stacked)
    )

    layer_out, grad_second, grad_second_b, first_scaled, normed_t, second_t, activated, slope, root, sums_two = feed_forward(
        place, gathered, contexts, tok_block, grad_top, vec, bias_all
    )

    barrier = lax.optimization_barrier
    out_blocks = [layer_out, swap_tp(layer_out, 1), swap_tp(layer_out, 2)]

    grad_first, first_t, g0, g1, g2, g3, grad_hidden, hidden_sums, sums_one = feed_back(
        place, gathered, grad_second, grad_second_b, first_scaled, slope, root, vec, part
    )
    heads_grads = [g0, swap_tp(g1, 1), swap_tp(g2, 2), swap_tp(g3, 3)]

    *made, whole = weight_grads(place, per, normed_t, second_t, first_t, stacked, grad_hidden, activated)
    made, whole, heads_grads, out_blocks = barrier((made, whole, heads_grads, out_blocks))
    whole = lax.psum_scatter(whole.reshape(-1, 2 * hh + part), ("tp", "shard", "ctx"), scatter_dimension=0, tiled=True)
    grad_heads = heads_grads
    corner = [out_blocks[1][: share // 2], out_blocks[2][share // 2 :]]
    if direct:
        got = swap_ctx(made[1])
        grad_heads, got, corner = barrier((grad_heads, got, corner))
        packs = [made[0][k].astype(F32) + got[k].astype(F32) for k in range(4)]
        sent = [packs[k].astype(BF) for k in (1, 2, 3)]
        grad_heads, sent = barrier((grad_heads, sent))
        sent = [swap_tp(sent[k - 1], k) for k in (1, 2, 3)]
    corner = [swap_tp(corner[0], 2), swap_tp(corner[1], 1)]

    spot = jnp.concatenate([(t * (share // BLOCK))[None].astype(jnp.int32), bounds])
    grad_proj, bias_sums = attention_backward(
        spot, q, q_turned, k_rows, k_turned, v_rows, grad_heads, full, log_total, seg_column, seg_row, cosine, sine, heads
    )
    grad_proj, bias_sums, corner, hidden_sums, sums_one, sums_two, out_blocks = barrier(
        (grad_proj, bias_sums, corner, hidden_sums, sums_one, sums_two, out_blocks)
    )
    if direct:
        grad_proj, sent, packs[0] = barrier((grad_proj, sent, packs[0]))

    three = branch(place, (3,), (BF,), grad_proj, qkv_wide)[0]
    three, grad_proj, corner, bias_sums, out_blocks = barrier((three, grad_proj, corner, bias_sums, out_blocks))
    low, high = swap_tp(three[: share // 2], 2), swap_tp(three[share // 2 :], 1)
    one, two, own = branch(place, (1, 2, 0), (F32, F32, F32), grad_proj, qkv_wide)
    grads = qkv_weight_grads(place, per, tokens, other_tokens, grad_proj, part)
    keep_a, send_a = pick(place, out_blocks[0], out_blocks[2])
    keep_b, send_b = pick(place, out_blocks[1], *corner)
    small = collect(place, hidden_sums, sums_one, sums_two, bias_sums)
    outs = [keep_a, keep_b, swap_ctx(send_a), swap_ctx(send_b)]
    if direct:
        qkv_sum, *qkv_pieces = settle(grads[0], swap_ctx(grads[1]))
        qkv_sum, qkv_pieces, low = barrier((qkv_sum, qkv_pieces, low))
    low, high, one, two, own, outs, small = barrier((low, high, one, two, own, outs, small))

    def send_shards(pieces, small, k):
        moved = [swap_shard(pieces[j - 1], j) for j in (1, 2, 3)]
        moved[0], small = barrier((moved[0], small))
        return moved, small + swap_tp(small, k)

    one, two = relay(one, two, low, high)
    one, two, outs, small = barrier((one, two, outs, small))
    one, two = swap_tp(one, 1), swap_tp(two, 2)
    outputs = join(place, outs[:2], outs[2:])
    if direct:
        moved, small = send_shards(qkv_pieces, small, 1)
        qkv_total = finish(3, qkv_sum, *moved)
        summed, *pieces = settle(packs[0], *sent)
        one, two, own, small, outputs, summed, pieces, qkv_total = barrier((one, two, own, small, outputs, summed, pieces, qkv_total))
    else:
        one, two, own, small, outputs = barrier((one, two, own, small, outputs))

    block = add_block(own, grad_first, one, two)
    ready = [block, swap_tp(block, 1), swap_tp(block, 2)]
    if direct:
        moved, small = send_shards(pieces, small, 2)
        total = finish(1, summed, *moved)
        ready, total, small = barrier((ready, total, small))
    else:
        qkv_total = lax.psum_scatter(grads[0], ("shard", "ctx"), scatter_dimension=0, tiled=True).reshape(rows, 3, part)
        total = lax.psum_scatter(made[0].reshape(-1, 2 * hh), ("tp", "shard", "ctx"), scatter_dimension=0, tiled=True).astype(F32)
    corner = [swap_tp(ready[1][: share // 2], 2), swap_tp(ready[2][share // 2 :], 1)]
    keep_a, send_a = pick(place, ready[0], ready[2])
    other_a = swap_ctx(send_a)
    grad_ffn_weight, grad_out_weight = place_feed(whole, total)
    if direct:
        small = small + swap_shard(small, 1)
        small = small + swap_shard(small, 2)
        small = small + swap_ctx(small)
    else:
        small = lax.psum(small, ("shard", "ctx", "tp"))
    corner, grad_ffn_weight, grad_out_weight, small, keep_a, other_a, qkv_total = barrier(
        (corner, grad_ffn_weight, grad_out_weight, small, keep_a, other_a, qkv_total)
    )
    keep_b, send_b = pick(place, ready[1], *corner)
    grad_tokens = join(place, [keep_a, keep_b], [other_a, swap_ctx(send_b)])

    grad_qkv_weight = qkv_total
    grad_ffn_bias = take(small, t)
    vectors = small[4:10]
    grad_qkv_bias = take(small[10:14], t).reshape(3, WIDE)[:, :part]
    return (
        outputs,
        grad_tokens,
        grad_qkv_weight,
        grad_out_weight,
        grad_ffn_weight,
        grad_qkv_bias,
        grad_ffn_bias,
        vectors[:2],
        vectors[2:],
    )


def solution(mesh):
    return jax.shard_map(
        body,
        mesh=mesh,
        in_specs=(
            P("shard", "ctx", None),
            P("shard", "ctx"),
            P("shard", "ctx"),
            P(("shard", "ctx"), None, "tp"),
            P(("shard", "ctx"), "tp"),
            P(("shard", "ctx"), None, "tp"),
            P(None, "tp"),
            P("tp"),
            P(),
            P(),
            P("shard", "ctx", None),
        ),
        out_specs=(
            P("shard", "ctx", None),
            P("shard", "ctx", None),
            P(("shard", "ctx"), None, "tp"),
            P(("shard", "ctx"), "tp"),
            P(("shard", "ctx"), None, "tp"),
            P(None, "tp"),
            P("tp"),
            P(),
            P(),
        ),
        check_vma=False,
    )
```

```python
from functools import partial

import jax
import jax.numpy as jnp
import numpy as np
from jax import lax
from jax.experimental import pallas as pl
from jax.experimental.pallas import tpu as pltpu
from jax.sharding import PartitionSpec as P

HEAD = 64
WIDE = 256
BLOCK = 256
CHUNK = 256
EPSILON = 1e-12
F32 = jnp.float32
BF = jnp.bfloat16
NEG = -1e30
COST = pl.CostEstimate(flops=0, bytes_accessed=0, transcendentals=0)


def swap_pairs(x):
    lane = lax.broadcasted_iota(jnp.int32, x.shape, 1)
    n = x.shape[1]
    return jnp.where(lane % 2 == 0, pltpu.roll(x, n - 1, 1), pltpu.roll(x, 1, 1))


def nt(a, b):
    return lax.dot_general(a, b, (((1,), (1,)), ((), ())), preferred_element_type=F32)


def nn(a, b):
    return lax.dot_general(a, b, (((1,), (0,)), ((), ())), preferred_element_type=F32)


def twice(x):
    return jnp.concatenate([x, x], axis=1)


def lanes_of_heads(x, heads):
    lane = lax.broadcasted_iota(jnp.int32, x.shape, 1) // HEAD
    return [jnp.where(lane == h, x, jnp.zeros_like(x)) for h in range(heads)]


def whole_block(shape, buffers=1):
    return pl.BlockSpec(shape, lambda *_: (0,) * len(shape), pipeline_mode=pl.Buffered(buffers))


def smem():
    return pl.BlockSpec(memory_space=pltpu.SMEM)


def params(mib):
    return pltpu.CompilerParams(dimension_semantics=("arbitrary",), vmem_limit_bytes=mib * 1024 * 1024)


def qkv_kernel(count, per, part, place, *refs):
    pieces = []
    for x in refs[:count]:
        pieces += [x] if len(x.shape) == 2 else [x.at[n] for n in range(x.shape[0])]
    bias, own, other, cos, sin, q_o, k_o, v_o, kt_o, qt_o, w_o = refs[count:]
    piece_rows = pieces[0].shape[0]
    pad = jnp.zeros((piece_rows, WIDE - part), BF)
    for n in range(per):
        sl = pl.ds(pl.multiple_of(place[n], 16), piece_rows)
        for m in range(3):
            w_o[sl, m * WIDE : (m + 1) * WIDE] = jnp.concatenate([pieces[n][:, m * part : (m + 1) * part], pad], axis=1)
    half_len = other.shape[0]

    def run(x, sl):
        c, s = twice(cos[sl, :]), twice(sin[sl, :])
        p = nn(x, w_o[:, 0:WIDE]) + bias[0:1, :]
        q = ((p * c + swap_pairs(p) * s).astype(BF).astype(F32) * (HEAD**-0.5)).astype(BF)
        q_o[sl, :] = q
        qt_o[:, sl] = q.T
        p = nn(x, w_o[:, WIDE : 2 * WIDE]) + bias[1:2, :]
        k = (p * c + swap_pairs(p) * s).astype(BF)
        k_o[sl, :] = k
        kt_o[:, sl] = k.T
        v_o[sl, :] = (nn(x, w_o[:, 2 * WIDE : 3 * WIDE]) + bias[2:3, :]).astype(BF)

    def step(r, _):
        rows = pl.ds(pl.multiple_of(r * BLOCK, BLOCK), BLOCK)
        core = place[per]
        run(own[0, rows, :], pl.ds(pl.multiple_of(core * half_len + r * BLOCK, BLOCK), BLOCK))
        run(other[rows, :], pl.ds(pl.multiple_of((1 - core) * half_len + r * BLOCK, BLOCK), BLOCK))
        return 0

    lax.fori_loop(0, half_len // BLOCK, step, 0)


def project_qkv(place, pieces, per, bias, tokens, other, cos, sin, part):
    half_len, width = other.shape
    length, count = 2 * half_len, len(pieces)
    return pl.pallas_call(
        partial(qkv_kernel, count, per, part),
        grid_spec=pltpu.PrefetchScalarGridSpec(
            num_scalar_prefetch=1,
            grid=(1,),
            in_specs=[whole_block(p.shape) for p in pieces]
            + [whole_block(bias.shape), pl.BlockSpec((1, half_len, width), lambda i, s: (s[per], 0, 0))]
            + [whole_block(x.shape) for x in (other, cos, sin)],
            out_specs=[whole_block((length, WIDE))] * 3 + [whole_block((WIDE, length))] * 2 + [whole_block((width, 3 * WIDE))],
        ),
        out_shape=[jax.ShapeDtypeStruct((length, WIDE), BF)] * 3
        + [jax.ShapeDtypeStruct((WIDE, length), BF)] * 2
        + [jax.ShapeDtypeStruct((width, 3 * WIDE), BF)],
        compiler_params=params(32),
        cost_estimate=COST,
        name="project_qkv",
    )(place, *pieces, bias, tokens, other, cos, sin)


def forward_kernel(heads, place, q, k, v, segc, segr, ctx_o, lse_o, full_o, acc, s_sc, m_sc, l_sc, qc_sc):
    i = place[0] + pl.program_id(0)
    start, count = place[1 + 2 * i], place[2 + 2 * i]
    qc_sc[...] = jnp.concatenate(lanes_of_heads(q[...], heads), axis=0)
    seg_q = segc[...]
    m_sc[...] = jnp.full(m_sc.shape, NEG, F32)
    l_sc[...] = jnp.zeros(l_sc.shape, F32)

    def at(j):
        return pl.ds(pl.multiple_of(start + j * CHUNK, 128), CHUNK)

    def of(h):
        return slice(h * BLOCK, (h + 1) * BLOCK)

    def pass1(j, _):
        s = nt(qc_sc[...], k[at(j), :])
        keep = seg_q == segr[0:1, at(j)]
        for h in range(heads):
            sh = jnp.where(keep, s[of(h), :], NEG)
            s_sc[j, of(h), :] = sh
            m_sc[of(h), :] = jnp.maximum(m_sc[of(h), :], jnp.maximum(sh[:, :128], sh[:, 128:]))
        return 0

    lax.fori_loop(0, count, pass1, 0)
    m_sc[...] = jnp.broadcast_to(jnp.max(m_sc[...], axis=1, keepdims=True), m_sc.shape)

    def pass2(j, _):
        for h in range(heads):
            e = jnp.exp(s_sc[j, of(h), :] - twice(m_sc[of(h), :]))
            s_sc[j, of(h), :] = e
            l_sc[of(h), :] += e[:, :128] + e[:, 128:]
        return 0

    lax.fori_loop(0, count, pass2, 0)
    total = jnp.sum(l_sc[...], axis=1, keepdims=True)
    lse = m_sc[:, 0:1] + jnp.log(total)
    l_sc[...] = jnp.broadcast_to(1.0 / total, l_sc.shape)
    lane = lax.broadcasted_iota(jnp.int32, (BLOCK, 128), 1)
    tile = jnp.zeros((BLOCK, 128), F32)
    for h in range(heads):
        tile = jnp.where(lane == h, lse[of(h), :], tile)
    lse_o[...] = tile.T[0:8, :]
    acc[...] = jnp.zeros(acc.shape, F32)
    full_o[...] = jnp.zeros(full_o.shape, F32)

    def pass3(j, _):
        ps, less = [], []
        for h in range(heads):
            p = s_sc[j, of(h), :] * twice(l_sc[of(h), :])
            b = p.astype(BF)
            ps.append(b)
            less.append((p - b.astype(F32)).astype(BF))
        vs = jnp.concatenate(lanes_of_heads(v[at(j), :], heads), axis=0)
        acc[...] += nn(jnp.concatenate(ps, axis=1), vs)
        full_o[...] += nn(jnp.concatenate(less, axis=1), vs)
        return 0

    lax.fori_loop(0, count, pass3, 0)
    ctx_o[...] = acc[:, : heads * HEAD].astype(BF)
    full_o[...] += acc[...]


def attention_forward(place, q, k, v, segc, segr, heads, share):
    length = q.shape[0]
    grid = share // BLOCK
    rows = lambda i, s: (s[0] + i, 0)
    return pl.pallas_call(
        partial(forward_kernel, heads),
        grid_spec=pltpu.PrefetchScalarGridSpec(
            num_scalar_prefetch=1,
            grid=(grid,),
            in_specs=[
                pl.BlockSpec((BLOCK, WIDE), rows),
                whole_block(k.shape),
                whole_block(v.shape),
                pl.BlockSpec((BLOCK, 1), rows),
                whole_block(segr.shape),
            ],
            out_specs=[
                pl.BlockSpec((BLOCK, heads * HEAD), lambda i, s: (i, 0)),
                pl.BlockSpec((8, BLOCK), lambda i, s: (0, i)),
                pl.BlockSpec((BLOCK, WIDE), lambda i, s: (i, 0)),
            ],
            scratch_shapes=[
                pltpu.VMEM((BLOCK, WIDE), F32),
                pltpu.VMEM((length // CHUNK, heads * BLOCK, CHUNK), F32),
                pltpu.VMEM((heads * BLOCK, 128), F32),
                pltpu.VMEM((heads * BLOCK, 128), F32),
                pltpu.VMEM((heads * BLOCK, WIDE), BF),
            ],
        ),
        out_shape=[
            jax.ShapeDtypeStruct((share, heads * HEAD), BF),
            jax.ShapeDtypeStruct((8, share), F32),
            jax.ShapeDtypeStruct((share, WIDE), F32),
        ],
        compiler_params=params(16),
        cost_estimate=COST,
        name="attention_forward",
    )(place, q, k, v, segc, segr)


def backward_kernel(heads, place, q, qt, k, kt, v, d0, d1, d2, d3, full, lse, segc, segr, cos, sin, g_o, gb_o, dk_sc, dv_sc, qc_sc, dc_sc, dq_sc, d_sc, dt_sc, qs_sc):
    step_at = pl.program_id(0)
    blocks = k.shape[0] // BLOCK

    @pl.when(step_at < blocks)
    def _():
        backward_rows(heads, place, q, qt, k, kt, v, (d0, d1, d2, d3), full, lse, segc, segr, dk_sc, dv_sc, qc_sc, dc_sc, dq_sc, d_sc, dt_sc, qs_sc)

    @pl.when(step_at == 0)
    def _():
        gb_o[...] = jnp.zeros(gb_o.shape, F32)

    @pl.when(step_at >= blocks)
    def _():
        at = pl.ds(pl.multiple_of((step_at - blocks) * BLOCK, BLOCK), BLOCK)

        def turn(x):
            return (x * twice(cos[...]) - swap_pairs(x) * twice(sin[...])).astype(BF)

        def put(x, m):
            g_o[:, m * WIDE : (m + 1) * WIDE] = x
            gb_o[0:1, m * WIDE : (m + 1) * WIDE] += jnp.sum(x.astype(F32), axis=0, keepdims=True)

        put(turn(qs_sc[:, at].T * (HEAD**-0.5)), 0)
        put(turn(dk_sc[:, at].T), 1)
        put(dv_sc[:, at].astype(BF).T, 2)


def backward_rows(heads, place, q, qt, k, kt, v, do, full, lse, segc, segr, dk_sc, dv_sc, qc_sc, dc_sc, dq_sc, d_sc, dt_sc, qs_sc):
    step_at = pl.program_id(0)
    i = step_at ^ place[0]
    part = do[0].shape[1]
    per = do[0].shape[0] // BLOCK

    @pl.when(step_at == 0)
    def _():
        dk_sc[...] = jnp.zeros(dk_sc.shape, F32)
        dv_sc[...] = jnp.zeros(dv_sc.shape, F32)
        d_sc[...] = jnp.zeros(d_sc.shape, BF)

    for n, d in enumerate(do):

        @pl.when(step_at // per == n)
        def _(d=d):
            d_sc[:, 0:part] = d[pl.ds(pl.multiple_of(step_at % per * BLOCK, BLOCK), BLOCK), :]

    start, count = place[1 + 2 * i], place[2 + 2 * i]
    qc_sc[...] = jnp.concatenate(lanes_of_heads(q[...], heads), axis=0)
    dz = d_sc[...]
    dc_sc[...] = jnp.concatenate(lanes_of_heads(dz, heads), axis=0)
    dt_sc[...] = dz.T
    dq_sc[...] = jnp.zeros(dq_sc.shape, F32)
    own = pl.ds(pl.multiple_of(i * BLOCK, BLOCK), BLOCK)
    seg_q = segr[0:1, own]
    row = lax.broadcasted_iota(jnp.int32, (8, WIDE), 0)
    lane = lax.broadcasted_iota(jnp.int32, (8, WIDE), 1) // HEAD
    pick = jnp.where(row == lane, 1.0, 0.0).astype(F32)
    delta = lax.dot_general(
        pick, dz.astype(F32) * full[...], (((1,), (1,)), ((), ())), preferred_element_type=F32, precision=lax.Precision.HIGHEST
    )

    def of(h):
        return slice(h * BLOCK, (h + 1) * BLOCK)

    def step(j, _):
        at = pl.ds(pl.multiple_of(start + j * CHUNK, 128), CHUNK)
        s = nt(k[at, :], qc_sc[...])
        dp = nt(v[at, :], dc_sc[...])
        keep = segc[at, :] == seg_q
        for h in range(heads):
            mine = slice(h * HEAD, (h + 1) * HEAD)
            p = jnp.exp(jnp.where(keep, s[:, of(h)], NEG) - lse[h : h + 1, :])
            ds = (p * (dp[:, of(h)] - delta[h : h + 1, :])).astype(BF)
            dq_sc[mine, :] += nn(kt[mine, at], ds)
            dv_sc[mine, at] += nt(dt_sc[mine, :], p.astype(BF))
            dk_sc[mine, at] += nt(qt[mine, :], ds)
        return 0

    def pair(j, _):
        step(2 * j, 0)
        step(2 * j + 1, 0)
        return 0

    lax.fori_loop(0, count // 2, pair, 0)

    @pl.when(count % 2 == 1)
    def _():
        step(count - 1, 0)

    qs_sc[:, own] = dq_sc[...]


def attention_backward(place, q, qt, k, kt, v, do, full, lse, segc, segr, cos, sin, heads):
    length = k.shape[0]
    blocks = length // BLOCK
    first = lambda i: jnp.minimum(i, blocks - 1)
    second = lambda i: jnp.maximum(i - blocks, 0)
    return pl.pallas_call(
        partial(backward_kernel, heads),
        grid_spec=pltpu.PrefetchScalarGridSpec(
            num_scalar_prefetch=1,
            grid=(2 * blocks,),
            in_specs=[
                pl.BlockSpec((BLOCK, WIDE), lambda i, s: (first(i) ^ s[0], 0)),
                pl.BlockSpec((WIDE, BLOCK), lambda i, s: (0, first(i) ^ s[0])),
                whole_block(k.shape),
                whole_block(kt.shape),
                whole_block(v.shape),
                *[whole_block(d.shape) for d in do],
                pl.BlockSpec((BLOCK, WIDE), lambda i, s: (first(i), 0)),
                pl.BlockSpec((8, BLOCK), lambda i, s: (0, first(i))),
                whole_block(segc.shape),
                whole_block(segr.shape),
                pl.BlockSpec((BLOCK, 128), lambda i, s: (second(i), 0)),
                pl.BlockSpec((BLOCK, 128), lambda i, s: (second(i), 0)),
            ],
            out_specs=[pl.BlockSpec((BLOCK, 3 * WIDE), lambda i, s: (second(i), 0)), whole_block((8, 3 * WIDE))],
            scratch_shapes=[pltpu.VMEM((WIDE, length), F32)] * 2
            + [pltpu.VMEM((heads * BLOCK, WIDE), BF)] * 2
            + [pltpu.VMEM((WIDE, BLOCK), F32), pltpu.VMEM((BLOCK, WIDE), BF), pltpu.VMEM((WIDE, BLOCK), BF)]
            + [pltpu.VMEM((WIDE, length), F32)],
        ),
        out_shape=[jax.ShapeDtypeStruct((length, 3 * WIDE), BF), jax.ShapeDtypeStruct((8, 3 * WIDE), F32)],
        compiler_params=params(28),
        cost_estimate=COST,
        name="attention_backward",
    )(place, q, qt, k, kt, v, *do, full, lse, segc, segr, cos, sin)


def out_copies(place, gathered, w_out, sems):
    here = place[place.shape[0] - 1]
    feed = gathered.shape[2] - w_out.shape[2]
    return [pltpu.make_async_copy(gathered.at[here ^ k, :, feed:], w_out.at[k], sems.at[k]) for k in range(4)]


def row_mean(x):
    return jnp.mean(x, axis=1, keepdims=True)


def gelu_parts(x):
    e = jnp.exp2(x * x * (-0.5 * 1.4426950408889634))
    t = 1.0 / (1.0 + (0.3275911 * 0.7071067811865476) * jnp.abs(x))
    p = t * (0.127414796 + t * (-0.142248368 + t * (0.7107068705 + t * (-0.7265760135 + t * 0.5307027145))))
    tail = p * e
    phi = jnp.where(x >= 0, 1.0 - tail, tail)
    return phi, phi + x * e * 0.3989422804014327


ROWS = 512


def feed_kernel(place, gathered, w, c0, c1, c2, c3, tokb, gtop, vec, bias, *refs):
    (out_o, gs_o, gsb_o, fs_o, nbt_o, gst_o, act_o, gp_o, root_o, sum_o, nb_o, w_out, acc, normed, sems) = refs
    copies = out_copies(place, gathered, w_out, sems)
    k = pl.program_id(0)
    share = tokb.shape[0]
    part = c0.shape[1]
    chunks = [pl.ds(r * ROWS, ROWS) for r in range(share // ROWS)]

    @pl.when(k == 0)
    def _():
        for copy in copies:
            copy.start()
        for copy in copies:
            copy.wait()
        for sl in chunks:
            x = tokb[sl, :].astype(F32) + vec[4:5, :]
            for n, ctx in enumerate((c0, c1, c2, c3)):
                x = x + nt(ctx[sl, :], w_out[n, :, 0:part])
            x = x - row_mean(x)
            root = lax.rsqrt(row_mean(x * x) + EPSILON)
            x = x * root
            fs_o[sl, :] = x
            root_o[sl, :] = jnp.broadcast_to(root, (ROWS, 128))
            y = x * vec[0:1, :] + vec[2:3, :]
            normed[sl, :] = y
            nb_o[sl, :] = y.astype(BF)
            nbt_o[:, sl] = y.astype(BF).T
            acc[sl, :] = y + vec[5:6, :]

    hidden = act_o.shape[2]

    def rows_step(r, _):
        sl = pl.ds(pl.multiple_of(r * ROWS, ROWS), ROWS)
        h = nn(nb_o[sl, :], w[0, :, 0:hidden]) + bias[pl.ds(k, 1), :]
        phi, slope = gelu_parts(h)
        a = (h * phi).astype(BF)
        act_o[0, sl, :] = a
        gp_o[0, sl, :] = slope
        acc[sl, :] += nt(a, w[0, :, hidden:])
        return 0

    lax.fori_loop(0, share // ROWS, rows_step, 0, unroll=True)

    @pl.when(k == 3)
    def _():
        total = [jnp.zeros((1, tokb.shape[1]), F32)] * 3
        for sl in chunks:
            x = acc[sl, :]
            x = x - row_mean(x)
            root = lax.rsqrt(row_mean(x * x) + EPSILON)
            x = x * root
            out_o[sl, :] = (x * vec[1:2, :] + vec[3:4, :]).astype(BF)
            g = gtop[sl, :].astype(F32)
            gg = g * vec[1:2, :]
            gs = root * (gg - row_mean(gg) - x * row_mean(gg * x))
            gs_o[sl, :] = gs
            gsb_o[sl, :] = gs.astype(BF)
            gst_o[:, sl] = gs.astype(BF).T
            for n, y in enumerate((g * x, g, gs)):
                total[n] = total[n] + jnp.sum(y, axis=0, keepdims=True)
        sum_o[...] = jnp.concatenate(total + [jnp.zeros((5, tokb.shape[1]), F32)], axis=0)


def feed_specs(place, gathered, hidden):
    width, last = gathered.shape[1], place.shape[0] - 1
    return [pl.BlockSpec(memory_space=pl.ANY), pl.BlockSpec((1, width, 2 * hidden), lambda i, s: (s[last] ^ i, 0, 0))]


def feed_forward(place, gathered, contexts, tokb, gtop, vec, bias):
    share, width = tokb.shape
    hidden = bias.shape[1]
    block = lambda: pl.BlockSpec((1, share, hidden), lambda i, s: (i, 0, 0))
    sd, far = jax.ShapeDtypeStruct, pltpu.HBM
    return pl.pallas_call(
        feed_kernel,
        grid_spec=pltpu.PrefetchScalarGridSpec(
            num_scalar_prefetch=1,
            grid=(4,),
            in_specs=feed_specs(place, gathered, hidden) + [whole_block(x.shape) for x in (*contexts, tokb, gtop, vec, bias)],
            out_specs=[whole_block((share, width))] * 4
            + [whole_block((width, share))] * 2
            + [block(), block(), whole_block((share, 128)), whole_block((8, width))],
            scratch_shapes=[
                pltpu.VMEM((share, width), BF),
                pltpu.VMEM((4, width, gathered.shape[2] - 2 * hidden), BF),
                pltpu.VMEM((share, width), F32),
                pltpu.VMEM((share, width), F32),
                pltpu.SemaphoreType.DMA((4,)),
            ],
        ),
        out_shape=[
            sd((share, width), BF),
            sd((share, width), F32),
            sd((share, width), BF),
            sd((share, width), F32),
            far((width, share), BF),
            far((width, share), BF),
            far((4, share, hidden), BF),
            far((4, share, hidden), F32),
            sd((share, 128), F32),
            sd((8, width), F32),
        ],
        compiler_params=params(54),
        cost_estimate=COST,
        name="feed_forward",
    )(place, gathered, gathered, *contexts, tokb, gtop, vec, bias)


def feed_back_kernel(place, gathered, w, gs, gsb, fs, gp, root, vec, *refs):
    (gf_o, gft_o, gc0, gc1, gc2, gc3, gh_o, ghs_o, sum_o, w_out, acc, sems) = refs
    copies = out_copies(place, gathered, w_out, sems)
    k = pl.program_id(0)
    share, width = gs.shape
    hidden, part = gh_o.shape[2], gc0.shape[1]

    @pl.when(k == 0)
    def _():
        for copy in copies:
            copy.start()
        acc[...] = gs[...]

    def rows_step(r, total):
        sl = pl.ds(pl.multiple_of(r * ROWS, ROWS), ROWS)
        g = (nn(gsb[sl, :], w[0, :, hidden:]) * gp[0, sl, :]).astype(BF)
        gh_o[0, sl, :] = g
        acc[sl, :] += nt(g, w[0, :, 0:hidden])
        return total + jnp.sum(g.astype(F32), axis=0, keepdims=True)

    total = lax.fori_loop(0, share // ROWS, rows_step, jnp.zeros((1, hidden), F32), unroll=True)
    ghs_o[0] = jnp.broadcast_to(total, (8, hidden))

    @pl.when(k == 3)
    def _():
        for copy in copies:
            copy.wait()
        sums = [jnp.zeros((1, width), F32)] * 3
        for r in range(share // ROWS):
            sl = pl.ds(r * ROWS, ROWS)
            gn = acc[sl, :]
            x = fs[sl, :]
            gg = gn * vec[0:1, :]
            gf = root[sl, 0:1] * (gg - row_mean(gg) - x * row_mean(gg * x))
            gf_o[sl, :] = gf
            b = gf.astype(BF)
            gft_o[:, sl] = b.T
            for n, o in enumerate((gc0, gc1, gc2, gc3)):
                o[sl, :] = nn(b, w_out[n, :, 0:part]).astype(BF)
            for n, y in enumerate((gn * x, gn, gf)):
                sums[n] = sums[n] + jnp.sum(y, axis=0, keepdims=True)
        sum_o[...] = jnp.concatenate(sums + [jnp.zeros((5, width), F32)], axis=0)


def feed_back(place, gathered, gs, gsb, fs, gp, root, vec, part):
    share, width = gs.shape
    hidden = gp.shape[2]
    block = lambda: pl.BlockSpec((1, share, hidden), lambda i, s: (i, 0, 0))
    sd, far = jax.ShapeDtypeStruct, pltpu.HBM
    return pl.pallas_call(
        feed_back_kernel,
        grid_spec=pltpu.PrefetchScalarGridSpec(
            num_scalar_prefetch=1,
            grid=(4,),
            in_specs=feed_specs(place, gathered, hidden)
            + [whole_block(gs.shape), whole_block(gsb.shape), whole_block(fs.shape), block(), whole_block(root.shape), whole_block(vec.shape)],
            out_specs=[whole_block((share, width)), whole_block((width, share))]
            + [whole_block((share, part))] * 4
            + [block(), pl.BlockSpec((1, 8, hidden), lambda i, s: (i, 0, 0)), whole_block((8, width))],
            scratch_shapes=[
                pltpu.VMEM((4, width, gathered.shape[2] - 2 * hidden), BF),
                pltpu.VMEM((share, width), F32),
                pltpu.SemaphoreType.DMA((4,)),
            ],
        ),
        out_shape=[far((share, width), F32), far((width, share), BF)]
        + [sd((share, part), BF)] * 4
        + [far((4, share, hidden), BF), sd((4, 8, hidden), F32), sd((8, width), F32)],
        compiler_params=params(54),
        cost_estimate=COST,
        name="feed_back",
    )(place, gathered, gathered, gs, gsb, fs, gp, root, vec)


def split_rows(place, per, acc, source, near_o, far_o, lead, cols):
    if per == 1:
        near_o[(*lead, slice(None), cols)] = acc[:, source].astype(near_o.dtype)
        return
    rows = acc.shape[0] // per
    for n in range(per // 2):
        near, far = (pl.ds(pl.multiple_of(place[m], 16), rows) for m in (n, per // 2 + n))
        near_o[(*lead, n, slice(None), cols)] = acc[near, source].astype(near_o.dtype)
        far_o[(*lead, n, slice(None), cols)] = acc[far, source].astype(BF)


def weights_kernel(per, place, nbt, gst, gft, ctx, gh, act, *refs):
    hh = gh.shape[2] // 2
    if per > 1:
        near_o, far_o, out, acc = refs
    else:
        other, out = refs
    for n, (left, right) in enumerate(((nbt, gh), (gst, act))):
        made = nn(left[...], right[0])
        out[0, :, n * hh : (n + 1) * hh] = made[:, 0:hh].astype(BF)
        if per > 1:
            acc[...] = made[:, hh:]
            split_rows(place, per, acc, slice(None), near_o, far_o, (0,), slice(n * hh, (n + 1) * hh))
        else:
            other[0, :, n * hh : (n + 1) * hh] = made[:, hh:].astype(BF)
    out[0, :, 2 * hh :] = nn(gft[...], ctx[0]).astype(BF)


def weight_grads(place, per, nbt, gst, gft, contexts, gh, act):
    width, share = nbt.shape
    hidden, part = gh.shape[2], contexts.shape[2]
    last = place.shape[0] - 1
    block = lambda cols: pl.BlockSpec((1, share, cols), lambda i, s: (i, 0, 0))
    ordered = lambda cols: pl.BlockSpec((1, width, cols), lambda i, s: (i ^ s[last], 0, 0))
    if per > 1:
        shape = (4, per // 2, width // per, hidden)
        outs = [jax.ShapeDtypeStruct(shape, BF)] * 2
        specs = [pl.BlockSpec((1,) + shape[1:], lambda i, s: (i, 0, 0, 0))] * 2
        scratch = [pltpu.VMEM((width, hidden // 2), F32)]
    else:
        outs = [jax.ShapeDtypeStruct((4, width, hidden), BF)]
        specs = [ordered(hidden)]
        scratch = []
    return pl.pallas_call(
        partial(weights_kernel, per),
        grid_spec=pltpu.PrefetchScalarGridSpec(
            num_scalar_prefetch=1,
            grid=(4,),
            in_specs=[whole_block(x.shape) for x in (nbt, gst, gft)] + [block(part), block(hidden), block(hidden)],
            out_specs=specs + [ordered(hidden + part)],
            scratch_shapes=scratch,
        ),
        out_shape=outs + [jax.ShapeDtypeStruct((4, width, hidden + part), BF)],
        compiler_params=params(58),
        cost_estimate=COST,
        name="weight_grads",
    )(place, nbt, gst, gft, contexts, gh, act)


def qkv_weights_kernel(per, part, place, own, other, g, *refs):
    near_o, far_o = refs[:2] if per > 1 else (refs[0], None)
    acc = refs[-1]
    half_len = other.shape[0]
    core = place[per]
    rows = 512

    acc[...] = jnp.zeros(acc.shape, F32)

    def step(r, _):
        at = pl.ds(pl.multiple_of(r * rows, rows), rows)
        a = g[pl.ds(pl.multiple_of(core * half_len + r * rows, rows), rows), :]
        b = g[pl.ds(pl.multiple_of((1 - core) * half_len + r * rows, rows), rows), :]
        acc[...] += nn(own[0, at, :].T, a) + nn(other[at, :].T, b)
        return 0

    lax.fori_loop(0, half_len // rows, step, 0)
    for m in range(3):
        split_rows(place, per, acc, slice(m * WIDE, m * WIDE + part), near_o, far_o, (), slice(m * part, (m + 1) * part))


def qkv_weight_grads(place, per, tokens, other, g, part):
    half_len, width = other.shape
    if per > 1:
        shape = (per // 2, width // per, 3 * part)
        outs = [jax.ShapeDtypeStruct(shape, F32), jax.ShapeDtypeStruct(shape, BF)]
    else:
        outs = [jax.ShapeDtypeStruct((width, 3 * part), F32)]
    return pl.pallas_call(
        partial(qkv_weights_kernel, per, part),
        grid_spec=pltpu.PrefetchScalarGridSpec(
            num_scalar_prefetch=1,
            grid=(1,),
            in_specs=[pl.BlockSpec((1, half_len, width), lambda i, s: (s[per], 0, 0)), whole_block(other.shape), whole_block(g.shape)],
            out_specs=[whole_block(o.shape) for o in outs],
            scratch_shapes=[pltpu.VMEM((width, 3 * WIDE), F32)],
        ),
        out_shape=outs,
        compiler_params=params(32),
        cost_estimate=COST,
        name="qkv_weight_grads",
    )(place, tokens, other, g)


def branch_kernel(place, *refs):
    count = (len(refs) - 1) // 2
    w = refs[count]
    for g, o in zip(refs[:count], refs[count + 1 :]):
        rows = 256
        for r in range(g.shape[0] // rows):
            sl = slice(r * rows, (r + 1) * rows)
            o[sl, :] = nt(g[sl, :], w[...]).astype(o.dtype)


def branch(place, blocks, kinds, g, w):
    share, last = g.shape[0] // 4, place.shape[0] - 1
    return pl.pallas_call(
        branch_kernel,
        grid_spec=pltpu.PrefetchScalarGridSpec(
            num_scalar_prefetch=1,
            grid=(1,),
            in_specs=[pl.BlockSpec((share, g.shape[1]), lambda i, s, k=k: (s[last] ^ k, 0)) for k in blocks] + [whole_block(w.shape)],
            out_specs=[whole_block((share, w.shape[0]))] * len(blocks),
        ),
        out_shape=[jax.ShapeDtypeStruct((share, w.shape[0]), kind) for kind in kinds],
        compiler_params=params(24),
        cost_estimate=COST,
        name="branch",
    )(place, *[g] * len(blocks), w)


def pick_kernel(place, near, *refs):
    far, (keep, send) = refs[:-2], refs[-2:]
    last = place.shape[0] - 1
    mine = place[last] // 2 == place[last - 1]

    def put(out, parts):
        rows = out.shape[0] // len(parts)
        for n, x in enumerate(parts):
            out[n * rows : (n + 1) * rows, :] = x[...]

    @pl.when(mine)
    def _():
        put(keep, [near])
        put(send, far)

    @pl.when(jnp.logical_not(mine))
    def _():
        put(keep, far)
        put(send, [near])


def pick(place, near, *far):
    return pl.pallas_call(
        pick_kernel,
        grid_spec=pltpu.PrefetchScalarGridSpec(
            num_scalar_prefetch=1,
            grid=(1,),
            in_specs=[whole_block(x.shape) for x in (near, *far)],
            out_specs=[whole_block(near.shape)] * 2,
        ),
        out_shape=[jax.ShapeDtypeStruct(near.shape, near.dtype)] * 2,
        compiler_params=params(8),
        cost_estimate=COST,
        name="pick",
    )(place, near, *far)


def join_kernel(second, place, *refs):
    last = place.shape[0] - 1
    mine = place[last] // 2 == place[last - 1]
    if second:
        near, *far, other, _, out = refs
    else:
        near, *far, other, out = refs
    here = pl.program_id(0) == place[last - 1]

    def put(parts):
        rows = out.shape[1] // len(parts)
        for n, x in enumerate(parts):
            out[0, n * rows : (n + 1) * rows, :] = x[...]

    @pl.when(jnp.logical_and(here, mine))
    def _():
        put([near])

    @pl.when(jnp.logical_and(here, jnp.logical_not(mine)))
    def _():
        put(far)

    @pl.when(jnp.logical_not(here))
    def _():
        put([other])


def join(place, near, far, other, before=None):
    share, width = near.shape
    second = before is not None
    last = place.shape[0] - 1
    ins = [near, *far, other]
    specs = [whole_block(x.shape) for x in ins]
    if second:
        ins.append(before)
        specs.append(pl.BlockSpec(memory_space=pl.ANY))
    return pl.pallas_call(
        partial(join_kernel, second),
        grid_spec=pltpu.PrefetchScalarGridSpec(
            num_scalar_prefetch=1,
            grid=(2,),
            in_specs=specs,
            out_specs=pl.BlockSpec((1, share, width), lambda i, s: (i, (s[last] + int(second)) % 2, 0)),
        ),
        out_shape=jax.ShapeDtypeStruct((2, 2 * share, width), near.dtype),
        input_output_aliases={len(ins): 0} if second else {},
        compiler_params=params(12),
        cost_estimate=COST,
        name="join",
    )(place, *ins)


def relay_kernel(one, two, low, high, one_o, two_o):
    half = low.shape[0]
    one_o[0:half, :] = (one[0:half, :] + low[...].astype(F32)).astype(BF)
    one_o[half:, :] = one[half:, :].astype(BF)
    two_o[0:half, :] = two[0:half, :].astype(BF)
    two_o[half:, :] = (two[half:, :] + high[...].astype(F32)).astype(BF)


def relay(one, two, low, high):
    return pl.pallas_call(
        relay_kernel,
        in_specs=[pl.BlockSpec(memory_space=pltpu.VMEM)] * 4,
        out_specs=[pl.BlockSpec(memory_space=pltpu.VMEM)] * 2,
        out_shape=[jax.ShapeDtypeStruct(one.shape, BF)] * 2,
        compiler_params=pltpu.CompilerParams(vmem_limit_bytes=16 * 1024 * 1024),
        cost_estimate=COST,
        name="relay",
    )(one, two, low, high)


def collect_kernel(place, hidden_sums, one, two, bias, out):
    here = place[place.shape[0] - 1]
    out[...] = jnp.zeros(out.shape, F32)
    for k in range(4):
        out[pl.ds(here ^ k, 1), :] = hidden_sums[k, 0:1, :]
    for n, (x, row) in enumerate(((one, 0), (two, 0), (one, 1), (two, 1), (one, 2), (two, 2))):
        out[4 + n : 5 + n, :] = x[row : row + 1, :]
    out[pl.ds(10 + here, 1), :] = bias[0:1, :]


def collect(place, hidden_sums, one, two, bias):
    return pl.pallas_call(
        collect_kernel,
        grid_spec=pltpu.PrefetchScalarGridSpec(
            num_scalar_prefetch=1,
            grid=(1,),
            in_specs=[whole_block(x.shape) for x in (hidden_sums, one, two, bias)],
            out_specs=whole_block((16, one.shape[1])),
        ),
        out_shape=jax.ShapeDtypeStruct((16, one.shape[1]), F32),
        compiler_params=params(8),
        cost_estimate=COST,
        name="collect",
    )(place, hidden_sums, one, two, bias)


def settle_kernel(count, *refs):
    ins, outs = refs[:count], refs[count:]
    for j, out in enumerate(outs):
        total = ins[0][j].astype(F32)
        for x in ins[1:]:
            total = total + x[j].astype(F32)
        out[...] = total.astype(out.dtype)


def settle(*stacks):
    shape = stacks[0].shape
    vmem = pl.BlockSpec(memory_space=pltpu.VMEM)
    return pl.pallas_call(
        partial(settle_kernel, len(stacks)),
        in_specs=[vmem] * len(stacks),
        out_specs=[vmem] * shape[0],
        out_shape=[jax.ShapeDtypeStruct(shape[1:], F32 if j == 0 else BF) for j in range(shape[0])],
        compiler_params=pltpu.CompilerParams(vmem_limit_bytes=16 * 1024 * 1024),
        cost_estimate=COST,
        name="settle",
    )(*stacks)


def finish_kernel(parts, *refs):
    out = refs[-1]
    total = refs[0][...]
    for x in refs[1:-1]:
        total = total + x[...].astype(F32)
    if parts == 1:
        out[...] = total
    else:
        cols = total.shape[1] // parts
        for m in range(parts):
            out[:, m, :] = total[:, m * cols : (m + 1) * cols]


def finish(parts, *pieces):
    vmem = pl.BlockSpec(memory_space=pltpu.VMEM)
    rows, cols = pieces[0].shape
    return pl.pallas_call(
        partial(finish_kernel, parts),
        in_specs=[vmem] * len(pieces),
        out_specs=vmem,
        out_shape=jax.ShapeDtypeStruct((rows, cols) if parts == 1 else (rows, parts, cols // parts), F32),
        compiler_params=pltpu.CompilerParams(vmem_limit_bytes=8 * 1024 * 1024),
        cost_estimate=COST,
        name="finish",
    )(*pieces)


def place_kernel(whole, rest, feed_o, out_o):
    hh = rest.shape[1] // 2
    for m in range(2):
        feed_o[:, m, 0:hh] = whole[:, m * hh : (m + 1) * hh].astype(F32)
        feed_o[:, m, hh:] = rest[:, m * hh : (m + 1) * hh]
    out_o[...] = whole[:, 2 * hh :].astype(F32)


def place_feed(whole, rest):
    vmem = pl.BlockSpec(memory_space=pltpu.VMEM)
    rows, cols = rest.shape
    return pl.pallas_call(
        place_kernel,
        in_specs=[vmem] * 2,
        out_specs=[vmem] * 2,
        out_shape=[jax.ShapeDtypeStruct((rows, 2, cols), F32), jax.ShapeDtypeStruct((rows, whole.shape[1] - cols), F32)],
        compiler_params=pltpu.CompilerParams(vmem_limit_bytes=8 * 1024 * 1024),
        cost_estimate=COST,
        name="place_feed",
    )(whole, rest)


def block_kernel(own, first, one, two, out):
    out[...] = (own[...] + first[...] + one[...].astype(F32) + two[...].astype(F32)).astype(BF)


def add_block(own, first, one, two):
    vmem = pl.BlockSpec(memory_space=pltpu.VMEM)
    return pl.pallas_call(
        block_kernel,
        in_specs=[vmem] * 4,
        out_specs=vmem,
        out_shape=jax.ShapeDtypeStruct(own.shape, BF),
        compiler_params=pltpu.CompilerParams(vmem_limit_bytes=12 * 1024 * 1024),
        cost_estimate=COST,
        name="add_block",
    )(own, first, one, two)


def relay_kernel(one, two, low, high, one_o, two_o):
    half = low.shape[0]
    one_o[0:half, :] = (one[0:half, :] + low[...].astype(F32)).astype(BF)
    one_o[half:, :] = one[half:, :].astype(BF)
    two_o[0:half, :] = two[0:half, :].astype(BF)
    two_o[half:, :] = (two[half:, :] + high[...].astype(F32)).astype(BF)


def relay(one, two, low, high):
    return pl.pallas_call(
        relay_kernel,
        in_specs=[pl.BlockSpec(memory_space=pltpu.VMEM)] * 4,
        out_specs=[pl.BlockSpec(memory_space=pltpu.VMEM)] * 2,
        out_shape=[jax.ShapeDtypeStruct(one.shape, BF)] * 2,
        compiler_params=pltpu.CompilerParams(vmem_limit_bytes=16 * 1024 * 1024),
        cost_estimate=COST,
        name="relay",
    )(one, two, low, high)


def rotation_tables(offsets):
    lane = np.arange(128)
    frequency = (10000.0 ** (-2.0 * (lane % HEAD // 2) / HEAD)).astype(np.float32)
    angles = offsets.astype(F32)[:, None] * frequency[None, :]
    sign = np.where(lane % 2 == 0, -1.0, 1.0).astype(np.float32)
    return jnp.cos(angles), jnp.sin(angles) * sign


def key_bounds(segment):
    length = segment.shape[0]
    first, last = segment[::BLOCK], segment[BLOCK - 1 :: BLOCK]
    low = jnp.sum(segment[None, :] < first[:, None], axis=1)
    high = jnp.sum(segment[None, :] <= last[:, None], axis=1)
    low = low // 128 * 128
    count = (high - low + CHUNK - 1) // CHUNK
    return jnp.stack([jnp.minimum(low, length - CHUNK * count), count], axis=1).reshape(-1).astype(jnp.int32)


def swap_ctx(x):
    return lax.ppermute(x, "ctx", [(0, 1), (1, 0)])


def swap_tp(x, k):
    return lax.ppermute(x, "tp", [(i, i ^ k) for i in range(4)])


def swap_shard(x, k):
    return lax.ppermute(x, "shard", [(i, i ^ k) for i in range(4)])


def order_four(parts, index):
    a, b, c, d = parts
    odd, high = index % 2 == 1, index // 2 == 1
    a, b = jnp.where(odd, b, a), jnp.where(odd, a, b)
    c, d = jnp.where(odd, d, c), jnp.where(odd, c, d)
    return jnp.stack([jnp.where(high, c, a), jnp.where(high, d, b), jnp.where(high, a, c), jnp.where(high, b, d)])


def after(x, *others):
    return lax.optimization_barrier((x, others))[0]


def gather_tp(x, half):
    one, two = swap_tp(x, 1), swap_tp(x, 2)
    three = jnp.concatenate([swap_tp(one[:half], 2), swap_tp(two[half:], 1)])
    return [x, one, two, three]


def scatter_tp(parts):
    own, one, two, three = parts
    half = own.shape[0] // 2
    low, high = three[:half].astype(BF), three[half:].astype(BF)
    low, high = swap_tp(low, 2), swap_tp(high, 1)
    one = jnp.concatenate([one[:half] + low.astype(F32), one[half:]]).astype(BF)
    two = jnp.concatenate([two[:half], two[half:] + high.astype(F32)]).astype(BF)
    return own + swap_tp(one, 1).astype(F32) + swap_tp(two, 2).astype(F32)


def three_rows(x):
    high = lax.reduce_precision(x, 8, 7)
    middle = lax.reduce_precision(x - high, 8, 7)
    return jnp.stack([high, middle, x - high - middle]).astype(BF)


def contract_last(left, right):
    return lax.dot_general(left, right, (((1,), (1,)), ((), ())), preferred_element_type=F32)


def body(tokens, segment_ids, offsets, qkv_weight, out_weight, ffn_weight, qkv_bias, ffn_bias, norm_gain, shift_params, out_grad):
    t, c, z = lax.axis_index("tp"), lax.axis_index("ctx"), lax.axis_index("shard")
    shards = lax.axis_size("shard")
    half_len, width = tokens.shape[1:]
    rows, _, part = qkv_weight.shape
    hidden = ffn_weight.shape[2]
    heads = part // HEAD
    length = 2 * half_len
    share = length // 4
    first_core = c == 0
    direct = shards == 4

    def take(x, index):
        return lax.dynamic_index_in_dim(x, index, 0, keepdims=False)

    def by_core(own, other):
        return jnp.where(first_core, jnp.stack([own, other]), jnp.stack([other, own]))

    hh = hidden // 2
    gathered = jnp.concatenate([ffn_weight.reshape(rows, 2 * hidden), out_weight], axis=1)
    gathered = lax.all_gather(gathered, ("tp", "shard", "ctx"), axis=0, tiled=True).reshape(4, width, 2 * hidden + part)
    bias_all = ffn_bias.reshape(1, hidden)
    bias_all = jnp.concatenate([bias_all] + [swap_tp(bias_all, k) for k in (1, 2, 3)])
    qkv_rows = qkv_weight.reshape(rows, 3 * part)
    other_tokens = swap_ctx(take(tokens, 1 - c))
    if direct:
        places = [((z ^ j) * 2 + (c ^ f)) * rows for f in (0, 1) for j in range(4)]
        near = [qkv_rows] + [swap_shard(qkv_rows, j) for j in (1, 2, 3)]
        qkv_pieces = [*near, swap_ctx(jnp.stack(near))]
    else:
        places = [jnp.zeros_like(c)]
        qkv_pieces = [lax.all_gather(qkv_rows, ("shard", "ctx"), axis=0, tiled=True)]
    per = len(places)
    place = jnp.stack(places + [c, t]).astype(jnp.int32)
    bias_pad = jnp.pad(qkv_bias, ((0, 0), (0, WIDE - part)))
    vec = jnp.concatenate([norm_gain, shift_params, jnp.zeros((2, width), F32)])

    marks = jnp.stack([segment_ids, offsets])
    marks = by_core(take(marks.swapaxes(0, 1), c), swap_ctx(take(marks.swapaxes(0, 1), 1 - c)))
    segment, places = marks[:, 0].reshape(length), marks[:, 1].reshape(length)
    halves = lambda x: x.reshape(2, 2, share, width)
    here = t // 2 == c
    tok_block = jnp.where(here, take(take(halves(tokens), c), t % 2), take(other_tokens.reshape(2, share, width), t % 2))
    grad_block = halves(out_grad)
    grad_far = swap_ctx(take(take(grad_block, 1 - c), t % 2))
    grad_top = jnp.where(here, take(take(grad_block, c), t % 2), grad_far)

    cosine, sine = rotation_tables(places)
    bounds = key_bounds(segment)
    seg_column = segment[:, None]
    seg_row = jnp.broadcast_to(segment[None, :], (8, length))
    q, k_rows, v_rows, k_turned, q_turned, qkv_wide = project_qkv(place, qkv_pieces, per, bias_pad, tokens, other_tokens, cosine, sine, part)

    contexts, log_totals, fulls = [None] * 4, [None] * 4, [None] * 4

    def forward(j, q):
        spot = jnp.concatenate([((t ^ j) * (share // BLOCK))[None].astype(jnp.int32), bounds])
        context, log_totals[j], fulls[j] = attention_forward(spot, q, k_rows, v_rows, seg_column, seg_row, heads, share)
        contexts[j] = swap_tp(context, j) if j else context

    forward(3, q)
    q_next, log_totals[3] = lax.optimization_barrier((q, log_totals[3]))
    forward(1, q_next)
    q_next, log_totals[1], contexts[3] = lax.optimization_barrier((q, log_totals[1], contexts[3]))
    forward(2, q_next)
    q_next, log_totals[2], contexts[1] = lax.optimization_barrier((q, log_totals[2], contexts[1]))
    forward(0, q_next)
    stacked = jnp.stack(contexts)
    tok_block, log_total, full, stacked = lax.optimization_barrier(
        (tok_block, jnp.concatenate(log_totals, axis=1), jnp.concatenate(fulls), stacked)
    )

    layer_out, grad_second, grad_second_b, first_scaled, normed_t, second_t, activated, slope, root, sums_two = feed_forward(
        place, gathered, contexts, tok_block, grad_top, vec, bias_all
    )

    barrier = lax.optimization_barrier
    out_blocks = [layer_out, swap_tp(layer_out, 1), swap_tp(layer_out, 2)]

    grad_first, first_t, g0, g1, g2, g3, grad_hidden, hidden_sums, sums_one = feed_back(
        place, gathered, grad_second, grad_second_b, first_scaled, slope, root, vec, part
    )
    heads_grads = [g0, swap_tp(g1, 1), swap_tp(g2, 2), swap_tp(g3, 3)]

    *made, whole = weight_grads(place, per, normed_t, second_t, first_t, stacked, grad_hidden, activated)
    made, whole, heads_grads, out_blocks = barrier((made, whole, heads_grads, out_blocks))
    whole = lax.psum_scatter(whole.reshape(-1, 2 * hh + part), ("tp", "shard", "ctx"), scatter_dimension=0, tiled=True)
    grad_heads = heads_grads
    corner = [out_blocks[1][: share // 2], out_blocks[2][share // 2 :]]
    if direct:
        got = swap_ctx(made[1])
        grad_heads, got, corner = barrier((grad_heads, got, corner))
        packs = [made[0][k].astype(F32) + got[k].astype(F32) for k in range(4)]
        sent = [packs[k].astype(BF) for k in (1, 2, 3)]
        grad_heads, sent = barrier((grad_heads, sent))
        sent = [swap_tp(sent[k - 1], k) for k in (1, 2, 3)]
    corner = [swap_tp(corner[0], 2), swap_tp(corner[1], 1)]

    spot = jnp.concatenate([(t * (share // BLOCK))[None].astype(jnp.int32), bounds])
    grad_proj, bias_sums = attention_backward(
        spot, q, q_turned, k_rows, k_turned, v_rows, grad_heads, full, log_total, seg_column, seg_row, cosine, sine, heads
    )
    grad_proj, bias_sums, hidden_sums, sums_one, sums_two, out_blocks = barrier(
        (grad_proj, bias_sums, hidden_sums, sums_one, sums_two, out_blocks)
    )
    if direct:
        grad_proj, sent, packs[0] = barrier((grad_proj, sent, packs[0]))

    three = branch(place, (3,), (BF,), grad_proj, qkv_wide)[0]
    three, grad_proj, corner, bias_sums, out_blocks = barrier((three, grad_proj, corner, bias_sums, out_blocks))
    low, high = swap_tp(three[: share // 2], 2), swap_tp(three[share // 2 :], 1)
    one, two, own = branch(place, (1, 2, 0), (F32, F32, F32), grad_proj, qkv_wide)
    grads = qkv_weight_grads(place, per, tokens, other_tokens, grad_proj, part)
    keep_a, send_a = pick(place, out_blocks[0], out_blocks[2])
    keep_b, send_b = pick(place, out_blocks[1], *corner)
    small = collect(place, hidden_sums, sums_one, sums_two, bias_sums)
    outs = [swap_ctx(send_a), swap_ctx(send_b)]
    if direct:
        qkv_sum, *qkv_pieces = settle(grads[0], swap_ctx(grads[1]))
        qkv_sum, qkv_pieces, low = barrier((qkv_sum, qkv_pieces, low))
    low, high, one, two, own, outs, small = barrier((low, high, one, two, own, outs, small))

    def send_shards(pieces, small, k):
        moved = [swap_shard(pieces[j - 1], j) for j in (1, 2, 3)]
        moved[0], small = barrier((moved[0], small))
        return moved, small + swap_tp(small, k)

    one, two = relay(one, two, low, high)
    one, two, outs, small = barrier((one, two, outs, small))
    one, two = swap_tp(one, 1), swap_tp(two, 2)
    outputs = join(place, out_blocks[0], [out_blocks[2]], outs[0])
    outputs = join(place, out_blocks[1], corner, outs[1], outputs)
    if direct:
        moved, small = send_shards(qkv_pieces, small, 1)
        qkv_total = finish(3, qkv_sum, *moved)
        summed, *pieces = settle(packs[0], *sent)
        one, two, own, small, outputs, summed, pieces, qkv_total = barrier((one, two, own, small, outputs, summed, pieces, qkv_total))
    else:
        one, two, own, small, outputs = barrier((one, two, own, small, outputs))

    block = add_block(own, grad_first, one, two)
    ready = [block, swap_tp(block, 1), swap_tp(block, 2)]
    if direct:
        moved, small = send_shards(pieces, small, 2)
        total = finish(1, summed, *moved)
        ready, total, small = barrier((ready, total, small))
    else:
        qkv_total = lax.psum_scatter(grads[0], ("shard", "ctx"), scatter_dimension=0, tiled=True).reshape(rows, 3, part)
        total = lax.psum_scatter(made[0].reshape(-1, 2 * hh), ("tp", "shard", "ctx"), scatter_dimension=0, tiled=True).astype(F32)
    corner = [swap_tp(ready[1][: share // 2], 2), swap_tp(ready[2][share // 2 :], 1)]
    _, send_a = pick(place, ready[0], ready[2])
    grad_tokens = join(place, ready[0], [ready[2]], swap_ctx(send_a))
    grad_ffn_weight, grad_out_weight = place_feed(whole, total)
    if direct:
        small = small + swap_shard(small, 1)
        small, grad_tokens = barrier((small, grad_tokens))
        small = small + swap_shard(small, 2)
    else:
        small = lax.psum(small, ("shard", "ctx", "tp"))
    corner, small, grad_tokens, qkv_total = barrier((corner, small, grad_tokens, qkv_total))
    if direct:
        small = small + swap_ctx(small)
    send_b = jnp.where(here, jnp.concatenate(corner), ready[1])
    grad_tokens = join(place, ready[1], corner, swap_ctx(send_b), grad_tokens)

    grad_qkv_weight = qkv_total
    grad_ffn_bias = take(small, t)
    vectors = small[4:10]
    grad_qkv_bias = take(small[10:14], t).reshape(3, WIDE)[:, :part]
    return (
        outputs,
        grad_tokens,
        grad_qkv_weight,
        grad_out_weight,
        grad_ffn_weight,
        grad_qkv_bias,
        grad_ffn_bias,
        vectors[:2],
        vectors[2:],
    )


def solution(mesh):
    return jax.shard_map(
        body,
        mesh=mesh,
        in_specs=(
            P("shard", "ctx", None),
            P("shard", "ctx"),
            P("shard", "ctx"),
            P(("shard", "ctx"), None, "tp"),
            P(("shard", "ctx"), "tp"),
            P(("shard", "ctx"), None, "tp"),
            P(None, "tp"),
            P("tp"),
            P(),
            P(),
            P("shard", "ctx", None),
        ),
        out_specs=(
            P("shard", "ctx", None),
            P("shard", "ctx", None),
            P(("shard", "ctx"), None, "tp"),
            P(("shard", "ctx"), "tp"),
            P(("shard", "ctx"), None, "tp"),
            P(None, "tp"),
            P("tp"),
            P(),
            P(),
        ),
        check_vma=False,
    )
```

```python
from functools import partial

import jax
import jax.numpy as jnp
import numpy as np
from jax import lax
from jax.experimental import pallas as pl
from jax.experimental.pallas import tpu as pltpu
from jax.sharding import PartitionSpec as P

HEAD = 64
WIDE = 256
BLOCK = 256
CHUNK = 256
EPSILON = 1e-12
F32 = jnp.float32
BF = jnp.bfloat16
NEG = -1e30
COST = pl.CostEstimate(flops=0, bytes_accessed=0, transcendentals=0)


def swap_pairs(x):
    lane = lax.broadcasted_iota(jnp.int32, x.shape, 1)
    n = x.shape[1]
    return jnp.where(lane % 2 == 0, pltpu.roll(x, n - 1, 1), pltpu.roll(x, 1, 1))


def nt(a, b):
    return lax.dot_general(a, b, (((1,), (1,)), ((), ())), preferred_element_type=F32)


def nn(a, b):
    return lax.dot_general(a, b, (((1,), (0,)), ((), ())), preferred_element_type=F32)


def twice(x):
    return jnp.concatenate([x, x], axis=1)


def lanes_of_heads(x, heads):
    lane = lax.broadcasted_iota(jnp.int32, x.shape, 1) // HEAD
    return [jnp.where(lane == h, x, jnp.zeros_like(x)) for h in range(heads)]


def whole_block(shape, buffers=1):
    return pl.BlockSpec(shape, lambda *_: (0,) * len(shape), pipeline_mode=pl.Buffered(buffers))


def smem():
    return pl.BlockSpec(memory_space=pltpu.SMEM)


def params(mib):
    return pltpu.CompilerParams(dimension_semantics=("arbitrary",), vmem_limit_bytes=mib * 1024 * 1024)


def qkv_kernel(count, per, part, place, *refs):
    pieces = []
    for x in refs[:count]:
        pieces += [x] if len(x.shape) == 2 else [x.at[n] for n in range(x.shape[0])]
    bias, own, other, cos, sin, q_o, k_o, v_o, kt_o, qt_o, w_o = refs[count:]
    piece_rows = pieces[0].shape[0]
    pad = jnp.zeros((piece_rows, WIDE - part), BF)
    for n in range(per):
        sl = pl.ds(pl.multiple_of(place[n], 16), piece_rows)
        for m in range(3):
            w_o[sl, m * WIDE : (m + 1) * WIDE] = jnp.concatenate([pieces[n][:, m * part : (m + 1) * part], pad], axis=1)
    half_len = other.shape[0]

    def run(x, sl):
        c, s = twice(cos[sl, :]), twice(sin[sl, :])
        p = nn(x, w_o[:, 0:WIDE]) + bias[0:1, :]
        q = ((p * c + swap_pairs(p) * s).astype(BF).astype(F32) * (HEAD**-0.5)).astype(BF)
        q_o[sl, :] = q
        qt_o[:, sl] = q.T
        p = nn(x, w_o[:, WIDE : 2 * WIDE]) + bias[1:2, :]
        k = (p * c + swap_pairs(p) * s).astype(BF)
        k_o[sl, :] = k
        kt_o[:, sl] = k.T
        v_o[sl, :] = (nn(x, w_o[:, 2 * WIDE : 3 * WIDE]) + bias[2:3, :]).astype(BF)

    def step(r, _):
        rows = pl.ds(pl.multiple_of(r * BLOCK, BLOCK), BLOCK)
        core = place[per]
        run(own[0, rows, :], pl.ds(pl.multiple_of(core * half_len + r * BLOCK, BLOCK), BLOCK))
        run(other[rows, :], pl.ds(pl.multiple_of((1 - core) * half_len + r * BLOCK, BLOCK), BLOCK))
        return 0

    lax.fori_loop(0, half_len // BLOCK, step, 0)


def project_qkv(place, pieces, per, bias, tokens, other, cos, sin, part):
    half_len, width = other.shape
    length, count = 2 * half_len, len(pieces)
    return pl.pallas_call(
        partial(qkv_kernel, count, per, part),
        grid_spec=pltpu.PrefetchScalarGridSpec(
            num_scalar_prefetch=1,
            grid=(1,),
            in_specs=[whole_block(p.shape) for p in pieces]
            + [whole_block(bias.shape), pl.BlockSpec((1, half_len, width), lambda i, s: (s[per], 0, 0))]
            + [whole_block(x.shape) for x in (other, cos, sin)],
            out_specs=[whole_block((length, WIDE))] * 3 + [whole_block((WIDE, length))] * 2 + [whole_block((width, 3 * WIDE))],
        ),
        out_shape=[jax.ShapeDtypeStruct((length, WIDE), BF)] * 3
        + [jax.ShapeDtypeStruct((WIDE, length), BF)] * 2
        + [jax.ShapeDtypeStruct((width, 3 * WIDE), BF)],
        compiler_params=params(32),
        cost_estimate=COST,
        name="project_qkv",
    )(place, *pieces, bias, tokens, other, cos, sin)


def forward_kernel(heads, place, q, k, v, segc, segr, ctx_o, lse_o, full_o, acc, s_sc, m_sc, l_sc, qc_sc):
    i = place[0] + pl.program_id(0)
    start, count = place[1 + 2 * i], place[2 + 2 * i]
    qc_sc[...] = jnp.concatenate(lanes_of_heads(q[...], heads), axis=0)
    seg_q = segc[...]
    m_sc[...] = jnp.full(m_sc.shape, NEG, F32)
    l_sc[...] = jnp.zeros(l_sc.shape, F32)

    def at(j):
        return pl.ds(pl.multiple_of(start + j * CHUNK, 128), CHUNK)

    def of(h):
        return slice(h * BLOCK, (h + 1) * BLOCK)

    def pass1(j, _):
        s = nt(qc_sc[...], k[at(j), :])
        keep = seg_q == segr[0:1, at(j)]
        for h in range(heads):
            sh = jnp.where(keep, s[of(h), :], NEG)
            s_sc[j, of(h), :] = sh
            m_sc[of(h), :] = jnp.maximum(m_sc[of(h), :], jnp.maximum(sh[:, :128], sh[:, 128:]))
        return 0

    lax.fori_loop(0, count, pass1, 0)
    m_sc[...] = jnp.broadcast_to(jnp.max(m_sc[...], axis=1, keepdims=True), m_sc.shape)

    def pass2(j, _):
        for h in range(heads):
            e = jnp.exp(s_sc[j, of(h), :] - twice(m_sc[of(h), :]))
            s_sc[j, of(h), :] = e
            l_sc[of(h), :] += e[:, :128] + e[:, 128:]
        return 0

    lax.fori_loop(0, count, pass2, 0)
    total = jnp.sum(l_sc[...], axis=1, keepdims=True)
    lse = m_sc[:, 0:1] + jnp.log(total)
    l_sc[...] = jnp.broadcast_to(1.0 / total, l_sc.shape)
    lane = lax.broadcasted_iota(jnp.int32, (BLOCK, 128), 1)
    tile = jnp.zeros((BLOCK, 128), F32)
    for h in range(heads):
        tile = jnp.where(lane == h, lse[of(h), :], tile)
    lse_o[...] = tile.T[0:8, :]
    acc[...] = jnp.zeros(acc.shape, F32)
    full_o[...] = jnp.zeros(full_o.shape, F32)

    def pass3(j, _):
        ps, less = [], []
        for h in range(heads):
            p = s_sc[j, of(h), :] * twice(l_sc[of(h), :])
            b = p.astype(BF)
            ps.append(b)
            less.append((p - b.astype(F32)).astype(BF))
        vs = jnp.concatenate(lanes_of_heads(v[at(j), :], heads), axis=0)
        acc[...] += nn(jnp.concatenate(ps, axis=1), vs)
        full_o[...] += nn(jnp.concatenate(less, axis=1), vs)
        return 0

    lax.fori_loop(0, count, pass3, 0)
    ctx_o[...] = acc[:, : heads * HEAD].astype(BF)
    full_o[...] += acc[...]


def attention_forward(place, q, k, v, segc, segr, heads, share):
    length = q.shape[0]
    grid = share // BLOCK
    rows = lambda i, s: (s[0] + i, 0)
    return pl.pallas_call(
        partial(forward_kernel, heads),
        grid_spec=pltpu.PrefetchScalarGridSpec(
            num_scalar_prefetch=1,
            grid=(grid,),
            in_specs=[
                pl.BlockSpec((BLOCK, WIDE), rows),
                whole_block(k.shape),
                whole_block(v.shape),
                pl.BlockSpec((BLOCK, 1), rows),
                whole_block(segr.shape),
            ],
            out_specs=[
                pl.BlockSpec((BLOCK, heads * HEAD), lambda i, s: (i, 0)),
                pl.BlockSpec((8, BLOCK), lambda i, s: (0, i)),
                pl.BlockSpec((BLOCK, WIDE), lambda i, s: (i, 0)),
            ],
            scratch_shapes=[
                pltpu.VMEM((BLOCK, WIDE), F32),
                pltpu.VMEM((length // CHUNK, heads * BLOCK, CHUNK), F32),
                pltpu.VMEM((heads * BLOCK, 128), F32),
                pltpu.VMEM((heads * BLOCK, 128), F32),
                pltpu.VMEM((heads * BLOCK, WIDE), BF),
            ],
        ),
        out_shape=[
            jax.ShapeDtypeStruct((share, heads * HEAD), BF),
            jax.ShapeDtypeStruct((8, share), F32),
            jax.ShapeDtypeStruct((share, WIDE), F32),
        ],
        compiler_params=params(16),
        cost_estimate=COST,
        name="attention_forward",
    )(place, q, k, v, segc, segr)


def backward_kernel(heads, place, q, qt, k, kt, v, d0, d1, d2, d3, full, lse, segc, segr, cos, sin, g_o, gb_o, dk_sc, dv_sc, qc_sc, dc_sc, dq_sc, d_sc, dt_sc, qs_sc):
    step_at = pl.program_id(0)
    blocks = k.shape[0] // BLOCK

    @pl.when(step_at < blocks)
    def _():
        backward_rows(heads, place, q, qt, k, kt, v, (d0, d1, d2, d3), full, lse, segc, segr, dk_sc, dv_sc, qc_sc, dc_sc, dq_sc, d_sc, dt_sc, qs_sc)

    @pl.when(step_at == 0)
    def _():
        gb_o[...] = jnp.zeros(gb_o.shape, F32)

    @pl.when(step_at >= blocks)
    def _():
        at = pl.ds(pl.multiple_of((step_at - blocks) * BLOCK, BLOCK), BLOCK)

        def turn(x):
            return (x * twice(cos[...]) - swap_pairs(x) * twice(sin[...])).astype(BF)

        def put(x, m):
            g_o[:, m * WIDE : (m + 1) * WIDE] = x
            gb_o[0:1, m * WIDE : (m + 1) * WIDE] += jnp.sum(x.astype(F32), axis=0, keepdims=True)

        put(turn(qs_sc[:, at].T * (HEAD**-0.5)), 0)
        put(turn(dk_sc[:, at].T), 1)
        put(dv_sc[:, at].astype(BF).T, 2)


def backward_rows(heads, place, q, qt, k, kt, v, do, full, lse, segc, segr, dk_sc, dv_sc, qc_sc, dc_sc, dq_sc, d_sc, dt_sc, qs_sc):
    step_at = pl.program_id(0)
    i = step_at ^ place[0]
    part = do[0].shape[1]
    per = do[0].shape[0] // BLOCK

    @pl.when(step_at == 0)
    def _():
        dk_sc[...] = jnp.zeros(dk_sc.shape, F32)
        dv_sc[...] = jnp.zeros(dv_sc.shape, F32)
        d_sc[...] = jnp.zeros(d_sc.shape, BF)

    for n, d in enumerate(do):

        @pl.when(step_at // per == n)
        def _(d=d):
            d_sc[:, 0:part] = d[pl.ds(pl.multiple_of(step_at % per * BLOCK, BLOCK), BLOCK), :]

    start, count = place[1 + 2 * i], place[2 + 2 * i]
    qc_sc[...] = jnp.concatenate(lanes_of_heads(q[...], heads), axis=0)
    dz = d_sc[...]
    dc_sc[...] = jnp.concatenate(lanes_of_heads(dz, heads), axis=0)
    dt_sc[...] = dz.T
    dq_sc[...] = jnp.zeros(dq_sc.shape, F32)
    own = pl.ds(pl.multiple_of(i * BLOCK, BLOCK), BLOCK)
    seg_q = segr[0:1, own]
    row = lax.broadcasted_iota(jnp.int32, (8, WIDE), 0)
    lane = lax.broadcasted_iota(jnp.int32, (8, WIDE), 1) // HEAD
    pick = jnp.where(row == lane, 1.0, 0.0).astype(F32)
    delta = lax.dot_general(
        pick, dz.astype(F32) * full[...], (((1,), (1,)), ((), ())), preferred_element_type=F32, precision=lax.Precision.HIGHEST
    )

    def of(h):
        return slice(h * BLOCK, (h + 1) * BLOCK)

    def step(j, _):
        at = pl.ds(pl.multiple_of(start + j * CHUNK, 128), CHUNK)
        s = nt(k[at, :], qc_sc[...])
        dp = nt(v[at, :], dc_sc[...])
        keep = segc[at, :] == seg_q
        for h in range(heads):
            mine = slice(h * HEAD, (h + 1) * HEAD)
            p = jnp.exp(jnp.where(keep, s[:, of(h)], NEG) - lse[h : h + 1, :])
            ds = (p * (dp[:, of(h)] - delta[h : h + 1, :])).astype(BF)
            dq_sc[mine, :] += nn(kt[mine, at], ds)
            dv_sc[mine, at] += nt(dt_sc[mine, :], p.astype(BF))
            dk_sc[mine, at] += nt(qt[mine, :], ds)
        return 0

    def pair(j, _):
        step(2 * j, 0)
        step(2 * j + 1, 0)
        return 0

    lax.fori_loop(0, count // 2, pair, 0)

    @pl.when(count % 2 == 1)
    def _():
        step(count - 1, 0)

    qs_sc[:, own] = dq_sc[...]


def attention_backward(place, q, qt, k, kt, v, do, full, lse, segc, segr, cos, sin, heads):
    length = k.shape[0]
    blocks = length // BLOCK
    first = lambda i: jnp.minimum(i, blocks - 1)
    second = lambda i: jnp.maximum(i - blocks, 0)
    return pl.pallas_call(
        partial(backward_kernel, heads),
        grid_spec=pltpu.PrefetchScalarGridSpec(
            num_scalar_prefetch=1,
            grid=(2 * blocks,),
            in_specs=[
                pl.BlockSpec((BLOCK, WIDE), lambda i, s: (first(i) ^ s[0], 0)),
                pl.BlockSpec((WIDE, BLOCK), lambda i, s: (0, first(i) ^ s[0])),
                whole_block(k.shape),
                whole_block(kt.shape),
                whole_block(v.shape),
                *[whole_block(d.shape) for d in do],
                pl.BlockSpec((BLOCK, WIDE), lambda i, s: (first(i), 0)),
                pl.BlockSpec((8, BLOCK), lambda i, s: (0, first(i))),
                whole_block(segc.shape),
                whole_block(segr.shape),
                pl.BlockSpec((BLOCK, 128), lambda i, s: (second(i), 0)),
                pl.BlockSpec((BLOCK, 128), lambda i, s: (second(i), 0)),
            ],
            out_specs=[pl.BlockSpec((BLOCK, 3 * WIDE), lambda i, s: (second(i), 0)), whole_block((8, 3 * WIDE))],
            scratch_shapes=[pltpu.VMEM((WIDE, length), F32)] * 2
            + [pltpu.VMEM((heads * BLOCK, WIDE), BF)] * 2
            + [pltpu.VMEM((WIDE, BLOCK), F32), pltpu.VMEM((BLOCK, WIDE), BF), pltpu.VMEM((WIDE, BLOCK), BF)]
            + [pltpu.VMEM((WIDE, length), F32)],
        ),
        out_shape=[jax.ShapeDtypeStruct((length, 3 * WIDE), BF), jax.ShapeDtypeStruct((8, 3 * WIDE), F32)],
        compiler_params=params(28),
        cost_estimate=COST,
        name="attention_backward",
    )(place, q, qt, k, kt, v, *do, full, lse, segc, segr, cos, sin)


def out_copies(place, gathered, w_out, sems):
    here = place[place.shape[0] - 1]
    feed = gathered.shape[2] - w_out.shape[2]
    return [pltpu.make_async_copy(gathered.at[here ^ k, :, feed:], w_out.at[k], sems.at[k]) for k in range(4)]


def row_mean(x):
    return jnp.mean(x, axis=1, keepdims=True)


def gelu_parts(x):
    e = jnp.exp2(x * x * (-0.5 * 1.4426950408889634))
    t = 1.0 / (1.0 + (0.3275911 * 0.7071067811865476) * jnp.abs(x))
    p = t * (0.127414796 + t * (-0.142248368 + t * (0.7107068705 + t * (-0.7265760135 + t * 0.5307027145))))
    tail = p * e
    phi = jnp.where(x >= 0, 1.0 - tail, tail)
    return phi, phi + x * e * 0.3989422804014327


ROWS = 512


def feed_kernel(place, gathered, w, c0, c1, c2, c3, tokb, gtop, vec, bias, *refs):
    (out_o, gs_o, gsb_o, fs_o, nbt_o, gst_o, act_o, gp_o, root_o, sum_o, nb_o, w_out, acc, normed, sems) = refs
    copies = out_copies(place, gathered, w_out, sems)
    k = pl.program_id(0)
    share = tokb.shape[0]
    part = c0.shape[1]
    chunks = [pl.ds(r * ROWS, ROWS) for r in range(share // ROWS)]

    @pl.when(k == 0)
    def _():
        for copy in copies:
            copy.start()
        for copy in copies:
            copy.wait()
        for sl in chunks:
            x = tokb[sl, :].astype(F32) + vec[4:5, :]
            for n, ctx in enumerate((c0, c1, c2, c3)):
                x = x + nt(ctx[sl, :], w_out[n, :, 0:part])
            x = x - row_mean(x)
            root = lax.rsqrt(row_mean(x * x) + EPSILON)
            x = x * root
            fs_o[sl, :] = x
            root_o[sl, :] = jnp.broadcast_to(root, (ROWS, 128))
            y = x * vec[0:1, :] + vec[2:3, :]
            normed[sl, :] = y
            nb_o[sl, :] = y.astype(BF)
            nbt_o[:, sl] = y.astype(BF).T
            acc[sl, :] = y + vec[5:6, :]

    hidden = act_o.shape[2]

    def rows_step(r, _):
        sl = pl.ds(pl.multiple_of(r * ROWS, ROWS), ROWS)
        h = nn(nb_o[sl, :], w[0, :, 0:hidden]) + bias[pl.ds(k, 1), :]
        phi, slope = gelu_parts(h)
        a = (h * phi).astype(BF)
        act_o[0, sl, :] = a
        gp_o[0, sl, :] = slope
        acc[sl, :] += nt(a, w[0, :, hidden:])
        return 0

    lax.fori_loop(0, share // ROWS, rows_step, 0, unroll=True)

    @pl.when(k == 3)
    def _():
        total = [jnp.zeros((1, tokb.shape[1]), F32)] * 3
        for sl in chunks:
            x = acc[sl, :]
            x = x - row_mean(x)
            root = lax.rsqrt(row_mean(x * x) + EPSILON)
            x = x * root
            out_o[sl, :] = (x * vec[1:2, :] + vec[3:4, :]).astype(BF)
            g = gtop[sl, :].astype(F32)
            gg = g * vec[1:2, :]
            gs = root * (gg - row_mean(gg) - x * row_mean(gg * x))
            gs_o[sl, :] = gs
            gsb_o[sl, :] = gs.astype(BF)
            gst_o[:, sl] = gs.astype(BF).T
            for n, y in enumerate((g * x, g, gs)):
                total[n] = total[n] + jnp.sum(y, axis=0, keepdims=True)
        sum_o[...] = jnp.concatenate(total + [jnp.zeros((5, tokb.shape[1]), F32)], axis=0)


def feed_specs(place, gathered, hidden):
    width, last = gathered.shape[1], place.shape[0] - 1
    return [pl.BlockSpec(memory_space=pl.ANY), pl.BlockSpec((1, width, 2 * hidden), lambda i, s: (s[last] ^ i, 0, 0))]


def feed_forward(place, gathered, contexts, tokb, gtop, vec, bias):
    share, width = tokb.shape
    hidden = bias.shape[1]
    block = lambda: pl.BlockSpec((1, share, hidden), lambda i, s: (i, 0, 0))
    sd, far = jax.ShapeDtypeStruct, pltpu.HBM
    return pl.pallas_call(
        feed_kernel,
        grid_spec=pltpu.PrefetchScalarGridSpec(
            num_scalar_prefetch=1,
            grid=(4,),
            in_specs=feed_specs(place, gathered, hidden) + [whole_block(x.shape) for x in (*contexts, tokb, gtop, vec, bias)],
            out_specs=[whole_block((share, width))] * 4
            + [whole_block((width, share))] * 2
            + [block(), block(), whole_block((share, 128)), whole_block((8, width))],
            scratch_shapes=[
                pltpu.VMEM((share, width), BF),
                pltpu.VMEM((4, width, gathered.shape[2] - 2 * hidden), BF),
                pltpu.VMEM((share, width), F32),
                pltpu.VMEM((share, width), F32),
                pltpu.SemaphoreType.DMA((4,)),
            ],
        ),
        out_shape=[
            sd((share, width), BF),
            sd((share, width), F32),
            sd((share, width), BF),
            sd((share, width), F32),
            far((width, share), BF),
            far((width, share), BF),
            far((4, share, hidden), BF),
            far((4, share, hidden), F32),
            sd((share, 128), F32),
            sd((8, width), F32),
        ],
        compiler_params=params(54),
        cost_estimate=COST,
        name="feed_forward",
    )(place, gathered, gathered, *contexts, tokb, gtop, vec, bias)


def feed_back_kernel(place, gathered, w, gs, gsb, fs, gp, root, vec, *refs):
    (gf_o, gft_o, gc0, gc1, gc2, gc3, gh_o, ghs_o, sum_o, w_out, acc, sems) = refs
    copies = out_copies(place, gathered, w_out, sems)
    k = pl.program_id(0)
    share, width = gs.shape
    hidden, part = gh_o.shape[2], gc0.shape[1]

    @pl.when(k == 0)
    def _():
        for copy in copies:
            copy.start()
        acc[...] = gs[...]

    def rows_step(r, total):
        sl = pl.ds(pl.multiple_of(r * ROWS, ROWS), ROWS)
        g = (nn(gsb[sl, :], w[0, :, hidden:]) * gp[0, sl, :]).astype(BF)
        gh_o[0, sl, :] = g
        acc[sl, :] += nt(g, w[0, :, 0:hidden])
        return total + jnp.sum(g.astype(F32), axis=0, keepdims=True)

    total = lax.fori_loop(0, share // ROWS, rows_step, jnp.zeros((1, hidden), F32), unroll=True)
    ghs_o[0] = jnp.broadcast_to(total, (8, hidden))

    @pl.when(k == 3)
    def _():
        for copy in copies:
            copy.wait()
        sums = [jnp.zeros((1, width), F32)] * 3
        for r in range(share // ROWS):
            sl = pl.ds(r * ROWS, ROWS)
            gn = acc[sl, :]
            x = fs[sl, :]
            gg = gn * vec[0:1, :]
            gf = root[sl, 0:1] * (gg - row_mean(gg) - x * row_mean(gg * x))
            gf_o[sl, :] = gf
            b = gf.astype(BF)
            gft_o[:, sl] = b.T
            for n, o in enumerate((gc0, gc1, gc2, gc3)):
                o[sl, :] = nn(b, w_out[n, :, 0:part]).astype(BF)
            for n, y in enumerate((gn * x, gn, gf)):
                sums[n] = sums[n] + jnp.sum(y, axis=0, keepdims=True)
        sum_o[...] = jnp.concatenate(sums + [jnp.zeros((5, width), F32)], axis=0)


def feed_back(place, gathered, gs, gsb, fs, gp, root, vec, part):
    share, width = gs.shape
    hidden = gp.shape[2]
    block = lambda: pl.BlockSpec((1, share, hidden), lambda i, s: (i, 0, 0))
    sd, far = jax.ShapeDtypeStruct, pltpu.HBM
    return pl.pallas_call(
        feed_back_kernel,
        grid_spec=pltpu.PrefetchScalarGridSpec(
            num_scalar_prefetch=1,
            grid=(4,),
            in_specs=feed_specs(place, gathered, hidden)
            + [whole_block(gs.shape), whole_block(gsb.shape), whole_block(fs.shape), block(), whole_block(root.shape), whole_block(vec.shape)],
            out_specs=[whole_block((share, width)), whole_block((width, share))]
            + [whole_block((share, part))] * 4
            + [block(), pl.BlockSpec((1, 8, hidden), lambda i, s: (i, 0, 0)), whole_block((8, width))],
            scratch_shapes=[
                pltpu.VMEM((4, width, gathered.shape[2] - 2 * hidden), BF),
                pltpu.VMEM((share, width), F32),
                pltpu.SemaphoreType.DMA((4,)),
            ],
        ),
        out_shape=[far((share, width), F32), far((width, share), BF)]
        + [sd((share, part), BF)] * 4
        + [far((4, share, hidden), BF), sd((4, 8, hidden), F32), sd((8, width), F32)],
        compiler_params=params(54),
        cost_estimate=COST,
        name="feed_back",
    )(place, gathered, gathered, gs, gsb, fs, gp, root, vec)


def split_rows(place, per, acc, source, near_o, far_o, lead, cols):
    if per == 1:
        near_o[(*lead, slice(None), cols)] = acc[:, source].astype(near_o.dtype)
        return
    rows = acc.shape[0] // per
    for n in range(per // 2):
        near, far = (pl.ds(pl.multiple_of(place[m], 16), rows) for m in (n, per // 2 + n))
        near_o[(*lead, n, slice(None), cols)] = acc[near, source].astype(near_o.dtype)
        far_o[(*lead, n, slice(None), cols)] = acc[far, source].astype(BF)


def weights_kernel(per, place, nbt, gst, gft, ctx, gh, act, *refs):
    hh = gh.shape[2] // 2
    if per > 1:
        near_o, far_o, out, acc = refs
    else:
        other, out = refs
    for n, (left, right) in enumerate(((nbt, gh), (gst, act))):
        made = nn(left[...], right[0])
        out[0, :, n * hh : (n + 1) * hh] = made[:, 0:hh].astype(BF)
        if per > 1:
            acc[...] = made[:, hh:]
            split_rows(place, per, acc, slice(None), near_o, far_o, (0,), slice(n * hh, (n + 1) * hh))
        else:
            other[0, :, n * hh : (n + 1) * hh] = made[:, hh:].astype(BF)
    out[0, :, 2 * hh :] = nn(gft[...], ctx[0]).astype(BF)


def weight_grads(place, per, nbt, gst, gft, contexts, gh, act):
    width, share = nbt.shape
    hidden, part = gh.shape[2], contexts.shape[2]
    last = place.shape[0] - 1
    block = lambda cols: pl.BlockSpec((1, share, cols), lambda i, s: (i, 0, 0))
    ordered = lambda cols: pl.BlockSpec((1, width, cols), lambda i, s: (i ^ s[last], 0, 0))
    if per > 1:
        shape = (4, per // 2, width // per, hidden)
        outs = [jax.ShapeDtypeStruct(shape, BF)] * 2
        specs = [pl.BlockSpec((1,) + shape[1:], lambda i, s: (i, 0, 0, 0))] * 2
        scratch = [pltpu.VMEM((width, hidden // 2), F32)]
    else:
        outs = [jax.ShapeDtypeStruct((4, width, hidden), BF)]
        specs = [ordered(hidden)]
        scratch = []
    return pl.pallas_call(
        partial(weights_kernel, per),
        grid_spec=pltpu.PrefetchScalarGridSpec(
            num_scalar_prefetch=1,
            grid=(4,),
            in_specs=[whole_block(x.shape) for x in (nbt, gst, gft)] + [block(part), block(hidden), block(hidden)],
            out_specs=specs + [ordered(hidden + part)],
            scratch_shapes=scratch,
        ),
        out_shape=outs + [jax.ShapeDtypeStruct((4, width, hidden + part), BF)],
        compiler_params=params(58),
        cost_estimate=COST,
        name="weight_grads",
    )(place, nbt, gst, gft, contexts, gh, act)


def qkv_weights_kernel(per, part, place, own, other, g, *refs):
    near_o, far_o = refs[:2] if per > 1 else (refs[0], None)
    acc = refs[-1]
    half_len = other.shape[0]
    core = place[per]
    rows = 512

    acc[...] = jnp.zeros(acc.shape, F32)

    def step(r, _):
        at = pl.ds(pl.multiple_of(r * rows, rows), rows)
        a = g[pl.ds(pl.multiple_of(core * half_len + r * rows, rows), rows), :]
        b = g[pl.ds(pl.multiple_of((1 - core) * half_len + r * rows, rows), rows), :]
        acc[...] += nn(own[0, at, :].T, a) + nn(other[at, :].T, b)
        return 0

    lax.fori_loop(0, half_len // rows, step, 0)
    for m in range(3):
        split_rows(place, per, acc, slice(m * WIDE, m * WIDE + part), near_o, far_o, (), slice(m * part, (m + 1) * part))


def qkv_weight_grads(place, per, tokens, other, g, part):
    half_len, width = other.shape
    if per > 1:
        shape = (per // 2, width // per, 3 * part)
        outs = [jax.ShapeDtypeStruct(shape, F32), jax.ShapeDtypeStruct(shape, BF)]
    else:
        outs = [jax.ShapeDtypeStruct((width, 3 * part), F32)]
    return pl.pallas_call(
        partial(qkv_weights_kernel, per, part),
        grid_spec=pltpu.PrefetchScalarGridSpec(
            num_scalar_prefetch=1,
            grid=(1,),
            in_specs=[pl.BlockSpec((1, half_len, width), lambda i, s: (s[per], 0, 0)), whole_block(other.shape), whole_block(g.shape)],
            out_specs=[whole_block(o.shape) for o in outs],
            scratch_shapes=[pltpu.VMEM((width, 3 * WIDE), F32)],
        ),
        out_shape=outs,
        compiler_params=params(32),
        cost_estimate=COST,
        name="qkv_weight_grads",
    )(place, tokens, other, g)


def branch_kernel(place, *refs):
    count = (len(refs) - 1) // 2
    w = refs[count]
    for g, o in zip(refs[:count], refs[count + 1 :]):
        rows = 256
        for r in range(g.shape[0] // rows):
            sl = slice(r * rows, (r + 1) * rows)
            o[sl, :] = nt(g[sl, :], w[...]).astype(o.dtype)


def branch(place, blocks, kinds, g, w):
    share, last = g.shape[0] // 4, place.shape[0] - 1
    return pl.pallas_call(
        branch_kernel,
        grid_spec=pltpu.PrefetchScalarGridSpec(
            num_scalar_prefetch=1,
            grid=(1,),
            in_specs=[pl.BlockSpec((share, g.shape[1]), lambda i, s, k=k: (s[last] ^ k, 0)) for k in blocks] + [whole_block(w.shape)],
            out_specs=[whole_block((share, w.shape[0]))] * len(blocks),
        ),
        out_shape=[jax.ShapeDtypeStruct((share, w.shape[0]), kind) for kind in kinds],
        compiler_params=params(24),
        cost_estimate=COST,
        name="branch",
    )(place, *[g] * len(blocks), w)


def pick_kernel(place, near, *refs):
    far, (keep, send) = refs[:-2], refs[-2:]
    last = place.shape[0] - 1
    mine = place[last] // 2 == place[last - 1]

    def put(out, parts):
        rows = out.shape[0] // len(parts)
        for n, x in enumerate(parts):
            out[n * rows : (n + 1) * rows, :] = x[...]

    @pl.when(mine)
    def _():
        put(keep, [near])
        put(send, far)

    @pl.when(jnp.logical_not(mine))
    def _():
        put(keep, far)
        put(send, [near])


def pick(place, near, *far):
    return pl.pallas_call(
        pick_kernel,
        grid_spec=pltpu.PrefetchScalarGridSpec(
            num_scalar_prefetch=1,
            grid=(1,),
            in_specs=[whole_block(x.shape) for x in (near, *far)],
            out_specs=[whole_block(near.shape)] * 2,
        ),
        out_shape=[jax.ShapeDtypeStruct(near.shape, near.dtype)] * 2,
        compiler_params=params(8),
        cost_estimate=COST,
        name="pick",
    )(place, near, *far)


def join_kernel(second, place, *refs):
    last = place.shape[0] - 1
    mine = place[last] // 2 == place[last - 1]
    if second:
        near, *far, other, _, out = refs
    else:
        near, *far, other, out = refs
    here = pl.program_id(0) == place[last - 1]

    def put(parts):
        rows = out.shape[1] // len(parts)
        for n, x in enumerate(parts):
            out[0, n * rows : (n + 1) * rows, :] = x[...]

    @pl.when(jnp.logical_and(here, mine))
    def _():
        put([near])

    @pl.when(jnp.logical_and(here, jnp.logical_not(mine)))
    def _():
        put(far)

    @pl.when(jnp.logical_not(here))
    def _():
        put([other])


def join(place, near, far, other, before=None):
    share, width = near.shape
    second = before is not None
    last = place.shape[0] - 1
    ins = [near, *far, other]
    specs = [whole_block(x.shape) for x in ins]
    if second:
        ins.append(before)
        specs.append(pl.BlockSpec(memory_space=pl.ANY))
    return pl.pallas_call(
        partial(join_kernel, second),
        grid_spec=pltpu.PrefetchScalarGridSpec(
            num_scalar_prefetch=1,
            grid=(2,),
            in_specs=specs,
            out_specs=pl.BlockSpec((1, share, width), lambda i, s: (i, (s[last] + int(second)) % 2, 0)),
        ),
        out_shape=jax.ShapeDtypeStruct((2, 2 * share, width), near.dtype),
        input_output_aliases={len(ins): 0} if second else {},
        compiler_params=params(12),
        cost_estimate=COST,
        name="join",
    )(place, *ins)


def relay_kernel(one, two, low, high, one_o, two_o):
    half = low.shape[0]
    one_o[0:half, :] = (one[0:half, :] + low[...].astype(F32)).astype(BF)
    one_o[half:, :] = one[half:, :].astype(BF)
    two_o[0:half, :] = two[0:half, :].astype(BF)
    two_o[half:, :] = (two[half:, :] + high[...].astype(F32)).astype(BF)


def relay(one, two, low, high):
    return pl.pallas_call(
        relay_kernel,
        in_specs=[pl.BlockSpec(memory_space=pltpu.VMEM)] * 4,
        out_specs=[pl.BlockSpec(memory_space=pltpu.VMEM)] * 2,
        out_shape=[jax.ShapeDtypeStruct(one.shape, BF)] * 2,
        compiler_params=pltpu.CompilerParams(vmem_limit_bytes=16 * 1024 * 1024),
        cost_estimate=COST,
        name="relay",
    )(one, two, low, high)


def collect_kernel(place, hidden_sums, one, two, bias, out):
    here = place[place.shape[0] - 1]
    out[...] = jnp.zeros(out.shape, F32)
    for k in range(4):
        out[pl.ds(here ^ k, 1), :] = hidden_sums[k, 0:1, :]
    for n, (x, row) in enumerate(((one, 0), (two, 0), (one, 1), (two, 1), (one, 2), (two, 2))):
        out[4 + n : 5 + n, :] = x[row : row + 1, :]
    out[pl.ds(10 + here, 1), :] = bias[0:1, :]


def collect(place, hidden_sums, one, two, bias):
    return pl.pallas_call(
        collect_kernel,
        grid_spec=pltpu.PrefetchScalarGridSpec(
            num_scalar_prefetch=1,
            grid=(1,),
            in_specs=[whole_block(x.shape) for x in (hidden_sums, one, two, bias)],
            out_specs=whole_block((16, one.shape[1])),
        ),
        out_shape=jax.ShapeDtypeStruct((16, one.shape[1]), F32),
        compiler_params=params(8),
        cost_estimate=COST,
        name="collect",
    )(place, hidden_sums, one, two, bias)


def settle_kernel(count, *refs):
    ins, outs = refs[:count], refs[count:]
    for j, out in enumerate(outs):
        total = ins[0][j].astype(F32)
        for x in ins[1:]:
            total = total + x[j].astype(F32)
        out[...] = total.astype(out.dtype)


def settle(*stacks):
    shape = stacks[0].shape
    vmem = pl.BlockSpec(memory_space=pltpu.VMEM)
    return pl.pallas_call(
        partial(settle_kernel, len(stacks)),
        in_specs=[vmem] * len(stacks),
        out_specs=[vmem] * shape[0],
        out_shape=[jax.ShapeDtypeStruct(shape[1:], F32 if j == 0 else BF) for j in range(shape[0])],
        compiler_params=pltpu.CompilerParams(vmem_limit_bytes=16 * 1024 * 1024),
        cost_estimate=COST,
        name="settle",
    )(*stacks)


def finish_kernel(parts, *refs):
    out = refs[-1]
    total = refs[0][...]
    for x in refs[1:-1]:
        total = total + x[...].astype(F32)
    if parts == 1:
        out[...] = total
    else:
        cols = total.shape[1] // parts
        for m in range(parts):
            out[:, m, :] = total[:, m * cols : (m + 1) * cols]


def finish(parts, *pieces):
    vmem = pl.BlockSpec(memory_space=pltpu.VMEM)
    rows, cols = pieces[0].shape
    return pl.pallas_call(
        partial(finish_kernel, parts),
        in_specs=[vmem] * len(pieces),
        out_specs=vmem,
        out_shape=jax.ShapeDtypeStruct((rows, cols) if parts == 1 else (rows, parts, cols // parts), F32),
        compiler_params=pltpu.CompilerParams(vmem_limit_bytes=8 * 1024 * 1024),
        cost_estimate=COST,
        name="finish",
    )(*pieces)


def place_kernel(whole, rest, feed_o, out_o):
    hh = rest.shape[1] // 2
    for m in range(2):
        feed_o[:, m, 0:hh] = whole[:, m * hh : (m + 1) * hh].astype(F32)
        feed_o[:, m, hh:] = rest[:, m * hh : (m + 1) * hh]
    out_o[...] = whole[:, 2 * hh :].astype(F32)


def place_feed(whole, rest):
    vmem = pl.BlockSpec(memory_space=pltpu.VMEM)
    rows, cols = rest.shape
    return pl.pallas_call(
        place_kernel,
        in_specs=[vmem] * 2,
        out_specs=[vmem] * 2,
        out_shape=[jax.ShapeDtypeStruct((rows, 2, cols), F32), jax.ShapeDtypeStruct((rows, whole.shape[1] - cols), F32)],
        compiler_params=pltpu.CompilerParams(vmem_limit_bytes=8 * 1024 * 1024),
        cost_estimate=COST,
        name="place_feed",
    )(whole, rest)


def block_kernel(own, first, one, two, out):
    out[...] = (own[...] + first[...] + one[...].astype(F32) + two[...].astype(F32)).astype(BF)


def add_block(own, first, one, two):
    vmem = pl.BlockSpec(memory_space=pltpu.VMEM)
    return pl.pallas_call(
        block_kernel,
        in_specs=[vmem] * 4,
        out_specs=vmem,
        out_shape=jax.ShapeDtypeStruct(own.shape, BF),
        compiler_params=pltpu.CompilerParams(vmem_limit_bytes=12 * 1024 * 1024),
        cost_estimate=COST,
        name="add_block",
    )(own, first, one, two)


def relay_kernel(one, two, low, high, one_o, two_o):
    half = low.shape[0]
    one_o[0:half, :] = (one[0:half, :] + low[...].astype(F32)).astype(BF)
    one_o[half:, :] = one[half:, :].astype(BF)
    two_o[0:half, :] = two[0:half, :].astype(BF)
    two_o[half:, :] = (two[half:, :] + high[...].astype(F32)).astype(BF)


def relay(one, two, low, high):
    return pl.pallas_call(
        relay_kernel,
        in_specs=[pl.BlockSpec(memory_space=pltpu.VMEM)] * 4,
        out_specs=[pl.BlockSpec(memory_space=pltpu.VMEM)] * 2,
        out_shape=[jax.ShapeDtypeStruct(one.shape, BF)] * 2,
        compiler_params=pltpu.CompilerParams(vmem_limit_bytes=16 * 1024 * 1024),
        cost_estimate=COST,
        name="relay",
    )(one, two, low, high)


def rotation_tables(offsets):
    lane = np.arange(128)
    frequency = (10000.0 ** (-2.0 * (lane % HEAD // 2) / HEAD)).astype(np.float32)
    angles = offsets.astype(F32)[:, None] * frequency[None, :]
    sign = np.where(lane % 2 == 0, -1.0, 1.0).astype(np.float32)
    return jnp.cos(angles), jnp.sin(angles) * sign


def key_bounds(segment):
    length = segment.shape[0]
    first, last = segment[::BLOCK], segment[BLOCK - 1 :: BLOCK]
    low = jnp.sum(segment[None, :] < first[:, None], axis=1)
    high = jnp.sum(segment[None, :] <= last[:, None], axis=1)
    low = low // 128 * 128
    count = (high - low + CHUNK - 1) // CHUNK
    return jnp.stack([jnp.minimum(low, length - CHUNK * count), count], axis=1).reshape(-1).astype(jnp.int32)


def swap_ctx(x):
    return lax.ppermute(x, "ctx", [(0, 1), (1, 0)])


def swap_tp(x, k):
    return lax.ppermute(x, "tp", [(i, i ^ k) for i in range(4)])


def swap_shard(x, k):
    return lax.ppermute(x, "shard", [(i, i ^ k) for i in range(4)])


def order_four(parts, index):
    a, b, c, d = parts
    odd, high = index % 2 == 1, index // 2 == 1
    a, b = jnp.where(odd, b, a), jnp.where(odd, a, b)
    c, d = jnp.where(odd, d, c), jnp.where(odd, c, d)
    return jnp.stack([jnp.where(high, c, a), jnp.where(high, d, b), jnp.where(high, a, c), jnp.where(high, b, d)])


def after(x, *others):
    return lax.optimization_barrier((x, others))[0]


def gather_tp(x, half):
    one, two = swap_tp(x, 1), swap_tp(x, 2)
    three = jnp.concatenate([swap_tp(one[:half], 2), swap_tp(two[half:], 1)])
    return [x, one, two, three]


def scatter_tp(parts):
    own, one, two, three = parts
    half = own.shape[0] // 2
    low, high = three[:half].astype(BF), three[half:].astype(BF)
    low, high = swap_tp(low, 2), swap_tp(high, 1)
    one = jnp.concatenate([one[:half] + low.astype(F32), one[half:]]).astype(BF)
    two = jnp.concatenate([two[:half], two[half:] + high.astype(F32)]).astype(BF)
    return own + swap_tp(one, 1).astype(F32) + swap_tp(two, 2).astype(F32)


def three_rows(x):
    high = lax.reduce_precision(x, 8, 7)
    middle = lax.reduce_precision(x - high, 8, 7)
    return jnp.stack([high, middle, x - high - middle]).astype(BF)


def contract_last(left, right):
    return lax.dot_general(left, right, (((1,), (1,)), ((), ())), preferred_element_type=F32)


def body(tokens, segment_ids, offsets, qkv_weight, out_weight, ffn_weight, qkv_bias, ffn_bias, norm_gain, shift_params, out_grad):
    t, c, z = lax.axis_index("tp"), lax.axis_index("ctx"), lax.axis_index("shard")
    shards = lax.axis_size("shard")
    half_len, width = tokens.shape[1:]
    rows, _, part = qkv_weight.shape
    hidden = ffn_weight.shape[2]
    heads = part // HEAD
    length = 2 * half_len
    share = length // 4
    first_core = c == 0
    direct = shards == 4

    def take(x, index):
        return lax.dynamic_index_in_dim(x, index, 0, keepdims=False)

    def by_core(own, other):
        return jnp.where(first_core, jnp.stack([own, other]), jnp.stack([other, own]))

    hh = hidden // 2
    gathered = jnp.concatenate([ffn_weight.reshape(rows, 2 * hidden), out_weight], axis=1)
    gathered = lax.all_gather(gathered, ("tp", "shard", "ctx"), axis=0, tiled=True).reshape(4, width, 2 * hidden + part)
    bias_all = ffn_bias.reshape(1, hidden)
    bias_all = jnp.concatenate([bias_all] + [swap_tp(bias_all, k) for k in (1, 2, 3)])
    qkv_rows = qkv_weight.reshape(rows, 3 * part)
    other_tokens = swap_ctx(take(tokens, 1 - c))
    if direct:
        places = [((z ^ j) * 2 + (c ^ f)) * rows for f in (0, 1) for j in range(4)]
        near = [qkv_rows] + [swap_shard(qkv_rows, j) for j in (1, 2, 3)]
        qkv_pieces = [*near, swap_ctx(jnp.stack(near))]
    else:
        places = [jnp.zeros_like(c)]
        qkv_pieces = [lax.all_gather(qkv_rows, ("shard", "ctx"), axis=0, tiled=True)]
    per = len(places)
    place = jnp.stack(places + [c, t]).astype(jnp.int32)
    bias_pad = jnp.pad(qkv_bias, ((0, 0), (0, WIDE - part)))
    vec = jnp.concatenate([norm_gain, shift_params, jnp.zeros((2, width), F32)])

    marks = jnp.stack([segment_ids, offsets])
    marks = by_core(take(marks.swapaxes(0, 1), c), swap_ctx(take(marks.swapaxes(0, 1), 1 - c)))
    segment, places = marks[:, 0].reshape(length), marks[:, 1].reshape(length)
    halves = lambda x: x.reshape(2, 2, share, width)
    here = t // 2 == c
    tok_block = jnp.where(here, take(take(halves(tokens), c), t % 2), take(other_tokens.reshape(2, share, width), t % 2))
    grad_block = halves(out_grad)
    grad_far = swap_ctx(take(take(grad_block, 1 - c), t % 2))
    grad_top = jnp.where(here, take(take(grad_block, c), t % 2), grad_far)

    cosine, sine = rotation_tables(places)
    bounds = key_bounds(segment)
    seg_column = segment[:, None]
    seg_row = jnp.broadcast_to(segment[None, :], (8, length))
    q, k_rows, v_rows, k_turned, q_turned, qkv_wide = project_qkv(place, qkv_pieces, per, bias_pad, tokens, other_tokens, cosine, sine, part)

    contexts, log_totals, fulls = [None] * 4, [None] * 4, [None] * 4

    def forward(j, q):
        spot = jnp.concatenate([((t ^ j) * (share // BLOCK))[None].astype(jnp.int32), bounds])
        context, log_totals[j], fulls[j] = attention_forward(spot, q, k_rows, v_rows, seg_column, seg_row, heads, share)
        contexts[j] = swap_tp(context, j) if j else context

    forward(3, q)
    q_next, log_totals[3] = lax.optimization_barrier((q, log_totals[3]))
    forward(1, q_next)
    q_next, log_totals[1], contexts[3] = lax.optimization_barrier((q, log_totals[1], contexts[3]))
    forward(2, q_next)
    q_next, log_totals[2], contexts[1] = lax.optimization_barrier((q, log_totals[2], contexts[1]))
    forward(0, q_next)
    stacked = jnp.stack(contexts)
    tok_block, log_total, full, stacked = lax.optimization_barrier(
        (tok_block, jnp.concatenate(log_totals, axis=1), jnp.concatenate(fulls), stacked)
    )

    layer_out, grad_second, grad_second_b, first_scaled, normed_t, second_t, activated, slope, root, sums_two = feed_forward(
        place, gathered, contexts, tok_block, grad_top, vec, bias_all
    )

    barrier = lax.optimization_barrier
    out_blocks = [layer_out, swap_tp(layer_out, 1), swap_tp(layer_out, 2)]

    grad_first, first_t, g0, g1, g2, g3, grad_hidden, hidden_sums, sums_one = feed_back(
        place, gathered, grad_second, grad_second_b, first_scaled, slope, root, vec, part
    )
    heads_grads = [g0, swap_tp(g1, 1), swap_tp(g2, 2), swap_tp(g3, 3)]

    *made, whole = weight_grads(place, per, normed_t, second_t, first_t, stacked, grad_hidden, activated)
    made, whole, heads_grads, out_blocks = barrier((made, whole, heads_grads, out_blocks))
    whole = lax.psum_scatter(whole.reshape(-1, 2 * hh + part), ("tp", "shard", "ctx"), scatter_dimension=0, tiled=True)
    grad_heads = heads_grads
    corner = [out_blocks[1][: share // 2], out_blocks[2][share // 2 :]]
    if direct:
        got = swap_ctx(made[1])
        grad_heads, got, corner = barrier((grad_heads, got, corner))
        packs = [made[0][k].astype(F32) + got[k].astype(F32) for k in range(4)]
        sent = [packs[k].astype(BF) for k in (1, 2, 3)]
        grad_heads, sent = barrier((grad_heads, sent))
        sent = [swap_tp(sent[k - 1], k) for k in (1, 2, 3)]
    corner = [swap_tp(corner[0], 2), swap_tp(corner[1], 1)]

    spot = jnp.concatenate([(t * (share // BLOCK))[None].astype(jnp.int32), bounds])
    grad_proj, bias_sums = attention_backward(
        spot, q, q_turned, k_rows, k_turned, v_rows, grad_heads, full, log_total, seg_column, seg_row, cosine, sine, heads
    )
    grad_proj, bias_sums, hidden_sums, sums_one, sums_two, out_blocks = barrier(
        (grad_proj, bias_sums, hidden_sums, sums_one, sums_two, out_blocks)
    )
    if direct:
        grad_proj, sent, packs[0] = barrier((grad_proj, sent, packs[0]))

    three = branch(place, (3,), (BF,), grad_proj, qkv_wide)[0]
    three, grad_proj, corner, bias_sums, out_blocks = barrier((three, grad_proj, corner, bias_sums, out_blocks))
    low, high = swap_tp(three[: share // 2], 2), swap_tp(three[share // 2 :], 1)
    one, two, own = branch(place, (1, 2, 0), (F32, F32, F32), grad_proj, qkv_wide)
    grads = qkv_weight_grads(place, per, tokens, other_tokens, grad_proj, part)
    keep_a, send_a = pick(place, out_blocks[0], out_blocks[2])
    keep_b, send_b = pick(place, out_blocks[1], *corner)
    small = collect(place, hidden_sums, sums_one, sums_two, bias_sums)
    outs = [swap_ctx(send_a), swap_ctx(send_b)]
    if direct:
        small = small + swap_ctx(small)
        small = small + swap_shard(small, 1)
    if direct:
        qkv_sum, *qkv_pieces = settle(grads[0], swap_ctx(grads[1]))
        qkv_sum, qkv_pieces, low = barrier((qkv_sum, qkv_pieces, low))
    low, high, one, two, own, outs, small = barrier((low, high, one, two, own, outs, small))

    def send_shards(pieces, small, k):
        moved = [swap_shard(pieces[j - 1], j) for j in (1, 2, 3)]
        moved[0], small = barrier((moved[0], small))
        return moved, small + swap_tp(small, k)

    one, two = relay(one, two, low, high)
    one, two, outs, small = barrier((one, two, outs, small))
    one, two = swap_tp(one, 1), swap_tp(two, 2)
    outputs = join(place, out_blocks[0], [out_blocks[2]], outs[0])
    outputs = join(place, out_blocks[1], corner, outs[1], outputs)
    if direct:
        moved, small = send_shards(qkv_pieces, small, 1)
        qkv_total = finish(3, qkv_sum, *moved)
        summed, *pieces = settle(packs[0], *sent)
        one, two, own, small, outputs, summed, pieces, qkv_total = barrier((one, two, own, small, outputs, summed, pieces, qkv_total))
    else:
        one, two, own, small, outputs = barrier((one, two, own, small, outputs))

    block = add_block(own, grad_first, one, two)
    ready = [block, swap_tp(block, 1), swap_tp(block, 2)]
    if direct:
        moved, small = send_shards(pieces, small, 2)
        total = finish(1, summed, *moved)
        ready, total, small = barrier((ready, total, small))
    else:
        qkv_total = lax.psum_scatter(grads[0], ("shard", "ctx"), scatter_dimension=0, tiled=True).reshape(rows, 3, part)
        total = lax.psum_scatter(made[0].reshape(-1, 2 * hh), ("tp", "shard", "ctx"), scatter_dimension=0, tiled=True).astype(F32)
    corner = [swap_tp(ready[1][: share // 2], 2), swap_tp(ready[2][share // 2 :], 1)]
    _, send_a = pick(place, ready[0], ready[2])
    grad_tokens = join(place, ready[0], [ready[2]], swap_ctx(send_a))
    grad_ffn_weight, grad_out_weight = place_feed(whole, total)
    if direct:
        small, grad_tokens = barrier((small, grad_tokens))
        small = small + swap_shard(small, 2)
    else:
        small = lax.psum(small, ("shard", "ctx", "tp"))
    corner, small, grad_tokens, qkv_total = barrier((corner, small, grad_tokens, qkv_total))
    send_b = jnp.where(here, jnp.concatenate(corner), ready[1])
    grad_tokens = join(place, ready[1], corner, swap_ctx(send_b), grad_tokens)

    grad_qkv_weight = qkv_total
    grad_ffn_bias = take(small, t)
    vectors = small[4:10]
    grad_qkv_bias = take(small[10:14], t).reshape(3, WIDE)[:, :part]
    return (
        outputs,
        grad_tokens,
        grad_qkv_weight,
        grad_out_weight,
        grad_ffn_weight,
        grad_qkv_bias,
        grad_ffn_bias,
        vectors[:2],
        vectors[2:],
    )


def solution(mesh):
    return jax.shard_map(
        body,
        mesh=mesh,
        in_specs=(
            P("shard", "ctx", None),
            P("shard", "ctx"),
            P("shard", "ctx"),
            P(("shard", "ctx"), None, "tp"),
            P(("shard", "ctx"), "tp"),
            P(("shard", "ctx"), None, "tp"),
            P(None, "tp"),
            P("tp"),
            P(),
            P(),
            P("shard", "ctx", None),
        ),
        out_specs=(
            P("shard", "ctx", None),
            P("shard", "ctx", None),
            P(("shard", "ctx"), None, "tp"),
            P(("shard", "ctx"), "tp"),
            P(("shard", "ctx"), None, "tp"),
            P(None, "tp"),
            P("tp"),
            P(),
            P(),
        ),
        check_vma=False,
    )
```

```python
from functools import partial

import jax
import jax.numpy as jnp
import numpy as np
from jax import lax
from jax.experimental import pallas as pl
from jax.experimental.pallas import tpu as pltpu
from jax.sharding import PartitionSpec as P

HEAD = 64
WIDE = 256
BLOCK = 256
CHUNK = 256
EPSILON = 1e-12
F32 = jnp.float32
BF = jnp.bfloat16
NEG = -1e30
COST = pl.CostEstimate(flops=0, bytes_accessed=0, transcendentals=0)


def swap_pairs(x):
    lane = lax.broadcasted_iota(jnp.int32, x.shape, 1)
    n = x.shape[1]
    return jnp.where(lane % 2 == 0, pltpu.roll(x, n - 1, 1), pltpu.roll(x, 1, 1))


def nt(a, b):
    return lax.dot_general(a, b, (((1,), (1,)), ((), ())), preferred_element_type=F32)


def nn(a, b):
    return lax.dot_general(a, b, (((1,), (0,)), ((), ())), preferred_element_type=F32)


def twice(x):
    return jnp.concatenate([x, x], axis=1)


def lanes_of_heads(x, heads):
    lane = lax.broadcasted_iota(jnp.int32, x.shape, 1) // HEAD
    return [jnp.where(lane == h, x, jnp.zeros_like(x)) for h in range(heads)]


def whole_block(shape, buffers=1):
    return pl.BlockSpec(shape, lambda *_: (0,) * len(shape), pipeline_mode=pl.Buffered(buffers))


def smem():
    return pl.BlockSpec(memory_space=pltpu.SMEM)


def params(mib):
    return pltpu.CompilerParams(dimension_semantics=("arbitrary",), vmem_limit_bytes=mib * 1024 * 1024)


def qkv_kernel(count, per, part, place, *refs):
    pieces = []
    for x in refs[:count]:
        pieces += [x] if len(x.shape) == 2 else [x.at[n] for n in range(x.shape[0])]
    bias, own, other, cos, sin, q_o, k_o, v_o, kt_o, qt_o, w_o = refs[count:]
    piece_rows = pieces[0].shape[0]
    pad = jnp.zeros((piece_rows, WIDE - part), BF)
    for n in range(per):
        sl = pl.ds(pl.multiple_of(place[n], 16), piece_rows)
        for m in range(3):
            w_o[sl, m * WIDE : (m + 1) * WIDE] = jnp.concatenate([pieces[n][:, m * part : (m + 1) * part], pad], axis=1)
    half_len = other.shape[0]

    def run(x, sl):
        c, s = twice(cos[sl, :]), twice(sin[sl, :])
        p = nn(x, w_o[:, 0:WIDE]) + bias[0:1, :]
        q = ((p * c + swap_pairs(p) * s).astype(BF).astype(F32) * (HEAD**-0.5)).astype(BF)
        q_o[sl, :] = q
        qt_o[:, sl] = q.T
        p = nn(x, w_o[:, WIDE : 2 * WIDE]) + bias[1:2, :]
        k = (p * c + swap_pairs(p) * s).astype(BF)
        k_o[sl, :] = k
        kt_o[:, sl] = k.T
        v_o[sl, :] = (nn(x, w_o[:, 2 * WIDE : 3 * WIDE]) + bias[2:3, :]).astype(BF)

    def step(r, _):
        rows = pl.ds(pl.multiple_of(r * BLOCK, BLOCK), BLOCK)
        core = place[per]
        run(own[0, rows, :], pl.ds(pl.multiple_of(core * half_len + r * BLOCK, BLOCK), BLOCK))
        run(other[rows, :], pl.ds(pl.multiple_of((1 - core) * half_len + r * BLOCK, BLOCK), BLOCK))
        return 0

    lax.fori_loop(0, half_len // BLOCK, step, 0)


def project_qkv(place, pieces, per, bias, tokens, other, cos, sin, part):
    half_len, width = other.shape
    length, count = 2 * half_len, len(pieces)
    return pl.pallas_call(
        partial(qkv_kernel, count, per, part),
        grid_spec=pltpu.PrefetchScalarGridSpec(
            num_scalar_prefetch=1,
            grid=(1,),
            in_specs=[whole_block(p.shape) for p in pieces]
            + [whole_block(bias.shape), pl.BlockSpec((1, half_len, width), lambda i, s: (s[per], 0, 0))]
            + [whole_block(x.shape) for x in (other, cos, sin)],
            out_specs=[whole_block((length, WIDE))] * 3 + [whole_block((WIDE, length))] * 2 + [whole_block((width, 3 * WIDE))],
        ),
        out_shape=[jax.ShapeDtypeStruct((length, WIDE), BF)] * 3
        + [jax.ShapeDtypeStruct((WIDE, length), BF)] * 2
        + [jax.ShapeDtypeStruct((width, 3 * WIDE), BF)],
        compiler_params=params(32),
        cost_estimate=COST,
        name="project_qkv",
    )(place, *pieces, bias, tokens, other, cos, sin)


def forward_kernel(heads, place, q, k, v, segc, segr, ctx_o, lse_o, full_o, acc, s_sc, m_sc, l_sc, qc_sc):
    i = place[0] + pl.program_id(0)
    start, count = place[1 + 2 * i], place[2 + 2 * i]
    qc_sc[...] = jnp.concatenate(lanes_of_heads(q[...], heads), axis=0)
    seg_q = segc[...]
    m_sc[...] = jnp.full(m_sc.shape, NEG, F32)
    l_sc[...] = jnp.zeros(l_sc.shape, F32)

    def at(j):
        return pl.ds(pl.multiple_of(start + j * CHUNK, 128), CHUNK)

    def of(h):
        return slice(h * BLOCK, (h + 1) * BLOCK)

    def pass1(j, _):
        s = nt(qc_sc[...], k[at(j), :])
        keep = seg_q == segr[0:1, at(j)]
        for h in range(heads):
            sh = jnp.where(keep, s[of(h), :], NEG)
            s_sc[j, of(h), :] = sh
            m_sc[of(h), :] = jnp.maximum(m_sc[of(h), :], jnp.maximum(sh[:, :128], sh[:, 128:]))
        return 0

    lax.fori_loop(0, count, pass1, 0)
    m_sc[...] = jnp.broadcast_to(jnp.max(m_sc[...], axis=1, keepdims=True), m_sc.shape)

    def pass2(j, _):
        for h in range(heads):
            e = jnp.exp(s_sc[j, of(h), :] - twice(m_sc[of(h), :]))
            s_sc[j, of(h), :] = e
            l_sc[of(h), :] += e[:, :128] + e[:, 128:]
        return 0

    lax.fori_loop(0, count, pass2, 0)
    total = jnp.sum(l_sc[...], axis=1, keepdims=True)
    lse = m_sc[:, 0:1] + jnp.log(total)
    l_sc[...] = jnp.broadcast_to(1.0 / total, l_sc.shape)
    lane = lax.broadcasted_iota(jnp.int32, (BLOCK, 128), 1)
    tile = jnp.zeros((BLOCK, 128), F32)
    for h in range(heads):
        tile = jnp.where(lane == h, lse[of(h), :], tile)
    lse_o[...] = tile.T[0:8, :]
    acc[...] = jnp.zeros(acc.shape, F32)
    full_o[...] = jnp.zeros(full_o.shape, F32)

    def pass3(j, _):
        ps, less = [], []
        for h in range(heads):
            p = s_sc[j, of(h), :] * twice(l_sc[of(h), :])
            b = p.astype(BF)
            ps.append(b)
            less.append((p - b.astype(F32)).astype(BF))
        vs = jnp.concatenate(lanes_of_heads(v[at(j), :], heads), axis=0)
        acc[...] += nn(jnp.concatenate(ps, axis=1), vs)
        full_o[...] += nn(jnp.concatenate(less, axis=1), vs)
        return 0

    lax.fori_loop(0, count, pass3, 0)
    ctx_o[...] = acc[:, : heads * HEAD].astype(BF)
    full_o[...] += acc[...]


def attention_forward(place, q, k, v, segc, segr, heads, share):
    length = q.shape[0]
    grid = share // BLOCK
    rows = lambda i, s: (s[0] + i, 0)
    return pl.pallas_call(
        partial(forward_kernel, heads),
        grid_spec=pltpu.PrefetchScalarGridSpec(
            num_scalar_prefetch=1,
            grid=(grid,),
            in_specs=[
                pl.BlockSpec((BLOCK, WIDE), rows),
                whole_block(k.shape),
                whole_block(v.shape),
                pl.BlockSpec((BLOCK, 1), rows),
                whole_block(segr.shape),
            ],
            out_specs=[
                pl.BlockSpec((BLOCK, heads * HEAD), lambda i, s: (i, 0)),
                pl.BlockSpec((8, BLOCK), lambda i, s: (0, i)),
                pl.BlockSpec((BLOCK, WIDE), lambda i, s: (i, 0)),
            ],
            scratch_shapes=[
                pltpu.VMEM((BLOCK, WIDE), F32),
                pltpu.VMEM((length // CHUNK, heads * BLOCK, CHUNK), F32),
                pltpu.VMEM((heads * BLOCK, 128), F32),
                pltpu.VMEM((heads * BLOCK, 128), F32),
                pltpu.VMEM((heads * BLOCK, WIDE), BF),
            ],
        ),
        out_shape=[
            jax.ShapeDtypeStruct((share, heads * HEAD), BF),
            jax.ShapeDtypeStruct((8, share), F32),
            jax.ShapeDtypeStruct((share, WIDE), F32),
        ],
        compiler_params=params(16),
        cost_estimate=COST,
        name="attention_forward",
    )(place, q, k, v, segc, segr)


def backward_kernel(heads, place, q, qt, k, kt, v, d0, d1, d2, d3, full, lse, segc, segr, cos, sin, g_o, gb_o, dk_sc, dv_sc, qc_sc, dc_sc, dq_sc, d_sc, dt_sc, qs_sc):
    step_at = pl.program_id(0)
    blocks = k.shape[0] // BLOCK

    @pl.when(step_at < blocks)
    def _():
        backward_rows(heads, place, q, qt, k, kt, v, (d0, d1, d2, d3), full, lse, segc, segr, dk_sc, dv_sc, qc_sc, dc_sc, dq_sc, d_sc, dt_sc, qs_sc)

    @pl.when(step_at == 0)
    def _():
        gb_o[...] = jnp.zeros(gb_o.shape, F32)

    @pl.when(step_at >= blocks)
    def _():
        at = pl.ds(pl.multiple_of((step_at - blocks) * BLOCK, BLOCK), BLOCK)

        def turn(x):
            return (x * twice(cos[...]) - swap_pairs(x) * twice(sin[...])).astype(BF)

        def put(x, m):
            g_o[:, m * WIDE : (m + 1) * WIDE] = x
            gb_o[0:1, m * WIDE : (m + 1) * WIDE] += jnp.sum(x.astype(F32), axis=0, keepdims=True)

        put(turn(qs_sc[:, at].T * (HEAD**-0.5)), 0)
        put(turn(dk_sc[:, at].T), 1)
        put(dv_sc[:, at].astype(BF).T, 2)


def backward_rows(heads, place, q, qt, k, kt, v, do, full, lse, segc, segr, dk_sc, dv_sc, qc_sc, dc_sc, dq_sc, d_sc, dt_sc, qs_sc):
    step_at = pl.program_id(0)
    i = step_at ^ place[0]
    part = do[0].shape[1]
    per = do[0].shape[0] // BLOCK

    @pl.when(step_at == 0)
    def _():
        dk_sc[...] = jnp.zeros(dk_sc.shape, F32)
        dv_sc[...] = jnp.zeros(dv_sc.shape, F32)
        d_sc[...] = jnp.zeros(d_sc.shape, BF)

    for n, d in enumerate(do):

        @pl.when(step_at // per == n)
        def _(d=d):
            d_sc[:, 0:part] = d[pl.ds(pl.multiple_of(step_at % per * BLOCK, BLOCK), BLOCK), :]

    start, count = place[1 + 2 * i], place[2 + 2 * i]
    qc_sc[...] = jnp.concatenate(lanes_of_heads(q[...], heads), axis=0)
    dz = d_sc[...]
    dc_sc[...] = jnp.concatenate(lanes_of_heads(dz, heads), axis=0)
    dt_sc[...] = dz.T
    dq_sc[...] = jnp.zeros(dq_sc.shape, F32)
    own = pl.ds(pl.multiple_of(i * BLOCK, BLOCK), BLOCK)
    seg_q = segr[0:1, own]
    row = lax.broadcasted_iota(jnp.int32, (8, WIDE), 0)
    lane = lax.broadcasted_iota(jnp.int32, (8, WIDE), 1) // HEAD
    pick = jnp.where(row == lane, 1.0, 0.0).astype(F32)
    delta = lax.dot_general(
        pick, dz.astype(F32) * full[...], (((1,), (1,)), ((), ())), preferred_element_type=F32, precision=lax.Precision.HIGHEST
    )

    def of(h):
        return slice(h * BLOCK, (h + 1) * BLOCK)

    def step(j, _):
        at = pl.ds(pl.multiple_of(start + j * CHUNK, 128), CHUNK)
        s = nt(k[at, :], qc_sc[...])
        dp = nt(v[at, :], dc_sc[...])
        keep = segc[at, :] == seg_q
        for h in range(heads):
            mine = slice(h * HEAD, (h + 1) * HEAD)
            p = jnp.exp(jnp.where(keep, s[:, of(h)], NEG) - lse[h : h + 1, :])
            ds = (p * (dp[:, of(h)] - delta[h : h + 1, :])).astype(BF)
            dq_sc[mine, :] += nn(kt[mine, at], ds)
            dv_sc[mine, at] += nt(dt_sc[mine, :], p.astype(BF))
            dk_sc[mine, at] += nt(qt[mine, :], ds)
        return 0

    def pair(j, _):
        step(2 * j, 0)
        step(2 * j + 1, 0)
        return 0

    lax.fori_loop(0, count // 2, pair, 0)

    @pl.when(count % 2 == 1)
    def _():
        step(count - 1, 0)

    qs_sc[:, own] = dq_sc[...]


def attention_backward(place, q, qt, k, kt, v, do, full, lse, segc, segr, cos, sin, heads):
    length = k.shape[0]
    blocks = length // BLOCK
    first = lambda i: jnp.minimum(i, blocks - 1)
    second = lambda i: jnp.maximum(i - blocks, 0)
    return pl.pallas_call(
        partial(backward_kernel, heads),
        grid_spec=pltpu.PrefetchScalarGridSpec(
            num_scalar_prefetch=1,
            grid=(2 * blocks,),
            in_specs=[
                pl.BlockSpec((BLOCK, WIDE), lambda i, s: (first(i) ^ s[0], 0)),
                pl.BlockSpec((WIDE, BLOCK), lambda i, s: (0, first(i) ^ s[0])),
                whole_block(k.shape),
                whole_block(kt.shape),
                whole_block(v.shape),
                *[whole_block(d.shape) for d in do],
                pl.BlockSpec((BLOCK, WIDE), lambda i, s: (first(i), 0)),
                pl.BlockSpec((8, BLOCK), lambda i, s: (0, first(i))),
                whole_block(segc.shape),
                whole_block(segr.shape),
                pl.BlockSpec((BLOCK, 128), lambda i, s: (second(i), 0)),
                pl.BlockSpec((BLOCK, 128), lambda i, s: (second(i), 0)),
            ],
            out_specs=[pl.BlockSpec((BLOCK, 3 * WIDE), lambda i, s: (second(i), 0)), whole_block((8, 3 * WIDE))],
            scratch_shapes=[pltpu.VMEM((WIDE, length), F32)] * 2
            + [pltpu.VMEM((heads * BLOCK, WIDE), BF)] * 2
            + [pltpu.VMEM((WIDE, BLOCK), F32), pltpu.VMEM((BLOCK, WIDE), BF), pltpu.VMEM((WIDE, BLOCK), BF)]
            + [pltpu.VMEM((WIDE, length), F32)],
        ),
        out_shape=[jax.ShapeDtypeStruct((length, 3 * WIDE), BF), jax.ShapeDtypeStruct((8, 3 * WIDE), F32)],
        compiler_params=params(28),
        cost_estimate=COST,
        name="attention_backward",
    )(place, q, qt, k, kt, v, *do, full, lse, segc, segr, cos, sin)


def out_copies(place, gathered, w_out, sems):
    here = place[place.shape[0] - 1]
    feed = gathered.shape[2] - w_out.shape[2]
    return [pltpu.make_async_copy(gathered.at[here ^ k, :, feed:], w_out.at[k], sems.at[k]) for k in range(4)]


def row_mean(x):
    return jnp.mean(x, axis=1, keepdims=True)


def gelu_parts(x):
    e = jnp.exp2(x * x * (-0.5 * 1.4426950408889634))
    t = 1.0 / (1.0 + (0.3275911 * 0.7071067811865476) * jnp.abs(x))
    p = t * (0.127414796 + t * (-0.142248368 + t * (0.7107068705 + t * (-0.7265760135 + t * 0.5307027145))))
    tail = p * e
    phi = jnp.where(x >= 0, 1.0 - tail, tail)
    return phi, phi + x * e * 0.3989422804014327


ROWS = 512


def feed_kernel(place, gathered, w, c0, c1, c2, c3, tokb, gtop, vec, bias, *refs):
    (out_o, gs_o, gsb_o, fs_o, nbt_o, gst_o, act_o, gp_o, root_o, sum_o, nb_o, w_out, acc, normed, sems) = refs
    copies = out_copies(place, gathered, w_out, sems)
    k = pl.program_id(0)
    share = tokb.shape[0]
    part = c0.shape[1]
    chunks = [pl.ds(r * ROWS, ROWS) for r in range(share // ROWS)]

    @pl.when(k == 0)
    def _():
        for copy in copies:
            copy.start()
        for copy in copies:
            copy.wait()
        for sl in chunks:
            x = tokb[sl, :].astype(F32) + vec[4:5, :]
            for n, ctx in enumerate((c0, c1, c2, c3)):
                x = x + nt(ctx[sl, :], w_out[n, :, 0:part])
            x = x - row_mean(x)
            root = lax.rsqrt(row_mean(x * x) + EPSILON)
            x = x * root
            fs_o[sl, :] = x
            root_o[sl, :] = jnp.broadcast_to(root, (ROWS, 128))
            y = x * vec[0:1, :] + vec[2:3, :]
            normed[sl, :] = y
            nb_o[sl, :] = y.astype(BF)
            nbt_o[:, sl] = y.astype(BF).T
            acc[sl, :] = y + vec[5:6, :]

    hidden = act_o.shape[2]

    def rows_step(r, _):
        sl = pl.ds(pl.multiple_of(r * ROWS, ROWS), ROWS)
        h = nn(nb_o[sl, :], w[0, :, 0:hidden]) + bias[pl.ds(k, 1), :]
        phi, slope = gelu_parts(h)
        a = (h * phi).astype(BF)
        act_o[0, sl, :] = a
        gp_o[0, sl, :] = slope
        acc[sl, :] += nt(a, w[0, :, hidden:])
        return 0

    lax.fori_loop(0, share // ROWS, rows_step, 0, unroll=True)

    @pl.when(k == 3)
    def _():
        total = [jnp.zeros((1, tokb.shape[1]), F32)] * 3
        for sl in chunks:
            x = acc[sl, :]
            x = x - row_mean(x)
            root = lax.rsqrt(row_mean(x * x) + EPSILON)
            x = x * root
            out_o[sl, :] = (x * vec[1:2, :] + vec[3:4, :]).astype(BF)
            g = gtop[sl, :].astype(F32)
            gg = g * vec[1:2, :]
            gs = root * (gg - row_mean(gg) - x * row_mean(gg * x))
            gs_o[sl, :] = gs
            gsb_o[sl, :] = gs.astype(BF)
            gst_o[:, sl] = gs.astype(BF).T
            for n, y in enumerate((g * x, g, gs)):
                total[n] = total[n] + jnp.sum(y, axis=0, keepdims=True)
        sum_o[...] = jnp.concatenate(total + [jnp.zeros((5, tokb.shape[1]), F32)], axis=0)


def feed_specs(place, gathered, hidden):
    width, last = gathered.shape[1], place.shape[0] - 1
    return [pl.BlockSpec(memory_space=pl.ANY), pl.BlockSpec((1, width, 2 * hidden), lambda i, s: (s[last] ^ i, 0, 0))]


def feed_forward(place, gathered, contexts, tokb, gtop, vec, bias):
    share, width = tokb.shape
    hidden = bias.shape[1]
    block = lambda: pl.BlockSpec((1, share, hidden), lambda i, s: (i, 0, 0))
    sd, far = jax.ShapeDtypeStruct, pltpu.HBM
    return pl.pallas_call(
        feed_kernel,
        grid_spec=pltpu.PrefetchScalarGridSpec(
            num_scalar_prefetch=1,
            grid=(4,),
            in_specs=feed_specs(place, gathered, hidden) + [whole_block(x.shape) for x in (*contexts, tokb, gtop, vec, bias)],
            out_specs=[whole_block((share, width))] * 4
            + [whole_block((width, share))] * 2
            + [block(), block(), whole_block((share, 128)), whole_block((8, width))],
            scratch_shapes=[
                pltpu.VMEM((share, width), BF),
                pltpu.VMEM((4, width, gathered.shape[2] - 2 * hidden), BF),
                pltpu.VMEM((share, width), F32),
                pltpu.VMEM((share, width), F32),
                pltpu.SemaphoreType.DMA((4,)),
            ],
        ),
        out_shape=[
            sd((share, width), BF),
            sd((share, width), F32),
            sd((share, width), BF),
            sd((share, width), F32),
            far((width, share), BF),
            far((width, share), BF),
            far((4, share, hidden), BF),
            far((4, share, hidden), F32),
            sd((share, 128), F32),
            sd((8, width), F32),
        ],
        compiler_params=params(54),
        cost_estimate=COST,
        name="feed_forward",
    )(place, gathered, gathered, *contexts, tokb, gtop, vec, bias)


def feed_back_kernel(place, gathered, w, gs, gsb, fs, gp, root, vec, *refs):
    (gf_o, gft_o, gc0, gc1, gc2, gc3, gh_o, ghs_o, sum_o, w_out, acc, sems) = refs
    copies = out_copies(place, gathered, w_out, sems)
    k = pl.program_id(0)
    share, width = gs.shape
    hidden, part = gh_o.shape[2], gc0.shape[1]

    @pl.when(k == 0)
    def _():
        for copy in copies:
            copy.start()
        acc[...] = gs[...]

    def rows_step(r, total):
        sl = pl.ds(pl.multiple_of(r * ROWS, ROWS), ROWS)
        g = (nn(gsb[sl, :], w[0, :, hidden:]) * gp[0, sl, :]).astype(BF)
        gh_o[0, sl, :] = g
        acc[sl, :] += nt(g, w[0, :, 0:hidden])
        return total + jnp.sum(g.astype(F32), axis=0, keepdims=True)

    total = lax.fori_loop(0, share // ROWS, rows_step, jnp.zeros((1, hidden), F32), unroll=True)
    ghs_o[0] = jnp.broadcast_to(total, (8, hidden))

    @pl.when(k == 3)
    def _():
        for copy in copies:
            copy.wait()
        sums = [jnp.zeros((1, width), F32)] * 3
        for r in range(share // ROWS):
            sl = pl.ds(r * ROWS, ROWS)
            gn = acc[sl, :]
            x = fs[sl, :]
            gg = gn * vec[0:1, :]
            gf = root[sl, 0:1] * (gg - row_mean(gg) - x * row_mean(gg * x))
            gf_o[sl, :] = gf
            b = gf.astype(BF)
            gft_o[:, sl] = b.T
            for n, o in enumerate((gc0, gc1, gc2, gc3)):
                o[sl, :] = nn(b, w_out[n, :, 0:part]).astype(BF)
            for n, y in enumerate((gn * x, gn, gf)):
                sums[n] = sums[n] + jnp.sum(y, axis=0, keepdims=True)
        sum_o[...] = jnp.concatenate(sums + [jnp.zeros((5, width), F32)], axis=0)


def feed_back(place, gathered, gs, gsb, fs, gp, root, vec, part):
    share, width = gs.shape
    hidden = gp.shape[2]
    block = lambda: pl.BlockSpec((1, share, hidden), lambda i, s: (i, 0, 0))
    sd, far = jax.ShapeDtypeStruct, pltpu.HBM
    return pl.pallas_call(
        feed_back_kernel,
        grid_spec=pltpu.PrefetchScalarGridSpec(
            num_scalar_prefetch=1,
            grid=(4,),
            in_specs=feed_specs(place, gathered, hidden)
            + [whole_block(gs.shape), whole_block(gsb.shape), whole_block(fs.shape), block(), whole_block(root.shape), whole_block(vec.shape)],
            out_specs=[whole_block((share, width)), whole_block((width, share))]
            + [whole_block((share, part))] * 4
            + [block(), pl.BlockSpec((1, 8, hidden), lambda i, s: (i, 0, 0)), whole_block((8, width))],
            scratch_shapes=[
                pltpu.VMEM((4, width, gathered.shape[2] - 2 * hidden), BF),
                pltpu.VMEM((share, width), F32),
                pltpu.SemaphoreType.DMA((4,)),
            ],
        ),
        out_shape=[far((share, width), F32), far((width, share), BF)]
        + [sd((share, part), BF)] * 4
        + [far((4, share, hidden), BF), sd((4, 8, hidden), F32), sd((8, width), F32)],
        compiler_params=params(54),
        cost_estimate=COST,
        name="feed_back",
    )(place, gathered, gathered, gs, gsb, fs, gp, root, vec)


def split_rows(place, per, acc, source, near_o, far_o, lead, cols):
    if per == 1:
        near_o[(*lead, slice(None), cols)] = acc[:, source].astype(near_o.dtype)
        return
    rows = acc.shape[0] // per
    for n in range(per // 2):
        near, far = (pl.ds(pl.multiple_of(place[m], 16), rows) for m in (n, per // 2 + n))
        near_o[(*lead, n, slice(None), cols)] = acc[near, source].astype(near_o.dtype)
        far_o[(*lead, n, slice(None), cols)] = acc[far, source].astype(BF)


def weights_kernel(per, place, nbt, gst, gft, ctx, gh, act, *refs):
    hh = gh.shape[2] // 2
    if per > 1:
        near_o, far_o, out, acc = refs
    else:
        other, out = refs
    for n, (left, right) in enumerate(((nbt, gh), (gst, act))):
        made = nn(left[...], right[0])
        out[0, :, n * hh : (n + 1) * hh] = made[:, 0:hh].astype(BF)
        if per > 1:
            acc[...] = made[:, hh:]
            split_rows(place, per, acc, slice(None), near_o, far_o, (0,), slice(n * hh, (n + 1) * hh))
        else:
            other[0, :, n * hh : (n + 1) * hh] = made[:, hh:].astype(BF)
    out[0, :, 2 * hh :] = nn(gft[...], ctx[0]).astype(BF)


def weight_grads(place, per, nbt, gst, gft, contexts, gh, act):
    width, share = nbt.shape
    hidden, part = gh.shape[2], contexts.shape[2]
    last = place.shape[0] - 1
    block = lambda cols: pl.BlockSpec((1, share, cols), lambda i, s: (i, 0, 0))
    ordered = lambda cols: pl.BlockSpec((1, width, cols), lambda i, s: (i ^ s[last], 0, 0))
    if per > 1:
        shape = (4, per // 2, width // per, hidden)
        outs = [jax.ShapeDtypeStruct(shape, BF)] * 2
        specs = [pl.BlockSpec((1,) + shape[1:], lambda i, s: (i, 0, 0, 0))] * 2
        scratch = [pltpu.VMEM((width, hidden // 2), F32)]
    else:
        outs = [jax.ShapeDtypeStruct((4, width, hidden), BF)]
        specs = [ordered(hidden)]
        scratch = []
    return pl.pallas_call(
        partial(weights_kernel, per),
        grid_spec=pltpu.PrefetchScalarGridSpec(
            num_scalar_prefetch=1,
            grid=(4,),
            in_specs=[whole_block(x.shape) for x in (nbt, gst, gft)] + [block(part), block(hidden), block(hidden)],
            out_specs=specs + [ordered(hidden + part)],
            scratch_shapes=scratch,
        ),
        out_shape=outs + [jax.ShapeDtypeStruct((4, width, hidden + part), BF)],
        compiler_params=params(58),
        cost_estimate=COST,
        name="weight_grads",
    )(place, nbt, gst, gft, contexts, gh, act)


def qkv_weights_kernel(per, part, place, own, other, g, *refs):
    near_o, far_o = refs[:2] if per > 1 else (refs[0], None)
    acc = refs[-1]
    half_len = other.shape[0]
    core = place[per]
    rows = 512

    acc[...] = jnp.zeros(acc.shape, F32)

    def step(r, _):
        at = pl.ds(pl.multiple_of(r * rows, rows), rows)
        a = g[pl.ds(pl.multiple_of(core * half_len + r * rows, rows), rows), :]
        b = g[pl.ds(pl.multiple_of((1 - core) * half_len + r * rows, rows), rows), :]
        acc[...] += nn(own[0, at, :].T, a) + nn(other[at, :].T, b)
        return 0

    lax.fori_loop(0, half_len // rows, step, 0)
    for m in range(3):
        split_rows(place, per, acc, slice(m * WIDE, m * WIDE + part), near_o, far_o, (), slice(m * part, (m + 1) * part))


def qkv_weight_grads(place, per, tokens, other, g, part):
    half_len, width = other.shape
    if per > 1:
        shape = (per // 2, width // per, 3 * part)
        outs = [jax.ShapeDtypeStruct(shape, F32), jax.ShapeDtypeStruct(shape, BF)]
    else:
        outs = [jax.ShapeDtypeStruct((width, 3 * part), F32)]
    return pl.pallas_call(
        partial(qkv_weights_kernel, per, part),
        grid_spec=pltpu.PrefetchScalarGridSpec(
            num_scalar_prefetch=1,
            grid=(1,),
            in_specs=[pl.BlockSpec((1, half_len, width), lambda i, s: (s[per], 0, 0)), whole_block(other.shape), whole_block(g.shape)],
            out_specs=[whole_block(o.shape) for o in outs],
            scratch_shapes=[pltpu.VMEM((width, 3 * WIDE), F32)],
        ),
        out_shape=outs,
        compiler_params=params(32),
        cost_estimate=COST,
        name="qkv_weight_grads",
    )(place, tokens, other, g)


def branch_kernel(place, *refs):
    count = (len(refs) - 1) // 2
    w = refs[count]
    for g, o in zip(refs[:count], refs[count + 1 :]):
        rows = 256
        for r in range(g.shape[0] // rows):
            sl = slice(r * rows, (r + 1) * rows)
            o[sl, :] = nt(g[sl, :], w[...]).astype(o.dtype)


def branch(place, blocks, kinds, g, w):
    share, last = g.shape[0] // 4, place.shape[0] - 1
    return pl.pallas_call(
        branch_kernel,
        grid_spec=pltpu.PrefetchScalarGridSpec(
            num_scalar_prefetch=1,
            grid=(1,),
            in_specs=[pl.BlockSpec((share, g.shape[1]), lambda i, s, k=k: (s[last] ^ k, 0)) for k in blocks] + [whole_block(w.shape)],
            out_specs=[whole_block((share, w.shape[0]))] * len(blocks),
        ),
        out_shape=[jax.ShapeDtypeStruct((share, w.shape[0]), kind) for kind in kinds],
        compiler_params=params(24),
        cost_estimate=COST,
        name="branch",
    )(place, *[g] * len(blocks), w)


def pick_kernel(place, near, *refs):
    far, (keep, send) = refs[:-2], refs[-2:]
    last = place.shape[0] - 1
    mine = place[last] // 2 == place[last - 1]

    def put(out, parts):
        rows = out.shape[0] // len(parts)
        for n, x in enumerate(parts):
            out[n * rows : (n + 1) * rows, :] = x[...]

    @pl.when(mine)
    def _():
        put(keep, [near])
        put(send, far)

    @pl.when(jnp.logical_not(mine))
    def _():
        put(keep, far)
        put(send, [near])


def pick(place, near, *far):
    return pl.pallas_call(
        pick_kernel,
        grid_spec=pltpu.PrefetchScalarGridSpec(
            num_scalar_prefetch=1,
            grid=(1,),
            in_specs=[whole_block(x.shape) for x in (near, *far)],
            out_specs=[whole_block(near.shape)] * 2,
        ),
        out_shape=[jax.ShapeDtypeStruct(near.shape, near.dtype)] * 2,
        compiler_params=params(8),
        cost_estimate=COST,
        name="pick",
    )(place, near, *far)


def join_kernel(second, place, *refs):
    last = place.shape[0] - 1
    mine = place[last] // 2 == place[last - 1]
    if second:
        near, *far, other, _, out = refs
    else:
        near, *far, other, out = refs
    here = pl.program_id(0) == place[last - 1]

    def put(parts):
        rows = out.shape[1] // len(parts)
        for n, x in enumerate(parts):
            out[0, n * rows : (n + 1) * rows, :] = x[...]

    @pl.when(jnp.logical_and(here, mine))
    def _():
        put([near])

    @pl.when(jnp.logical_and(here, jnp.logical_not(mine)))
    def _():
        put(far)

    @pl.when(jnp.logical_not(here))
    def _():
        put([other])


def join(place, near, far, other, before=None):
    share, width = near.shape
    second = before is not None
    last = place.shape[0] - 1
    ins = [near, *far, other]
    specs = [whole_block(x.shape) for x in ins]
    if second:
        ins.append(before)
        specs.append(pl.BlockSpec(memory_space=pl.ANY))
    return pl.pallas_call(
        partial(join_kernel, second),
        grid_spec=pltpu.PrefetchScalarGridSpec(
            num_scalar_prefetch=1,
            grid=(2,),
            in_specs=specs,
            out_specs=pl.BlockSpec((1, share, width), lambda i, s: (i, (s[last] + int(second)) % 2, 0)),
        ),
        out_shape=jax.ShapeDtypeStruct((2, 2 * share, width), near.dtype),
        input_output_aliases={len(ins): 0} if second else {},
        compiler_params=params(12),
        cost_estimate=COST,
        name="join",
    )(place, *ins)


def relay_kernel(one, two, low, high, one_o, two_o):
    half = low.shape[0]
    one_o[0:half, :] = (one[0:half, :] + low[...].astype(F32)).astype(BF)
    one_o[half:, :] = one[half:, :].astype(BF)
    two_o[0:half, :] = two[0:half, :].astype(BF)
    two_o[half:, :] = (two[half:, :] + high[...].astype(F32)).astype(BF)


def relay(one, two, low, high):
    return pl.pallas_call(
        relay_kernel,
        in_specs=[pl.BlockSpec(memory_space=pltpu.VMEM)] * 4,
        out_specs=[pl.BlockSpec(memory_space=pltpu.VMEM)] * 2,
        out_shape=[jax.ShapeDtypeStruct(one.shape, BF)] * 2,
        compiler_params=pltpu.CompilerParams(vmem_limit_bytes=16 * 1024 * 1024),
        cost_estimate=COST,
        name="relay",
    )(one, two, low, high)


def collect_kernel(place, hidden_sums, one, two, bias, out):
    here = place[place.shape[0] - 1]
    out[...] = jnp.zeros(out.shape, F32)
    for k in range(4):
        out[pl.ds(here ^ k, 1), :] = hidden_sums[k, 0:1, :]
    for n, (x, row) in enumerate(((one, 0), (two, 0), (one, 1), (two, 1), (one, 2), (two, 2))):
        out[4 + n : 5 + n, :] = x[row : row + 1, :]
    out[pl.ds(10 + here, 1), :] = bias[0:1, :]


def collect(place, hidden_sums, one, two, bias):
    return pl.pallas_call(
        collect_kernel,
        grid_spec=pltpu.PrefetchScalarGridSpec(
            num_scalar_prefetch=1,
            grid=(1,),
            in_specs=[whole_block(x.shape) for x in (hidden_sums, one, two, bias)],
            out_specs=whole_block((16, one.shape[1])),
        ),
        out_shape=jax.ShapeDtypeStruct((16, one.shape[1]), F32),
        compiler_params=params(8),
        cost_estimate=COST,
        name="collect",
    )(place, hidden_sums, one, two, bias)


def settle_kernel(count, *refs):
    ins, outs = refs[:count], refs[count:]
    for j, out in enumerate(outs):
        total = ins[0][j].astype(F32)
        for x in ins[1:]:
            total = total + x[j].astype(F32)
        out[...] = total.astype(out.dtype)


def settle(*stacks):
    shape = stacks[0].shape
    vmem = pl.BlockSpec(memory_space=pltpu.VMEM)
    return pl.pallas_call(
        partial(settle_kernel, len(stacks)),
        in_specs=[vmem] * len(stacks),
        out_specs=[vmem] * shape[0],
        out_shape=[jax.ShapeDtypeStruct(shape[1:], F32 if j == 0 else BF) for j in range(shape[0])],
        compiler_params=pltpu.CompilerParams(vmem_limit_bytes=16 * 1024 * 1024),
        cost_estimate=COST,
        name="settle",
    )(*stacks)


def finish_kernel(parts, *refs):
    out = refs[-1]
    total = refs[0][...]
    for x in refs[1:-1]:
        total = total + x[...].astype(F32)
    if parts == 1:
        out[...] = total
    else:
        cols = total.shape[1] // parts
        for m in range(parts):
            out[:, m, :] = total[:, m * cols : (m + 1) * cols]


def finish(parts, *pieces):
    vmem = pl.BlockSpec(memory_space=pltpu.VMEM)
    rows, cols = pieces[0].shape
    return pl.pallas_call(
        partial(finish_kernel, parts),
        in_specs=[vmem] * len(pieces),
        out_specs=vmem,
        out_shape=jax.ShapeDtypeStruct((rows, cols) if parts == 1 else (rows, parts, cols // parts), F32),
        compiler_params=pltpu.CompilerParams(vmem_limit_bytes=8 * 1024 * 1024),
        cost_estimate=COST,
        name="finish",
    )(*pieces)


def place_kernel(whole, rest, feed_o, out_o):
    hh = rest.shape[1] // 2
    for m in range(2):
        feed_o[:, m, 0:hh] = whole[:, m * hh : (m + 1) * hh].astype(F32)
        feed_o[:, m, hh:] = rest[:, m * hh : (m + 1) * hh]
    out_o[...] = whole[:, 2 * hh :].astype(F32)


def place_feed(whole, rest):
    vmem = pl.BlockSpec(memory_space=pltpu.VMEM)
    rows, cols = rest.shape
    return pl.pallas_call(
        place_kernel,
        in_specs=[vmem] * 2,
        out_specs=[vmem] * 2,
        out_shape=[jax.ShapeDtypeStruct((rows, 2, cols), F32), jax.ShapeDtypeStruct((rows, whole.shape[1] - cols), F32)],
        compiler_params=pltpu.CompilerParams(vmem_limit_bytes=8 * 1024 * 1024),
        cost_estimate=COST,
        name="place_feed",
    )(whole, rest)


def block_kernel(own, first, one, two, out):
    out[...] = (own[...] + first[...] + one[...].astype(F32) + two[...].astype(F32)).astype(BF)


def add_block(own, first, one, two):
    vmem = pl.BlockSpec(memory_space=pltpu.VMEM)
    return pl.pallas_call(
        block_kernel,
        in_specs=[vmem] * 4,
        out_specs=vmem,
        out_shape=jax.ShapeDtypeStruct(own.shape, BF),
        compiler_params=pltpu.CompilerParams(vmem_limit_bytes=12 * 1024 * 1024),
        cost_estimate=COST,
        name="add_block",
    )(own, first, one, two)


def relay_kernel(one, two, low, high, one_o, two_o):
    half = low.shape[0]
    one_o[0:half, :] = (one[0:half, :] + low[...].astype(F32)).astype(BF)
    one_o[half:, :] = one[half:, :].astype(BF)
    two_o[0:half, :] = two[0:half, :].astype(BF)
    two_o[half:, :] = (two[half:, :] + high[...].astype(F32)).astype(BF)


def relay(one, two, low, high):
    return pl.pallas_call(
        relay_kernel,
        in_specs=[pl.BlockSpec(memory_space=pltpu.VMEM)] * 4,
        out_specs=[pl.BlockSpec(memory_space=pltpu.VMEM)] * 2,
        out_shape=[jax.ShapeDtypeStruct(one.shape, BF)] * 2,
        compiler_params=pltpu.CompilerParams(vmem_limit_bytes=16 * 1024 * 1024),
        cost_estimate=COST,
        name="relay",
    )(one, two, low, high)


def rotation_tables(offsets):
    lane = np.arange(128)
    frequency = (10000.0 ** (-2.0 * (lane % HEAD // 2) / HEAD)).astype(np.float32)
    angles = offsets.astype(F32)[:, None] * frequency[None, :]
    sign = np.where(lane % 2 == 0, -1.0, 1.0).astype(np.float32)
    return jnp.cos(angles), jnp.sin(angles) * sign


def key_bounds(segment):
    length = segment.shape[0]
    first, last = segment[::BLOCK], segment[BLOCK - 1 :: BLOCK]
    low = jnp.sum(segment[None, :] < first[:, None], axis=1)
    high = jnp.sum(segment[None, :] <= last[:, None], axis=1)
    low = low // 128 * 128
    count = (high - low + CHUNK - 1) // CHUNK
    return jnp.stack([jnp.minimum(low, length - CHUNK * count), count], axis=1).reshape(-1).astype(jnp.int32)


def swap_ctx(x):
    return lax.ppermute(x, "ctx", [(0, 1), (1, 0)])


def swap_tp(x, k):
    return lax.ppermute(x, "tp", [(i, i ^ k) for i in range(4)])


def swap_shard(x, k):
    return lax.ppermute(x, "shard", [(i, i ^ k) for i in range(4)])


def order_four(parts, index):
    a, b, c, d = parts
    odd, high = index % 2 == 1, index // 2 == 1
    a, b = jnp.where(odd, b, a), jnp.where(odd, a, b)
    c, d = jnp.where(odd, d, c), jnp.where(odd, c, d)
    return jnp.stack([jnp.where(high, c, a), jnp.where(high, d, b), jnp.where(high, a, c), jnp.where(high, b, d)])


def after(x, *others):
    return lax.optimization_barrier((x, others))[0]


def gather_tp(x, half):
    one, two = swap_tp(x, 1), swap_tp(x, 2)
    three = jnp.concatenate([swap_tp(one[:half], 2), swap_tp(two[half:], 1)])
    return [x, one, two, three]


def scatter_tp(parts):
    own, one, two, three = parts
    half = own.shape[0] // 2
    low, high = three[:half].astype(BF), three[half:].astype(BF)
    low, high = swap_tp(low, 2), swap_tp(high, 1)
    one = jnp.concatenate([one[:half] + low.astype(F32), one[half:]]).astype(BF)
    two = jnp.concatenate([two[:half], two[half:] + high.astype(F32)]).astype(BF)
    return own + swap_tp(one, 1).astype(F32) + swap_tp(two, 2).astype(F32)


def three_rows(x):
    high = lax.reduce_precision(x, 8, 7)
    middle = lax.reduce_precision(x - high, 8, 7)
    return jnp.stack([high, middle, x - high - middle]).astype(BF)


def contract_last(left, right):
    return lax.dot_general(left, right, (((1,), (1,)), ((), ())), preferred_element_type=F32)


def body(tokens, segment_ids, offsets, qkv_weight, out_weight, ffn_weight, qkv_bias, ffn_bias, norm_gain, shift_params, out_grad):
    t, c, z = lax.axis_index("tp"), lax.axis_index("ctx"), lax.axis_index("shard")
    shards = lax.axis_size("shard")
    half_len, width = tokens.shape[1:]
    rows, _, part = qkv_weight.shape
    hidden = ffn_weight.shape[2]
    heads = part // HEAD
    length = 2 * half_len
    share = length // 4
    first_core = c == 0
    direct = shards == 4

    def take(x, index):
        return lax.dynamic_index_in_dim(x, index, 0, keepdims=False)

    def by_core(own, other):
        return jnp.where(first_core, jnp.stack([own, other]), jnp.stack([other, own]))

    hh = hidden // 2
    gathered = jnp.concatenate([ffn_weight.reshape(rows, 2 * hidden), out_weight], axis=1)
    gathered = lax.all_gather(gathered, ("tp", "shard", "ctx"), axis=0, tiled=True).reshape(4, width, 2 * hidden + part)
    bias_all = ffn_bias.reshape(1, hidden)
    bias_all = jnp.concatenate([bias_all] + [swap_tp(bias_all, k) for k in (1, 2, 3)])
    qkv_rows = qkv_weight.reshape(rows, 3 * part)
    other_tokens = swap_ctx(take(tokens, 1 - c))
    if direct:
        places = [((z ^ j) * 2 + (c ^ f)) * rows for f in (0, 1) for j in range(4)]
        near = [qkv_rows] + [swap_shard(qkv_rows, j) for j in (1, 2, 3)]
        qkv_pieces = [*near, swap_ctx(jnp.stack(near))]
    else:
        places = [jnp.zeros_like(c)]
        qkv_pieces = [lax.all_gather(qkv_rows, ("shard", "ctx"), axis=0, tiled=True)]
    per = len(places)
    place = jnp.stack(places + [c, t]).astype(jnp.int32)
    bias_pad = jnp.pad(qkv_bias, ((0, 0), (0, WIDE - part)))
    vec = jnp.concatenate([norm_gain, shift_params, jnp.zeros((2, width), F32)])

    marks = jnp.stack([segment_ids, offsets])
    marks = by_core(take(marks.swapaxes(0, 1), c), swap_ctx(take(marks.swapaxes(0, 1), 1 - c)))
    segment, places = marks[:, 0].reshape(length), marks[:, 1].reshape(length)
    halves = lambda x: x.reshape(2, 2, share, width)
    here = t // 2 == c
    tok_block = jnp.where(here, take(take(halves(tokens), c), t % 2), take(other_tokens.reshape(2, share, width), t % 2))
    grad_block = halves(out_grad)
    grad_far = swap_ctx(take(take(grad_block, 1 - c), t % 2))
    grad_top = jnp.where(here, take(take(grad_block, c), t % 2), grad_far)

    cosine, sine = rotation_tables(places)
    bounds = key_bounds(segment)
    seg_column = segment[:, None]
    seg_row = jnp.broadcast_to(segment[None, :], (8, length))
    q, k_rows, v_rows, k_turned, q_turned, qkv_wide = project_qkv(place, qkv_pieces, per, bias_pad, tokens, other_tokens, cosine, sine, part)

    contexts, log_totals, fulls = [None] * 4, [None] * 4, [None] * 4

    def forward(j, q):
        spot = jnp.concatenate([((t ^ j) * (share // BLOCK))[None].astype(jnp.int32), bounds])
        context, log_totals[j], fulls[j] = attention_forward(spot, q, k_rows, v_rows, seg_column, seg_row, heads, share)
        contexts[j] = swap_tp(context, j) if j else context

    forward(3, q)
    q_next, log_totals[3] = lax.optimization_barrier((q, log_totals[3]))
    forward(1, q_next)
    q_next, log_totals[1], contexts[3] = lax.optimization_barrier((q, log_totals[1], contexts[3]))
    forward(2, q_next)
    q_next, log_totals[2], contexts[1] = lax.optimization_barrier((q, log_totals[2], contexts[1]))
    forward(0, q_next)
    stacked = jnp.stack(contexts)
    tok_block, log_total, full, stacked = lax.optimization_barrier(
        (tok_block, jnp.concatenate(log_totals, axis=1), jnp.concatenate(fulls), stacked)
    )

    layer_out, grad_second, grad_second_b, first_scaled, normed_t, second_t, activated, slope, root, sums_two = feed_forward(
        place, gathered, contexts, tok_block, grad_top, vec, bias_all
    )

    barrier = lax.optimization_barrier
    out_blocks = [layer_out, swap_tp(layer_out, 1), swap_tp(layer_out, 2)]

    grad_first, first_t, g0, g1, g2, g3, grad_hidden, hidden_sums, sums_one = feed_back(
        place, gathered, grad_second, grad_second_b, first_scaled, slope, root, vec, part
    )
    heads_grads = [g0, swap_tp(g1, 1), swap_tp(g2, 2), swap_tp(g3, 3)]

    *made, whole = weight_grads(place, per, normed_t, second_t, first_t, stacked, grad_hidden, activated)
    made, whole, heads_grads, out_blocks = barrier((made, whole, heads_grads, out_blocks))
    whole = lax.psum_scatter(whole.reshape(-1, 2 * hh + part), ("tp", "shard", "ctx"), scatter_dimension=0, tiled=True)
    grad_heads = heads_grads
    corner = [out_blocks[1][: share // 2], out_blocks[2][share // 2 :]]
    if direct:
        got = swap_ctx(made[1])
        grad_heads, got, corner = barrier((grad_heads, got, corner))
        packs = [made[0][k].astype(F32) + got[k].astype(F32) for k in range(4)]
        sent = [packs[k].astype(BF) for k in (1, 2, 3)]
        grad_heads, sent = barrier((grad_heads, sent))
        sent = [swap_tp(sent[k - 1], k) for k in (1, 2, 3)]
    corner = [swap_tp(corner[0], 2), swap_tp(corner[1], 1)]

    spot = jnp.concatenate([(t * (share // BLOCK))[None].astype(jnp.int32), bounds])
    grad_proj, bias_sums = attention_backward(
        spot, q, q_turned, k_rows, k_turned, v_rows, grad_heads, full, log_total, seg_column, seg_row, cosine, sine, heads
    )
    grad_proj, bias_sums, hidden_sums, sums_one, sums_two, out_blocks = barrier(
        (grad_proj, bias_sums, hidden_sums, sums_one, sums_two, out_blocks)
    )
    if direct:
        grad_proj, sent, packs[0] = barrier((grad_proj, sent, packs[0]))

    three = branch(place, (3,), (BF,), grad_proj, qkv_wide)[0]
    three, grad_proj, corner, bias_sums, out_blocks = barrier((three, grad_proj, corner, bias_sums, out_blocks))
    low, high = swap_tp(three[: share // 2], 2), swap_tp(three[share // 2 :], 1)
    one, two, own = branch(place, (1, 2, 0), (F32, F32, F32), grad_proj, qkv_wide)
    grads = qkv_weight_grads(place, per, tokens, other_tokens, grad_proj, part)
    keep_a, send_a = pick(place, out_blocks[0], out_blocks[2])
    keep_b, send_b = pick(place, out_blocks[1], *corner)
    small = collect(place, hidden_sums, sums_one, sums_two, bias_sums)
    outs = [swap_ctx(send_a), swap_ctx(send_b)]
    if direct:
        small = small + swap_ctx(small)
        small = small + swap_shard(small, 1)
    if direct:
        qkv_sum, *qkv_pieces = settle(grads[0], swap_ctx(grads[1]))
        qkv_sum, qkv_pieces, low = barrier((qkv_sum, qkv_pieces, low))
    low, high, one, two, own, outs, small = barrier((low, high, one, two, own, outs, small))

    def send_shards(pieces, small, k):
        moved = [swap_shard(pieces[j - 1], j) for j in (1, 2, 3)]
        moved[0], small = barrier((moved[0], small))
        return moved, small + swap_tp(small, k)

    one, two = relay(one, two, low, high)
    one, two, outs, small = barrier((one, two, outs, small))
    one, two = swap_tp(one, 1), swap_tp(two, 2)
    outputs = join(place, out_blocks[0], [out_blocks[2]], outs[0])
    outputs = join(place, out_blocks[1], corner, outs[1], outputs)
    if direct:
        moved, small = send_shards(qkv_pieces, small, 1)
        small = small + swap_shard(small, 2)
        qkv_total = finish(3, qkv_sum, *moved)
        summed, *pieces = settle(packs[0], *sent)
        one, two, own, small, outputs, summed, pieces, qkv_total = barrier((one, two, own, small, outputs, summed, pieces, qkv_total))
    else:
        one, two, own, small, outputs = barrier((one, two, own, small, outputs))

    block = add_block(own, grad_first, one, two)
    ready = [block, swap_tp(block, 1), swap_tp(block, 2)]
    if direct:
        moved, small = send_shards(pieces, small, 2)
        total = finish(1, summed, *moved)
        ready, total, small = barrier((ready, total, small))
    else:
        qkv_total = lax.psum_scatter(grads[0], ("shard", "ctx"), scatter_dimension=0, tiled=True).reshape(rows, 3, part)
        total = lax.psum_scatter(made[0].reshape(-1, 2 * hh), ("tp", "shard", "ctx"), scatter_dimension=0, tiled=True).astype(F32)
    corner = [swap_tp(ready[1][: share // 2], 2), swap_tp(ready[2][share // 2 :], 1)]
    _, send_a = pick(place, ready[0], ready[2])
    grad_tokens = join(place, ready[0], [ready[2]], swap_ctx(send_a))
    grad_ffn_weight, grad_out_weight = place_feed(whole, total)
    if direct:
        small, grad_tokens = barrier((small, grad_tokens))
    else:
        small = lax.psum(small, ("shard", "ctx", "tp"))
    corner, small, grad_tokens, qkv_total = barrier((corner, small, grad_tokens, qkv_total))
    send_b = jnp.where(here, jnp.concatenate(corner), ready[1])
    grad_tokens = join(place, ready[1], corner, swap_ctx(send_b), grad_tokens)

    grad_qkv_weight = qkv_total
    grad_ffn_bias = take(small, t)
    vectors = small[4:10]
    grad_qkv_bias = take(small[10:14], t).reshape(3, WIDE)[:, :part]
    return (
        outputs,
        grad_tokens,
        grad_qkv_weight,
        grad_out_weight,
        grad_ffn_weight,
        grad_qkv_bias,
        grad_ffn_bias,
        vectors[:2],
        vectors[2:],
    )


def solution(mesh):
    return jax.shard_map(
        body,
        mesh=mesh,
        in_specs=(
            P("shard", "ctx", None),
            P("shard", "ctx"),
            P("shard", "ctx"),
            P(("shard", "ctx"), None, "tp"),
            P(("shard", "ctx"), "tp"),
            P(("shard", "ctx"), None, "tp"),
            P(None, "tp"),
            P("tp"),
            P(),
            P(),
            P("shard", "ctx", None),
        ),
        out_specs=(
            P("shard", "ctx", None),
            P("shard", "ctx", None),
            P(("shard", "ctx"), None, "tp"),
            P(("shard", "ctx"), "tp"),
            P(("shard", "ctx"), None, "tp"),
            P(None, "tp"),
            P("tp"),
            P(),
            P(),
        ),
        check_vma=False,
    )
```
